32 devices in a mesh: rep: 4 (over y, core), shard: 8 (over z, x).
Axes of the slice: x: 2, y: 2, z: 4, core: 2. Of those that a mesh axis runs over, the one named last changes fastest.
Arguments:
- tokens: bfloat16 [10240, 1536], P(('rep', 'shard')), may hold values from -6 to 6
- cotangent: bfloat16 [10240, 1536], P(('rep', 'shard')), may hold values from -6 to 6
- cond: float32 [11, 1536], replicated, may hold values from -6 to 6
- seq_lengths: int32 [11], replicated, may hold values from 0 to 1178, as said below
- stream_mask: int32 [10240], P(('rep', 'shard')), may hold values from 0 to 1, as said below
- w_mod: float32 [2, 1536, 9216], P(None, 'shard', 'rep'), may hold values from -0.15625 to 0.15625
- m_mod: float32 [2, 1536, 9216], P(None, 'shard', 'rep'), may hold values from -40 to 40
- v_mod: float32 [2, 1536, 9216], P(None, 'shard', 'rep'), may hold values from 1.8432 to 29.696
- w_qkv: float32 [2, 1536, 4608], P(None, 'shard', 'rep'), may hold values from -0.15625 to 0.15625
- m_qkv: float32 [2, 1536, 4608], P(None, 'shard', 'rep'), may hold values from -48 to 48
- v_qkv: float32 [2, 1536, 4608], P(None, 'shard', 'rep'), may hold values from 2.56 to 39.936
- w_out: float32 [2, 1536, 1536], P(None, 'shard', 'rep'), may hold values from -0.75 to 0.75
- m_out: float32 [2, 1536, 1536], P(None, 'shard', 'rep'), may hold values from -14 to 14
- v_out: float32 [2, 1536, 1536], P(None, 'shard', 'rep'), may hold values from 0.2048 to 3.2768
- w_fc1: float32 [2, 1536, 6144], P(None, 'shard', 'rep'), may hold values from -0.15625 to 0.15625
- m_fc1: float32 [2, 1536, 6144], P(None, 'shard', 'rep'), may hold values from -28 to 28
- v_fc1: float32 [2, 1536, 6144], P(None, 'shard', 'rep'), may hold values from 0.8192 to 13.312
- w_fc2: float32 [2, 6144, 1536], P(None, 'shard', 'rep'), may hold values from -0.078125 to 0.078125
- m_fc2: float32 [2, 6144, 1536], P(None, 'shard', 'rep'), may hold values from -32 to 32
- v_fc2: float32 [2, 6144, 1536], P(None, 'shard', 'rep'), may hold values from 1.28 to 20.48
- gains: float32 [2, 128], replicated, may hold values from 0.5 to 1.5
- m_gains: float32 [2, 128], replicated, may hold values from -192 to 192
- v_gains: float32 [2, 128], replicated, may hold values from 46.08 to 737.28
Outputs:
- output: bfloat16 [10240, 1536], P(('rep', 'shard'))
- d_tokens: float32 [10240, 1536], P(('rep', 'shard'))
- new_w_mod: float32 [2, 1536, 9216], P(None, 'shard', 'rep')
- new_m_mod: float32 [2, 1536, 9216], P(None, 'shard', 'rep')
- new_v_mod: float32 [2, 1536, 9216], P(None, 'shard', 'rep')
- copy_w_mod: bfloat16 [2, 1536, 9216], P(None, 'shard', 'rep')
- new_w_qkv: float32 [2, 1536, 4608], P(None, 'shard', 'rep')
- new_m_qkv: float32 [2, 1536, 4608], P(None, 'shard', 'rep')
- new_v_qkv: float32 [2, 1536, 4608], P(None, 'shard', 'rep')
- copy_w_qkv: bfloat16 [2, 1536, 4608], P(None, 'shard', 'rep')
- new_w_out: float32 [2, 1536, 1536], P(None, 'shard', 'rep')
- new_m_out: float32 [2, 1536, 1536], P(None, 'shard', 'rep')
- new_v_out: float32 [2, 1536, 1536], P(None, 'shard', 'rep')
- copy_w_out: bfloat16 [2, 1536, 1536], P(None, 'shard', 'rep')
- new_w_fc1: float32 [2, 1536, 6144], P(None, 'shard', 'rep')
- new_m_fc1: float32 [2, 1536, 6144], P(None, 'shard', 'rep')
- new_v_fc1: float32 [2, 1536, 6144], P(None, 'shard', 'rep')
- copy_w_fc1: bfloat16 [2, 1536, 6144], P(None, 'shard', 'rep')
- new_w_fc2: float32 [2, 6144, 1536], P(None, 'shard', 'rep')
- new_m_fc2: float32 [2, 6144, 1536], P(None, 'shard', 'rep')
- new_v_fc2: float32 [2, 6144, 1536], P(None, 'shard', 'rep')
- copy_w_fc2: bfloat16 [2, 6144, 1536], P(None, 'shard', 'rep')
- new_gains: float32 [2, 128], replicated
- new_m_gains: float32 [2, 128], replicated
- new_v_gains: float32 [2, 128], replicated
The draws below stay inside these ranges and needn't reach their ends.
Inputs may be any that keep to these rules, and one draw needn't show every extreme that they name: `seq_lengths`: slots hold sequences in order and sum to 10240; the first is 1178; once a slot is 0 all later ones are 0; every nonzero one but the last nonzero one is at least 1024, so the 320 tokens of one device meet at most two sequences. `stream_mask`: the 320 tokens of one device hold at most min(320, 154) text tokens, all in one run, and the first device holds exactly that many.
All inputs are finite; a program needn't handle non-finite values.
Results may differ from the reference program's by a relative error of at most 0.035.
Values may be sent and summed in bfloat16 or wider, within the bound.
A program may use at most 512 MiB of HBM per device.

```python
import math
import jax
import jax.numpy as jnp
from jax import lax

D = 1536
H = 24
HD = 64
FF = 6144
TOK_DEV = 320
MAXLEN = 1178
MINLEN = 1024
TXT = 154
STEP = 7
TOKENS = 10240
SLOTS = 11
REACH = 4


def sequence_layout(layout_key):
    drawn = jax.random.randint(layout_key, (SLOTS,), MINLEN, MAXLEN + 1).astype(jnp.int32)
    drawn = drawn.at[0].set(MAXLEN)
    finish = jnp.minimum(jnp.cumsum(drawn), TOKENS).astype(jnp.int32)
    begins = jnp.concatenate([jnp.zeros((1,), jnp.int32), finish[:-1]])
    return (begins, finish)


def draw_seq_lengths(key, part):
    begins, finish = sequence_layout(jax.random.fold_in(key, 11))
    return (finish - begins).astype(jnp.int32)


def draw_stream_mask(key, part):
    begins, finish = sequence_layout(jax.random.fold_in(key, 11))
    position = jnp.arange(TOKENS, dtype=jnp.int32)
    inside = (position[:, None] >= begins[None, :]) & (position[:, None] < finish[None, :]) & (position[:, None] < begins[None, :] + TXT)
    textual = jnp.any(inside, axis=1)
    return jnp.where(textual, 0, 1).astype(jnp.int32)


def levels(own_key, extent, pieces, least, top_value):
    loudness, own = 1.0, jax.random.fold_in(own_key, 6)
    for dim, blocks in pieces:
        steps = jnp.exp(jax.random.uniform(jax.random.fold_in(own, dim), (blocks,), jnp.float32, least / len(pieces), top_value / len(pieces)))
        loudness = loudness * jnp.repeat(steps, extent[dim] // blocks).reshape([-1 if axis == dim else 1 for axis in range(len(extent))])
    return loudness


def scatter_about(rng, extent, scale, most, shards=(), held_as=jnp.bfloat16):
    result = scale * jax.random.normal(rng, extent, jnp.float32)
    if shards:
        result = result * levels(rng, extent, shards, -0.22, 0.18)
    return jnp.clip(result, -most, most).astype(held_as)


def setup_inputs(seed: int = 0) -> dict:
    arg_keys = jax.random.split(jax.random.key(seed), 24)
    tokens = scatter_about(arg_keys[0], (TOKENS, D), 1.0, 6.0, ((0, 32),))
    cotangent = scatter_about(arg_keys[1], (TOKENS, D), 1.0, 6.0, ((0, 32),))
    cond = scatter_about(arg_keys[2], (SLOTS, D), 1.0, 6.0, (), jnp.float32)
    seq_lengths = draw_seq_lengths(jax.random.fold_in(arg_keys[23], 71), 0)
    stream_mask = draw_stream_mask(jax.random.fold_in(arg_keys[23], 71), 0)
    w_mod = scatter_about(arg_keys[5], (2, D, 6 * D), D ** -0.5, 0.15625, ((1, 8), (2, 4)), jnp.float32)
    m_mod = scatter_about(arg_keys[6], (2, D, 6 * D), (0.066 * TOKENS ** 0.5), 40.0, ((1, 8), (2, 4)), jnp.float32)
    v_mod = jnp.clip(jnp.exp(math.log(29.696) - 2.779509 * jax.random.uniform(arg_keys[7], (2, D, 6 * D), jnp.float32) ** levels(arg_keys[7], (2, D, 6 * D), ((1, 8), (2, 4)), -0.2, 0.2)), 1.8432, 29.696)
    w_qkv = scatter_about(arg_keys[8], (2, D, 3 * D), D ** -0.5, 0.15625, ((1, 8), (2, 4)), jnp.float32)
    m_qkv = scatter_about(arg_keys[9], (2, D, 3 * D), (0.077 * TOKENS ** 0.5), 48.0, ((1, 8), (2, 4)), jnp.float32)
    v_qkv = jnp.clip(jnp.exp(math.log(39.936) - 2.747271 * jax.random.uniform(arg_keys[10], (2, D, 3 * D), jnp.float32) ** levels(arg_keys[10], (2, D, 3 * D), ((1, 8), (2, 4)), -0.2, 0.2)), 2.56, 39.936)
    w_out = scatter_about(arg_keys[11], (2, D, D), HD ** -0.5, 0.75, ((1, 8), (2, 4)), jnp.float32)
    m_out = scatter_about(arg_keys[12], (2, D, D), (0.022 * TOKENS ** 0.5), 14.0, ((1, 8), (2, 4)), jnp.float32)
    v_out = jnp.clip(jnp.exp(math.log(3.2768) - 2.7725887 * jax.random.uniform(arg_keys[13], (2, D, D), jnp.float32) ** levels(arg_keys[13], (2, D, D), ((1, 8), (2, 4)), -0.2, 0.2)), 0.2048, 3.2768)
    w_fc1 = scatter_about(arg_keys[14], (2, D, FF), D ** -0.5, 0.15625, ((1, 8), (2, 4)), jnp.float32)
    m_fc1 = scatter_about(arg_keys[15], (2, D, FF), (0.044 * TOKENS ** 0.5), 28.0, ((1, 8), (2, 4)), jnp.float32)
    v_fc1 = jnp.clip(jnp.exp(math.log(13.312) - 2.78809295 * jax.random.uniform(arg_keys[16], (2, D, FF), jnp.float32) ** levels(arg_keys[16], (2, D, FF), ((1, 8), (2, 4)), -0.2, 0.2)), 0.8192, 13.312)
    w_fc2 = scatter_about(arg_keys[17], (2, FF, D), FF ** -0.5, 0.078125, ((1, 8), (2, 4)), jnp.float32)
    m_fc2 = scatter_about(arg_keys[18], (2, FF, D), (0.055 * TOKENS ** 0.5), 32.0, ((1, 8), (2, 4)), jnp.float32)
    v_fc2 = jnp.clip(jnp.exp(math.log(20.48) - 2.7725887 * jax.random.uniform(arg_keys[19], (2, FF, D), jnp.float32) ** levels(arg_keys[19], (2, FF, D), ((1, 8), (2, 4)), -0.2, 0.2)), 1.28, 20.48)
    gains = jnp.clip(jax.random.uniform(arg_keys[20], (2, 2 * HD), jnp.float32, 0.5, 1.5), 0.5, 1.5)
    m_gains = scatter_about(arg_keys[21], (2, 2 * HD), (0.33 * TOKENS ** 0.5), 192.0, (), jnp.float32)
    v_gains = jnp.clip(jnp.exp(jax.random.uniform(arg_keys[22], (2, 2 * HD), jnp.float32, math.log(46.08), math.log(737.28))), 46.08, 737.28)
    return {"tokens": tokens, "cotangent": cotangent, "cond": cond, "seq_lengths": seq_lengths, "stream_mask": stream_mask, "w_mod": w_mod, "m_mod": m_mod, "v_mod": v_mod, "w_qkv": w_qkv, "m_qkv": m_qkv, "v_qkv": v_qkv, "w_out": w_out, "m_out": m_out, "v_out": v_out, "w_fc1": w_fc1, "m_fc1": m_fc1, "v_fc1": v_fc1, "w_fc2": w_fc2, "m_fc2": m_fc2, "v_fc2": v_fc2, "gains": gains, "m_gains": m_gains, "v_gains": v_gains}


@jax.custom_vjp
def low(v):
    return lax.optimization_barrier(v.astype(jnp.bfloat16)).astype(jnp.float32)

@jax.custom_vjp
def low_back(v):
    return v

def low_keep(v):
    return (low(v), None)

def low_pass(kept, grad):
    return (grad,)

def back_keep(v):
    return (v, None)

def back_low(kept, grad):
    return (low(grad),)
low.defvjp(low_keep, low_pass)
low_back.defvjp(back_keep, back_low)
norm_eps = 1e-06
adam_eps = 1e-08
score_scale = 0.125
masked_score = -1e+30
rate_mod = 0.03
rate_qkv = 0.03
rate_out = 0.15
rate_fc1 = 0.03
rate_fc2 = 0.015
rate_gains = 1.0

def layer_modulate(values, shift, scale):
    centred = values - lax.optimization_barrier(jnp.mean(values, axis=-1, keepdims=True))
    normed = centred * lax.rsqrt(lax.optimization_barrier(jnp.mean(centred * centred, axis=-1, keepdims=True)) + norm_eps)
    return normed * (1.0 + scale) + shift

def head_norm(values, gain):
    return values * lax.rsqrt(lax.optimization_barrier(jnp.mean(values * values, axis=-1, keepdims=True)) + norm_eps) * gain

def query_key_norm(query_pre, key_pre, gain_tok):
    half_width = gain_tok.shape[1] // 2
    return (head_norm(query_pre, gain_tok[:, None, :half_width]), head_norm(key_pre, gain_tok[:, None, half_width:]))

def adam_step(weight, moment_one, moment_two, grads, rate):
    new_one = 0.9 * moment_one + 0.1 * grads
    new_two = 0.999 * moment_two + 0.001 * grads * grads
    fixed_one = new_one / (1.0 - 0.9 ** STEP)
    fixed_two = new_two / (1.0 - 0.999 ** STEP)
    new_weight = weight - rate * (fixed_one / (jnp.sqrt(fixed_two) + adam_eps) + 0.01 * weight)
    return (new_weight, new_one, new_two, new_weight.astype(jnp.bfloat16))

def split_product(acts, weight, image_col):
    image_out = jnp.dot(acts, weight[0], precision=lax.Precision.HIGHEST, preferred_element_type=jnp.float32)
    text_out = jnp.dot(acts, weight[1], precision=lax.Precision.HIGHEST, preferred_element_type=jnp.float32)
    return jnp.where(image_col, image_out, text_out)

def attention_block(query_block, key_window, value_window, query_ids, key_ids):
    scores = jnp.einsum('qhd,khd->hqk', query_block, key_window, precision=lax.Precision.HIGHEST) * score_scale
    scores = low_back(scores)
    scores = jnp.where((query_ids[:, None] == key_ids[None, :])[None], scores, masked_score)
    probs = low(jax.nn.softmax(scores, axis=-1))
    return jnp.einsum('hqk,khd->qhd', probs, value_window, precision=lax.Precision.HIGHEST)

def reference(tokens, cotangent, cond, seq_lengths, stream_mask, w_mod, m_mod, v_mod, w_qkv, m_qkv, v_qkv, w_out, m_out, v_out, w_fc1, m_fc1, v_fc1, w_fc2, m_fc2, v_fc2, gains, m_gains, v_gains):
    stream_in = tokens.astype(jnp.float32)
    back_out = cotangent.astype(jnp.float32)
    seq_starts = jnp.cumsum(seq_lengths) - seq_lengths
    positions = jnp.arange(TOKENS, dtype=jnp.int32)
    seq_ids = (lax.optimization_barrier(jnp.sum((seq_starts[None, :] <= positions[:, None]).astype(jnp.int32), axis=1)) - 1).astype(jnp.int32)
    image_col = (stream_mask == 1)[:, None]
    silu_cond = low(jax.nn.silu(cond))
    pad_len = REACH * TOK_DEV
    window_len = (2 * REACH + 1) * TOK_DEV
    block_count = TOKENS // TOK_DEV
    key_ids = jnp.pad(seq_ids, (pad_len, pad_len), constant_values=-1)
    checked = jax.checkpoint(attention_block)

    def forward(block_in, params):
        weight_mod, weight_qkv, weight_out, weight_fc1, weight_fc2, gain_pair = params
        mods = low(jnp.einsum('sd,tde->ste', silu_cond, low(weight_mod), precision=lax.Precision.HIGHEST))
        picks = jnp.where(image_col, mods[seq_ids, 0], mods[seq_ids, 1])
        shift_one, scale_one, gate_one, shift_two, scale_two, gate_two = jnp.split(picks, 6, axis=1)
        act_one = low(layer_modulate(block_in, shift_one, scale_one))
        qkv_pre = low_back(split_product(act_one, low(weight_qkv), image_col))
        query_pre = qkv_pre[:, :D].reshape(TOKENS, H, HD)
        key_pre = qkv_pre[:, D:2 * D].reshape(TOKENS, H, HD)
        value_pre = qkv_pre[:, 2 * D:].reshape(TOKENS, H, HD)
        gain_tok = jnp.where(image_col, gain_pair[0][None], gain_pair[1][None])
        query_f, key_f = query_key_norm(query_pre, key_pre, gain_tok)
        query_f = low(query_f)
        key_f = low(key_f)
        value_f = low(value_pre)
        key_pad = jnp.pad(key_f, ((pad_len, pad_len), (0, 0), (0, 0)))
        value_pad = jnp.pad(value_f, ((pad_len, pad_len), (0, 0), (0, 0)))

        def one_block(block_index):
            start_row = block_index * TOK_DEV
            return checked(lax.dynamic_slice_in_dim(query_f, start_row, TOK_DEV, 0), lax.dynamic_slice_in_dim(key_pad, start_row, window_len, 0), lax.dynamic_slice_in_dim(value_pad, start_row, window_len, 0), lax.dynamic_slice_in_dim(seq_ids, start_row, TOK_DEV, 0), lax.dynamic_slice_in_dim(key_ids, start_row, window_len, 0))
        attended = lax.map(one_block, jnp.arange(block_count, dtype=jnp.int32)).reshape(TOKENS, D)
        attended = low_back(low(attended))
        branch = low_back(split_product(attended, low(weight_out), image_col))
        mid = block_in + gate_one * branch
        act_two = low(layer_modulate(mid, shift_two, scale_two))
        up_proj = low_back(split_product(act_two, low(weight_fc1), image_col))
        gelu_act = low(jax.nn.gelu(up_proj, approximate=True))
        down_proj = low_back(split_product(gelu_act, low(weight_fc2), image_col))
        return mid + gate_two * down_proj
    output, pull = jax.vjp(forward, stream_in, (w_mod, w_qkv, w_out, w_fc1, w_fc2, gains))
    d_tokens, grads = pull(back_out)
    g_mod, g_qkv, g_out, g_fc1, g_fc2, g_gains = grads
    up_mod = adam_step(w_mod, m_mod, v_mod, g_mod, rate_mod)
    up_qkv = adam_step(w_qkv, m_qkv, v_qkv, g_qkv, rate_qkv)
    up_out = adam_step(w_out, m_out, v_out, g_out, rate_out)
    up_fc1 = adam_step(w_fc1, m_fc1, v_fc1, g_fc1, rate_fc1)
    up_fc2 = adam_step(w_fc2, m_fc2, v_fc2, g_fc2, rate_fc2)
    up_gains = adam_step(gains, m_gains, v_gains, g_gains, rate_gains)
    return (output.astype(jnp.bfloat16), d_tokens, up_mod[0], up_mod[1], up_mod[2], up_mod[3], up_qkv[0], up_qkv[1], up_qkv[2], up_qkv[3], up_out[0], up_out[1], up_out[2], up_out[3], up_fc1[0], up_fc1[1], up_fc1[2], up_fc1[3], up_fc2[0], up_fc2[1], up_fc2[2], up_fc2[3], up_gains[0], up_gains[1], up_gains[2])
```

```python
import functools

import jax
import jax.numpy as jnp
from jax import lax
from jax.experimental import pallas as pl
from jax.experimental.pallas import tpu as pltpu
from jax.sharding import PartitionSpec as P

HD = 64
MAXLEN = 1178
STEP = 7

norm_eps = 1e-06
adam_eps = 1e-08
score_scale = 0.125
rate_mod = 0.03
rate_qkv = 0.03
rate_out = 0.15
rate_fc1 = 0.03
rate_fc2 = 0.015
rate_gains = 1.0

bf16 = jnp.bfloat16
f32 = jnp.float32
QB = 256
KB = 256
TXT = 154
WINDOW = (TXT + 15 + 15) // 16 * 16
COLS = 512
GELU_A = 0.7978845608028654
GELU_B = 0.044715
NN = (((1,), (0,)), ((), ()))
NT = (((1,), (1,)), ((), ()))
TN = (((0,), (0,)), ((), ()))


def layer_modulate(values, shift, scale):
    centred = values - jnp.mean(values, axis=-1, keepdims=True)
    normed = centred * lax.rsqrt(jnp.mean(centred * centred, axis=-1, keepdims=True) + norm_eps)
    return normed * (1.0 + scale) + shift


def adam_step(weight, moment_one, moment_two, grads, rate):
    new_one = 0.9 * moment_one + 0.1 * grads
    new_two = 0.999 * moment_two + 0.001 * grads * grads
    fixed_one = new_one / (1.0 - 0.9**STEP)
    fixed_two = new_two / (1.0 - 0.999**STEP)
    new_weight = weight - rate * (fixed_one / (jnp.sqrt(fixed_two) + adam_eps) + 0.01 * weight)
    return (new_weight, new_one, new_two, new_weight.astype(bf16))


def segment_index(position, seq_starts, all_tokens):
    counted = jnp.sum((seq_starts[None, :] <= position[:, None]).astype(jnp.int32), axis=1) - 1
    inside = (position >= 0) & (position < all_tokens)
    return jnp.where(inside, counted, -1)


def fill_window(own_ref, before_ref, after_ref, keys, values):
    halo, own = before_ref.shape[0], own_ref.shape[0]
    heads = keys.shape[0]
    width = heads * HD
    parts = ((before_ref, 0, 0, halo), (own_ref, width, halo, own), (after_ref, 0, halo + own, halo))
    for source, skip, first, count in parts:
        for head in range(heads):
            for index, dest in ((0, keys), (1, values)):
                start = skip + index * width + head * HD
                dest[head, first : first + count, :HD] = source[:, start : start + HD]


def attend_kernel(
    lo_ref, hi_ref, own_ref, before_ref, after_ref, qid_ref, kid_ref, o_ref, l_ref, keys, values, acc
):
    step = pl.program_id(0)
    heads = keys.shape[0]

    @pl.when(step == 0)
    def _():
        lane = lax.broadcasted_iota(jnp.int32, values.shape[1:], 1)
        for head in range(heads):
            values[head] = (lane == HD).astype(bf16)
        fill_window(own_ref, before_ref, after_ref, keys, values)

    qid = qid_ref[...]
    diagonal = lax.broadcasted_iota(jnp.int32, (QB, QB), 0) == lax.broadcasted_iota(
        jnp.int32, (QB, QB), 1
    )
    own_rows = pl.ds(pl.multiple_of(step * QB, QB), QB)
    queries = [own_ref[own_rows, head * HD : (head + 1) * HD] for head in range(heads)]
    acc[...] = jnp.zeros_like(acc)

    @pl.loop(lo_ref[step], hi_ref[step])
    def _(block):
        rows = pl.ds(pl.multiple_of(block * KB, KB), KB)
        same = qid == kid_ref[pl.ds(block, 1), :]
        for head in range(heads):
            scores = lax.dot_general(
                queries[head], keys[head, rows, :], NT, preferred_element_type=f32
            )
            lifted = jnp.where(same, jnp.exp(scores), 0.0).astype(bf16)
            acc[head] += jnp.dot(lifted, values[head, rows, :], preferred_element_type=f32)

    for head in range(heads):
        total = acc[head, :, HD : HD + 1]
        o_ref[:, head * HD : (head + 1) * HD] = (acc[head, :, :HD] / total).astype(bf16)
        l_ref[0, head : head + 1, :] = jnp.sum(
            jnp.where(diagonal, jnp.log(total), 0.0), axis=0, keepdims=True
        )


def attend_back_kernel(
    lo_ref,
    hi_ref,
    own_ref,
    before_ref,
    after_ref,
    do_ref,
    o_ref,
    qid_ref,
    kid_ref,
    l_ref,
    dq_ref,
    d_before_ref,
    d_after_ref,
    d_own_ref,
    keys,
    values,
    d_keys,
    d_values,
    d_query,
):
    step = pl.program_id(0)
    heads = keys.shape[0]
    width = heads * HD

    @pl.when(step == 0)
    def _():
        fill_window(own_ref, before_ref, after_ref, keys, values)
        d_keys[...] = jnp.zeros_like(d_keys)
        d_values[...] = jnp.zeros_like(d_values)

    qid = qid_ref[0]
    ones = jnp.ones((8, HD), bf16)
    own_rows = pl.ds(pl.multiple_of(step * QB, QB), QB)
    queries, outs, dots = [], [], []
    for head in range(heads):
        lanes = slice(head * HD, (head + 1) * HD)
        queries.append(own_ref[own_rows, lanes])
        outs.append(do_ref[:, lanes])
        product = outs[head].astype(f32) * o_ref[:, lanes].astype(f32)
        coarse = product.astype(bf16)
        fine = (product - coarse.astype(f32)).astype(bf16)
        total = lax.dot_general(ones, coarse, NT, preferred_element_type=f32)
        dots.append((total + lax.dot_general(ones, fine, NT, preferred_element_type=f32))[:1])
    d_query[...] = jnp.zeros_like(d_query)

    @pl.loop(lo_ref[step], hi_ref[step])
    def _(block):
        rows = pl.ds(pl.multiple_of(block * KB, KB), KB)
        same = kid_ref[rows, :] == qid
        for head in range(heads):
            key = keys[head, rows, :]
            scores = lax.dot_general(key, queries[head], NT, preferred_element_type=f32)
            probs = jnp.where(same, jnp.exp(scores - l_ref[0, head : head + 1, :]), 0.0)
            d_values[head, rows, :] += jnp.dot(
                probs.astype(bf16), outs[head], preferred_element_type=f32
            )
            d_probs = lax.dot_general(
                values[head, rows, :], outs[head], NT, preferred_element_type=f32
            )
            d_scores = (probs * (d_probs - dots[head])).astype(bf16)
            d_keys[head, rows, :] += jnp.dot(d_scores, queries[head], preferred_element_type=f32)
            d_query[head] += lax.dot_general(d_scores, key, TN, preferred_element_type=f32)

    for head in range(heads):
        dq_ref[:, head * HD : (head + 1) * HD] = (d_query[head] * score_scale).astype(bf16)

    @pl.when(step == pl.num_programs(0) - 1)
    def _():
        halo, own = d_before_ref.shape[0], d_own_ref.shape[0]
        for index, source in ((0, d_keys), (1, d_values)):
            for head in range(heads):
                span = slice(index * width + head * HD, index * width + (head + 1) * HD)
                d_before_ref[:, span] = source[head, :halo, :].astype(bf16)
                d_own_ref[:, span] = source[head, halo : halo + own, :]
                d_after_ref[:, span] = source[head, halo + own :, :].astype(bf16)


def resident(shape):
    return pl.BlockSpec(shape, lambda *index: (0,) * len(shape))


def attention(own, before, after, lo, hi, qid, kid):
    count, width = own.shape[0], own.shape[1] // 3
    heads = width // HD
    window = count + 2 * before.shape[0]
    steps = count // QB
    return pl.pallas_call(
        attend_kernel,
        grid_spec=pltpu.PrefetchScalarGridSpec(
            num_scalar_prefetch=2,
            grid=(steps,),
            in_specs=[
                resident(own.shape),
                resident(before.shape),
                resident(after.shape),
                pl.BlockSpec((QB, 1), lambda i, lo, hi: (i, 0)),
                resident((window // KB, KB)),
            ],
            out_specs=[
                pl.BlockSpec((QB, width), lambda i, lo, hi: (i, 0)),
                pl.BlockSpec((1, 8, QB), lambda i, lo, hi: (i, 0, 0)),
            ],
            scratch_shapes=[
                pltpu.VMEM((heads, window, HD), bf16),
                pltpu.VMEM((heads, window, 2 * HD), bf16),
                pltpu.VMEM((heads, QB, 2 * HD), f32),
            ],
        ),
        out_shape=[
            jax.ShapeDtypeStruct((count, width), bf16),
            jax.ShapeDtypeStruct((steps, 8, QB), f32),
        ],
        compiler_params=pltpu.CompilerParams(vmem_limit_bytes=40 << 20),
        cost_estimate=pl.CostEstimate(flops=40 << 30, bytes_accessed=8 << 20, transcendentals=12 << 20),
        name="attend",
    )(lo, hi, own, before, after, qid[:, None], kid.reshape(window // KB, KB))


def attention_back(own, before, after, d_out, out, lo, hi, qid, kid, logsum):
    count, width = own.shape[0], own.shape[1] // 3
    heads = width // HD
    halo = before.shape[0]
    window = count + 2 * halo
    steps = count // QB
    rows = pl.BlockSpec((QB, width), lambda i, lo, hi: (i, 0))
    return pl.pallas_call(
        attend_back_kernel,
        grid_spec=pltpu.PrefetchScalarGridSpec(
            num_scalar_prefetch=2,
            grid=(steps,),
            in_specs=[
                resident(own.shape),
                resident(before.shape),
                resident(after.shape),
                rows,
                rows,
                pl.BlockSpec((1, 1, QB), lambda i, lo, hi: (i, 0, 0)),
                resident((window, 1)),
                pl.BlockSpec((1, 8, QB), lambda i, lo, hi: (i, 0, 0)),
            ],
            out_specs=[
                rows,
                resident((halo, 2 * width)),
                resident((halo, 2 * width)),
                resident((count, 2 * width)),
            ],
            scratch_shapes=[pltpu.VMEM((heads, window, HD), bf16)] * 2
            + [pltpu.VMEM((heads, window, HD), f32)] * 2
            + [pltpu.VMEM((heads, QB, HD), f32)],
        ),
        out_shape=[
            jax.ShapeDtypeStruct((count, width), bf16),
            jax.ShapeDtypeStruct((halo, 2 * width), bf16),
            jax.ShapeDtypeStruct((halo, 2 * width), bf16),
            jax.ShapeDtypeStruct((count, 2 * width), f32),
        ],
        compiler_params=pltpu.CompilerParams(vmem_limit_bytes=58 << 20),
        cost_estimate=pl.CostEstimate(flops=90 << 30, bytes_accessed=24 << 20, transcendentals=12 << 20),
        name="attend_back",
    )(lo, hi, own, before, after, d_out, out, qid.reshape(steps, 1, QB), kid[:, None], logsum)


def text_windows(spots, blocks, count, work):
    for p in range(blocks):

        @pl.when(spots[blocks + p] == 1)
        def _(p=p):
            first = pl.multiple_of(spots[p], 16)
            base = p * (count // blocks)
            work(p, first, pl.ds(pl.multiple_of(base + first, 16), WINDOW))


def flat(value):
    return value.reshape(-1, value.shape[-1])


def product(x_ref, rows, weight, dims):
    total = None
    for cols, get in weight:
        term = lax.dot_general(x_ref[rows, cols], get(), dims, preferred_element_type=f32)
        total = term if total is None else total + term
    return total


def group_sums(values, blocks_of):
    coarse = values.astype(bf16)
    fine = (values - coarse.astype(f32)).astype(bf16)
    return jnp.dot(coarse, blocks_of, preferred_element_type=f32) + jnp.dot(
        fine, blocks_of, preferred_element_type=f32
    )


def head_blocks(width):
    row = lax.broadcasted_iota(jnp.int32, (width, width), 0) // HD
    col = lax.broadcasted_iota(jnp.int32, (width, width), 1) // HD
    return (row == col).astype(bf16)


def qkv_kernel(blocks, spots, x_ref, w0, w1, image_ref, gain_ref, packed_ref, pre_ref):
    kind = pl.program_id(0)
    every = slice(None)
    size, width = packed_ref.shape[1], packed_ref.shape[2] // 3
    rep = spots[2 * blocks]
    spread = head_blocks(2 * width)

    def finish(t, values, gain):
        if t < 2:
            mean = group_sums(values * values, spread) * (1.0 / HD)
            values = values * lax.rsqrt(mean + norm_eps) * gain
        values = values.astype(bf16)
        return values * jnp.asarray(score_scale, bf16) if t == 0 else values

    for t in range(3):

        @pl.when(kind == t)
        def _(t=t):
            @pl.loop(0, blocks)
            def _(p):
                rows = pl.ds(pl.multiple_of(p * size, size), size)
                values = product(x_ref, rows, [(every, lambda: flat(w0[...]))], NN)
                if t < 2:
                    pre_ref[rows, :] = values
                values = finish(t, values, gain_ref[0, :1])
                for g in range(2):
                    packed_ref[pl.ds((rep ^ p) * 2 + g, 1), :, t * width : (t + 1) * width] = values[
                        :, g * width : (g + 1) * width
                    ][None]

            def text(p, first, rows):
                values = product(x_ref, rows, [(every, lambda: flat(w1[...]))], NN)
                image = image_ref[rows, :] == 1
                if t < 2:
                    pre_ref[rows, :] = jnp.where(image, pre_ref[rows, :], values)
                values = finish(t, values, gain_ref[0, 1:])
                for g in range(2):
                    place = (
                        pl.ds((rep ^ p) * 2 + g, 1),
                        pl.ds(first, WINDOW),
                        slice(t * width, (t + 1) * width),
                    )
                    packed_ref[place] = jnp.where(
                        image[None], packed_ref[place], values[:, g * width : (g + 1) * width][None]
                    )

            text_windows(spots, blocks, x_ref.shape[0], text)


def column_weights(weight, tile):
    shards, _, rows, _ = weight.shape
    return [
        pl.BlockSpec((shards, 1, rows, tile), lambda j, s, stream=stream: (0, stream, 0, j))
        for stream in range(2)
    ]


def tiled_gains(gains, heads):
    return jnp.stack([jnp.tile(gains[:, :HD], (1, heads)), jnp.tile(gains[:, HD:], (1, heads))])


def qkv_product(spots, x, weight, image, gains):
    count, depth = x.shape
    blocks = (spots.shape[0] - 1) // 2
    part = weight.shape[3] // 3
    size = count // blocks
    return pl.pallas_call(
        functools.partial(qkv_kernel, blocks),
        grid_spec=pltpu.PrefetchScalarGridSpec(
            num_scalar_prefetch=1,
            grid=(3,),
            in_specs=[
                resident(x.shape),
                *column_weights(weight, part),
                resident(image.shape),
                pl.BlockSpec((1, 2, part), lambda j, s: (jnp.minimum(j, 1), 0, 0)),
            ],
            out_specs=[
                resident((2 * blocks, size, 3 * part // 2)),
                pl.BlockSpec((count, part), lambda j, s: (0, jnp.minimum(j, 1))),
            ],
        ),
        out_shape=[
            jax.ShapeDtypeStruct((2 * blocks, size, 3 * part // 2), bf16),
            jax.ShapeDtypeStruct((count, 2 * part), f32),
        ],
        compiler_params=pltpu.CompilerParams(vmem_limit_bytes=40 << 20),
        cost_estimate=pl.CostEstimate(flops=7 << 30, bytes_accessed=20 << 20, transcendentals=0),
        name="qkv_product",
    )(spots, x, weight, weight, image, tiled_gains(gains, part // HD))


def norm_back_kernel(blocks, spots, came_ref, pre_ref, image_ref, gain_ref, out_ref, sum_ref, both):
    @pl.when(pl.program_id(0) == 0)
    def _():
        sum_ref[...] = jnp.zeros_like(sum_ref)

    part = both.shape[1]
    width = part // 2
    image = image_ref[...] == 1
    spread = head_blocks(part)
    for t in range(3):
        for g in range(2):
            both[:, g * width : (g + 1) * width] = came_ref[g, :, t * width : (t + 1) * width].astype(
                f32
            )
        grad = both[...]
        if t < 2:
            pre = pre_ref[:, t * part : (t + 1) * part]
            scale = lax.rsqrt(group_sums(pre * pre, spread) * (1.0 / HD) + norm_eps)
            gain = jnp.where(image, gain_ref[t, :1], gain_ref[t, 1:])
            each = grad * pre * scale
            total = jnp.sum(each, axis=0, keepdims=True)
            text = jnp.sum(jnp.where(image, 0.0, each), axis=0, keepdims=True)
            sum_ref[2 * t : 2 * t + 1, :] += total - text
            sum_ref[2 * t + 1 : 2 * t + 2, :] += text
            grad = grad * gain
            mean = group_sums(grad * pre, spread) * (1.0 / HD)
            grad = scale * (grad - pre * (scale * scale * mean))
        out_ref[:, t * part : (t + 1) * part] = grad.astype(bf16)


def norm_back(spots, came, pre, image, gains):
    blocks = (spots.shape[0] - 1) // 2
    _, size, width3 = came.shape
    part = 2 * width3 // 3
    tiled = tiled_gains(gains, part // HD)
    return pl.pallas_call(
        functools.partial(norm_back_kernel, blocks),
        grid_spec=pltpu.PrefetchScalarGridSpec(
            num_scalar_prefetch=1,
            grid=(blocks,),
            in_specs=[
                pl.BlockSpec((2, size, width3), lambda p, s: (s[2 * blocks] ^ p, 0, 0)),
                pl.BlockSpec((size, 2 * part), lambda p, s: (p, 0)),
                pl.BlockSpec((size, 1), lambda p, s: (p, 0)),
                resident(tiled.shape),
            ],
            out_specs=[
                pl.BlockSpec((size, 3 * part), lambda p, s: (p, 0)),
                resident((4, part)),
            ],
            scratch_shapes=[pltpu.VMEM((size, part), f32)],
        ),
        out_shape=[
            jax.ShapeDtypeStruct((blocks * size, 3 * part), bf16),
            jax.ShapeDtypeStruct((4, part), f32),
        ],
        compiler_params=pltpu.CompilerParams(vmem_limit_bytes=32 << 20),
        cost_estimate=pl.CostEstimate(flops=4 << 30, bytes_accessed=12 << 20, transcendentals=0),
        name="norm_back",
    )(spots, came, pre, image, tiled)


def forward_kernel(blocks, gathers, gelu, spots, x_ref, w0, w1, image_ref, *rest):
    rep = spots[2 * blocks]
    out_ref = rest[0]
    if gathers:
        x_out = rest[1]
        size, width = x_ref.shape[1:]

        @pl.when(pl.program_id(0) == 0)
        def _():
            for p in range(blocks):
                for g in range(2):
                    x_out[p * size : (p + 1) * size, g * width : (g + 1) * width] = x_ref[
                        pl.ds((rep ^ p) * 2 + g, 1)
                    ][0]

        x_ref = x_out
    every = slice(None)
    count = x_ref.shape[0]

    def finish(values):
        if not gelu:
            return (values.astype(bf16),)
        square = values * values
        bend = jnp.tanh(values * (GELU_A + GELU_A * GELU_B * square))
        half = 0.5 * (1.0 + bend)
        slope = half + 0.5 * values * (1.0 - bend * bend) * (GELU_A + 3.0 * GELU_A * GELU_B * square)
        return (values * half).astype(bf16), slope.astype(bf16)

    outs = rest if gelu else (out_ref,)
    chunk = count // (blocks if gelu else 2)

    @pl.loop(0, count // chunk)
    def _(p):
        rows = pl.ds(pl.multiple_of(p * chunk, chunk), chunk)
        values = product(x_ref, rows, [(every, lambda: flat(w0[...]))], NN)
        for out, value in zip(outs, finish(values)):
            out[rows, :] = value

    def text(p, first, rows):
        values = product(x_ref, rows, [(every, lambda: flat(w1[...]))], NN)
        image = image_ref[rows, :] == 1
        for out, value in zip(outs, finish(values)):
            out[rows, :] = jnp.where(image, out[rows, :], value)

    text_windows(spots, blocks, count, text)


def forward_product(spots, x, weight, image, gathers=False, gelu=False):
    blocks = (spots.shape[0] - 1) // 2
    if weight.ndim == 5:
        tiles, q, _, rows, tile = weight.shape
        weights = [
            pl.BlockSpec((1, q, 1, rows, tile), lambda j, s, stream=stream: (j, 0, stream, 0, 0))
            for stream in range(2)
        ]
        depth = q * rows
    else:
        depth, tile = weight.shape[0] * weight.shape[2], COLS
        tiles = weight.shape[3] // tile
        weights = column_weights(weight, tile)
    count = image.shape[0]
    column = pl.BlockSpec((count, tile), lambda j, s: (0, j))
    whole = jax.ShapeDtypeStruct((count, tiles * tile), bf16)
    out_specs, out_shape = [column], [whole]
    if gathers:
        out_specs.append(resident((count, depth)))
        out_shape.append(jax.ShapeDtypeStruct((count, depth), bf16))
    if gelu:
        out_specs.append(column)
        out_shape.append(whole)
    return pl.pallas_call(
        functools.partial(forward_kernel, blocks, gathers, gelu),
        grid_spec=pltpu.PrefetchScalarGridSpec(
            num_scalar_prefetch=1,
            grid=(tiles,),
            in_specs=[resident(x.shape), *weights, resident(image.shape)],
            out_specs=out_specs,
        ),
        out_shape=out_shape,
        compiler_params=pltpu.CompilerParams(vmem_limit_bytes=40 << 20),
        cost_estimate=pl.CostEstimate(
            flops=3 * count * depth * tiles * tile, bytes_accessed=20 << 20, transcendentals=0
        ),
        name="forward_product",
    )(spots, x, weight, weight, image)


def backward_kernel(blocks, turned, scaled, packs, spots, dy_ref, w0, w1, image_ref, *rest):
    rest = list(rest)
    factor_ref = rest.pop(0) if scaled else None
    out_ref = rest[0]
    if turned:
        tiles, tile = w0.shape[0], w0.shape[4]
        weights = [
            [
                (slice(n * tile, (n + 1) * tile), lambda w=w, n=n: flat(w[n, :, 0]))
                for n in range(tiles)
            ]
            for w in (w0, w1)
        ]
    else:
        every = slice(None)
        weights = [[(every, lambda w=w: flat(w[...]))] for w in (w0, w1)]
    count = dy_ref.shape[0]
    size = count // blocks
    rep = spots[2 * blocks]
    part = pl.program_id(0)

    def finish(rows, values):
        if scaled:
            values = values * factor_ref[rows, :].astype(f32)
        return values.astype(bf16)

    chunk = size if packs or scaled else count // 2

    @pl.loop(0, count // chunk)
    def _(p):
        rows = pl.ds(pl.multiple_of(p * chunk, chunk), chunk)
        values = finish(rows, product(dy_ref, rows, weights[0], NT))
        if packs:
            out_ref[pl.ds((rep ^ p) * 2 + part, 1)] = values[None]
        else:
            out_ref[rows, :] = values

    def text(p, first, rows):
        values = finish(rows, product(dy_ref, rows, weights[1], NT))
        image = image_ref[rows, :] == 1
        if packs:
            place = (pl.ds((rep ^ p) * 2 + part, 1), pl.ds(first, WINDOW), slice(None))
            out_ref[place] = jnp.where(image[None], out_ref[place], values[None])
        else:
            out_ref[rows, :] = jnp.where(image, out_ref[rows, :], values)

    text_windows(spots, blocks, count, text)


def backward_product(spots, dy, weight, image, factor=None, packs=False):
    blocks = (spots.shape[0] - 1) // 2
    turned = weight.ndim == 5
    count = image.shape[0]
    if turned:
        tiles, q, _, rows, tile = weight.shape
        step = q * rows // 2 if packs else min(q * rows, 768)
        grid = (q * rows // step,)
        if rows < step:
            block = (tiles, step // rows, 1, rows, tile)
            weights = [
                pl.BlockSpec(block, lambda j, s, stream=stream: (0, j, stream, 0, 0))
                for stream in range(2)
            ]
        else:
            per = rows // step
            weights = [
                pl.BlockSpec(
                    (tiles, 1, 1, step, tile),
                    lambda j, s, stream=stream: (0, j // per, stream, j % per, 0),
                )
                for stream in range(2)
            ]
        depth = q * rows
    else:
        shards, _, rows, width = weight.shape
        depth = shards * rows
        bunch = max(1, 768 // rows)
        step = bunch * rows
        grid = (depth // step,)
        weights = [
            pl.BlockSpec((bunch, 1, rows, width), lambda j, s, stream=stream: (j, stream, 0, 0))
            for stream in range(2)
        ]
    column = pl.BlockSpec((count, step), lambda j, s: (0, j))
    in_specs = [resident(dy.shape), *weights, resident(image.shape)]
    operands = [spots, dy, weight, weight, image]
    if factor is not None:
        in_specs.append(column)
        operands.append(factor)
    if packs:
        shape = (2 * blocks, count // blocks, step)
        out_spec, out_shape = resident(shape), jax.ShapeDtypeStruct(shape, bf16)
    else:
        out_spec, out_shape = column, jax.ShapeDtypeStruct((count, depth), bf16)
    return pl.pallas_call(
        functools.partial(backward_kernel, blocks, turned, factor is not None, packs),
        grid_spec=pltpu.PrefetchScalarGridSpec(
            num_scalar_prefetch=1,
            grid=grid,
            in_specs=in_specs,
            out_specs=out_spec,
        ),
        out_shape=out_shape,
        compiler_params=pltpu.CompilerParams(vmem_limit_bytes=48 << 20),
        cost_estimate=pl.CostEstimate(
            flops=3 * count * depth * dy.shape[1], bytes_accessed=20 << 20, transcendentals=0
        ),
        name="backward_product",
    )(*operands)


def gradient_kernel(blocks, spots, x_ref, dy_ref, image_ref, out, turned_x, masked, acc):
    count, width = dy_ref.shape
    size = count // blocks
    cols_at_once = acc.shape[1]

    @pl.when(pl.program_id(0) == 0)
    def _():
        @pl.loop(0, blocks)
        def _(p):
            rows = pl.ds(pl.multiple_of(p * size, size), size)
            kept = dy_ref[rows, :]
            masked[rows, :] = jnp.where(image_ref[rows, :] == 1, kept, jnp.zeros_like(kept))

    turned_x[...] = x_ref[...].T

    def store(stream, n, values):
        values = values.astype(bf16)
        if len(out.shape) == 5:
            tile, per = out.shape[4], out.shape[3]
            for t in range(cols_at_once // tile):
                for q in range(out.shape[1]):
                    out[n * (cols_at_once // tile) + t, q, stream] = values[
                        q * per : (q + 1) * per, t * tile : (t + 1) * tile
                    ]
        else:
            per = out.shape[2]
            for k in range(out.shape[0]):
                out[k, stream, :, n * cols_at_once : (n + 1) * cols_at_once] = values[
                    k * per : (k + 1) * per
                ]

    for n in range(width // cols_at_once):
        cols = slice(n * cols_at_once, (n + 1) * cols_at_once)
        store(0, n, jnp.dot(turned_x[...], masked[:, cols], preferred_element_type=f32))
        acc[...] = jnp.zeros_like(acc)

        def text(p, first, rows, cols=cols):
            kept = dy_ref[rows, cols]
            kept = jnp.where(image_ref[rows, :] == 1, jnp.zeros_like(kept), kept)
            acc[...] += lax.dot_general(x_ref[rows, :], kept, TN, preferred_element_type=f32)

        text_windows(spots, blocks, count, text)
        store(1, n, acc[...])


def gradient(spots, x, dy, image, shape):
    blocks = (spots.shape[0] - 1) // 2
    count, depth = x.shape
    width = dy.shape[1]
    step = 384
    cols = 1152 if width % 768 else 768
    if len(shape) == 4:
        per = step // shape[2]
        out_spec = pl.BlockSpec((per, 2, shape[2], width), lambda j, s: (j, 0, 0, 0))
    else:
        tiles, q, _, rows, tile = shape
        if rows < step:
            block = (tiles, step // rows, 2, rows, tile)
            out_spec = pl.BlockSpec(block, lambda j, s: (0, j, 0, 0, 0))
        else:
            per = rows // step
            out_spec = pl.BlockSpec(
                (tiles, 1, 2, step, tile), lambda j, s: (0, j // per, 0, j % per, 0)
            )
    return pl.pallas_call(
        functools.partial(gradient_kernel, blocks),
        grid_spec=pltpu.PrefetchScalarGridSpec(
            num_scalar_prefetch=1,
            grid=(depth // step,),
            in_specs=[
                pl.BlockSpec((count, step), lambda j, s: (0, j)),
                resident(dy.shape),
                resident(image.shape),
            ],
            out_specs=out_spec,
            scratch_shapes=[
                pltpu.VMEM((step, count), bf16),
                pltpu.VMEM((count, width), bf16),
                pltpu.VMEM((step, cols), f32),
            ],
        ),
        out_shape=jax.ShapeDtypeStruct(shape, bf16),
        compiler_params=pltpu.CompilerParams(vmem_limit_bytes=48 << 20),
        cost_estimate=pl.CostEstimate(
            flops=3 * count * depth * width, bytes_accessed=20 << 20, transcendentals=0
        ),
        name="gradient",
    )(spots, x, dy, image)


def over_rep(value, target):
    count = lax.axis_size("rep")
    return lax.ppermute(value, "rep", [(r, target(r)) for r in range(count)])


def sibling(value):
    return over_rep(value, lambda r: r ^ 1)


def across(value):
    return over_rep(value, lambda r: r ^ 2)


def gather_rep(value):
    far = across(value)
    return [value, sibling(value), far, sibling(far)]


def reduce_rep(parts):
    near = sibling((parts[1], parts[3]))
    far = across((parts[2].astype(f32) + near[1].astype(f32)).astype(bf16))
    return parts[0].astype(f32) + near[0].astype(f32) + far.astype(f32)


def turn(value):
    reps, shards = lax.axis_size("rep"), lax.axis_size("shard")
    q = shards // reps
    pairs = []
    for r in range(reps):
        for s in range(shards):
            pairs.append((r * shards + s, (s // q) * shards + r * q + s % q))
    return lax.ppermute(value, ("rep", "shard"), pairs)


def gather_weight(weight_low):
    return lax.all_gather(weight_low, "shard", axis=0, tiled=False)


def gather_turned(moved):
    full = gather_weight(moved)
    reps = lax.axis_size("rep")
    return full.reshape(reps, full.shape[0] // reps, *full.shape[1:])


def scatter_weight(terms):
    blocks = terms.reshape(lax.axis_size("shard"), -1, *terms.shape[-3:])
    return lax.psum_scatter(
        blocks.reshape(-1, *terms.shape[-2:]), "shard", scatter_dimension=0, tiled=True
    ).reshape(terms.shape[-3:])


def body(
    tokens,
    cotangent,
    cond,
    seq_lengths,
    stream_mask,
    w_mod,
    m_mod,
    v_mod,
    w_qkv,
    m_qkv,
    v_qkv,
    w_out,
    m_out,
    v_out,
    w_fc1,
    m_fc1,
    v_fc1,
    w_fc2,
    m_fc2,
    v_fc2,
    gains,
    m_gains,
    v_gains,
):
    tok_rows, model_width = tokens.shape
    slot_count = seq_lengths.shape[0]
    reps, shards = lax.axis_size("rep"), lax.axis_size("shard")
    rep_index, shard_index = lax.axis_index("rep"), lax.axis_index("shard")
    device_index = rep_index * shards + shard_index
    all_tokens = tok_rows * reps * shards
    reach = (MAXLEN - 2) // tok_rows + 1
    part_width = model_width // reps
    part_rows = w_mod.shape[1]
    mod_cols = w_mod.shape[2]

    seq_starts = jnp.cumsum(seq_lengths) - seq_lengths
    local_pos = device_index * tok_rows + jnp.arange(tok_rows, dtype=jnp.int32)
    seq_ids = segment_index(local_pos, seq_starts, all_tokens)
    image_col = (stream_mask == 1)[:, None]
    image_group = jnp.concatenate(gather_rep(stream_mask)) == 1
    image = image_group[:, None].astype(jnp.int32)
    text_group = ~image_group.reshape(reps, tok_rows)
    text_first = jnp.argmax(text_group, axis=1).astype(jnp.int32)
    spots = jnp.concatenate(
        [
            jnp.minimum(text_first // 16 * 16, tok_rows - WINDOW),
            jnp.any(text_group, axis=1).astype(jnp.int32),
            rep_index[None].astype(jnp.int32),
        ]
    )

    silu_cond = jax.nn.silu(cond).astype(bf16)
    cond_rows = lax.dynamic_slice_in_dim(silu_cond, shard_index * part_rows, part_rows, 1)
    mod_terms = jnp.concatenate(
        [
            jnp.dot(cond_rows, w_mod[s].astype(bf16), preferred_element_type=f32)
            for s in range(2)
        ],
        axis=0,
    ).astype(bf16)
    device_count = reps * shards
    firsts = segment_index(
        jnp.arange(device_count, dtype=jnp.int32) * tok_rows, seq_starts, all_tokens
    )
    seconds = jnp.minimum(firsts + 1, slot_count - 1)
    stream_offset = jnp.arange(2, dtype=jnp.int32) * slot_count
    wanted = jnp.stack([firsts, seconds], axis=1)[:, :, None] + stream_offset
    hot = (wanted.reshape(-1, 1) == jnp.arange(2 * slot_count, dtype=jnp.int32)).astype(bf16)
    mod_sent = jnp.dot(hot, mod_terms, preferred_element_type=f32).astype(bf16)
    mod_got = lax.all_to_all(
        mod_sent.reshape(device_count, 4, mod_cols), ("rep", "shard"), 0, 0, tiled=True
    )
    mod_sum = jnp.sum(mod_got.reshape(reps, shards, 4, mod_cols).astype(f32), axis=1).astype(bf16)
    mod_rows = jnp.concatenate([mod_sum[r] for r in range(reps)], axis=1)

    qkv_low = w_qkv.astype(bf16)
    chunks = [
        over_rep(
            qkv_low[:, :, i * part_width : (i + 1) * part_width],
            lambda r, i=i: (3 * r + i) % reps,
        )
        for i in range(3)
    ]
    turns = rep_index % 3

    def rolled(parts, amount):
        return [
            jnp.where(
                amount == 0,
                parts[t],
                jnp.where(amount == 1, parts[(t + 1) % 3], parts[(t + 2) % 3]),
            )
            for t in range(3)
        ]

    qkv_weights = gather_weight(jnp.concatenate(rolled(chunks, turns), axis=2))
    fc1_weights = gather_weight(w_fc1.astype(bf16))
    out_turned = turn(w_out.astype(bf16))
    fc2_turned = turn(w_fc2.astype(bf16))

    first_seq = seq_ids[0]
    second_seq = jnp.minimum(first_seq + 1, slot_count - 1)
    is_second = (seq_ids != first_seq)[:, None]

    def mod_block(index):
        span = slice(index * model_width, (index + 1) * model_width)
        rows = mod_rows[:, span].astype(f32)
        pick = [jnp.where(is_second, rows[2 + s][None], rows[s][None]) for s in range(2)]
        return jnp.where(image_col, pick[0], pick[1])

    shift_one, scale_one, gate_one, shift_two, scale_two, gate_two = [
        mod_block(i) for i in range(6)
    ]
    stream_in = tokens.astype(f32)
    back_out = cotangent.astype(f32)
    act_one = layer_modulate(stream_in, shift_one, scale_one).astype(bf16)
    act_one_group = jnp.concatenate(gather_rep(act_one))
    d_down = (gate_two * back_out).astype(bf16)
    d_down_group = jnp.concatenate(gather_rep(d_down))

    act_one_group, out_turned, fc2_turned = lax.optimization_barrier(
        (act_one_group, out_turned, fc2_turned)
    )
    out_weights = gather_turned(out_turned)
    fc2_weights = gather_turned(fc2_turned)

    packed, qk_pre = qkv_product(spots, act_one_group, qkv_weights, image, gains)

    bunch = 2 * reps
    bunches = shards // bunch
    half_width = part_width // 2
    groups = [[q * bunch + i for i in range(bunch)] for q in range(bunches)]

    def exchange(value):
        return lax.all_to_all(
            value, "shard", 0, 0, axis_index_groups=None if bunches == 1 else groups, tiled=True
        )

    stretch_count = reps * bunches
    stretch_rows = bunch * tok_rows
    halo = reach * tok_rows

    def stretch_shift(value, steps):
        def place(stretch, g):
            return (stretch % bunches) * bunch + (stretch // bunches) * 2 + g

        pairs = [
            (place(t, g), place(t + steps, g))
            for t in range(stretch_count)
            for g in range(2)
            if 0 <= t + steps < stretch_count
        ]
        return lax.ppermute(value, "shard", pairs)

    own = exchange(packed).reshape(stretch_rows, 3 * half_width)
    pair_own = own[:, half_width:]
    pair_before = stretch_shift(pair_own[-halo:], 1)
    pair_after = stretch_shift(pair_own[:halo], -1)
    window_rows = stretch_rows + 2 * halo
    stretch = ((shard_index % bunch) // 2) * bunches + shard_index // bunch
    stretch_first = stretch * stretch_rows
    qid = segment_index(
        stretch_first + jnp.arange(stretch_rows, dtype=jnp.int32), seq_starts, all_tokens
    )
    kid = segment_index(
        stretch_first - halo + jnp.arange(window_rows, dtype=jnp.int32), seq_starts, all_tokens
    )
    seq_ends = seq_starts + seq_lengths
    low_pos = seq_starts[qid[::QB]] - (stretch_first - halo)
    high_pos = seq_ends[qid[QB - 1 :: QB]] - (stretch_first - halo)
    lo = jnp.clip(low_pos // KB, 0, window_rows // KB).astype(jnp.int32)
    hi = jnp.clip((high_pos + KB - 1) // KB, 0, window_rows // KB).astype(jnp.int32)
    attended_own, logsum = attention(own, pair_before, pair_after, lo, hi, qid, kid)
    attended_came = exchange(attended_own.reshape(bunch, tok_rows, half_width))

    def split_group(value):
        return [value[p * tok_rows : (p + 1) * tok_rows] for p in range(reps)]

    branch_terms, attended_low = forward_product(
        spots, attended_came, out_weights, image, gathers=True
    )
    branch = reduce_rep(split_group(branch_terms))
    branch, fc1_weights = lax.optimization_barrier((branch, fc1_weights))
    mid = stream_in + gate_one * branch
    act_two = layer_modulate(mid, shift_two, scale_two).astype(bf16)
    act_two_group = jnp.concatenate(gather_rep(act_two))
    gelu_low, gelu_slope = forward_product(spots, act_two_group, fc1_weights, image, gelu=True)
    down_proj = reduce_rep(split_group(forward_product(spots, gelu_low, fc2_weights, image)[0]))
    output = mid + gate_two * down_proj

    d_gate_two = back_out * down_proj
    d_up = backward_product(spots, d_down_group, fc2_weights, image, factor=gelu_slope)
    g_fc2 = turn(
        scatter_weight(gradient(spots, gelu_low, d_down_group, image, fc2_weights.shape))
    )
    d_act_two = reduce_rep(split_group(backward_product(spots, d_up, fc1_weights, image)))
    g_fc1 = scatter_weight(gradient(spots, act_two_group, d_up, image, fc1_weights.shape))
    d_mid_norm, d_shift_two, d_scale_two = jax.vjp(layer_modulate, mid, shift_two, scale_two)[1](
        d_act_two
    )
    d_mid = back_out + d_mid_norm
    d_branch = (gate_one * d_mid).astype(bf16)
    d_gate_one = d_mid * branch
    d_branch_group = jnp.concatenate(gather_rep(d_branch))
    d_attended = backward_product(spots, d_branch_group, out_weights, image, packs=True)
    g_out = turn(
        scatter_weight(gradient(spots, attended_low, d_branch_group, image, out_weights.shape))
    )
    d_attended_own = exchange(d_attended).reshape(stretch_rows, half_width)
    d_query_own, d_before, d_after, d_pair_own = attention_back(
        own, pair_before, pair_after, d_attended_own, attended_own, lo, hi, qid, kid, logsum
    )
    from_later = stretch_shift(d_before, -1).astype(f32)
    from_earlier = stretch_shift(d_after, 1).astype(f32)
    rest = jnp.zeros((stretch_rows - halo, 2 * half_width), f32)
    d_pair_own = (
        d_pair_own
        + jnp.concatenate([rest, from_later], axis=0)
        + jnp.concatenate([from_earlier, rest], axis=0)
    )
    d_own = jnp.concatenate([d_query_own, d_pair_own.astype(bf16)], axis=1)
    d_came = exchange(d_own.reshape(bunch, tok_rows, 3 * half_width))
    d_qkv, gain_sums = norm_back(spots, d_came, qk_pre, image, gains)
    d_act_one = reduce_rep(split_group(backward_product(spots, d_qkv, qkv_weights, image)))
    g_qkv_group = scatter_weight(gradient(spots, act_one_group, d_qkv, image, qkv_weights.shape))
    g_parts = [
        g_qkv_group[:, :, t * part_width : (t + 1) * part_width] for t in range(3)
    ]
    g_parts = rolled(g_parts, (3 - turns) % 3)
    g_qkv = jnp.concatenate(
        [over_rep(g_parts[i], lambda d, i=i: (3 * (d - i)) % reps) for i in range(3)], axis=2
    )

    d_in_norm, d_shift_one, d_scale_one = jax.vjp(layer_modulate, stream_in, shift_one, scale_one)[
        1
    ](d_act_one)
    d_tokens = d_mid + d_in_norm
    d_mod_tok = jnp.concatenate(
        [d_shift_one, d_scale_one, d_gate_one, d_shift_two, d_scale_two, d_gate_two], axis=1
    )
    image_flag = image_col[:, 0]
    second_flag = is_second[:, 0]
    selector = jnp.stack(
        [
            ~second_flag & image_flag,
            ~second_flag & ~image_flag,
            second_flag & image_flag,
            second_flag & ~image_flag,
        ],
        axis=1,
    ).astype(f32)
    pooled = jnp.einsum("tp,te->pe", selector, d_mod_tok, precision=lax.Precision.HIGHEST)
    gain_sums = jnp.sum(gain_sums.reshape(2, 2, part_width // HD, HD), axis=2)
    gain_part = jnp.concatenate([gain_sums[0], gain_sums[1]], axis=1)
    gain_rows = jnp.concatenate([gain_part, jnp.zeros_like(gain_part)], axis=0)
    leaving = jnp.stack(
        [
            jnp.concatenate([pooled[:, r * mod_cols : (r + 1) * mod_cols], gain_rows], axis=1)
            for r in range(reps)
        ]
    )
    leaving = jnp.broadcast_to(leaving[:, None], (reps, shards, *leaving.shape[1:]))
    came = lax.all_to_all(
        leaving.reshape(device_count, *leaving.shape[2:]), ("rep", "shard"), 0, 0, tiled=True
    )
    g_gains = jnp.sum(came[:, :2, mod_cols:], axis=0)
    came = came[:, :, :mod_cols].reshape(2 * device_count, 2, mod_cols)
    seqs = jnp.stack([firsts, seconds], axis=1).reshape(-1)
    hot_seq = (seqs[:, None] == jnp.arange(slot_count, dtype=jnp.int32)).astype(bf16)
    cond_seq = jnp.dot(hot_seq, cond_rows, preferred_element_type=f32)
    g_mod = jnp.stack(
        [
            lax.dot_general(
                cond_seq,
                came[:, s],
                (((0,), (0,)), ((), ())),
                precision=lax.Precision.HIGHEST,
                preferred_element_type=f32,
            )
            for s in range(2)
        ]
    )
    up_mod = adam_step(w_mod, m_mod, v_mod, g_mod, rate_mod)
    up_qkv = adam_step(w_qkv, m_qkv, v_qkv, g_qkv.astype(f32), rate_qkv)
    up_out = adam_step(w_out, m_out, v_out, g_out.astype(f32), rate_out)
    up_fc1 = adam_step(w_fc1, m_fc1, v_fc1, g_fc1.astype(f32), rate_fc1)
    up_fc2 = adam_step(w_fc2, m_fc2, v_fc2, g_fc2.astype(f32), rate_fc2)
    up_gains = adam_step(gains, m_gains, v_gains, g_gains, rate_gains)
    return (
        output.astype(bf16),
        d_tokens,
        *up_mod,
        *up_qkv,
        *up_out,
        *up_fc1,
        *up_fc2,
        *up_gains[:3],
    )


def solution(mesh):
    rows = P(("rep", "shard"), None)
    held = P(None, "shard", "rep")
    return jax.shard_map(
        body,
        mesh=mesh,
        in_specs=(rows, rows, P(), P(), P(("rep", "shard")), *([held] * 15), P(), P(), P()),
        out_specs=(rows, rows, *([held] * 20), P(), P(), P()),
        check_vma=False,
    )
```

```python
import functools

import jax
import jax.numpy as jnp
from jax import lax
from jax.experimental import pallas as pl
from jax.experimental.pallas import tpu as pltpu
from jax.sharding import PartitionSpec as P

HD = 64
MAXLEN = 1178
STEP = 7

norm_eps = 1e-06
adam_eps = 1e-08
score_scale = 0.125
rate_mod = 0.03
rate_qkv = 0.03
rate_out = 0.15
rate_fc1 = 0.03
rate_fc2 = 0.015
rate_gains = 1.0

bf16 = jnp.bfloat16
f32 = jnp.float32
QB = 256
KB = 256
TXT = 154
WINDOW = (TXT + 15 + 15) // 16 * 16
COLS = 512
GELU_A = 0.7978845608028654
GELU_B = 0.044715
NN = (((1,), (0,)), ((), ()))
NT = (((1,), (1,)), ((), ()))
TN = (((0,), (0,)), ((), ()))


def layer_modulate(values, shift, scale):
    centred = values - jnp.mean(values, axis=-1, keepdims=True)
    normed = centred * lax.rsqrt(jnp.mean(centred * centred, axis=-1, keepdims=True) + norm_eps)
    return normed * (1.0 + scale) + shift


def adam_step(weight, moment_one, moment_two, grads, rate):
    new_one = 0.9 * moment_one + 0.1 * grads
    new_two = 0.999 * moment_two + 0.001 * grads * grads
    fixed_one = new_one / (1.0 - 0.9**STEP)
    fixed_two = new_two / (1.0 - 0.999**STEP)
    new_weight = weight - rate * (fixed_one / (jnp.sqrt(fixed_two) + adam_eps) + 0.01 * weight)
    return (new_weight, new_one, new_two, new_weight.astype(bf16))


def segment_index(position, seq_starts, all_tokens):
    counted = jnp.sum((seq_starts[None, :] <= position[:, None]).astype(jnp.int32), axis=1) - 1
    inside = (position >= 0) & (position < all_tokens)
    return jnp.where(inside, counted, -1)


def fill_window(own_ref, before_ref, after_ref, keys, values):
    halo, own = before_ref.shape[0], own_ref.shape[0]
    heads = keys.shape[0]
    width = heads * HD
    parts = ((before_ref, 0, halo), (own_ref, halo, own), (after_ref, halo + own, halo))
    for source, first, count in parts:
        for head in range(heads):
            for index, dest in ((0, keys), (1, values)):
                start = index * width + head * HD
                dest[head, first : first + count, :HD] = source[:, start : start + HD]


def attend_kernel(
    lo_ref, hi_ref, q_ref, own_ref, before_ref, after_ref, qid_ref, kid_ref, o_ref, l_ref, keys, values, acc
):
    step = pl.program_id(0)
    heads = keys.shape[0]

    @pl.when(step == 0)
    def _():
        lane = lax.broadcasted_iota(jnp.int32, values.shape[1:], 1)
        for head in range(heads):
            values[head] = (lane == HD).astype(bf16)
        fill_window(own_ref, before_ref, after_ref, keys, values)

    qid = qid_ref[...]
    diagonal = lax.broadcasted_iota(jnp.int32, (QB, QB), 0) == lax.broadcasted_iota(
        jnp.int32, (QB, QB), 1
    )
    queries = [q_ref[:, head * HD : (head + 1) * HD] for head in range(heads)]
    acc[...] = jnp.zeros_like(acc)

    @pl.loop(lo_ref[step], hi_ref[step])
    def _(block):
        rows = pl.ds(pl.multiple_of(block * KB, KB), KB)
        same = qid == kid_ref[pl.ds(block, 1), :]
        for head in range(heads):
            scores = lax.dot_general(
                queries[head], keys[head, rows, :], NT, preferred_element_type=f32
            )
            lifted = jnp.where(same, jnp.exp(scores), 0.0).astype(bf16)
            acc[head] += jnp.dot(lifted, values[head, rows, :], preferred_element_type=f32)

    for head in range(heads):
        total = acc[head, :, HD : HD + 1]
        o_ref[:, head * HD : (head + 1) * HD] = (acc[head, :, :HD] / total).astype(bf16)
        l_ref[0, head : head + 1, :] = jnp.sum(
            jnp.where(diagonal, jnp.log(total), 0.0), axis=0, keepdims=True
        )


def attend_back_kernel(
    lo_ref,
    hi_ref,
    q_ref,
    own_ref,
    before_ref,
    after_ref,
    do_ref,
    o_ref,
    qid_ref,
    kid_ref,
    l_ref,
    dq_ref,
    d_before_ref,
    d_after_ref,
    d_own_ref,
    keys,
    values,
    d_keys,
    d_values,
    d_query,
):
    step = pl.program_id(0)
    heads = keys.shape[0]
    width = heads * HD

    @pl.when(step == 0)
    def _():
        fill_window(own_ref, before_ref, after_ref, keys, values)
        d_keys[...] = jnp.zeros_like(d_keys)
        d_values[...] = jnp.zeros_like(d_values)

    qid = qid_ref[0]
    ones = jnp.ones((8, HD), bf16)
    queries, outs, dots = [], [], []
    for head in range(heads):
        lanes = slice(head * HD, (head + 1) * HD)
        queries.append(q_ref[:, lanes])
        outs.append(do_ref[:, lanes])
        product = outs[head].astype(f32) * o_ref[:, lanes].astype(f32)
        coarse = product.astype(bf16)
        fine = (product - coarse.astype(f32)).astype(bf16)
        total = lax.dot_general(ones, coarse, NT, preferred_element_type=f32)
        dots.append((total + lax.dot_general(ones, fine, NT, preferred_element_type=f32))[:1])
    d_query[...] = jnp.zeros_like(d_query)

    @pl.loop(lo_ref[step], hi_ref[step])
    def _(block):
        rows = pl.ds(pl.multiple_of(block * KB, KB), KB)
        same = kid_ref[rows, :] == qid
        for head in range(heads):
            key = keys[head, rows, :]
            scores = lax.dot_general(key, queries[head], NT, preferred_element_type=f32)
            probs = jnp.where(same, jnp.exp(scores - l_ref[0, head : head + 1, :]), 0.0)
            d_values[head, rows, :] += jnp.dot(
                probs.astype(bf16), outs[head], preferred_element_type=f32
            )
            d_probs = lax.dot_general(
                values[head, rows, :], outs[head], NT, preferred_element_type=f32
            )
            d_scores = (probs * (d_probs - dots[head])).astype(bf16)
            d_keys[head, rows, :] += jnp.dot(d_scores, queries[head], preferred_element_type=f32)
            d_query[head] += lax.dot_general(d_scores, key, TN, preferred_element_type=f32)

    for head in range(heads):
        dq_ref[:, head * HD : (head + 1) * HD] = (d_query[head] * score_scale).astype(bf16)

    @pl.when(step == pl.num_programs(0) - 1)
    def _():
        halo, own = d_before_ref.shape[0], d_own_ref.shape[0]
        for index, source in ((0, d_keys), (1, d_values)):
            for head in range(heads):
                span = slice(index * width + head * HD, index * width + (head + 1) * HD)
                d_before_ref[:, span] = source[head, :halo, :].astype(bf16)
                d_own_ref[:, span] = source[head, halo : halo + own, :]
                d_after_ref[:, span] = source[head, halo + own :, :].astype(bf16)


def resident(shape):
    return pl.BlockSpec(shape, lambda *index: (0,) * len(shape))


def attention(query, own, before, after, lo, hi, qid, kid):
    count, width = query.shape
    heads = width // HD
    window = count + 2 * before.shape[0]
    steps = count // QB
    return pl.pallas_call(
        attend_kernel,
        grid_spec=pltpu.PrefetchScalarGridSpec(
            num_scalar_prefetch=2,
            grid=(steps,),
            in_specs=[
                pl.BlockSpec((QB, width), lambda i, lo, hi: (i, 0)),
                resident(own.shape),
                resident(before.shape),
                resident(after.shape),
                pl.BlockSpec((QB, 1), lambda i, lo, hi: (i, 0)),
                resident((window // KB, KB)),
            ],
            out_specs=[
                pl.BlockSpec((QB, width), lambda i, lo, hi: (i, 0)),
                pl.BlockSpec((1, 8, QB), lambda i, lo, hi: (i, 0, 0)),
            ],
            scratch_shapes=[
                pltpu.VMEM((heads, window, HD), bf16),
                pltpu.VMEM((heads, window, 2 * HD), bf16),
                pltpu.VMEM((heads, QB, 2 * HD), f32),
            ],
        ),
        out_shape=[
            jax.ShapeDtypeStruct((count, width), bf16),
            jax.ShapeDtypeStruct((steps, 8, QB), f32),
        ],
        compiler_params=pltpu.CompilerParams(vmem_limit_bytes=40 << 20),
        cost_estimate=pl.CostEstimate(flops=1 << 30, bytes_accessed=4 << 20, transcendentals=0),
        name="attend",
    )(lo, hi, query, own, before, after, qid[:, None], kid.reshape(window // KB, KB))


def attention_back(query, own, before, after, d_out, out, lo, hi, qid, kid, logsum):
    count, width = query.shape
    heads = width // HD
    halo = before.shape[0]
    window = count + 2 * halo
    steps = count // QB
    rows = pl.BlockSpec((QB, width), lambda i, lo, hi: (i, 0))
    return pl.pallas_call(
        attend_back_kernel,
        grid_spec=pltpu.PrefetchScalarGridSpec(
            num_scalar_prefetch=2,
            grid=(steps,),
            in_specs=[
                rows,
                resident(own.shape),
                resident(before.shape),
                resident(after.shape),
                rows,
                rows,
                pl.BlockSpec((1, 1, QB), lambda i, lo, hi: (i, 0, 0)),
                resident((window, 1)),
                pl.BlockSpec((1, 8, QB), lambda i, lo, hi: (i, 0, 0)),
            ],
            out_specs=[
                rows,
                resident((halo, 2 * width)),
                resident((halo, 2 * width)),
                resident((count, 2 * width)),
            ],
            scratch_shapes=[pltpu.VMEM((heads, window, HD), bf16)] * 2
            + [pltpu.VMEM((heads, window, HD), f32)] * 2
            + [pltpu.VMEM((heads, QB, HD), f32)],
        ),
        out_shape=[
            jax.ShapeDtypeStruct((count, width), bf16),
            jax.ShapeDtypeStruct((halo, 2 * width), bf16),
            jax.ShapeDtypeStruct((halo, 2 * width), bf16),
            jax.ShapeDtypeStruct((count, 2 * width), f32),
        ],
        compiler_params=pltpu.CompilerParams(vmem_limit_bytes=58 << 20),
        cost_estimate=pl.CostEstimate(flops=24 << 30, bytes_accessed=8 << 20, transcendentals=0),
        name="attend_back",
    )(lo, hi, query, own, before, after, d_out, out, qid.reshape(steps, 1, QB), kid[:, None], logsum)


def text_windows(spots, blocks, count, work):
    for p in range(blocks):

        @pl.when(spots[blocks + p] == 1)
        def _(p=p):
            first = pl.multiple_of(spots[p], 16)
            base = p * (count // blocks)
            work(p, first, pl.ds(pl.multiple_of(base + first, 16), WINDOW))


def flat(value):
    return value.reshape(-1, value.shape[-1])


def product(x_ref, rows, weight, dims):
    total = None
    for cols, get in weight:
        term = lax.dot_general(x_ref[rows, cols], get(), dims, preferred_element_type=f32)
        total = term if total is None else total + term
    return total


def group_sums(values, blocks_of):
    coarse = values.astype(bf16)
    fine = (values - coarse.astype(f32)).astype(bf16)
    return jnp.dot(coarse, blocks_of, preferred_element_type=f32) + jnp.dot(
        fine, blocks_of, preferred_element_type=f32
    )


def head_blocks(width):
    row = lax.broadcasted_iota(jnp.int32, (width, width), 0) // HD
    col = lax.broadcasted_iota(jnp.int32, (width, width), 1) // HD
    return (row == col).astype(bf16)


def qkv_kernel(blocks, spots, x_ref, w0, w1, image_ref, gain_ref, q_ref, kv_ref, pre_ref):
    kind = pl.program_id(0)
    every = slice(None)
    size, width = q_ref.shape[1:]
    rep = spots[2 * blocks]
    spread = head_blocks(2 * width)

    def finish(t, values, gain):
        if t < 2:
            mean = group_sums(values * values, spread) * (1.0 / HD)
            values = values * lax.rsqrt(mean + norm_eps) * gain
        values = values.astype(bf16)
        return values * jnp.asarray(score_scale, bf16) if t == 0 else values

    for t in range(3):

        @pl.when(kind == t)
        def _(t=t):
            packed_ref = kv_ref if t else q_ref
            lanes = slice((t - 1) * width, t * width) if t else slice(0, width)

            @pl.loop(0, blocks)
            def _(p):
                rows = pl.ds(pl.multiple_of(p * size, size), size)
                values = product(x_ref, rows, [(every, lambda: flat(w0[...]))], NN)
                if t < 2:
                    pre_ref[rows, :] = values
                values = finish(t, values, gain_ref[0, :1])
                for g in range(2):
                    packed_ref[pl.ds((rep ^ p) * 2 + g, 1), :, lanes] = values[
                        :, g * width : (g + 1) * width
                    ][None]

            def text(p, first, rows):
                values = product(x_ref, rows, [(every, lambda: flat(w1[...]))], NN)
                image = image_ref[rows, :] == 1
                if t < 2:
                    pre_ref[rows, :] = jnp.where(image, pre_ref[rows, :], values)
                values = finish(t, values, gain_ref[0, 1:])
                for g in range(2):
                    place = (
                        pl.ds((rep ^ p) * 2 + g, 1),
                        pl.ds(first, WINDOW),
                        lanes,
                    )
                    packed_ref[place] = jnp.where(
                        image[None], packed_ref[place], values[:, g * width : (g + 1) * width][None]
                    )

            text_windows(spots, blocks, x_ref.shape[0], text)


def column_weights(weight, tile):
    shards, _, rows, _ = weight.shape
    return [
        pl.BlockSpec((shards, 1, rows, tile), lambda j, s, stream=stream: (0, stream, 0, j))
        for stream in range(2)
    ]


def tiled_gains(gains, heads):
    return jnp.stack([jnp.tile(gains[:, :HD], (1, heads)), jnp.tile(gains[:, HD:], (1, heads))])


def qkv_product(spots, x, weight, image, gains):
    count, depth = x.shape
    blocks = (spots.shape[0] - 1) // 2
    part = weight.shape[3] // 3
    size = count // blocks
    return pl.pallas_call(
        functools.partial(qkv_kernel, blocks),
        grid_spec=pltpu.PrefetchScalarGridSpec(
            num_scalar_prefetch=1,
            grid=(3,),
            in_specs=[
                resident(x.shape),
                *column_weights(weight, part),
                resident(image.shape),
                pl.BlockSpec((1, 2, part), lambda j, s: (jnp.minimum(j, 1), 0, 0)),
            ],
            out_specs=[
                resident((2 * blocks, size, part // 2)),
                resident((2 * blocks, size, part)),
                pl.BlockSpec((count, part), lambda j, s: (0, jnp.minimum(j, 1))),
            ],
        ),
        out_shape=[
            jax.ShapeDtypeStruct((2 * blocks, size, part // 2), bf16),
            jax.ShapeDtypeStruct((2 * blocks, size, part), bf16),
            jax.ShapeDtypeStruct((count, 2 * part), f32),
        ],
        compiler_params=pltpu.CompilerParams(vmem_limit_bytes=40 << 20),
        cost_estimate=pl.CostEstimate(flops=1 << 30, bytes_accessed=4 << 20, transcendentals=0),
        name="qkv_product",
    )(spots, x, weight, weight, image, tiled_gains(gains, part // HD))


def norm_back_kernel(blocks, spots, q_ref, kv_ref, pre_ref, image_ref, gain_ref, out_ref, sum_ref, both):
    @pl.when(pl.program_id(0) == 0)
    def _():
        sum_ref[...] = jnp.zeros_like(sum_ref)

    part = both.shape[1]
    width = part // 2
    image = image_ref[...] == 1
    spread = head_blocks(part)
    for t in range(3):
        came_ref = kv_ref if t else q_ref
        lanes = slice((t - 1) * width, t * width) if t else slice(0, width)
        for g in range(2):
            both[:, g * width : (g + 1) * width] = came_ref[g, :, lanes].astype(f32)
        grad = both[...]
        if t < 2:
            pre = pre_ref[:, t * part : (t + 1) * part]
            scale = lax.rsqrt(group_sums(pre * pre, spread) * (1.0 / HD) + norm_eps)
            gain = jnp.where(image, gain_ref[t, :1], gain_ref[t, 1:])
            each = grad * pre * scale
            total = jnp.sum(each, axis=0, keepdims=True)
            text = jnp.sum(jnp.where(image, 0.0, each), axis=0, keepdims=True)
            sum_ref[2 * t : 2 * t + 1, :] += total - text
            sum_ref[2 * t + 1 : 2 * t + 2, :] += text
            grad = grad * gain
            mean = group_sums(grad * pre, spread) * (1.0 / HD)
            grad = scale * (grad - pre * (scale * scale * mean))
        out_ref[:, t * part : (t + 1) * part] = grad.astype(bf16)


def norm_back(spots, came_query, came_pair, pre, image, gains):
    blocks = (spots.shape[0] - 1) // 2
    _, size, part = came_pair.shape
    tiled = tiled_gains(gains, part // HD)
    return pl.pallas_call(
        functools.partial(norm_back_kernel, blocks),
        grid_spec=pltpu.PrefetchScalarGridSpec(
            num_scalar_prefetch=1,
            grid=(blocks,),
            in_specs=[
                pl.BlockSpec((2, size, part // 2), lambda p, s: (s[2 * blocks] ^ p, 0, 0)),
                pl.BlockSpec((2, size, part), lambda p, s: (s[2 * blocks] ^ p, 0, 0)),
                pl.BlockSpec((size, 2 * part), lambda p, s: (p, 0)),
                pl.BlockSpec((size, 1), lambda p, s: (p, 0)),
                resident(tiled.shape),
            ],
            out_specs=[
                pl.BlockSpec((size, 3 * part), lambda p, s: (p, 0)),
                resident((4, part)),
            ],
            scratch_shapes=[pltpu.VMEM((size, part), f32)],
        ),
        out_shape=[
            jax.ShapeDtypeStruct((blocks * size, 3 * part), bf16),
            jax.ShapeDtypeStruct((4, part), f32),
        ],
        compiler_params=pltpu.CompilerParams(vmem_limit_bytes=32 << 20),
        cost_estimate=pl.CostEstimate(flops=4 << 30, bytes_accessed=12 << 20, transcendentals=0),
        name="norm_back",
    )(spots, came_query, came_pair, pre, image, tiled)


def forward_kernel(blocks, gathers, gelu, spots, x_ref, w0, w1, image_ref, *rest):
    rep = spots[2 * blocks]
    out_ref = rest[0]
    if gathers:
        x_out = rest[1]
        size, width = x_ref.shape[1:]

        @pl.when(pl.program_id(0) == 0)
        def _():
            for p in range(blocks):
                for g in range(2):
                    x_out[p * size : (p + 1) * size, g * width : (g + 1) * width] = x_ref[
                        pl.ds((rep ^ p) * 2 + g, 1)
                    ][0]

        x_ref = x_out
    every = slice(None)
    count = x_ref.shape[0]

    def finish(values):
        if not gelu:
            return (values.astype(bf16),)
        square = values * values
        bend = jnp.tanh(values * (GELU_A + GELU_A * GELU_B * square))
        half = 0.5 * (1.0 + bend)
        slope = half + 0.5 * values * (1.0 - bend * bend) * (GELU_A + 3.0 * GELU_A * GELU_B * square)
        return (values * half).astype(bf16), slope.astype(bf16)

    outs = rest if gelu else (out_ref,)
    chunk = count // (blocks if gelu else 2)

    @pl.loop(0, count // chunk)
    def _(p):
        rows = pl.ds(pl.multiple_of(p * chunk, chunk), chunk)
        values = product(x_ref, rows, [(every, lambda: flat(w0[...]))], NN)
        for out, value in zip(outs, finish(values)):
            out[rows, :] = value

    def text(p, first, rows):
        values = product(x_ref, rows, [(every, lambda: flat(w1[...]))], NN)
        image = image_ref[rows, :] == 1
        for out, value in zip(outs, finish(values)):
            out[rows, :] = jnp.where(image, out[rows, :], value)

    text_windows(spots, blocks, count, text)


def forward_product(spots, x, weight, image, gathers=False, gelu=False):
    blocks = (spots.shape[0] - 1) // 2
    if weight.ndim == 5:
        tiles, q, _, rows, tile = weight.shape
        weights = [
            pl.BlockSpec((1, q, 1, rows, tile), lambda j, s, stream=stream: (j, 0, stream, 0, 0))
            for stream in range(2)
        ]
        depth = q * rows
    else:
        depth, tile = weight.shape[0] * weight.shape[2], COLS
        tiles = weight.shape[3] // tile
        weights = column_weights(weight, tile)
    count = image.shape[0]
    column = pl.BlockSpec((count, tile), lambda j, s: (0, j))
    whole = jax.ShapeDtypeStruct((count, tiles * tile), bf16)
    out_specs, out_shape = [column], [whole]
    if gathers:
        out_specs.append(resident((count, depth)))
        out_shape.append(jax.ShapeDtypeStruct((count, depth), bf16))
    if gelu:
        out_specs.append(column)
        out_shape.append(whole)
    return pl.pallas_call(
        functools.partial(forward_kernel, blocks, gathers, gelu),
        grid_spec=pltpu.PrefetchScalarGridSpec(
            num_scalar_prefetch=1,
            grid=(tiles,),
            in_specs=[resident(x.shape), *weights, resident(image.shape)],
            out_specs=out_specs,
        ),
        out_shape=out_shape,
        compiler_params=pltpu.CompilerParams(vmem_limit_bytes=40 << 20),
        cost_estimate=pl.CostEstimate(
            flops=count * depth // 4 * tiles * tile, bytes_accessed=4 << 20, transcendentals=0
        ),
        name="forward_product",
    )(spots, x, weight, weight, image)


def backward_kernel(blocks, turned, scaled, packs, spots, dy_ref, w0, w1, image_ref, *rest):
    rest = list(rest)
    factor_ref = rest.pop(0) if scaled else None
    out_ref = rest[0]
    if turned:
        tiles, tile = w0.shape[0], w0.shape[4]
        weights = [
            [
                (slice(n * tile, (n + 1) * tile), lambda w=w, n=n: flat(w[n, :, 0]))
                for n in range(tiles)
            ]
            for w in (w0, w1)
        ]
    else:
        every = slice(None)
        weights = [[(every, lambda w=w: flat(w[...]))] for w in (w0, w1)]
    count = dy_ref.shape[0]
    size = count // blocks
    rep = spots[2 * blocks]
    part = pl.program_id(0)

    def finish(rows, values):
        if scaled:
            values = values * factor_ref[rows, :].astype(f32)
        return values.astype(bf16)

    chunk = size if packs or scaled else count // 2

    @pl.loop(0, count // chunk)
    def _(p):
        rows = pl.ds(pl.multiple_of(p * chunk, chunk), chunk)
        values = finish(rows, product(dy_ref, rows, weights[0], NT))
        if packs:
            out_ref[pl.ds((rep ^ p) * 2 + part, 1)] = values[None]
        else:
            out_ref[rows, :] = values

    def text(p, first, rows):
        values = finish(rows, product(dy_ref, rows, weights[1], NT))
        image = image_ref[rows, :] == 1
        if packs:
            place = (pl.ds((rep ^ p) * 2 + part, 1), pl.ds(first, WINDOW), slice(None))
            out_ref[place] = jnp.where(image[None], out_ref[place], values[None])
        else:
            out_ref[rows, :] = jnp.where(image, out_ref[rows, :], values)

    text_windows(spots, blocks, count, text)


def backward_product(spots, dy, weight, image, factor=None, packs=False):
    blocks = (spots.shape[0] - 1) // 2
    turned = weight.ndim == 5
    count = image.shape[0]
    if turned:
        tiles, q, _, rows, tile = weight.shape
        step = q * rows // 2 if packs else min(q * rows, 768)
        grid = (q * rows // step,)
        if rows < step:
            block = (tiles, step // rows, 1, rows, tile)
            weights = [
                pl.BlockSpec(block, lambda j, s, stream=stream: (0, j, stream, 0, 0))
                for stream in range(2)
            ]
        else:
            per = rows // step
            weights = [
                pl.BlockSpec(
                    (tiles, 1, 1, step, tile),
                    lambda j, s, stream=stream: (0, j // per, stream, j % per, 0),
                )
                for stream in range(2)
            ]
        depth = q * rows
    else:
        shards, _, rows, width = weight.shape
        depth = shards * rows
        bunch = max(1, 768 // rows)
        step = bunch * rows
        grid = (depth // step,)
        weights = [
            pl.BlockSpec((bunch, 1, rows, width), lambda j, s, stream=stream: (j, stream, 0, 0))
            for stream in range(2)
        ]
    column = pl.BlockSpec((count, step), lambda j, s: (0, j))
    in_specs = [resident(dy.shape), *weights, resident(image.shape)]
    operands = [spots, dy, weight, weight, image]
    if factor is not None:
        in_specs.append(column)
        operands.append(factor)
    if packs:
        shape = (2 * blocks, count // blocks, step)
        out_spec, out_shape = resident(shape), jax.ShapeDtypeStruct(shape, bf16)
    else:
        out_spec, out_shape = column, jax.ShapeDtypeStruct((count, depth), bf16)
    return pl.pallas_call(
        functools.partial(backward_kernel, blocks, turned, factor is not None, packs),
        grid_spec=pltpu.PrefetchScalarGridSpec(
            num_scalar_prefetch=1,
            grid=grid,
            in_specs=in_specs,
            out_specs=out_spec,
        ),
        out_shape=out_shape,
        compiler_params=pltpu.CompilerParams(vmem_limit_bytes=48 << 20),
        cost_estimate=pl.CostEstimate(
            flops=count * depth // 4 * dy.shape[1], bytes_accessed=4 << 20, transcendentals=0
        ),
        name="backward_product",
    )(*operands)


def gradient_kernel(blocks, spots, x_ref, dy_ref, image_ref, out, turned_x, masked, acc):
    count, width = dy_ref.shape
    size = count // blocks
    cols_at_once = acc.shape[1]

    @pl.when(pl.program_id(0) == 0)
    def _():
        @pl.loop(0, blocks)
        def _(p):
            rows = pl.ds(pl.multiple_of(p * size, size), size)
            kept = dy_ref[rows, :]
            masked[rows, :] = jnp.where(image_ref[rows, :] == 1, kept, jnp.zeros_like(kept))

    turned_x[...] = x_ref[...].T

    def store(stream, n, values):
        values = values.astype(bf16)
        if len(out.shape) == 5:
            tile, per = out.shape[4], out.shape[3]
            for t in range(cols_at_once // tile):
                for q in range(out.shape[1]):
                    out[n * (cols_at_once // tile) + t, q, stream] = values[
                        q * per : (q + 1) * per, t * tile : (t + 1) * tile
                    ]
        else:
            per = out.shape[2]
            for k in range(out.shape[0]):
                out[k, stream, :, n * cols_at_once : (n + 1) * cols_at_once] = values[
                    k * per : (k + 1) * per
                ]

    for n in range(width // cols_at_once):
        cols = slice(n * cols_at_once, (n + 1) * cols_at_once)
        store(0, n, jnp.dot(turned_x[...], masked[:, cols], preferred_element_type=f32))
        acc[...] = jnp.zeros_like(acc)

        def text(p, first, rows, cols=cols):
            kept = dy_ref[rows, cols]
            kept = jnp.where(image_ref[rows, :] == 1, jnp.zeros_like(kept), kept)
            acc[...] += lax.dot_general(x_ref[rows, :], kept, TN, preferred_element_type=f32)

        text_windows(spots, blocks, count, text)
        store(1, n, acc[...])


def gradient(spots, x, dy, image, shape):
    blocks = (spots.shape[0] - 1) // 2
    count, depth = x.shape
    width = dy.shape[1]
    step = 384
    cols = 1152 if width % 768 else 768
    if len(shape) == 4:
        per = step // shape[2]
        out_spec = pl.BlockSpec((per, 2, shape[2], width), lambda j, s: (j, 0, 0, 0))
    else:
        tiles, q, _, rows, tile = shape
        if rows < step:
            block = (tiles, step // rows, 2, rows, tile)
            out_spec = pl.BlockSpec(block, lambda j, s: (0, j, 0, 0, 0))
        else:
            per = rows // step
            out_spec = pl.BlockSpec(
                (tiles, 1, 2, step, tile), lambda j, s: (0, j // per, 0, j % per, 0)
            )
    return pl.pallas_call(
        functools.partial(gradient_kernel, blocks),
        grid_spec=pltpu.PrefetchScalarGridSpec(
            num_scalar_prefetch=1,
            grid=(depth // step,),
            in_specs=[
                pl.BlockSpec((count, step), lambda j, s: (0, j)),
                resident(dy.shape),
                resident(image.shape),
            ],
            out_specs=out_spec,
            scratch_shapes=[
                pltpu.VMEM((step, count), bf16),
                pltpu.VMEM((count, width), bf16),
                pltpu.VMEM((step, cols), f32),
            ],
        ),
        out_shape=jax.ShapeDtypeStruct(shape, bf16),
        compiler_params=pltpu.CompilerParams(vmem_limit_bytes=48 << 20),
        cost_estimate=pl.CostEstimate(
            flops=count * depth // 4 * width, bytes_accessed=4 << 20, transcendentals=0
        ),
        name="gradient",
    )(spots, x, dy, image)


def over_rep(value, target):
    count = lax.axis_size("rep")
    return lax.ppermute(value, "rep", [(r, target(r)) for r in range(count)])


def sibling(value):
    return over_rep(value, lambda r: r ^ 1)


def across(value):
    return over_rep(value, lambda r: r ^ 2)


def gather_rep(value):
    far = across(value)
    return [value, sibling(value), far, sibling(far)]


def reduce_rep(parts):
    near = sibling((parts[1], parts[3]))
    far = across((parts[2].astype(f32) + near[1].astype(f32)).astype(bf16))
    return parts[0].astype(f32) + near[0].astype(f32) + far.astype(f32)


def turn(value):
    reps, shards = lax.axis_size("rep"), lax.axis_size("shard")
    q = shards // reps
    pairs = []
    for r in range(reps):
        for s in range(shards):
            pairs.append((r * shards + s, (s // q) * shards + r * q + s % q))
    return lax.ppermute(value, ("rep", "shard"), pairs)


def gather_weight(weight_low):
    return lax.all_gather(weight_low, "shard", axis=0, tiled=False)


def gather_turned(moved):
    full = gather_weight(moved)
    reps = lax.axis_size("rep")
    return full.reshape(reps, full.shape[0] // reps, *full.shape[1:])


def ring_place(shards):
    mine = lax.axis_index("shard")
    odd = mine % 2
    return (1 - odd) * (mine // 2) + odd * (shards - 1 - mine // 2)


def ring_owner(place, shards):
    place = (place + 2 * shards) % shards
    back = place // ((shards + 1) // 2)
    return (1 - back) * (2 * place) + back * (2 * (shards - 1 - place) + 1)


def ring_kernel(shards, count, *refs):
    sources, dests = refs[:count], refs[count : 2 * count]
    send_sem, recv_sem, own_sem = refs[2 * count :]
    place = ring_place(shards)
    mine = ring_owner(place, shards)
    peers = [ring_owner(place + 1, shards), ring_owner(place - 1, shards)]

    barrier = pltpu.get_barrier_semaphore()
    for peer in peers:
        pl.semaphore_signal(
            barrier, inc=1, device_id={"shard": peer}, device_id_type=pl.DeviceIdType.MESH
        )
    pl.semaphore_wait(barrier, 2)

    kept = [
        pltpu.make_async_copy(sources[w], dests[w].at[mine], own_sem.at[w]) for w in range(count)
    ]
    for copy in kept:
        copy.start()
    chains = [(w, way) for w in range(count) for way in range(2)]
    copies = {}
    for step in range(shards - 1):
        for chain in chains:
            w, way = chain
            if step:
                copies[chain, step - 1].wait_recv()
            owner = ring_owner(place - step if way == 0 else place + step, shards)
            dest = dests[w].at[owner, way]
            copies[chain, step] = pltpu.make_async_remote_copy(
                src_ref=dest if step else sources[w].at[way],
                dst_ref=dest,
                send_sem=send_sem.at[w, way, step],
                recv_sem=recv_sem.at[w, way, step],
                device_id={"shard": peers[way]},
                device_id_type=pl.DeviceIdType.MESH,
            )
            copies[chain, step].start()
    for chain in chains:
        copies[chain, shards - 2].wait_recv()
        for step in range(shards - 1):
            copies[chain, step].wait_send()
    for copy in kept:
        copy.wait()


def ring_gather(*blocks):
    shards = lax.axis_size("shard")
    count = len(blocks)
    anywhere = pl.BlockSpec(memory_space=pl.ANY)
    return pl.pallas_call(
        functools.partial(ring_kernel, shards, count),
        in_specs=[anywhere] * count,
        out_specs=[anywhere] * count,
        out_shape=[jax.ShapeDtypeStruct((shards, *b.shape), b.dtype) for b in blocks],
        scratch_shapes=[
            pltpu.SemaphoreType.DMA((count, 2, shards - 1)),
            pltpu.SemaphoreType.DMA((count, 2, shards - 1)),
            pltpu.SemaphoreType.DMA((count,)),
        ],
        compiler_params=pltpu.CompilerParams(collective_id=0, has_side_effects=True),
        cost_estimate=pl.CostEstimate(flops=1 << 20, bytes_accessed=8 << 20, transcendentals=0),
        name="ring_gather",
    )(*blocks)


def ring_scatter_kernel(terms, out, held, send_sem, recv_sem):
    shards, _, rows, _ = terms.shape
    pieces = held.shape[1]
    part = rows // pieces
    place = ring_place(shards)
    mine = ring_owner(place, shards)
    peers = [ring_owner(place + 1, shards), ring_owner(place - 1, shards)]

    barrier = pltpu.get_barrier_semaphore()
    for peer in peers:
        pl.semaphore_signal(
            barrier, inc=1, device_id={"shard": peer}, device_id_type=pl.DeviceIdType.MESH
        )
    pl.semaphore_wait(barrier, 2)

    chains = [(way, piece) for piece in range(pieces) for way in range(2)]
    copies = {}
    for step in range(shards):
        for way, piece in chains:
            span = slice(piece * part, (piece + 1) * part)
            if step < shards - 1:
                owner = ring_owner(place - 1 - step if way == 0 else place + 1 + step, shards)
            else:
                owner = mine
            source = terms.at[owner, way, span]
            if step:
                copies[way, piece, step - 1].wait_recv()
                arrived = held.at[way, piece, step - 1]
                total = arrived[...].astype(f32) + source[...].astype(f32)
                if step == shards - 1:
                    out[way, span] = total.astype(bf16)
                    continue
                arrived[...] = total.astype(bf16)
                source = arrived
            copies[way, piece, step] = pltpu.make_async_remote_copy(
                src_ref=source,
                dst_ref=held.at[way, piece, step],
                send_sem=send_sem.at[way, piece, step],
                recv_sem=recv_sem.at[way, piece, step],
                device_id={"shard": peers[way]},
                device_id_type=pl.DeviceIdType.MESH,
            )
            copies[way, piece, step].start()
    for copy in copies.values():
        copy.wait_send()


def ring_scatter(terms):
    shards, _, rows, width = terms.shape
    pieces = 2 if rows % 32 == 0 else 1
    sems = pltpu.SemaphoreType.DMA((2, pieces, shards - 1))
    return pl.pallas_call(
        ring_scatter_kernel,
        in_specs=[pl.BlockSpec(memory_space=pltpu.VMEM)],
        out_specs=pl.BlockSpec(memory_space=pltpu.VMEM),
        out_shape=jax.ShapeDtypeStruct((2, rows, width), bf16),
        scratch_shapes=[
            pltpu.VMEM((2, pieces, shards - 1, rows // pieces, width), bf16),
            sems,
            sems,
        ],
        compiler_params=pltpu.CompilerParams(
            collective_id=1, has_side_effects=True, vmem_limit_bytes=32 << 20
        ),
        cost_estimate=pl.CostEstimate(flops=1 << 20, bytes_accessed=256 << 20, transcendentals=0),
        name="ring_scatter",
    )(terms)


def scatter_weight(terms):
    blocks = terms.reshape(lax.axis_size("shard"), -1, *terms.shape[-3:])
    return lax.psum_scatter(
        blocks.reshape(-1, *terms.shape[-2:]), "shard", scatter_dimension=0, tiled=True
    ).reshape(terms.shape[-3:])


def body(
    tokens,
    cotangent,
    cond,
    seq_lengths,
    stream_mask,
    w_mod,
    m_mod,
    v_mod,
    w_qkv,
    m_qkv,
    v_qkv,
    w_out,
    m_out,
    v_out,
    w_fc1,
    m_fc1,
    v_fc1,
    w_fc2,
    m_fc2,
    v_fc2,
    gains,
    m_gains,
    v_gains,
):
    tok_rows, model_width = tokens.shape
    slot_count = seq_lengths.shape[0]
    reps, shards = lax.axis_size("rep"), lax.axis_size("shard")
    rep_index, shard_index = lax.axis_index("rep"), lax.axis_index("shard")
    device_index = rep_index * shards + shard_index
    all_tokens = tok_rows * reps * shards
    reach = (MAXLEN - 2) // tok_rows + 1
    part_width = model_width // reps
    part_rows = w_mod.shape[1]
    mod_cols = w_mod.shape[2]

    seq_starts = jnp.cumsum(seq_lengths) - seq_lengths
    local_pos = device_index * tok_rows + jnp.arange(tok_rows, dtype=jnp.int32)
    seq_ids = segment_index(local_pos, seq_starts, all_tokens)
    image_col = (stream_mask == 1)[:, None]
    image_group = jnp.concatenate(gather_rep(stream_mask)) == 1
    image = image_group[:, None].astype(jnp.int32)
    text_group = ~image_group.reshape(reps, tok_rows)
    text_first = jnp.argmax(text_group, axis=1).astype(jnp.int32)
    spots = jnp.concatenate(
        [
            jnp.minimum(text_first // 16 * 16, tok_rows - WINDOW),
            jnp.any(text_group, axis=1).astype(jnp.int32),
            rep_index[None].astype(jnp.int32),
        ]
    )

    silu_cond = jax.nn.silu(cond).astype(bf16)
    cond_rows = lax.dynamic_slice_in_dim(silu_cond, shard_index * part_rows, part_rows, 1)
    mod_terms = jnp.concatenate(
        [
            jnp.dot(cond_rows, w_mod[s].astype(bf16), preferred_element_type=f32)
            for s in range(2)
        ],
        axis=0,
    ).astype(bf16)
    device_count = reps * shards
    firsts = segment_index(
        jnp.arange(device_count, dtype=jnp.int32) * tok_rows, seq_starts, all_tokens
    )
    seconds = jnp.minimum(firsts + 1, slot_count - 1)
    stream_offset = jnp.arange(2, dtype=jnp.int32) * slot_count
    wanted = jnp.stack([firsts, seconds], axis=1)[:, :, None] + stream_offset
    hot = (wanted.reshape(-1, 1) == jnp.arange(2 * slot_count, dtype=jnp.int32)).astype(bf16)
    mod_sent = jnp.dot(hot, mod_terms, preferred_element_type=f32).astype(bf16)
    mod_got = lax.all_to_all(
        mod_sent.reshape(device_count, 4, mod_cols), ("rep", "shard"), 0, 0, tiled=True
    )
    mod_sum = jnp.sum(mod_got.reshape(reps, shards, 4, mod_cols).astype(f32), axis=1).astype(bf16)
    mod_rows = jnp.concatenate([mod_sum[r] for r in range(reps)], axis=1)

    qkv_low = w_qkv.astype(bf16)
    chunks = [
        over_rep(
            qkv_low[:, :, i * part_width : (i + 1) * part_width],
            lambda r, i=i: (3 * r + i) % reps,
        )
        for i in range(3)
    ]
    turns = rep_index % 3

    def rolled(parts, amount):
        return [
            jnp.where(
                amount == 0,
                parts[t],
                jnp.where(amount == 1, parts[(t + 1) % 3], parts[(t + 2) % 3]),
            )
            for t in range(3)
        ]

    qkv_weights = gather_weight(jnp.concatenate(rolled(chunks, turns), axis=2))
    first_seq = seq_ids[0]
    second_seq = jnp.minimum(first_seq + 1, slot_count - 1)
    is_second = (seq_ids != first_seq)[:, None]

    def mod_block(index):
        span = slice(index * model_width, (index + 1) * model_width)
        rows = mod_rows[:, span].astype(f32)
        pick = [jnp.where(is_second, rows[2 + s][None], rows[s][None]) for s in range(2)]
        return jnp.where(image_col, pick[0], pick[1])

    shift_one, scale_one, gate_one, shift_two, scale_two, gate_two = [
        mod_block(i) for i in range(6)
    ]
    stream_in = tokens.astype(f32)
    back_out = cotangent.astype(f32)
    act_one = layer_modulate(stream_in, shift_one, scale_one).astype(bf16)
    act_one_group = jnp.concatenate(gather_rep(act_one))
    d_down = (gate_two * back_out).astype(bf16)
    d_down_group = jnp.concatenate(gather_rep(d_down))

    fc1_low, act_one_group = lax.optimization_barrier((w_fc1.astype(bf16), act_one_group))
    (fc1_weights,) = ring_gather(fc1_low)
    act_one_group, fc1_weights = lax.optimization_barrier((act_one_group, fc1_weights))

    query_sent, pair_sent, qk_pre = qkv_product(spots, act_one_group, qkv_weights, image, gains)
    out_low, fc2_low, pair_sent = lax.optimization_barrier(
        (w_out.astype(bf16), w_fc2.astype(bf16), pair_sent)
    )
    out_turned, fc2_turned = turn(out_low), turn(fc2_low)

    bunch = 2 * reps
    bunches = shards // bunch
    half_width = part_width // 2
    groups = [[q * bunch + i for i in range(bunch)] for q in range(bunches)]

    def exchange(value):
        return lax.all_to_all(
            value, "shard", 0, 0, axis_index_groups=None if bunches == 1 else groups, tiled=True
        )

    stretch_count = reps * bunches
    stretch_rows = bunch * tok_rows
    halo = reach * tok_rows

    def stretch_shift(value, steps):
        def place(stretch, g):
            return (stretch % bunches) * bunch + (stretch // bunches) * 2 + g

        pairs = [
            (place(t, g), place(t + steps, g))
            for t in range(stretch_count)
            for g in range(2)
            if 0 <= t + steps < stretch_count
        ]
        return lax.ppermute(value, "shard", pairs)

    pair_own = exchange(pair_sent).reshape(stretch_rows, 2 * half_width)
    query_sent, pair_own = lax.optimization_barrier((query_sent, pair_own))
    query_own = exchange(query_sent).reshape(stretch_rows, half_width)
    out_turned, fc2_turned, query_own = lax.optimization_barrier(
        (out_turned, fc2_turned, query_own)
    )
    out_weights = gather_turned(out_turned)
    fc2_weights = gather_turned(fc2_turned)
    pair_before = stretch_shift(pair_own[-halo:], 1)
    pair_after = stretch_shift(pair_own[:halo], -1)
    window_rows = stretch_rows + 2 * halo
    stretch = ((shard_index % bunch) // 2) * bunches + shard_index // bunch
    stretch_first = stretch * stretch_rows
    qid = segment_index(
        stretch_first + jnp.arange(stretch_rows, dtype=jnp.int32), seq_starts, all_tokens
    )
    kid = segment_index(
        stretch_first - halo + jnp.arange(window_rows, dtype=jnp.int32), seq_starts, all_tokens
    )
    seq_ends = seq_starts + seq_lengths
    low_pos = seq_starts[qid[::QB]] - (stretch_first - halo)
    high_pos = seq_ends[qid[QB - 1 :: QB]] - (stretch_first - halo)
    lo = jnp.clip(low_pos // KB, 0, window_rows // KB).astype(jnp.int32)
    hi = jnp.clip((high_pos + KB - 1) // KB, 0, window_rows // KB).astype(jnp.int32)
    attended_own, logsum = attention(
        query_own, pair_own, pair_before, pair_after, lo, hi, qid, kid
    )
    attended_came = exchange(attended_own.reshape(bunch, tok_rows, half_width))

    def split_group(value):
        return [value[p * tok_rows : (p + 1) * tok_rows] for p in range(reps)]

    branch_terms, attended_low = forward_product(
        spots, attended_came, out_weights, image, gathers=True
    )
    branch = reduce_rep(split_group(branch_terms))
    mid = stream_in + gate_one * branch
    act_two = layer_modulate(mid, shift_two, scale_two).astype(bf16)
    act_two_group = jnp.concatenate(gather_rep(act_two))
    gelu_low, gelu_slope = forward_product(spots, act_two_group, fc1_weights, image, gelu=True)
    down_terms = forward_product(spots, gelu_low, fc2_weights, image)[0]

    fc2_terms = gradient(spots, gelu_low, d_down_group, image, fc2_weights.shape)
    fc2_terms, gelu_slope = lax.optimization_barrier((fc2_terms, gelu_slope))
    fc2_own = scatter_weight(fc2_terms)
    d_up = backward_product(spots, d_down_group, fc2_weights, image, factor=gelu_slope)
    d_act_two = reduce_rep(split_group(backward_product(spots, d_up, fc1_weights, image)))
    d_mid_norm, d_shift_two, d_scale_two = jax.vjp(layer_modulate, mid, shift_two, scale_two)[1](
        d_act_two
    )
    d_mid = back_out + d_mid_norm
    d_branch = (gate_one * d_mid).astype(bf16)
    fc1_terms = gradient(spots, act_two_group, d_up, image, fc1_weights.shape)
    fc1_terms, d_branch = lax.optimization_barrier((fc1_terms, d_branch))
    g_fc1 = scatter_weight(fc1_terms)
    d_gate_one = d_mid * branch
    d_branch_group = jnp.concatenate(gather_rep(d_branch))
    d_attended = backward_product(spots, d_branch_group, out_weights, image, packs=True)
    out_terms = gradient(spots, attended_low, d_branch_group, image, out_weights.shape)
    out_came = lax.all_to_all(
        out_terms.reshape(shards, -1, out_terms.shape[-1]), "shard", 0, 0, tiled=True
    )
    d_attended_own = exchange(d_attended).reshape(stretch_rows, half_width)
    d_query_own, d_before, d_after, d_pair_own = attention_back(
        query_own,
        pair_own,
        pair_before,
        pair_after,
        d_attended_own,
        attended_own,
        lo,
        hi,
        qid,
        kid,
        logsum,
    )
    d_query_came = exchange(d_query_own.reshape(bunch, tok_rows, half_width))
    from_later = stretch_shift(d_before, -1).astype(f32)
    from_earlier = stretch_shift(d_after, 1).astype(f32)
    rest = jnp.zeros((stretch_rows - halo, 2 * half_width), f32)
    d_pair_own = (
        d_pair_own
        + jnp.concatenate([rest, from_later], axis=0)
        + jnp.concatenate([from_earlier, rest], axis=0)
    )
    d_pair_own, out_came = lax.optimization_barrier((d_pair_own, out_came))
    g_out = turn(jnp.sum(out_came.astype(f32), axis=0).astype(bf16).reshape(w_out.shape))
    d_pair_came = exchange(d_pair_own.astype(bf16).reshape(bunch, tok_rows, 2 * half_width))
    d_pair_came, down_terms = lax.optimization_barrier((d_pair_came, down_terms))
    down_proj = reduce_rep(split_group(down_terms))
    output = mid + gate_two * down_proj
    d_gate_two = back_out * down_proj
    d_qkv, gain_sums = norm_back(spots, d_query_came, d_pair_came, qk_pre, image, gains)
    d_act_one = reduce_rep(split_group(backward_product(spots, d_qkv, qkv_weights, image)))
    qkv_terms = gradient(spots, act_one_group, d_qkv, image, qkv_weights.shape)
    d_in_norm, d_shift_one, d_scale_one = jax.vjp(layer_modulate, stream_in, shift_one, scale_one)[
        1
    ](d_act_one)
    d_tokens = d_mid + d_in_norm
    d_mod_tok = jnp.concatenate(
        [d_shift_one, d_scale_one, d_gate_one, d_shift_two, d_scale_two, d_gate_two], axis=1
    )
    image_flag = image_col[:, 0]
    second_flag = is_second[:, 0]
    selector = jnp.stack(
        [
            ~second_flag & image_flag,
            ~second_flag & ~image_flag,
            second_flag & image_flag,
            second_flag & ~image_flag,
        ],
        axis=1,
    ).astype(f32)
    pooled = jnp.einsum("tp,te->pe", selector, d_mod_tok, precision=lax.Precision.HIGHEST)
    gain_sums = jnp.sum(gain_sums.reshape(2, 2, part_width // HD, HD), axis=2)
    gain_part = jnp.concatenate([gain_sums[0], gain_sums[1]], axis=1)
    gain_rows = jnp.concatenate([gain_part, jnp.zeros_like(gain_part)], axis=0)
    leaving = jnp.stack(
        [
            jnp.concatenate([pooled[:, r * mod_cols : (r + 1) * mod_cols], gain_rows], axis=1)
            for r in range(reps)
        ]
    )
    qkv_terms, g_fc1, fc2_own, leaving = lax.optimization_barrier(
        (qkv_terms, g_fc1, fc2_own, leaving)
    )
    leaving = jnp.broadcast_to(leaving[:, None], (reps, shards, *leaving.shape[1:]))
    came = lax.all_to_all(
        leaving.reshape(device_count, *leaving.shape[2:]), ("rep", "shard"), 0, 0, tiled=True
    )
    g_fc2 = turn(fc2_own)
    g_qkv_group = ring_scatter(qkv_terms)
    g_qkv_group, came = lax.optimization_barrier((g_qkv_group, came))
    g_parts = [
        g_qkv_group[:, :, t * part_width : (t + 1) * part_width] for t in range(3)
    ]
    g_parts = rolled(g_parts, (3 - turns) % 3)
    g_qkv = jnp.concatenate(
        [over_rep(g_parts[i], lambda d, i=i: (3 * (d - i)) % reps) for i in range(3)], axis=2
    )

    g_gains = jnp.sum(came[:, :2, mod_cols:], axis=0)
    came = came[:, :, :mod_cols].reshape(2 * device_count, 2, mod_cols)
    seqs = jnp.stack([firsts, seconds], axis=1).reshape(-1)
    hot_seq = (seqs[:, None] == jnp.arange(slot_count, dtype=jnp.int32)).astype(bf16)
    cond_seq = jnp.dot(hot_seq, cond_rows, preferred_element_type=f32)
    g_mod = jnp.stack(
        [
            lax.dot_general(
                cond_seq,
                came[:, s],
                (((0,), (0,)), ((), ())),
                precision=lax.Precision.HIGHEST,
                preferred_element_type=f32,
            )
            for s in range(2)
        ]
    )
    up_mod = adam_step(w_mod, m_mod, v_mod, g_mod, rate_mod)
    up_qkv = adam_step(w_qkv, m_qkv, v_qkv, g_qkv.astype(f32), rate_qkv)
    up_out = adam_step(w_out, m_out, v_out, g_out.astype(f32), rate_out)
    up_fc1 = adam_step(w_fc1, m_fc1, v_fc1, g_fc1.astype(f32), rate_fc1)
    up_fc2 = adam_step(w_fc2, m_fc2, v_fc2, g_fc2.astype(f32), rate_fc2)
    up_gains = adam_step(gains, m_gains, v_gains, g_gains, rate_gains)
    return (
        output.astype(bf16),
        d_tokens,
        *up_mod,
        *up_qkv,
        *up_out,
        *up_fc1,
        *up_fc2,
        *up_gains[:3],
    )


def solution(mesh):
    rows = P(("rep", "shard"), None)
    held = P(None, "shard", "rep")
    return jax.shard_map(
        body,
        mesh=mesh,
        in_specs=(rows, rows, P(), P(), P(("rep", "shard")), *([held] * 15), P(), P(), P()),
        out_specs=(rows, rows, *([held] * 20), P(), P(), P()),
        check_vma=False,
    )
```

```python
import functools

import jax
import jax.numpy as jnp
from jax import lax
from jax.experimental import pallas as pl
from jax.experimental.pallas import tpu as pltpu
from jax.sharding import PartitionSpec as P

HD = 64
MAXLEN = 1178
STEP = 7

norm_eps = 1e-06
adam_eps = 1e-08
score_scale = 0.125
rate_mod = 0.03
rate_qkv = 0.03
rate_out = 0.15
rate_fc1 = 0.03
rate_fc2 = 0.015
rate_gains = 1.0

bf16 = jnp.bfloat16
f32 = jnp.float32
QB = 256
KB = 256
TXT = 154
WINDOW = (TXT + 15 + 15) // 16 * 16
COLS = 512
GELU_A = 0.7978845608028654
GELU_B = 0.044715
NN = (((1,), (0,)), ((), ()))
NT = (((1,), (1,)), ((), ()))
TN = (((0,), (0,)), ((), ()))


def layer_modulate(values, shift, scale):
    centred = values - jnp.mean(values, axis=-1, keepdims=True)
    normed = centred * lax.rsqrt(jnp.mean(centred * centred, axis=-1, keepdims=True) + norm_eps)
    return normed * (1.0 + scale) + shift


def adam_step(weight, moment_one, moment_two, grads, rate):
    new_one = 0.9 * moment_one + 0.1 * grads
    new_two = 0.999 * moment_two + 0.001 * grads * grads
    fixed_one = new_one / (1.0 - 0.9**STEP)
    fixed_two = new_two / (1.0 - 0.999**STEP)
    new_weight = weight - rate * (fixed_one / (jnp.sqrt(fixed_two) + adam_eps) + 0.01 * weight)
    return (new_weight, new_one, new_two, new_weight.astype(bf16))


def segment_index(position, seq_starts, all_tokens):
    counted = jnp.sum((seq_starts[None, :] <= position[:, None]).astype(jnp.int32), axis=1) - 1
    inside = (position >= 0) & (position < all_tokens)
    return jnp.where(inside, counted, -1)


def fill_window(own_ref, before_ref, after_ref, keys, values):
    halo, own = before_ref.shape[0], own_ref.shape[0]
    heads = keys.shape[0]
    width = heads * HD
    parts = ((before_ref, 0, halo), (own_ref, halo, own), (after_ref, halo + own, halo))
    for source, first, count in parts:
        for head in range(heads):
            for index, dest in ((0, keys), (1, values)):
                start = index * width + head * HD
                dest[head, first : first + count, :HD] = source[:, start : start + HD]


def attend_kernel(
    lo_ref, hi_ref, q_ref, own_ref, before_ref, after_ref, qid_ref, kid_ref, o_ref, l_ref, keys, values, acc
):
    step = pl.program_id(0)
    heads = keys.shape[0]

    @pl.when(step == 0)
    def _():
        lane = lax.broadcasted_iota(jnp.int32, values.shape[1:], 1)
        for head in range(heads):
            values[head] = (lane == HD).astype(bf16)
        fill_window(own_ref, before_ref, after_ref, keys, values)

    qid = qid_ref[...]
    diagonal = lax.broadcasted_iota(jnp.int32, (QB, QB), 0) == lax.broadcasted_iota(
        jnp.int32, (QB, QB), 1
    )
    queries = [q_ref[:, head * HD : (head + 1) * HD] for head in range(heads)]
    acc[...] = jnp.zeros_like(acc)

    @pl.loop(lo_ref[step], hi_ref[step])
    def _(block):
        rows = pl.ds(pl.multiple_of(block * KB, KB), KB)
        same = qid == kid_ref[pl.ds(block, 1), :]
        for head in range(heads):
            scores = lax.dot_general(
                queries[head], keys[head, rows, :], NT, preferred_element_type=f32
            )
            lifted = jnp.where(same, jnp.exp(scores), 0.0).astype(bf16)
            acc[head] += jnp.dot(lifted, values[head, rows, :], preferred_element_type=f32)

    for head in range(heads):
        total = acc[head, :, HD : HD + 1]
        o_ref[:, head * HD : (head + 1) * HD] = (acc[head, :, :HD] / total).astype(bf16)
        l_ref[0, head : head + 1, :] = jnp.sum(
            jnp.where(diagonal, jnp.log(total), 0.0), axis=0, keepdims=True
        )


def attend_back_kernel(
    lo_ref,
    hi_ref,
    q_ref,
    own_ref,
    before_ref,
    after_ref,
    do_ref,
    o_ref,
    qid_ref,
    kid_ref,
    l_ref,
    dq_ref,
    d_before_ref,
    d_after_ref,
    d_own_ref,
    keys,
    values,
    d_keys,
    d_values,
    d_query,
):
    step = pl.program_id(0)
    heads = keys.shape[0]
    width = heads * HD

    @pl.when(step == 0)
    def _():
        fill_window(own_ref, before_ref, after_ref, keys, values)
        d_keys[...] = jnp.zeros_like(d_keys)
        d_values[...] = jnp.zeros_like(d_values)

    qid = qid_ref[0]
    ones = jnp.ones((8, HD), bf16)
    queries, outs, dots = [], [], []
    for head in range(heads):
        lanes = slice(head * HD, (head + 1) * HD)
        queries.append(q_ref[:, lanes])
        outs.append(do_ref[:, lanes])
        product = outs[head].astype(f32) * o_ref[:, lanes].astype(f32)
        coarse = product.astype(bf16)
        fine = (product - coarse.astype(f32)).astype(bf16)
        total = lax.dot_general(ones, coarse, NT, preferred_element_type=f32)
        dots.append((total + lax.dot_general(ones, fine, NT, preferred_element_type=f32))[:1])
    d_query[...] = jnp.zeros_like(d_query)

    @pl.loop(lo_ref[step], hi_ref[step])
    def _(block):
        rows = pl.ds(pl.multiple_of(block * KB, KB), KB)
        same = kid_ref[rows, :] == qid
        for head in range(heads):
            key = keys[head, rows, :]
            scores = lax.dot_general(key, queries[head], NT, preferred_element_type=f32)
            probs = jnp.where(same, jnp.exp(scores - l_ref[0, head : head + 1, :]), 0.0)
            d_values[head, rows, :] += jnp.dot(
                probs.astype(bf16), outs[head], preferred_element_type=f32
            )
            d_probs = lax.dot_general(
                values[head, rows, :], outs[head], NT, preferred_element_type=f32
            )
            d_scores = (probs * (d_probs - dots[head])).astype(bf16)
            d_keys[head, rows, :] += jnp.dot(d_scores, queries[head], preferred_element_type=f32)
            d_query[head] += lax.dot_general(d_scores, key, TN, preferred_element_type=f32)

    for head in range(heads):
        dq_ref[:, head * HD : (head + 1) * HD] = (d_query[head] * score_scale).astype(bf16)

    @pl.when(step == pl.num_programs(0) - 1)
    def _():
        halo, own = d_before_ref.shape[0], d_own_ref.shape[0]
        for index, source in ((0, d_keys), (1, d_values)):
            for head in range(heads):
                span = slice(index * width + head * HD, index * width + (head + 1) * HD)
                d_before_ref[:, span] = source[head, :halo, :].astype(bf16)
                d_own_ref[:, span] = source[head, halo : halo + own, :]
                d_after_ref[:, span] = source[head, halo + own :, :].astype(bf16)


def resident(shape):
    return pl.BlockSpec(shape, lambda *index: (0,) * len(shape))


def attention(query, own, before, after, lo, hi, qid, kid):
    count, width = query.shape
    heads = width // HD
    window = count + 2 * before.shape[0]
    steps = count // QB
    return pl.pallas_call(
        attend_kernel,
        grid_spec=pltpu.PrefetchScalarGridSpec(
            num_scalar_prefetch=2,
            grid=(steps,),
            in_specs=[
                pl.BlockSpec((QB, width), lambda i, lo, hi: (i, 0)),
                resident(own.shape),
                resident(before.shape),
                resident(after.shape),
                pl.BlockSpec((QB, 1), lambda i, lo, hi: (i, 0)),
                resident((window // KB, KB)),
            ],
            out_specs=[
                pl.BlockSpec((QB, width), lambda i, lo, hi: (i, 0)),
                pl.BlockSpec((1, 8, QB), lambda i, lo, hi: (i, 0, 0)),
            ],
            scratch_shapes=[
                pltpu.VMEM((heads, window, HD), bf16),
                pltpu.VMEM((heads, window, 2 * HD), bf16),
                pltpu.VMEM((heads, QB, 2 * HD), f32),
            ],
        ),
        out_shape=[
            jax.ShapeDtypeStruct((count, width), bf16),
            jax.ShapeDtypeStruct((steps, 8, QB), f32),
        ],
        compiler_params=pltpu.CompilerParams(vmem_limit_bytes=40 << 20),
        cost_estimate=pl.CostEstimate(flops=1 << 30, bytes_accessed=4 << 20, transcendentals=0),
        name="attend",
    )(lo, hi, query, own, before, after, qid[:, None], kid.reshape(window // KB, KB))


def attention_back(query, own, before, after, d_out, out, lo, hi, qid, kid, logsum):
    count, width = query.shape
    heads = width // HD
    halo = before.shape[0]
    window = count + 2 * halo
    steps = count // QB
    rows = pl.BlockSpec((QB, width), lambda i, lo, hi: (i, 0))
    return pl.pallas_call(
        attend_back_kernel,
        grid_spec=pltpu.PrefetchScalarGridSpec(
            num_scalar_prefetch=2,
            grid=(steps,),
            in_specs=[
                rows,
                resident(own.shape),
                resident(before.shape),
                resident(after.shape),
                rows,
                rows,
                pl.BlockSpec((1, 1, QB), lambda i, lo, hi: (i, 0, 0)),
                resident((window, 1)),
                pl.BlockSpec((1, 8, QB), lambda i, lo, hi: (i, 0, 0)),
            ],
            out_specs=[
                rows,
                resident((halo, 2 * width)),
                resident((halo, 2 * width)),
                resident((count, 2 * width)),
            ],
            scratch_shapes=[pltpu.VMEM((heads, window, HD), bf16)] * 2
            + [pltpu.VMEM((heads, window, HD), f32)] * 2
            + [pltpu.VMEM((heads, QB, HD), f32)],
        ),
        out_shape=[
            jax.ShapeDtypeStruct((count, width), bf16),
            jax.ShapeDtypeStruct((halo, 2 * width), bf16),
            jax.ShapeDtypeStruct((halo, 2 * width), bf16),
            jax.ShapeDtypeStruct((count, 2 * width), f32),
        ],
        compiler_params=pltpu.CompilerParams(vmem_limit_bytes=58 << 20),
        cost_estimate=pl.CostEstimate(flops=24 << 30, bytes_accessed=8 << 20, transcendentals=0),
        name="attend_back",
    )(lo, hi, query, own, before, after, d_out, out, qid.reshape(steps, 1, QB), kid[:, None], logsum)


def text_windows(spots, blocks, count, work):
    for p in range(blocks):

        @pl.when(spots[blocks + p] == 1)
        def _(p=p):
            first = pl.multiple_of(spots[p], 16)
            base = p * (count // blocks)
            work(p, first, pl.ds(pl.multiple_of(base + first, 16), WINDOW))


def flat(value):
    return value.reshape(-1, value.shape[-1])


def product(x_ref, rows, weight, dims):
    total = None
    for cols, get in weight:
        term = lax.dot_general(x_ref[rows, cols], get(), dims, preferred_element_type=f32)
        total = term if total is None else total + term
    return total


def group_sums(values, blocks_of):
    coarse = values.astype(bf16)
    fine = (values - coarse.astype(f32)).astype(bf16)
    return jnp.dot(coarse, blocks_of, preferred_element_type=f32) + jnp.dot(
        fine, blocks_of, preferred_element_type=f32
    )


def head_blocks(width):
    row = lax.broadcasted_iota(jnp.int32, (width, width), 0) // HD
    col = lax.broadcasted_iota(jnp.int32, (width, width), 1) // HD
    return (row == col).astype(bf16)


def qkv_kernel(blocks, spots, x_ref, w0, w1, image_ref, gain_ref, q_ref, kv_ref, pre_ref):
    kind = pl.program_id(0)
    every = slice(None)
    size, width = q_ref.shape[1:]
    rep = spots[2 * blocks]
    spread = head_blocks(2 * width)

    def finish(t, values, gain):
        if t < 2:
            mean = group_sums(values * values, spread) * (1.0 / HD)
            values = values * lax.rsqrt(mean + norm_eps) * gain
        values = values.astype(bf16)
        return values * jnp.asarray(score_scale, bf16) if t == 0 else values

    for t in range(3):

        @pl.when(kind == t)
        def _(t=t):
            packed_ref = kv_ref if t else q_ref
            lanes = slice((t - 1) * width, t * width) if t else slice(0, width)

            @pl.loop(0, blocks)
            def _(p):
                rows = pl.ds(pl.multiple_of(p * size, size), size)
                values = product(x_ref, rows, [(every, lambda: flat(w0[...]))], NN)
                if t < 2:
                    pre_ref[rows, :] = values
                values = finish(t, values, gain_ref[0, :1])
                for g in range(2):
                    packed_ref[pl.ds((rep ^ p) * 2 + g, 1), :, lanes] = values[
                        :, g * width : (g + 1) * width
                    ][None]

            def text(p, first, rows):
                values = product(x_ref, rows, [(every, lambda: flat(w1[...]))], NN)
                image = image_ref[rows, :] == 1
                if t < 2:
                    pre_ref[rows, :] = jnp.where(image, pre_ref[rows, :], values)
                values = finish(t, values, gain_ref[0, 1:])
                for g in range(2):
                    place = (
                        pl.ds((rep ^ p) * 2 + g, 1),
                        pl.ds(first, WINDOW),
                        lanes,
                    )
                    packed_ref[place] = jnp.where(
                        image[None], packed_ref[place], values[:, g * width : (g + 1) * width][None]
                    )

            text_windows(spots, blocks, x_ref.shape[0], text)


def column_weights(weight, tile):
    shards, _, rows, _ = weight.shape
    return [
        pl.BlockSpec((shards, 1, rows, tile), lambda j, s, stream=stream: (0, stream, 0, j))
        for stream in range(2)
    ]


def tiled_gains(gains, heads):
    return jnp.stack([jnp.tile(gains[:, :HD], (1, heads)), jnp.tile(gains[:, HD:], (1, heads))])


def qkv_product(spots, x, weight, image, gains):
    count, depth = x.shape
    blocks = (spots.shape[0] - 1) // 2
    part = weight.shape[3] // 3
    size = count // blocks
    return pl.pallas_call(
        functools.partial(qkv_kernel, blocks),
        grid_spec=pltpu.PrefetchScalarGridSpec(
            num_scalar_prefetch=1,
            grid=(3,),
            in_specs=[
                resident(x.shape),
                *column_weights(weight, part),
                resident(image.shape),
                pl.BlockSpec((1, 2, part), lambda j, s: (jnp.minimum(j, 1), 0, 0)),
            ],
            out_specs=[
                resident((2 * blocks, size, part // 2)),
                resident((2 * blocks, size, part)),
                pl.BlockSpec((count, part), lambda j, s: (0, jnp.minimum(j, 1))),
            ],
        ),
        out_shape=[
            jax.ShapeDtypeStruct((2 * blocks, size, part // 2), bf16),
            jax.ShapeDtypeStruct((2 * blocks, size, part), bf16),
            jax.ShapeDtypeStruct((count, 2 * part), f32),
        ],
        compiler_params=pltpu.CompilerParams(vmem_limit_bytes=40 << 20),
        cost_estimate=pl.CostEstimate(flops=1 << 30, bytes_accessed=4 << 20, transcendentals=0),
        name="qkv_product",
    )(spots, x, weight, weight, image, tiled_gains(gains, part // HD))


def norm_back_kernel(blocks, spots, q_ref, kv_ref, pre_ref, image_ref, gain_ref, out_ref, sum_ref, both):
    @pl.when(pl.program_id(0) == 0)
    def _():
        sum_ref[...] = jnp.zeros_like(sum_ref)

    part = both.shape[1]
    width = part // 2
    image = image_ref[...] == 1
    spread = head_blocks(part)
    for t in range(3):
        came_ref = kv_ref if t else q_ref
        lanes = slice((t - 1) * width, t * width) if t else slice(0, width)
        for g in range(2):
            both[:, g * width : (g + 1) * width] = came_ref[g, :, lanes].astype(f32)
        grad = both[...]
        if t < 2:
            pre = pre_ref[:, t * part : (t + 1) * part]
            scale = lax.rsqrt(group_sums(pre * pre, spread) * (1.0 / HD) + norm_eps)
            gain = jnp.where(image, gain_ref[t, :1], gain_ref[t, 1:])
            each = grad * pre * scale
            total = jnp.sum(each, axis=0, keepdims=True)
            text = jnp.sum(jnp.where(image, 0.0, each), axis=0, keepdims=True)
            sum_ref[2 * t : 2 * t + 1, :] += total - text
            sum_ref[2 * t + 1 : 2 * t + 2, :] += text
            grad = grad * gain
            mean = group_sums(grad * pre, spread) * (1.0 / HD)
            grad = scale * (grad - pre * (scale * scale * mean))
        out_ref[:, t * part : (t + 1) * part] = grad.astype(bf16)


def norm_back(spots, came_query, came_pair, pre, image, gains):
    blocks = (spots.shape[0] - 1) // 2
    _, size, part = came_pair.shape
    tiled = tiled_gains(gains, part // HD)
    return pl.pallas_call(
        functools.partial(norm_back_kernel, blocks),
        grid_spec=pltpu.PrefetchScalarGridSpec(
            num_scalar_prefetch=1,
            grid=(blocks,),
            in_specs=[
                pl.BlockSpec((2, size, part // 2), lambda p, s: (s[2 * blocks] ^ p, 0, 0)),
                pl.BlockSpec((2, size, part), lambda p, s: (s[2 * blocks] ^ p, 0, 0)),
                pl.BlockSpec((size, 2 * part), lambda p, s: (p, 0)),
                pl.BlockSpec((size, 1), lambda p, s: (p, 0)),
                resident(tiled.shape),
            ],
            out_specs=[
                pl.BlockSpec((size, 3 * part), lambda p, s: (p, 0)),
                resident((4, part)),
            ],
            scratch_shapes=[pltpu.VMEM((size, part), f32)],
        ),
        out_shape=[
            jax.ShapeDtypeStruct((blocks * size, 3 * part), bf16),
            jax.ShapeDtypeStruct((4, part), f32),
        ],
        compiler_params=pltpu.CompilerParams(vmem_limit_bytes=32 << 20),
        cost_estimate=pl.CostEstimate(flops=4 << 30, bytes_accessed=12 << 20, transcendentals=0),
        name="norm_back",
    )(spots, came_query, came_pair, pre, image, tiled)


def forward_kernel(blocks, gathers, gelu, spots, x_ref, w0, w1, image_ref, *rest):
    rep = spots[2 * blocks]
    out_ref = rest[0]
    if gathers:
        x_out = rest[1]
        size, width = x_ref.shape[1:]

        @pl.when(pl.program_id(0) == 0)
        def _():
            for p in range(blocks):
                for g in range(2):
                    x_out[p * size : (p + 1) * size, g * width : (g + 1) * width] = x_ref[
                        pl.ds((rep ^ p) * 2 + g, 1)
                    ][0]

        x_ref = x_out
    every = slice(None)
    count = x_ref.shape[0]

    def finish(values):
        if not gelu:
            return (values.astype(bf16),)
        square = values * values
        bend = jnp.tanh(values * (GELU_A + GELU_A * GELU_B * square))
        half = 0.5 * (1.0 + bend)
        slope = half + 0.5 * values * (1.0 - bend * bend) * (GELU_A + 3.0 * GELU_A * GELU_B * square)
        return (values * half).astype(bf16), slope.astype(bf16)

    outs = rest if gelu else (out_ref,)
    chunk = count // (blocks if gelu else 2)

    @pl.loop(0, count // chunk)
    def _(p):
        rows = pl.ds(pl.multiple_of(p * chunk, chunk), chunk)
        values = product(x_ref, rows, [(every, lambda: flat(w0[...]))], NN)
        for out, value in zip(outs, finish(values)):
            out[rows, :] = value

    def text(p, first, rows):
        values = product(x_ref, rows, [(every, lambda: flat(w1[...]))], NN)
        image = image_ref[rows, :] == 1
        for out, value in zip(outs, finish(values)):
            out[rows, :] = jnp.where(image, out[rows, :], value)

    text_windows(spots, blocks, count, text)


def forward_product(spots, x, weight, image, gathers=False, gelu=False):
    blocks = (spots.shape[0] - 1) // 2
    if weight.ndim == 5:
        tiles, q, _, rows, tile = weight.shape
        weights = [
            pl.BlockSpec((1, q, 1, rows, tile), lambda j, s, stream=stream: (j, 0, stream, 0, 0))
            for stream in range(2)
        ]
        depth = q * rows
    else:
        depth, tile = weight.shape[0] * weight.shape[2], COLS
        tiles = weight.shape[3] // tile
        weights = column_weights(weight, tile)
    count = image.shape[0]
    column = pl.BlockSpec((count, tile), lambda j, s: (0, j))
    whole = jax.ShapeDtypeStruct((count, tiles * tile), bf16)
    out_specs, out_shape = [column], [whole]
    if gathers:
        out_specs.append(resident((count, depth)))
        out_shape.append(jax.ShapeDtypeStruct((count, depth), bf16))
    if gelu:
        out_specs.append(column)
        out_shape.append(whole)
    return pl.pallas_call(
        functools.partial(forward_kernel, blocks, gathers, gelu),
        grid_spec=pltpu.PrefetchScalarGridSpec(
            num_scalar_prefetch=1,
            grid=(tiles,),
            in_specs=[resident(x.shape), *weights, resident(image.shape)],
            out_specs=out_specs,
        ),
        out_shape=out_shape,
        compiler_params=pltpu.CompilerParams(vmem_limit_bytes=40 << 20),
        cost_estimate=pl.CostEstimate(
            flops=count * depth // 4 * tiles * tile, bytes_accessed=4 << 20, transcendentals=0
        ),
        name="forward_product",
    )(spots, x, weight, weight, image)


def backward_kernel(blocks, turned, scaled, packs, spots, dy_ref, w0, w1, image_ref, *rest):
    rest = list(rest)
    factor_ref = rest.pop(0) if scaled else None
    out_ref = rest[0]
    if turned:
        tiles, tile = w0.shape[0], w0.shape[4]
        weights = [
            [
                (slice(n * tile, (n + 1) * tile), lambda w=w, n=n: flat(w[n, :, 0]))
                for n in range(tiles)
            ]
            for w in (w0, w1)
        ]
    else:
        every = slice(None)
        weights = [[(every, lambda w=w: flat(w[...]))] for w in (w0, w1)]
    count = dy_ref.shape[0]
    size = count // blocks
    rep = spots[2 * blocks]
    part = pl.program_id(0)

    def finish(rows, values):
        if scaled:
            values = values * factor_ref[rows, :].astype(f32)
        return values.astype(bf16)

    chunk = size if packs or scaled else count // 2

    @pl.loop(0, count // chunk)
    def _(p):
        rows = pl.ds(pl.multiple_of(p * chunk, chunk), chunk)
        values = finish(rows, product(dy_ref, rows, weights[0], NT))
        if packs:
            out_ref[pl.ds((rep ^ p) * 2 + part, 1)] = values[None]
        else:
            out_ref[rows, :] = values

    def text(p, first, rows):
        values = finish(rows, product(dy_ref, rows, weights[1], NT))
        image = image_ref[rows, :] == 1
        if packs:
            place = (pl.ds((rep ^ p) * 2 + part, 1), pl.ds(first, WINDOW), slice(None))
            out_ref[place] = jnp.where(image[None], out_ref[place], values[None])
        else:
            out_ref[rows, :] = jnp.where(image, out_ref[rows, :], values)

    text_windows(spots, blocks, count, text)


def backward_product(spots, dy, weight, image, factor=None, packs=False):
    blocks = (spots.shape[0] - 1) // 2
    turned = weight.ndim == 5
    count = image.shape[0]
    if turned:
        tiles, q, _, rows, tile = weight.shape
        step = q * rows // 2 if packs else min(q * rows, 768)
        grid = (q * rows // step,)
        if rows < step:
            block = (tiles, step // rows, 1, rows, tile)
            weights = [
                pl.BlockSpec(block, lambda j, s, stream=stream: (0, j, stream, 0, 0))
                for stream in range(2)
            ]
        else:
            per = rows // step
            weights = [
                pl.BlockSpec(
                    (tiles, 1, 1, step, tile),
                    lambda j, s, stream=stream: (0, j // per, stream, j % per, 0),
                )
                for stream in range(2)
            ]
        depth = q * rows
    else:
        shards, _, rows, width = weight.shape
        depth = shards * rows
        bunch = max(1, 768 // rows)
        step = bunch * rows
        grid = (depth // step,)
        weights = [
            pl.BlockSpec((bunch, 1, rows, width), lambda j, s, stream=stream: (j, stream, 0, 0))
            for stream in range(2)
        ]
    column = pl.BlockSpec((count, step), lambda j, s: (0, j))
    in_specs = [resident(dy.shape), *weights, resident(image.shape)]
    operands = [spots, dy, weight, weight, image]
    if factor is not None:
        in_specs.append(column)
        operands.append(factor)
    if packs:
        shape = (2 * blocks, count // blocks, step)
        out_spec, out_shape = resident(shape), jax.ShapeDtypeStruct(shape, bf16)
    else:
        out_spec, out_shape = column, jax.ShapeDtypeStruct((count, depth), bf16)
    return pl.pallas_call(
        functools.partial(backward_kernel, blocks, turned, factor is not None, packs),
        grid_spec=pltpu.PrefetchScalarGridSpec(
            num_scalar_prefetch=1,
            grid=grid,
            in_specs=in_specs,
            out_specs=out_spec,
        ),
        out_shape=out_shape,
        compiler_params=pltpu.CompilerParams(vmem_limit_bytes=48 << 20),
        cost_estimate=pl.CostEstimate(
            flops=count * depth // 4 * dy.shape[1], bytes_accessed=4 << 20, transcendentals=0
        ),
        name="backward_product",
    )(*operands)


def gradient_kernel(blocks, spots, x_ref, dy_ref, image_ref, *rest):
    *outs, turned_x, masked, acc = rest
    count, width = dy_ref.shape
    size = count // blocks
    cols_at_once = acc.shape[1]

    @pl.when(pl.program_id(0) == 0)
    def _():
        @pl.loop(0, blocks)
        def _(p):
            rows = pl.ds(pl.multiple_of(p * size, size), size)
            kept = dy_ref[rows, :]
            masked[rows, :] = jnp.where(image_ref[rows, :] == 1, kept, jnp.zeros_like(kept))

    turned_x[...] = x_ref[...].T

    def store(stream, n, values):
        values = values.astype(bf16)
        out = outs[min(stream, len(outs) - 1)]
        stream = stream if len(outs) == 1 else 0
        if len(out.shape) == 5:
            tile, per = out.shape[4], out.shape[3]
            for t in range(cols_at_once // tile):
                for q in range(out.shape[1]):
                    out[n * (cols_at_once // tile) + t, q, stream] = values[
                        q * per : (q + 1) * per, t * tile : (t + 1) * tile
                    ]
        else:
            per = out.shape[2]
            for k in range(out.shape[0]):
                out[k, stream, :, n * cols_at_once : (n + 1) * cols_at_once] = values[
                    k * per : (k + 1) * per
                ]

    for n in range(width // cols_at_once):
        cols = slice(n * cols_at_once, (n + 1) * cols_at_once)
        store(0, n, jnp.dot(turned_x[...], masked[:, cols], preferred_element_type=f32))
        acc[...] = jnp.zeros_like(acc)

        def text(p, first, rows, cols=cols):
            kept = dy_ref[rows, cols]
            kept = jnp.where(image_ref[rows, :] == 1, jnp.zeros_like(kept), kept)
            acc[...] += lax.dot_general(x_ref[rows, :], kept, TN, preferred_element_type=f32)

        text_windows(spots, blocks, count, text)
        store(1, n, acc[...])


def gradient(spots, x, dy, image, shape, split=False):
    blocks = (spots.shape[0] - 1) // 2
    count, depth = x.shape
    width = dy.shape[1]
    step = 384
    cols = 1152 if width % 768 else 768
    if len(shape) == 4:
        per = step // shape[2]
        streams = 1 if split else 2
        out_spec = pl.BlockSpec((per, streams, shape[2], width), lambda j, s: (j, 0, 0, 0))
    else:
        tiles, q, _, rows, tile = shape
        if rows < step:
            block = (tiles, step // rows, 2, rows, tile)
            out_spec = pl.BlockSpec(block, lambda j, s: (0, j, 0, 0, 0))
        else:
            per = rows // step
            out_spec = pl.BlockSpec(
                (tiles, 1, 2, step, tile), lambda j, s: (0, j // per, 0, j % per, 0)
            )
    half = jax.ShapeDtypeStruct((shape[0], 1, *shape[2:]), bf16)
    return pl.pallas_call(
        functools.partial(gradient_kernel, blocks),
        grid_spec=pltpu.PrefetchScalarGridSpec(
            num_scalar_prefetch=1,
            grid=(depth // step,),
            in_specs=[
                pl.BlockSpec((count, step), lambda j, s: (0, j)),
                resident(dy.shape),
                resident(image.shape),
            ],
            out_specs=[out_spec, out_spec] if split else out_spec,
            scratch_shapes=[
                pltpu.VMEM((step, count), bf16),
                pltpu.VMEM((count, width), bf16),
                pltpu.VMEM((step, cols), f32),
            ],
        ),
        out_shape=[half, half] if split else jax.ShapeDtypeStruct(shape, bf16),
        compiler_params=pltpu.CompilerParams(vmem_limit_bytes=48 << 20),
        cost_estimate=pl.CostEstimate(
            flops=count * depth // 4 * width, bytes_accessed=4 << 20, transcendentals=0
        ),
        name="gradient",
    )(spots, x, dy, image)


def over_rep(value, target):
    count = lax.axis_size("rep")
    return lax.ppermute(value, "rep", [(r, target(r)) for r in range(count)])


def sibling(value):
    return over_rep(value, lambda r: r ^ 1)


def across(value):
    return over_rep(value, lambda r: r ^ 2)


def gather_rep(value):
    far = across(value)
    return [value, sibling(value), far, sibling(far)]


def reduce_rep(parts):
    near = sibling((parts[1], parts[3]))
    far = across((parts[2].astype(f32) + near[1].astype(f32)).astype(bf16))
    return parts[0].astype(f32) + near[0].astype(f32) + far.astype(f32)


def turn(value):
    reps, shards = lax.axis_size("rep"), lax.axis_size("shard")
    q = shards // reps
    pairs = []
    for r in range(reps):
        for s in range(shards):
            pairs.append((r * shards + s, (s // q) * shards + r * q + s % q))
    return lax.ppermute(value, ("rep", "shard"), pairs)


def gather_weight(weight_low):
    return lax.all_gather(weight_low, "shard", axis=0, tiled=False)


def gather_turned(moved):
    full = gather_weight(moved)
    reps = lax.axis_size("rep")
    return full.reshape(reps, full.shape[0] // reps, *full.shape[1:])


def ring_place(shards):
    mine = lax.axis_index("shard")
    odd = mine % 2
    return (1 - odd) * (mine // 2) + odd * (shards - 1 - mine // 2)


def ring_owner(place, shards):
    place = (place + 2 * shards) % shards
    back = place // ((shards + 1) // 2)
    return (1 - back) * (2 * place) + back * (2 * (shards - 1 - place) + 1)


def ring_kernel(shards, count, *refs):
    sources, dests = refs[:count], refs[count : 2 * count]
    send_sem, recv_sem, own_sem = refs[2 * count :]
    place = ring_place(shards)
    mine = ring_owner(place, shards)
    peers = [ring_owner(place + 1, shards), ring_owner(place - 1, shards)]

    barrier = pltpu.get_barrier_semaphore()
    for peer in peers:
        pl.semaphore_signal(
            barrier, inc=1, device_id={"shard": peer}, device_id_type=pl.DeviceIdType.MESH
        )
    pl.semaphore_wait(barrier, 2)

    kept = [
        pltpu.make_async_copy(sources[w], dests[w].at[mine], own_sem.at[w]) for w in range(count)
    ]
    for copy in kept:
        copy.start()
    chains = [(w, way) for w in range(count) for way in range(2)]
    copies = {}
    for step in range(shards - 1):
        for chain in chains:
            w, way = chain
            if step:
                copies[chain, step - 1].wait_recv()
            owner = ring_owner(place - step if way == 0 else place + step, shards)
            dest = dests[w].at[owner, way]
            copies[chain, step] = pltpu.make_async_remote_copy(
                src_ref=dest if step else sources[w].at[way],
                dst_ref=dest,
                send_sem=send_sem.at[w, way, step],
                recv_sem=recv_sem.at[w, way, step],
                device_id={"shard": peers[way]},
                device_id_type=pl.DeviceIdType.MESH,
            )
            copies[chain, step].start()
    for chain in chains:
        copies[chain, shards - 2].wait_recv()
        for step in range(shards - 1):
            copies[chain, step].wait_send()
    for copy in kept:
        copy.wait()


def ring_gather(*blocks):
    shards = lax.axis_size("shard")
    count = len(blocks)
    anywhere = pl.BlockSpec(memory_space=pl.ANY)
    return pl.pallas_call(
        functools.partial(ring_kernel, shards, count),
        in_specs=[anywhere] * count,
        out_specs=[anywhere] * count,
        out_shape=[jax.ShapeDtypeStruct((shards, *b.shape), b.dtype) for b in blocks],
        scratch_shapes=[
            pltpu.SemaphoreType.DMA((count, 2, shards - 1)),
            pltpu.SemaphoreType.DMA((count, 2, shards - 1)),
            pltpu.SemaphoreType.DMA((count,)),
        ],
        compiler_params=pltpu.CompilerParams(collective_id=0, has_side_effects=True),
        cost_estimate=pl.CostEstimate(flops=1 << 20, bytes_accessed=256 << 20, transcendentals=0),
        name="ring_gather",
    )(*blocks)


def as_turned(full):
    reps = lax.axis_size("rep")
    return full.reshape(reps, full.shape[0] // reps, *full.shape[1:])


def ring_scatter_kernel(count, *refs):
    sources, outs, helds = refs[:count], refs[count : 2 * count], refs[2 * count : 3 * count]
    send_sem, recv_sem = refs[3 * count :]
    shards = sources[0].shape[0]
    pieces = helds[0].shape[1]
    place = ring_place(shards)
    mine = ring_owner(place, shards)
    peers = [ring_owner(place + 1, shards), ring_owner(place - 1, shards)]

    barrier = pltpu.get_barrier_semaphore()
    for peer in peers:
        pl.semaphore_signal(
            barrier, inc=1, device_id={"shard": peer}, device_id_type=pl.DeviceIdType.MESH
        )
    pl.semaphore_wait(barrier, 2)

    chains = [
        (w, way, piece) for piece in range(pieces) for w in range(count) for way in range(2)
    ]
    copies = {}
    for step in range(shards):
        for chain in chains:
            w, way, piece = chain
            part = sources[w].shape[2] // pieces
            span = slice(piece * part, (piece + 1) * part)
            if step < shards - 1:
                owner = ring_owner(place - 1 - step if way == 0 else place + 1 + step, shards)
            else:
                owner = mine
            source = sources[w].at[owner, way, span]
            if step:
                copies[chain, step - 1].wait_recv()
                arrived = helds[w].at[way, piece, step - 1]
                total = arrived[...].astype(f32) + source[...].astype(f32)
                if step == shards - 1:
                    outs[w][way, span] = total.astype(bf16)
                    continue
                arrived[...] = total.astype(bf16)
                source = arrived
            copies[chain, step] = pltpu.make_async_remote_copy(
                src_ref=source,
                dst_ref=helds[w].at[way, piece, step],
                send_sem=send_sem.at[w, way, piece, step],
                recv_sem=recv_sem.at[w, way, piece, step],
                device_id={"shard": peers[way]},
                device_id_type=pl.DeviceIdType.MESH,
            )
            copies[chain, step].start()
    for copy in copies.values():
        copy.wait_send()


def ring_scatter(*terms):
    shards, _, rows, _ = terms[0].shape
    count = len(terms)
    pieces = 2 if rows % 32 == 0 else 1
    sems = pltpu.SemaphoreType.DMA((count, 2, pieces, shards - 1))
    whole = pl.BlockSpec(memory_space=pltpu.VMEM)
    return pl.pallas_call(
        functools.partial(ring_scatter_kernel, count),
        in_specs=[whole] * count,
        out_specs=[whole] * count,
        out_shape=[jax.ShapeDtypeStruct(t.shape[1:], bf16) for t in terms],
        scratch_shapes=[
            pltpu.VMEM((2, pieces, shards - 1, t.shape[2] // pieces, t.shape[3]), bf16)
            for t in terms
        ]
        + [sems, sems],
        compiler_params=pltpu.CompilerParams(
            collective_id=1, has_side_effects=True, vmem_limit_bytes=36 << 20
        ),
        cost_estimate=pl.CostEstimate(flops=1 << 20, bytes_accessed=256 << 20, transcendentals=0),
        name="ring_scatter",
    )(*terms)


def scatter_weight(terms):
    return lax.psum_scatter(
        terms.reshape(-1, *terms.shape[-2:]), "shard", scatter_dimension=0, tiled=True
    ).reshape(terms.shape[-3:])


def body(
    tokens,
    cotangent,
    cond,
    seq_lengths,
    stream_mask,
    w_mod,
    m_mod,
    v_mod,
    w_qkv,
    m_qkv,
    v_qkv,
    w_out,
    m_out,
    v_out,
    w_fc1,
    m_fc1,
    v_fc1,
    w_fc2,
    m_fc2,
    v_fc2,
    gains,
    m_gains,
    v_gains,
):
    tok_rows, model_width = tokens.shape
    slot_count = seq_lengths.shape[0]
    reps, shards = lax.axis_size("rep"), lax.axis_size("shard")
    rep_index, shard_index = lax.axis_index("rep"), lax.axis_index("shard")
    device_index = rep_index * shards + shard_index
    all_tokens = tok_rows * reps * shards
    reach = (MAXLEN - 2) // tok_rows + 1
    part_width = model_width // reps
    part_rows = w_mod.shape[1]
    mod_cols = w_mod.shape[2]

    seq_starts = jnp.cumsum(seq_lengths) - seq_lengths
    local_pos = device_index * tok_rows + jnp.arange(tok_rows, dtype=jnp.int32)
    seq_ids = segment_index(local_pos, seq_starts, all_tokens)
    image_col = (stream_mask == 1)[:, None]
    image_group = jnp.concatenate(gather_rep(stream_mask)) == 1
    image = image_group[:, None].astype(jnp.int32)
    text_group = ~image_group.reshape(reps, tok_rows)
    text_first = jnp.argmax(text_group, axis=1).astype(jnp.int32)
    spots = jnp.concatenate(
        [
            jnp.minimum(text_first // 16 * 16, tok_rows - WINDOW),
            jnp.any(text_group, axis=1).astype(jnp.int32),
            rep_index[None].astype(jnp.int32),
        ]
    )

    silu_cond = jax.nn.silu(cond).astype(bf16)
    cond_rows = lax.dynamic_slice_in_dim(silu_cond, shard_index * part_rows, part_rows, 1)
    mod_terms = jnp.concatenate(
        [
            jnp.dot(cond_rows, w_mod[s].astype(bf16), preferred_element_type=f32)
            for s in range(2)
        ],
        axis=0,
    ).astype(bf16)
    device_count = reps * shards
    firsts = segment_index(
        jnp.arange(device_count, dtype=jnp.int32) * tok_rows, seq_starts, all_tokens
    )
    seconds = jnp.minimum(firsts + 1, slot_count - 1)
    stream_offset = jnp.arange(2, dtype=jnp.int32) * slot_count
    wanted = jnp.stack([firsts, seconds], axis=1)[:, :, None] + stream_offset
    hot = (wanted.reshape(-1, 1) == jnp.arange(2 * slot_count, dtype=jnp.int32)).astype(bf16)
    mod_sent = jnp.dot(hot, mod_terms, preferred_element_type=f32).astype(bf16)
    mod_got = lax.all_to_all(
        mod_sent.reshape(device_count, 4, mod_cols), ("rep", "shard"), 0, 0, tiled=True
    )
    mod_sum = jnp.sum(mod_got.reshape(reps, shards, 4, mod_cols).astype(f32), axis=1).astype(bf16)
    mod_rows = jnp.concatenate([mod_sum[r] for r in range(reps)], axis=1)

    qkv_low = w_qkv.astype(bf16)
    chunks = [
        over_rep(
            qkv_low[:, :, i * part_width : (i + 1) * part_width],
            lambda r, i=i: (3 * r + i) % reps,
        )
        for i in range(3)
    ]
    turns = rep_index % 3

    def rolled(parts, amount):
        return [
            jnp.where(
                amount == 0,
                parts[t],
                jnp.where(amount == 1, parts[(t + 1) % 3], parts[(t + 2) % 3]),
            )
            for t in range(3)
        ]

    qkv_weights = gather_weight(jnp.concatenate(rolled(chunks, turns), axis=2))
    first_seq = seq_ids[0]
    second_seq = jnp.minimum(first_seq + 1, slot_count - 1)
    is_second = (seq_ids != first_seq)[:, None]

    def mod_block(index):
        span = slice(index * model_width, (index + 1) * model_width)
        rows = mod_rows[:, span].astype(f32)
        pick = [jnp.where(is_second, rows[2 + s][None], rows[s][None]) for s in range(2)]
        return jnp.where(image_col, pick[0], pick[1])

    shift_one, scale_one, gate_one, shift_two, scale_two, gate_two = [
        mod_block(i) for i in range(6)
    ]
    stream_in = tokens.astype(f32)
    back_out = cotangent.astype(f32)
    act_one = layer_modulate(stream_in, shift_one, scale_one).astype(bf16)
    act_one_group = jnp.concatenate(gather_rep(act_one))
    d_down = (gate_two * back_out).astype(bf16)
    d_down_group = jnp.concatenate(gather_rep(d_down))

    out_turned, fc1_low, act_one_group = lax.optimization_barrier(
        (turn(w_out.astype(bf16)), w_fc1.astype(bf16), act_one_group)
    )
    out_full, fc1_weights = ring_gather(out_turned, fc1_low)
    out_weights = as_turned(out_full)
    fc2_low, act_one = lax.optimization_barrier((w_fc2.astype(bf16), act_one))
    fc2_turned = turn(fc2_low)
    act_one_group, fc1_weights, d_down_group, fc2_turned = lax.optimization_barrier(
        (act_one_group, fc1_weights, d_down_group, fc2_turned)
    )

    query_sent, pair_sent, qk_pre = qkv_product(spots, act_one_group, qkv_weights, image, gains)

    bunch = 2 * reps
    bunches = shards // bunch
    half_width = part_width // 2
    groups = [[q * bunch + i for i in range(bunch)] for q in range(bunches)]

    def exchange(value):
        return lax.all_to_all(
            value, "shard", 0, 0, axis_index_groups=None if bunches == 1 else groups, tiled=True
        )

    stretch_count = reps * bunches
    stretch_rows = bunch * tok_rows
    halo = reach * tok_rows

    def stretch_shift(value, steps):
        def place(stretch, g):
            return (stretch % bunches) * bunch + (stretch // bunches) * 2 + g

        pairs = [
            (place(t, g), place(t + steps, g))
            for t in range(stretch_count)
            for g in range(2)
            if 0 <= t + steps < stretch_count
        ]
        return lax.ppermute(value, "shard", pairs)

    pair_own = exchange(pair_sent).reshape(stretch_rows, 2 * half_width)
    pair_before = stretch_shift(pair_own[-halo:], 1)
    pair_after = stretch_shift(pair_own[:halo], -1)
    query_sent, pair_before, pair_after = lax.optimization_barrier(
        (query_sent, pair_before, pair_after)
    )
    query_own = exchange(query_sent).reshape(stretch_rows, half_width)
    fc2_turned, query_own = lax.optimization_barrier((fc2_turned, query_own))
    fc2_weights = as_turned(gather_weight(fc2_turned))
    window_rows = stretch_rows + 2 * halo
    stretch = ((shard_index % bunch) // 2) * bunches + shard_index // bunch
    stretch_first = stretch * stretch_rows
    qid = segment_index(
        stretch_first + jnp.arange(stretch_rows, dtype=jnp.int32), seq_starts, all_tokens
    )
    kid = segment_index(
        stretch_first - halo + jnp.arange(window_rows, dtype=jnp.int32), seq_starts, all_tokens
    )
    seq_ends = seq_starts + seq_lengths
    low_pos = seq_starts[qid[::QB]] - (stretch_first - halo)
    high_pos = seq_ends[qid[QB - 1 :: QB]] - (stretch_first - halo)
    lo = jnp.clip(low_pos // KB, 0, window_rows // KB).astype(jnp.int32)
    hi = jnp.clip((high_pos + KB - 1) // KB, 0, window_rows // KB).astype(jnp.int32)
    attended_own, logsum = attention(
        query_own, pair_own, pair_before, pair_after, lo, hi, qid, kid
    )
    attended_came = exchange(attended_own.reshape(bunch, tok_rows, half_width))

    def split_group(value):
        return [value[p * tok_rows : (p + 1) * tok_rows] for p in range(reps)]

    branch_terms, attended_low = forward_product(
        spots, attended_came, out_weights, image, gathers=True
    )
    branch = reduce_rep(split_group(branch_terms))
    mid = stream_in + gate_one * branch
    act_two = layer_modulate(mid, shift_two, scale_two).astype(bf16)
    act_two_group = jnp.concatenate(gather_rep(act_two))
    gelu_low, gelu_slope = forward_product(spots, act_two_group, fc1_weights, image, gelu=True)
    down_terms = forward_product(spots, gelu_low, fc2_weights, image)[0]

    fc2_terms = gradient(spots, gelu_low, d_down_group, image, fc2_weights.shape)
    fc2_terms, gelu_slope = lax.optimization_barrier((fc2_terms, gelu_slope))
    fc2_own = scatter_weight(fc2_terms)
    d_up = backward_product(spots, d_down_group, fc2_weights, image, factor=gelu_slope)
    d_act_two = reduce_rep(split_group(backward_product(spots, d_up, fc1_weights, image)))
    d_mid_norm, d_shift_two, d_scale_two = jax.vjp(layer_modulate, mid, shift_two, scale_two)[1](
        d_act_two
    )
    d_mid = back_out + d_mid_norm
    d_branch = (gate_one * d_mid).astype(bf16)
    fc1_image, fc1_text = gradient(
        spots, act_two_group, d_up, image, fc1_weights.shape, split=True
    )
    fc1_image, fc1_text, d_branch = lax.optimization_barrier((fc1_image, fc1_text, d_branch))
    fc1_image = scatter_weight(fc1_image)
    d_gate_one = d_mid * branch
    d_branch_group = jnp.concatenate(gather_rep(d_branch))
    d_attended = backward_product(spots, d_branch_group, out_weights, image, packs=True)
    out_terms = gradient(spots, attended_low, d_branch_group, image, out_weights.shape)
    d_attended_own = exchange(d_attended).reshape(stretch_rows, half_width)
    d_attended_own, out_terms = lax.optimization_barrier((d_attended_own, out_terms))
    d_query_own, d_before, d_after, d_pair_own = attention_back(
        query_own,
        pair_own,
        pair_before,
        pair_after,
        d_attended_own,
        attended_own,
        lo,
        hi,
        qid,
        kid,
        logsum,
    )
    d_query_came = exchange(d_query_own.reshape(bunch, tok_rows, half_width))
    from_later = stretch_shift(d_before, -1).astype(f32)
    from_earlier = stretch_shift(d_after, 1).astype(f32)
    rest = jnp.zeros((stretch_rows - halo, 2 * half_width), f32)
    d_pair_own = (
        d_pair_own
        + jnp.concatenate([rest, from_later], axis=0)
        + jnp.concatenate([from_earlier, rest], axis=0)
    )
    d_pair_came = exchange(d_pair_own.astype(bf16).reshape(bunch, tok_rows, 2 * half_width))
    up_fc2 = adam_step(w_fc2, m_fc2, v_fc2, turn(fc2_own).astype(f32), rate_fc2)
    d_pair_came, down_terms, fc1_text, up_fc2 = lax.optimization_barrier(
        (d_pair_came, down_terms, fc1_text, up_fc2)
    )
    fc1_text = scatter_weight(fc1_text)
    down_proj = reduce_rep(split_group(down_terms))
    output = mid + gate_two * down_proj
    d_gate_two = back_out * down_proj
    d_qkv, gain_sums = norm_back(spots, d_query_came, d_pair_came, qk_pre, image, gains)
    d_act_one = reduce_rep(split_group(backward_product(spots, d_qkv, qkv_weights, image)))
    qkv_terms = gradient(spots, act_one_group, d_qkv, image, qkv_weights.shape)
    d_in_norm, d_shift_one, d_scale_one = jax.vjp(layer_modulate, stream_in, shift_one, scale_one)[
        1
    ](d_act_one)
    d_tokens = d_mid + d_in_norm
    d_mod_tok = jnp.concatenate(
        [d_shift_one, d_scale_one, d_gate_one, d_shift_two, d_scale_two, d_gate_two], axis=1
    )
    image_flag = image_col[:, 0]
    second_flag = is_second[:, 0]
    selector = jnp.stack(
        [
            ~second_flag & image_flag,
            ~second_flag & ~image_flag,
            second_flag & image_flag,
            second_flag & ~image_flag,
        ],
        axis=1,
    ).astype(f32)
    pooled = jnp.einsum("tp,te->pe", selector, d_mod_tok, precision=lax.Precision.HIGHEST)
    gain_sums = jnp.sum(gain_sums.reshape(2, 2, part_width // HD, HD), axis=2)
    gain_part = jnp.concatenate([gain_sums[0], gain_sums[1]], axis=1)
    gain_rows = jnp.concatenate([gain_part, jnp.zeros_like(gain_part)], axis=0)
    leaving = jnp.stack(
        [
            jnp.concatenate([pooled[:, r * mod_cols : (r + 1) * mod_cols], gain_rows], axis=1)
            for r in range(reps)
        ]
    )
    qkv_terms, out_terms, fc1_image, leaving = lax.optimization_barrier(
        (qkv_terms, out_terms, fc1_image, leaving)
    )
    leaving = jnp.broadcast_to(leaving[:, None], (reps, shards, *leaving.shape[1:]))
    came = lax.all_to_all(
        leaving.reshape(device_count, *leaving.shape[2:]), ("rep", "shard"), 0, 0, tiled=True
    )
    out_terms = out_terms.reshape(shards, 2, -1, out_terms.shape[-1])
    g_qkv_group, g_out = ring_scatter(qkv_terms, out_terms)
    g_qkv_group, g_out, came = lax.optimization_barrier((g_qkv_group, g_out, came))
    g_out = turn(g_out)
    g_fc1 = jnp.concatenate([fc1_image, fc1_text], axis=0)
    g_parts = [
        g_qkv_group[:, :, t * part_width : (t + 1) * part_width] for t in range(3)
    ]
    g_parts = rolled(g_parts, (3 - turns) % 3)
    g_qkv = jnp.concatenate(
        [over_rep(g_parts[i], lambda d, i=i: (3 * (d - i)) % reps) for i in range(3)], axis=2
    )

    g_gains = jnp.sum(came[:, :2, mod_cols:], axis=0)
    came = came[:, :, :mod_cols].reshape(2 * device_count, 2, mod_cols)
    seqs = jnp.stack([firsts, seconds], axis=1).reshape(-1)
    hot_seq = (seqs[:, None] == jnp.arange(slot_count, dtype=jnp.int32)).astype(bf16)
    cond_seq = jnp.dot(hot_seq, cond_rows, preferred_element_type=f32)
    g_mod = jnp.stack(
        [
            lax.dot_general(
                cond_seq,
                came[:, s],
                (((0,), (0,)), ((), ())),
                precision=lax.Precision.HIGHEST,
                preferred_element_type=f32,
            )
            for s in range(2)
        ]
    )
    up_mod = adam_step(w_mod, m_mod, v_mod, g_mod, rate_mod)
    up_qkv = adam_step(w_qkv, m_qkv, v_qkv, g_qkv.astype(f32), rate_qkv)
    up_out = adam_step(w_out, m_out, v_out, g_out.astype(f32), rate_out)
    up_fc1 = adam_step(w_fc1, m_fc1, v_fc1, g_fc1.astype(f32), rate_fc1)
    up_gains = adam_step(gains, m_gains, v_gains, g_gains, rate_gains)
    return (
        output.astype(bf16),
        d_tokens,
        *up_mod,
        *up_qkv,
        *up_out,
        *up_fc1,
        *up_fc2,
        *up_gains[:3],
    )


def solution(mesh):
    rows = P(("rep", "shard"), None)
    held = P(None, "shard", "rep")
    return jax.shard_map(
        body,
        mesh=mesh,
        in_specs=(rows, rows, P(), P(), P(("rep", "shard")), *([held] * 15), P(), P(), P()),
        out_specs=(rows, rows, *([held] * 20), P(), P(), P()),
        check_vma=False,
    )
```

```python
import functools

import jax
import jax.numpy as jnp
from jax import lax
from jax.experimental import pallas as pl
from jax.experimental.pallas import tpu as pltpu
from jax.sharding import PartitionSpec as P

HD = 64
MAXLEN = 1178
STEP = 7

norm_eps = 1e-06
adam_eps = 1e-08
score_scale = 0.125
rate_mod = 0.03
rate_qkv = 0.03
rate_out = 0.15
rate_fc1 = 0.03
rate_fc2 = 0.015
rate_gains = 1.0

bf16 = jnp.bfloat16
f32 = jnp.float32
QB = 256
KB = 256
TXT = 154
WINDOW = (TXT + 15 + 15) // 16 * 16
COLS = 512
GELU_A = 0.7978845608028654
GELU_B = 0.044715
NN = (((1,), (0,)), ((), ()))
NT = (((1,), (1,)), ((), ()))
TN = (((0,), (0,)), ((), ()))


def layer_modulate(values, shift, scale):
    centred = values - jnp.mean(values, axis=-1, keepdims=True)
    normed = centred * lax.rsqrt(jnp.mean(centred * centred, axis=-1, keepdims=True) + norm_eps)
    return normed * (1.0 + scale) + shift


def adam_step(weight, moment_one, moment_two, grads, rate):
    new_one = 0.9 * moment_one + 0.1 * grads
    new_two = 0.999 * moment_two + 0.001 * grads * grads
    fixed_one = new_one / (1.0 - 0.9**STEP)
    fixed_two = new_two / (1.0 - 0.999**STEP)
    new_weight = weight - rate * (fixed_one / (jnp.sqrt(fixed_two) + adam_eps) + 0.01 * weight)
    return (new_weight, new_one, new_two, new_weight.astype(bf16))


def segment_index(position, seq_starts, all_tokens):
    counted = jnp.sum((seq_starts[None, :] <= position[:, None]).astype(jnp.int32), axis=1) - 1
    inside = (position >= 0) & (position < all_tokens)
    return jnp.where(inside, counted, -1)


def fill_window(own_ref, before_ref, after_ref, keys, values):
    halo, own = before_ref.shape[0], own_ref.shape[0]
    heads = keys.shape[0]
    width = heads * HD
    parts = ((before_ref, 0, halo), (own_ref, halo, own), (after_ref, halo + own, halo))
    for source, first, count in parts:
        for head in range(heads):
            for index, dest in ((0, keys), (1, values)):
                start = index * width + head * HD
                dest[head, first : first + count, :HD] = source[:, start : start + HD]


def attend_kernel(
    lo_ref, hi_ref, q_ref, own_ref, before_ref, after_ref, qid_ref, kid_ref, o_ref, l_ref, keys, values, acc
):
    step = pl.program_id(0)
    heads = keys.shape[0]

    @pl.when(step == 0)
    def _():
        lane = lax.broadcasted_iota(jnp.int32, values.shape[1:], 1)
        for head in range(heads):
            values[head] = (lane == HD).astype(bf16)
        fill_window(own_ref, before_ref, after_ref, keys, values)

    qid = qid_ref[...]
    diagonal = lax.broadcasted_iota(jnp.int32, (QB, QB), 0) == lax.broadcasted_iota(
        jnp.int32, (QB, QB), 1
    )
    queries = [q_ref[:, head * HD : (head + 1) * HD] for head in range(heads)]
    acc[...] = jnp.zeros_like(acc)

    @pl.loop(lo_ref[step], hi_ref[step])
    def _(block):
        rows = pl.ds(pl.multiple_of(block * KB, KB), KB)
        same = qid == kid_ref[pl.ds(block, 1), :]
        for head in range(heads):
            scores = lax.dot_general(
                queries[head], keys[head, rows, :], NT, preferred_element_type=f32
            )
            lifted = jnp.where(same, jnp.exp(scores), 0.0).astype(bf16)
            acc[head] += jnp.dot(lifted, values[head, rows, :], preferred_element_type=f32)

    for head in range(heads):
        total = acc[head, :, HD : HD + 1]
        o_ref[:, head * HD : (head + 1) * HD] = (acc[head, :, :HD] / total).astype(bf16)
        l_ref[0, head : head + 1, :] = jnp.sum(
            jnp.where(diagonal, jnp.log(total), 0.0), axis=0, keepdims=True
        )


def attend_back_kernel(
    lo_ref,
    hi_ref,
    q_ref,
    own_ref,
    before_ref,
    after_ref,
    do_ref,
    o_ref,
    qid_ref,
    kid_ref,
    l_ref,
    dq_ref,
    d_before_ref,
    d_after_ref,
    d_own_ref,
    keys,
    values,
    d_keys,
    d_values,
    d_query,
):
    step = pl.program_id(0)
    heads = keys.shape[0]
    width = heads * HD

    @pl.when(step == 0)
    def _():
        fill_window(own_ref, before_ref, after_ref, keys, values)
        d_keys[...] = jnp.zeros_like(d_keys)
        d_values[...] = jnp.zeros_like(d_values)

    qid = qid_ref[0]
    ones = jnp.ones((8, HD), bf16)
    queries, outs, dots = [], [], []
    for head in range(heads):
        lanes = slice(head * HD, (head + 1) * HD)
        queries.append(q_ref[:, lanes])
        outs.append(do_ref[:, lanes])
        product = outs[head].astype(f32) * o_ref[:, lanes].astype(f32)
        coarse = product.astype(bf16)
        fine = (product - coarse.astype(f32)).astype(bf16)
        total = lax.dot_general(ones, coarse, NT, preferred_element_type=f32)
        dots.append((total + lax.dot_general(ones, fine, NT, preferred_element_type=f32))[:1])
    d_query[...] = jnp.zeros_like(d_query)

    @pl.loop(lo_ref[step], hi_ref[step])
    def _(block):
        rows = pl.ds(pl.multiple_of(block * KB, KB), KB)
        same = kid_ref[rows, :] == qid
        for head in range(heads):
            key = keys[head, rows, :]
            scores = lax.dot_general(key, queries[head], NT, preferred_element_type=f32)
            probs = jnp.where(same, jnp.exp(scores - l_ref[0, head : head + 1, :]), 0.0)
            d_values[head, rows, :] += jnp.dot(
                probs.astype(bf16), outs[head], preferred_element_type=f32
            )
            d_probs = lax.dot_general(
                values[head, rows, :], outs[head], NT, preferred_element_type=f32
            )
            d_scores = (probs * (d_probs - dots[head])).astype(bf16)
            d_keys[head, rows, :] += jnp.dot(d_scores, queries[head], preferred_element_type=f32)
            d_query[head] += lax.dot_general(d_scores, key, TN, preferred_element_type=f32)

    for head in range(heads):
        dq_ref[:, head * HD : (head + 1) * HD] = (d_query[head] * score_scale).astype(bf16)

    @pl.when(step == pl.num_programs(0) - 1)
    def _():
        halo, own = d_before_ref.shape[0], d_own_ref.shape[0]
        for index, source in ((0, d_keys), (1, d_values)):
            for head in range(heads):
                span = slice(index * width + head * HD, index * width + (head + 1) * HD)
                d_before_ref[:, span] = source[head, :halo, :].astype(bf16)
                d_own_ref[:, span] = source[head, halo : halo + own, :]
                d_after_ref[:, span] = source[head, halo + own :, :].astype(bf16)


def resident(shape):
    return pl.BlockSpec(shape, lambda *index: (0,) * len(shape))


def attention(query, own, before, after, lo, hi, qid, kid):
    count, width = query.shape
    heads = width // HD
    window = count + 2 * before.shape[0]
    steps = count // QB
    return pl.pallas_call(
        attend_kernel,
        grid_spec=pltpu.PrefetchScalarGridSpec(
            num_scalar_prefetch=2,
            grid=(steps,),
            in_specs=[
                pl.BlockSpec((QB, width), lambda i, lo, hi: (i, 0)),
                resident(own.shape),
                resident(before.shape),
                resident(after.shape),
                pl.BlockSpec((QB, 1), lambda i, lo, hi: (i, 0)),
                resident((window // KB, KB)),
            ],
            out_specs=[
                pl.BlockSpec((QB, width), lambda i, lo, hi: (i, 0)),
                pl.BlockSpec((1, 8, QB), lambda i, lo, hi: (i, 0, 0)),
            ],
            scratch_shapes=[
                pltpu.VMEM((heads, window, HD), bf16),
                pltpu.VMEM((heads, window, 2 * HD), bf16),
                pltpu.VMEM((heads, QB, 2 * HD), f32),
            ],
        ),
        out_shape=[
            jax.ShapeDtypeStruct((count, width), bf16),
            jax.ShapeDtypeStruct((steps, 8, QB), f32),
        ],
        compiler_params=pltpu.CompilerParams(vmem_limit_bytes=40 << 20),
        cost_estimate=pl.CostEstimate(flops=1 << 30, bytes_accessed=4 << 20, transcendentals=0),
        name="attend",
    )(lo, hi, query, own, before, after, qid[:, None], kid.reshape(window // KB, KB))


def attention_back(query, own, before, after, d_out, out, lo, hi, qid, kid, logsum):
    count, width = query.shape
    heads = width // HD
    halo = before.shape[0]
    window = count + 2 * halo
    steps = count // QB
    rows = pl.BlockSpec((QB, width), lambda i, lo, hi: (i, 0))
    return pl.pallas_call(
        attend_back_kernel,
        grid_spec=pltpu.PrefetchScalarGridSpec(
            num_scalar_prefetch=2,
            grid=(steps,),
            in_specs=[
                rows,
                resident(own.shape),
                resident(before.shape),
                resident(after.shape),
                rows,
                rows,
                pl.BlockSpec((1, 1, QB), lambda i, lo, hi: (i, 0, 0)),
                resident((window, 1)),
                pl.BlockSpec((1, 8, QB), lambda i, lo, hi: (i, 0, 0)),
            ],
            out_specs=[
                rows,
                resident((halo, 2 * width)),
                resident((halo, 2 * width)),
                resident((count, 2 * width)),
            ],
            scratch_shapes=[pltpu.VMEM((heads, window, HD), bf16)] * 2
            + [pltpu.VMEM((heads, window, HD), f32)] * 2
            + [pltpu.VMEM((heads, QB, HD), f32)],
        ),
        out_shape=[
            jax.ShapeDtypeStruct((count, width), bf16),
            jax.ShapeDtypeStruct((halo, 2 * width), bf16),
            jax.ShapeDtypeStruct((halo, 2 * width), bf16),
            jax.ShapeDtypeStruct((count, 2 * width), f32),
        ],
        compiler_params=pltpu.CompilerParams(vmem_limit_bytes=58 << 20),
        cost_estimate=pl.CostEstimate(flops=24 << 30, bytes_accessed=8 << 20, transcendentals=0),
        name="attend_back",
    )(lo, hi, query, own, before, after, d_out, out, qid.reshape(steps, 1, QB), kid[:, None], logsum)


def text_windows(spots, blocks, count, work):
    for p in range(blocks):

        @pl.when(spots[blocks + p] == 1)
        def _(p=p):
            first = pl.multiple_of(spots[p], 16)
            base = p * (count // blocks)
            work(p, first, pl.ds(pl.multiple_of(base + first, 16), WINDOW))


def flat(value):
    return value.reshape(-1, value.shape[-1])


def product(x_ref, rows, weight, dims):
    total = None
    for cols, get in weight:
        term = lax.dot_general(x_ref[rows, cols], get(), dims, preferred_element_type=f32)
        total = term if total is None else total + term
    return total


def group_sums(values, blocks_of):
    coarse = values.astype(bf16)
    fine = (values - coarse.astype(f32)).astype(bf16)
    return jnp.dot(coarse, blocks_of, preferred_element_type=f32) + jnp.dot(
        fine, blocks_of, preferred_element_type=f32
    )


def head_blocks(width):
    row = lax.broadcasted_iota(jnp.int32, (width, width), 0) // HD
    col = lax.broadcasted_iota(jnp.int32, (width, width), 1) // HD
    return (row == col).astype(bf16)


def qkv_kernel(blocks, spots, x_ref, w0, w1, image_ref, gain_ref, q_ref, kv_ref, pre_ref):
    kind = pl.program_id(0)
    every = slice(None)
    size, width = q_ref.shape[1:]
    rep = spots[2 * blocks]
    spread = head_blocks(2 * width)

    def finish(t, values, gain):
        if t < 2:
            mean = group_sums(values * values, spread) * (1.0 / HD)
            values = values * lax.rsqrt(mean + norm_eps) * gain
        values = values.astype(bf16)
        return values * jnp.asarray(score_scale, bf16) if t == 0 else values

    for t in range(3):

        @pl.when(kind == t)
        def _(t=t):
            packed_ref = kv_ref if t else q_ref
            lanes = slice((t - 1) * width, t * width) if t else slice(0, width)

            @pl.loop(0, blocks)
            def _(p):
                rows = pl.ds(pl.multiple_of(p * size, size), size)
                values = product(x_ref, rows, [(every, lambda: flat(w0[...]))], NN)
                if t < 2:
                    pre_ref[rows, :] = values
                values = finish(t, values, gain_ref[0, :1])
                for g in range(2):
                    packed_ref[pl.ds((rep ^ p) * 2 + g, 1), :, lanes] = values[
                        :, g * width : (g + 1) * width
                    ][None]

            def text(p, first, rows):
                values = product(x_ref, rows, [(every, lambda: flat(w1[...]))], NN)
                image = image_ref[rows, :] == 1
                if t < 2:
                    pre_ref[rows, :] = jnp.where(image, pre_ref[rows, :], values)
                values = finish(t, values, gain_ref[0, 1:])
                for g in range(2):
                    place = (
                        pl.ds((rep ^ p) * 2 + g, 1),
                        pl.ds(first, WINDOW),
                        lanes,
                    )
                    packed_ref[place] = jnp.where(
                        image[None], packed_ref[place], values[:, g * width : (g + 1) * width][None]
                    )

            text_windows(spots, blocks, x_ref.shape[0], text)


def column_weights(weight, tile):
    shards, _, rows, _ = weight.shape
    return [
        pl.BlockSpec((shards, 1, rows, tile), lambda j, s, stream=stream: (0, stream, 0, j))
        for stream in range(2)
    ]


def tiled_gains(gains, heads):
    return jnp.stack([jnp.tile(gains[:, :HD], (1, heads)), jnp.tile(gains[:, HD:], (1, heads))])


def qkv_product(spots, x, weight, image, gains):
    count, depth = x.shape
    blocks = (spots.shape[0] - 1) // 2
    part = weight.shape[3] // 3
    size = count // blocks
    return pl.pallas_call(
        functools.partial(qkv_kernel, blocks),
        grid_spec=pltpu.PrefetchScalarGridSpec(
            num_scalar_prefetch=1,
            grid=(3,),
            in_specs=[
                resident(x.shape),
                *column_weights(weight, part),
                resident(image.shape),
                pl.BlockSpec((1, 2, part), lambda j, s: (jnp.minimum(j, 1), 0, 0)),
            ],
            out_specs=[
                resident((2 * blocks, size, part // 2)),
                resident((2 * blocks, size, part)),
                pl.BlockSpec((count, part), lambda j, s: (0, jnp.minimum(j, 1))),
            ],
        ),
        out_shape=[
            jax.ShapeDtypeStruct((2 * blocks, size, part // 2), bf16),
            jax.ShapeDtypeStruct((2 * blocks, size, part), bf16),
            jax.ShapeDtypeStruct((count, 2 * part), f32),
        ],
        compiler_params=pltpu.CompilerParams(vmem_limit_bytes=40 << 20),
        cost_estimate=pl.CostEstimate(flops=1 << 30, bytes_accessed=4 << 20, transcendentals=0),
        name="qkv_product",
    )(spots, x, weight, weight, image, tiled_gains(gains, part // HD))


def norm_back_kernel(blocks, spots, q_ref, kv_ref, pre_ref, image_ref, gain_ref, out_ref, sum_ref, both):
    @pl.when(pl.program_id(0) == 0)
    def _():
        sum_ref[...] = jnp.zeros_like(sum_ref)

    part = both.shape[1]
    width = part // 2
    image = image_ref[...] == 1
    spread = head_blocks(part)
    for t in range(3):
        came_ref = kv_ref if t else q_ref
        lanes = slice((t - 1) * width, t * width) if t else slice(0, width)
        for g in range(2):
            both[:, g * width : (g + 1) * width] = came_ref[g, :, lanes].astype(f32)
        grad = both[...]
        if t < 2:
            pre = pre_ref[:, t * part : (t + 1) * part]
            scale = lax.rsqrt(group_sums(pre * pre, spread) * (1.0 / HD) + norm_eps)
            gain = jnp.where(image, gain_ref[t, :1], gain_ref[t, 1:])
            each = grad * pre * scale
            total = jnp.sum(each, axis=0, keepdims=True)
            text = jnp.sum(jnp.where(image, 0.0, each), axis=0, keepdims=True)
            sum_ref[2 * t : 2 * t + 1, :] += total - text
            sum_ref[2 * t + 1 : 2 * t + 2, :] += text
            grad = grad * gain
            mean = group_sums(grad * pre, spread) * (1.0 / HD)
            grad = scale * (grad - pre * (scale * scale * mean))
        out_ref[:, t * part : (t + 1) * part] = grad.astype(bf16)


def norm_back(spots, came_query, came_pair, pre, image, gains):
    blocks = (spots.shape[0] - 1) // 2
    _, size, part = came_pair.shape
    tiled = tiled_gains(gains, part // HD)
    return pl.pallas_call(
        functools.partial(norm_back_kernel, blocks),
        grid_spec=pltpu.PrefetchScalarGridSpec(
            num_scalar_prefetch=1,
            grid=(blocks,),
            in_specs=[
                pl.BlockSpec((2, size, part // 2), lambda p, s: (s[2 * blocks] ^ p, 0, 0)),
                pl.BlockSpec((2, size, part), lambda p, s: (s[2 * blocks] ^ p, 0, 0)),
                pl.BlockSpec((size, 2 * part), lambda p, s: (p, 0)),
                pl.BlockSpec((size, 1), lambda p, s: (p, 0)),
                resident(tiled.shape),
            ],
            out_specs=[
                pl.BlockSpec((size, 3 * part), lambda p, s: (p, 0)),
                resident((4, part)),
            ],
            scratch_shapes=[pltpu.VMEM((size, part), f32)],
        ),
        out_shape=[
            jax.ShapeDtypeStruct((blocks * size, 3 * part), bf16),
            jax.ShapeDtypeStruct((4, part), f32),
        ],
        compiler_params=pltpu.CompilerParams(vmem_limit_bytes=32 << 20),
        cost_estimate=pl.CostEstimate(flops=4 << 30, bytes_accessed=12 << 20, transcendentals=0),
        name="norm_back",
    )(spots, came_query, came_pair, pre, image, tiled)


def forward_kernel(blocks, gathers, gelu, spots, x_ref, w0, w1, image_ref, *rest):
    rep = spots[2 * blocks]
    out_ref = rest[0]
    if gathers:
        x_out = rest[1]
        size, width = x_ref.shape[1:]

        @pl.when(pl.program_id(0) == 0)
        def _():
            for p in range(blocks):
                for g in range(2):
                    x_out[p * size : (p + 1) * size, g * width : (g + 1) * width] = x_ref[
                        pl.ds((rep ^ p) * 2 + g, 1)
                    ][0]

        x_ref = x_out
    every = slice(None)
    count = x_ref.shape[0]

    def finish(values):
        if not gelu:
            return (values.astype(bf16),)
        square = values * values
        bend = jnp.tanh(values * (GELU_A + GELU_A * GELU_B * square))
        half = 0.5 * (1.0 + bend)
        slope = half + 0.5 * values * (1.0 - bend * bend) * (GELU_A + 3.0 * GELU_A * GELU_B * square)
        return (values * half).astype(bf16), slope.astype(bf16)

    outs = rest if gelu else (out_ref,)
    chunk = count // (blocks if gelu else 2)

    @pl.loop(0, count // chunk)
    def _(p):
        rows = pl.ds(pl.multiple_of(p * chunk, chunk), chunk)
        values = product(x_ref, rows, [(every, lambda: flat(w0[...]))], NN)
        for out, value in zip(outs, finish(values)):
            out[rows, :] = value

    def text(p, first, rows):
        values = product(x_ref, rows, [(every, lambda: flat(w1[...]))], NN)
        image = image_ref[rows, :] == 1
        for out, value in zip(outs, finish(values)):
            out[rows, :] = jnp.where(image, out[rows, :], value)

    text_windows(spots, blocks, count, text)


def forward_product(spots, x, weight, image, gathers=False, gelu=False):
    blocks = (spots.shape[0] - 1) // 2
    if weight.ndim == 5:
        tiles, q, _, rows, tile = weight.shape
        weights = [
            pl.BlockSpec((1, q, 1, rows, tile), lambda j, s, stream=stream: (j, 0, stream, 0, 0))
            for stream in range(2)
        ]
        depth = q * rows
    else:
        depth, tile = weight.shape[0] * weight.shape[2], COLS
        tiles = weight.shape[3] // tile
        weights = column_weights(weight, tile)
    count = image.shape[0]
    column = pl.BlockSpec((count, tile), lambda j, s: (0, j))
    whole = jax.ShapeDtypeStruct((count, tiles * tile), bf16)
    out_specs, out_shape = [column], [whole]
    if gathers:
        out_specs.append(resident((count, depth)))
        out_shape.append(jax.ShapeDtypeStruct((count, depth), bf16))
    if gelu:
        out_specs.append(column)
        out_shape.append(whole)
    return pl.pallas_call(
        functools.partial(forward_kernel, blocks, gathers, gelu),
        grid_spec=pltpu.PrefetchScalarGridSpec(
            num_scalar_prefetch=1,
            grid=(tiles,),
            in_specs=[resident(x.shape), *weights, resident(image.shape)],
            out_specs=out_specs,
        ),
        out_shape=out_shape,
        compiler_params=pltpu.CompilerParams(vmem_limit_bytes=40 << 20),
        cost_estimate=pl.CostEstimate(
            flops=count * depth // 4 * tiles * tile, bytes_accessed=4 << 20, transcendentals=0
        ),
        name="forward_product",
    )(spots, x, weight, weight, image)


def backward_kernel(blocks, turned, scaled, packs, spots, dy_ref, w0, w1, image_ref, *rest):
    rest = list(rest)
    factor_ref = rest.pop(0) if scaled else None
    out_ref = rest[0]
    if turned:
        tiles, tile = w0.shape[0], w0.shape[4]
        weights = [
            [
                (slice(n * tile, (n + 1) * tile), lambda w=w, n=n: flat(w[n, :, 0]))
                for n in range(tiles)
            ]
            for w in (w0, w1)
        ]
    else:
        every = slice(None)
        weights = [[(every, lambda w=w: flat(w[...]))] for w in (w0, w1)]
    count = dy_ref.shape[0]
    size = count // blocks
    rep = spots[2 * blocks]
    part = pl.program_id(0)

    def finish(rows, values):
        if scaled:
            values = values * factor_ref[rows, :].astype(f32)
        return values.astype(bf16)

    chunk = size if packs or scaled else count // 2

    @pl.loop(0, count // chunk)
    def _(p):
        rows = pl.ds(pl.multiple_of(p * chunk, chunk), chunk)
        values = finish(rows, product(dy_ref, rows, weights[0], NT))
        if packs:
            out_ref[pl.ds((rep ^ p) * 2 + part, 1)] = values[None]
        else:
            out_ref[rows, :] = values

    def text(p, first, rows):
        values = finish(rows, product(dy_ref, rows, weights[1], NT))
        image = image_ref[rows, :] == 1
        if packs:
            place = (pl.ds((rep ^ p) * 2 + part, 1), pl.ds(first, WINDOW), slice(None))
            out_ref[place] = jnp.where(image[None], out_ref[place], values[None])
        else:
            out_ref[rows, :] = jnp.where(image, out_ref[rows, :], values)

    text_windows(spots, blocks, count, text)


def backward_product(spots, dy, weight, image, factor=None, packs=False):
    blocks = (spots.shape[0] - 1) // 2
    turned = weight.ndim == 5
    count = image.shape[0]
    if turned:
        tiles, q, _, rows, tile = weight.shape
        step = q * rows // 2 if packs else min(q * rows, 768)
        grid = (q * rows // step,)
        if rows < step:
            block = (tiles, step // rows, 1, rows, tile)
            weights = [
                pl.BlockSpec(block, lambda j, s, stream=stream: (0, j, stream, 0, 0))
                for stream in range(2)
            ]
        else:
            per = rows // step
            weights = [
                pl.BlockSpec(
                    (tiles, 1, 1, step, tile),
                    lambda j, s, stream=stream: (0, j // per, stream, j % per, 0),
                )
                for stream in range(2)
            ]
        depth = q * rows
    else:
        shards, _, rows, width = weight.shape
        depth = shards * rows
        bunch = max(1, 768 // rows)
        step = bunch * rows
        grid = (depth // step,)
        weights = [
            pl.BlockSpec((bunch, 1, rows, width), lambda j, s, stream=stream: (j, stream, 0, 0))
            for stream in range(2)
        ]
    column = pl.BlockSpec((count, step), lambda j, s: (0, j))
    in_specs = [resident(dy.shape), *weights, resident(image.shape)]
    operands = [spots, dy, weight, weight, image]
    if factor is not None:
        in_specs.append(column)
        operands.append(factor)
    if packs:
        shape = (2 * blocks, count // blocks, step)
        out_spec, out_shape = resident(shape), jax.ShapeDtypeStruct(shape, bf16)
    else:
        out_spec, out_shape = column, jax.ShapeDtypeStruct((count, depth), bf16)
    return pl.pallas_call(
        functools.partial(backward_kernel, blocks, turned, factor is not None, packs),
        grid_spec=pltpu.PrefetchScalarGridSpec(
            num_scalar_prefetch=1,
            grid=grid,
            in_specs=in_specs,
            out_specs=out_spec,
        ),
        out_shape=out_shape,
        compiler_params=pltpu.CompilerParams(vmem_limit_bytes=48 << 20),
        cost_estimate=pl.CostEstimate(
            flops=count * depth // 4 * dy.shape[1], bytes_accessed=4 << 20, transcendentals=0
        ),
        name="backward_product",
    )(*operands)


def gradient_kernel(blocks, spots, x_ref, dy_ref, image_ref, *rest):
    *outs, turned_x, masked, acc = rest
    count, width = dy_ref.shape
    size = count // blocks
    cols_at_once = acc.shape[1]

    @pl.when(pl.program_id(0) == 0)
    def _():
        @pl.loop(0, blocks)
        def _(p):
            rows = pl.ds(pl.multiple_of(p * size, size), size)
            kept = dy_ref[rows, :]
            masked[rows, :] = jnp.where(image_ref[rows, :] == 1, kept, jnp.zeros_like(kept))

    turned_x[...] = x_ref[...].T

    def store(stream, n, values):
        values = values.astype(bf16)
        out = outs[min(stream, len(outs) - 1)]
        stream = stream if len(outs) == 1 else 0
        if len(out.shape) == 5:
            tile, per = out.shape[4], out.shape[3]
            for t in range(cols_at_once // tile):
                for q in range(out.shape[1]):
                    out[n * (cols_at_once // tile) + t, q, stream] = values[
                        q * per : (q + 1) * per, t * tile : (t + 1) * tile
                    ]
        else:
            per = out.shape[2]
            for k in range(out.shape[0]):
                out[k, stream, :, n * cols_at_once : (n + 1) * cols_at_once] = values[
                    k * per : (k + 1) * per
                ]

    for n in range(width // cols_at_once):
        cols = slice(n * cols_at_once, (n + 1) * cols_at_once)
        store(0, n, jnp.dot(turned_x[...], masked[:, cols], preferred_element_type=f32))
        acc[...] = jnp.zeros_like(acc)

        def text(p, first, rows, cols=cols):
            kept = dy_ref[rows, cols]
            kept = jnp.where(image_ref[rows, :] == 1, jnp.zeros_like(kept), kept)
            acc[...] += lax.dot_general(x_ref[rows, :], kept, TN, preferred_element_type=f32)

        text_windows(spots, blocks, count, text)
        store(1, n, acc[...])


def gradient(spots, x, dy, image, shape, split=False):
    blocks = (spots.shape[0] - 1) // 2
    count, depth = x.shape
    width = dy.shape[1]
    step = 384
    cols = 1152 if width % 768 else 768
    if len(shape) == 4:
        per = step // shape[2]
        streams = 1 if split else 2
        out_spec = pl.BlockSpec((per, streams, shape[2], width), lambda j, s: (j, 0, 0, 0))
    else:
        tiles, q, _, rows, tile = shape
        if rows < step:
            block = (tiles, step // rows, 2, rows, tile)
            out_spec = pl.BlockSpec(block, lambda j, s: (0, j, 0, 0, 0))
        else:
            per = rows // step
            out_spec = pl.BlockSpec(
                (tiles, 1, 2, step, tile), lambda j, s: (0, j // per, 0, j % per, 0)
            )
    half = jax.ShapeDtypeStruct((shape[0], 1, *shape[2:]), bf16)
    return pl.pallas_call(
        functools.partial(gradient_kernel, blocks),
        grid_spec=pltpu.PrefetchScalarGridSpec(
            num_scalar_prefetch=1,
            grid=(depth // step,),
            in_specs=[
                pl.BlockSpec((count, step), lambda j, s: (0, j)),
                resident(dy.shape),
                resident(image.shape),
            ],
            out_specs=[out_spec, out_spec] if split else out_spec,
            scratch_shapes=[
                pltpu.VMEM((step, count), bf16),
                pltpu.VMEM((count, width), bf16),
                pltpu.VMEM((step, cols), f32),
            ],
        ),
        out_shape=[half, half] if split else jax.ShapeDtypeStruct(shape, bf16),
        compiler_params=pltpu.CompilerParams(vmem_limit_bytes=48 << 20),
        cost_estimate=pl.CostEstimate(
            flops=count * depth // 4 * width, bytes_accessed=4 << 20, transcendentals=0
        ),
        name="gradient",
    )(spots, x, dy, image)


def over_rep(value, target):
    count = lax.axis_size("rep")
    return lax.ppermute(value, "rep", [(r, target(r)) for r in range(count)])


def sibling(value):
    return over_rep(value, lambda r: r ^ 1)


def across(value):
    return over_rep(value, lambda r: r ^ 2)


def gather_rep(value):
    far = across(value)
    return [value, sibling(value), far, sibling(far)]


def reduce_rep(parts):
    near = sibling((parts[1], parts[3]))
    far = across((parts[2].astype(f32) + near[1].astype(f32)).astype(bf16))
    return parts[0].astype(f32) + near[0].astype(f32) + far.astype(f32)


def turn(value):
    reps, shards = lax.axis_size("rep"), lax.axis_size("shard")
    q = shards // reps
    pairs = []
    for r in range(reps):
        for s in range(shards):
            pairs.append((r * shards + s, (s // q) * shards + r * q + s % q))
    return lax.ppermute(value, ("rep", "shard"), pairs)


def gather_weight(weight_low):
    return lax.all_gather(weight_low, "shard", axis=0, tiled=False)


def gather_turned(moved):
    full = gather_weight(moved)
    reps = lax.axis_size("rep")
    return full.reshape(reps, full.shape[0] // reps, *full.shape[1:])


def ring_place(shards):
    mine = lax.axis_index("shard")
    odd = mine % 2
    return (1 - odd) * (mine // 2) + odd * (shards - 1 - mine // 2)


def ring_owner(place, shards):
    place = (place + 2 * shards) % shards
    back = place // ((shards + 1) // 2)
    return (1 - back) * (2 * place) + back * (2 * (shards - 1 - place) + 1)


def ring_kernel(shards, count, *refs):
    sources, dests = refs[:count], refs[count : 2 * count]
    send_sem, recv_sem, own_sem = refs[2 * count :]
    place = ring_place(shards)
    mine = ring_owner(place, shards)
    peers = [ring_owner(place + 1, shards), ring_owner(place - 1, shards)]

    barrier = pltpu.get_barrier_semaphore()
    for peer in peers:
        pl.semaphore_signal(
            barrier, inc=1, device_id={"shard": peer}, device_id_type=pl.DeviceIdType.MESH
        )
    pl.semaphore_wait(barrier, 2)

    kept = [
        pltpu.make_async_copy(sources[w], dests[w].at[mine], own_sem.at[w]) for w in range(count)
    ]
    for copy in kept:
        copy.start()
    chains = [(w, way) for w in range(count) for way in range(2)]
    copies = {}
    for step in range(shards - 1):
        for chain in chains:
            w, way = chain
            if step:
                copies[chain, step - 1].wait_recv()
            owner = ring_owner(place - step if way == 0 else place + step, shards)
            dest = dests[w].at[owner, way]
            copies[chain, step] = pltpu.make_async_remote_copy(
                src_ref=dest if step else sources[w].at[way],
                dst_ref=dest,
                send_sem=send_sem.at[w, way, step],
                recv_sem=recv_sem.at[w, way, step],
                device_id={"shard": peers[way]},
                device_id_type=pl.DeviceIdType.MESH,
            )
            copies[chain, step].start()
    for chain in chains:
        copies[chain, shards - 2].wait_recv()
        for step in range(shards - 1):
            copies[chain, step].wait_send()
    for copy in kept:
        copy.wait()


def ring_gather(*blocks):
    shards = lax.axis_size("shard")
    count = len(blocks)
    anywhere = pl.BlockSpec(memory_space=pl.ANY)
    return pl.pallas_call(
        functools.partial(ring_kernel, shards, count),
        in_specs=[anywhere] * count,
        out_specs=[anywhere] * count,
        out_shape=[jax.ShapeDtypeStruct((shards, *b.shape), b.dtype) for b in blocks],
        scratch_shapes=[
            pltpu.SemaphoreType.DMA((count, 2, shards - 1)),
            pltpu.SemaphoreType.DMA((count, 2, shards - 1)),
            pltpu.SemaphoreType.DMA((count,)),
        ],
        compiler_params=pltpu.CompilerParams(collective_id=0, has_side_effects=True),
        cost_estimate=pl.CostEstimate(flops=1 << 20, bytes_accessed=256 << 20, transcendentals=0),
        name="ring_gather",
    )(*blocks)


def as_turned(full):
    reps = lax.axis_size("rep")
    return full.reshape(reps, full.shape[0] // reps, *full.shape[1:])


def ring_scatter_kernel(count, *refs):
    sources, outs, helds = refs[:count], refs[count : 2 * count], refs[2 * count : 3 * count]
    send_sem, recv_sem = refs[3 * count :]
    shards = sources[0].shape[0]
    pieces = helds[0].shape[1]
    place = ring_place(shards)
    mine = ring_owner(place, shards)
    peers = [ring_owner(place + 1, shards), ring_owner(place - 1, shards)]

    barrier = pltpu.get_barrier_semaphore()
    for peer in peers:
        pl.semaphore_signal(
            barrier, inc=1, device_id={"shard": peer}, device_id_type=pl.DeviceIdType.MESH
        )
    pl.semaphore_wait(barrier, 2)

    chains = [
        (w, way, piece) for piece in range(pieces) for w in range(count) for way in range(2)
    ]
    copies = {}
    for step in range(shards):
        for chain in chains:
            w, way, piece = chain
            part = sources[w].shape[2] // pieces
            span = slice(piece * part, (piece + 1) * part)
            if step < shards - 1:
                owner = ring_owner(place - 1 - step if way == 0 else place + 1 + step, shards)
            else:
                owner = mine
            source = sources[w].at[owner, way, span]
            if step:
                copies[chain, step - 1].wait_recv()
                arrived = helds[w].at[way, piece, step - 1]
                total = arrived[...].astype(f32) + source[...].astype(f32)
                if step == shards - 1:
                    outs[w][way, span] = total.astype(bf16)
                    continue
                arrived[...] = total.astype(bf16)
                source = arrived
            copies[chain, step] = pltpu.make_async_remote_copy(
                src_ref=source,
                dst_ref=helds[w].at[way, piece, step],
                send_sem=send_sem.at[w, way, piece, step],
                recv_sem=recv_sem.at[w, way, piece, step],
                device_id={"shard": peers[way]},
                device_id_type=pl.DeviceIdType.MESH,
            )
            copies[chain, step].start()
    for copy in copies.values():
        copy.wait_send()


def ring_scatter(*terms):
    shards, _, rows, _ = terms[0].shape
    count = len(terms)
    pieces = 2 if rows % 32 == 0 else 1
    sems = pltpu.SemaphoreType.DMA((count, 2, pieces, shards - 1))
    whole = pl.BlockSpec(memory_space=pltpu.VMEM)
    return pl.pallas_call(
        functools.partial(ring_scatter_kernel, count),
        in_specs=[whole] * count,
        out_specs=[whole] * count,
        out_shape=[jax.ShapeDtypeStruct(t.shape[1:], bf16) for t in terms],
        scratch_shapes=[
            pltpu.VMEM((2, pieces, shards - 1, t.shape[2] // pieces, t.shape[3]), bf16)
            for t in terms
        ]
        + [sems, sems],
        compiler_params=pltpu.CompilerParams(
            collective_id=1, has_side_effects=True, vmem_limit_bytes=36 << 20
        ),
        cost_estimate=pl.CostEstimate(flops=1 << 20, bytes_accessed=256 << 20, transcendentals=0),
        name="ring_scatter",
    )(*terms)


def scatter_weight(terms):
    return lax.psum_scatter(
        terms.reshape(-1, *terms.shape[-2:]), "shard", scatter_dimension=0, tiled=True
    ).reshape(terms.shape[-3:])


def body(
    tokens,
    cotangent,
    cond,
    seq_lengths,
    stream_mask,
    w_mod,
    m_mod,
    v_mod,
    w_qkv,
    m_qkv,
    v_qkv,
    w_out,
    m_out,
    v_out,
    w_fc1,
    m_fc1,
    v_fc1,
    w_fc2,
    m_fc2,
    v_fc2,
    gains,
    m_gains,
    v_gains,
):
    tok_rows, model_width = tokens.shape
    slot_count = seq_lengths.shape[0]
    reps, shards = lax.axis_size("rep"), lax.axis_size("shard")
    rep_index, shard_index = lax.axis_index("rep"), lax.axis_index("shard")
    device_index = rep_index * shards + shard_index
    all_tokens = tok_rows * reps * shards
    reach = (MAXLEN - 2) // tok_rows + 1
    part_width = model_width // reps
    part_rows = w_mod.shape[1]
    mod_cols = w_mod.shape[2]

    seq_starts = jnp.cumsum(seq_lengths) - seq_lengths
    local_pos = device_index * tok_rows + jnp.arange(tok_rows, dtype=jnp.int32)
    seq_ids = segment_index(local_pos, seq_starts, all_tokens)
    image_col = (stream_mask == 1)[:, None]
    image_group = jnp.concatenate(gather_rep(stream_mask)) == 1
    image = image_group[:, None].astype(jnp.int32)
    text_group = ~image_group.reshape(reps, tok_rows)
    text_first = jnp.argmax(text_group, axis=1).astype(jnp.int32)
    spots = jnp.concatenate(
        [
            jnp.minimum(text_first // 16 * 16, tok_rows - WINDOW),
            jnp.any(text_group, axis=1).astype(jnp.int32),
            rep_index[None].astype(jnp.int32),
        ]
    )

    silu_cond = jax.nn.silu(cond).astype(bf16)
    cond_rows = lax.dynamic_slice_in_dim(silu_cond, shard_index * part_rows, part_rows, 1)
    mod_terms = jnp.concatenate(
        [
            jnp.dot(cond_rows, w_mod[s].astype(bf16), preferred_element_type=f32)
            for s in range(2)
        ],
        axis=0,
    ).astype(bf16)
    device_count = reps * shards
    firsts = segment_index(
        jnp.arange(device_count, dtype=jnp.int32) * tok_rows, seq_starts, all_tokens
    )
    seconds = jnp.minimum(firsts + 1, slot_count - 1)
    stream_offset = jnp.arange(2, dtype=jnp.int32) * slot_count
    wanted = jnp.stack([firsts, seconds], axis=1)[:, :, None] + stream_offset
    hot = (wanted.reshape(-1, 1) == jnp.arange(2 * slot_count, dtype=jnp.int32)).astype(bf16)
    mod_sent = jnp.dot(hot, mod_terms, preferred_element_type=f32).astype(bf16)
    mod_got = lax.all_to_all(
        mod_sent.reshape(device_count, 4, mod_cols), ("rep", "shard"), 0, 0, tiled=True
    )
    mod_sum = jnp.sum(mod_got.reshape(reps, shards, 4, mod_cols).astype(f32), axis=1).astype(bf16)
    mod_rows = jnp.concatenate([mod_sum[r] for r in range(reps)], axis=1)

    qkv_low = w_qkv.astype(bf16)
    chunks = [
        over_rep(
            qkv_low[:, :, i * part_width : (i + 1) * part_width],
            lambda r, i=i: (3 * r + i) % reps,
        )
        for i in range(3)
    ]
    turns = rep_index % 3

    def rolled(parts, amount):
        return [
            jnp.where(
                amount == 0,
                parts[t],
                jnp.where(amount == 1, parts[(t + 1) % 3], parts[(t + 2) % 3]),
            )
            for t in range(3)
        ]

    qkv_weights, out_full = ring_gather(
        jnp.concatenate(rolled(chunks, turns), axis=2), turn(w_out.astype(bf16))
    )
    out_weights = as_turned(out_full)
    qkv_weights, mod_rows, fc1_low = lax.optimization_barrier(
        (qkv_weights, mod_rows, w_fc1.astype(bf16))
    )
    fc1_weights = gather_weight(fc1_low)
    first_seq = seq_ids[0]
    second_seq = jnp.minimum(first_seq + 1, slot_count - 1)
    is_second = (seq_ids != first_seq)[:, None]

    def mod_block(index):
        span = slice(index * model_width, (index + 1) * model_width)
        rows = mod_rows[:, span].astype(f32)
        pick = [jnp.where(is_second, rows[2 + s][None], rows[s][None]) for s in range(2)]
        return jnp.where(image_col, pick[0], pick[1])

    shift_one, scale_one, gate_one, shift_two, scale_two, gate_two = [
        mod_block(i) for i in range(6)
    ]
    stream_in = tokens.astype(f32)
    back_out = cotangent.astype(f32)
    act_one = layer_modulate(stream_in, shift_one, scale_one).astype(bf16)
    act_one_group = jnp.concatenate(gather_rep(act_one))
    d_down = (gate_two * back_out).astype(bf16)
    d_down_group = jnp.concatenate(gather_rep(d_down))

    fc2_low, act_one = lax.optimization_barrier((w_fc2.astype(bf16), act_one))
    fc2_turned = turn(fc2_low)

    query_sent, pair_sent, qk_pre = qkv_product(spots, act_one_group, qkv_weights, image, gains)
    pair_sent, fc2_turned = lax.optimization_barrier((pair_sent, fc2_turned))

    bunch = 2 * reps
    bunches = shards // bunch
    half_width = part_width // 2
    groups = [[q * bunch + i for i in range(bunch)] for q in range(bunches)]

    def exchange(value):
        return lax.all_to_all(
            value, "shard", 0, 0, axis_index_groups=None if bunches == 1 else groups, tiled=True
        )

    stretch_count = reps * bunches
    stretch_rows = bunch * tok_rows
    halo = reach * tok_rows

    def stretch_shift(value, steps):
        def place(stretch, g):
            return (stretch % bunches) * bunch + (stretch // bunches) * 2 + g

        pairs = [
            (place(t, g), place(t + steps, g))
            for t in range(stretch_count)
            for g in range(2)
            if 0 <= t + steps < stretch_count
        ]
        return lax.ppermute(value, "shard", pairs)

    pair_own = exchange(pair_sent).reshape(stretch_rows, 2 * half_width)
    pair_before = stretch_shift(pair_own[-halo:], 1)
    pair_after = stretch_shift(pair_own[:halo], -1)
    query_sent, pair_before, pair_after = lax.optimization_barrier(
        (query_sent, pair_before, pair_after)
    )
    query_own = exchange(query_sent).reshape(stretch_rows, half_width)
    fc2_turned, query_own, fc1_weights, d_down_group = lax.optimization_barrier(
        (fc2_turned, query_own, fc1_weights, d_down_group)
    )
    fc2_weights = as_turned(gather_weight(fc2_turned))
    window_rows = stretch_rows + 2 * halo
    stretch = ((shard_index % bunch) // 2) * bunches + shard_index // bunch
    stretch_first = stretch * stretch_rows
    qid = segment_index(
        stretch_first + jnp.arange(stretch_rows, dtype=jnp.int32), seq_starts, all_tokens
    )
    kid = segment_index(
        stretch_first - halo + jnp.arange(window_rows, dtype=jnp.int32), seq_starts, all_tokens
    )
    seq_ends = seq_starts + seq_lengths
    low_pos = seq_starts[qid[::QB]] - (stretch_first - halo)
    high_pos = seq_ends[qid[QB - 1 :: QB]] - (stretch_first - halo)
    lo = jnp.clip(low_pos // KB, 0, window_rows // KB).astype(jnp.int32)
    hi = jnp.clip((high_pos + KB - 1) // KB, 0, window_rows // KB).astype(jnp.int32)
    attended_own, logsum = attention(
        query_own, pair_own, pair_before, pair_after, lo, hi, qid, kid
    )
    attended_came = exchange(attended_own.reshape(bunch, tok_rows, half_width))

    def split_group(value):
        return [value[p * tok_rows : (p + 1) * tok_rows] for p in range(reps)]

    branch_terms, attended_low = forward_product(
        spots, attended_came, out_weights, image, gathers=True
    )
    branch = reduce_rep(split_group(branch_terms))
    mid = stream_in + gate_one * branch
    act_two = layer_modulate(mid, shift_two, scale_two).astype(bf16)
    act_two_group = jnp.concatenate(gather_rep(act_two))
    gelu_low, gelu_slope = forward_product(spots, act_two_group, fc1_weights, image, gelu=True)
    down_terms = forward_product(spots, gelu_low, fc2_weights, image)[0]

    fc2_terms = gradient(spots, gelu_low, d_down_group, image, fc2_weights.shape)
    fc2_terms, gelu_slope = lax.optimization_barrier((fc2_terms, gelu_slope))
    fc2_own = scatter_weight(fc2_terms)
    d_up = backward_product(spots, d_down_group, fc2_weights, image, factor=gelu_slope)
    d_act_two = reduce_rep(split_group(backward_product(spots, d_up, fc1_weights, image)))
    d_mid_norm, d_shift_two, d_scale_two = jax.vjp(layer_modulate, mid, shift_two, scale_two)[1](
        d_act_two
    )
    d_mid = back_out + d_mid_norm
    d_branch = (gate_one * d_mid).astype(bf16)
    fc1_image, fc1_text = gradient(
        spots, act_two_group, d_up, image, fc1_weights.shape, split=True
    )
    fc1_image, fc1_text, d_branch = lax.optimization_barrier((fc1_image, fc1_text, d_branch))
    fc1_image = scatter_weight(fc1_image)
    d_gate_one = d_mid * branch
    d_branch_group = jnp.concatenate(gather_rep(d_branch))
    d_attended = backward_product(spots, d_branch_group, out_weights, image, packs=True)
    out_terms = gradient(spots, attended_low, d_branch_group, image, out_weights.shape)
    d_attended_own = exchange(d_attended).reshape(stretch_rows, half_width)
    d_attended_own, out_terms = lax.optimization_barrier((d_attended_own, out_terms))
    d_query_own, d_before, d_after, d_pair_own = attention_back(
        query_own,
        pair_own,
        pair_before,
        pair_after,
        d_attended_own,
        attended_own,
        lo,
        hi,
        qid,
        kid,
        logsum,
    )
    d_query_came = exchange(d_query_own.reshape(bunch, tok_rows, half_width))
    from_later = stretch_shift(d_before, -1).astype(f32)
    from_earlier = stretch_shift(d_after, 1).astype(f32)
    rest = jnp.zeros((stretch_rows - halo, 2 * half_width), f32)
    d_pair_own = (
        d_pair_own
        + jnp.concatenate([rest, from_later], axis=0)
        + jnp.concatenate([from_earlier, rest], axis=0)
    )
    d_pair_came = exchange(d_pair_own.astype(bf16).reshape(bunch, tok_rows, 2 * half_width))
    up_fc2 = adam_step(w_fc2, m_fc2, v_fc2, turn(fc2_own).astype(f32), rate_fc2)
    d_pair_came, down_terms, fc1_text, up_fc2 = lax.optimization_barrier(
        (d_pair_came, down_terms, fc1_text, up_fc2)
    )
    fc1_text = scatter_weight(fc1_text)
    down_proj = reduce_rep(split_group(down_terms))
    output = mid + gate_two * down_proj
    d_gate_two = back_out * down_proj
    d_qkv, gain_sums = norm_back(spots, d_query_came, d_pair_came, qk_pre, image, gains)
    d_act_one = reduce_rep(split_group(backward_product(spots, d_qkv, qkv_weights, image)))
    qkv_terms = gradient(spots, act_one_group, d_qkv, image, qkv_weights.shape)
    d_in_norm, d_shift_one, d_scale_one = jax.vjp(layer_modulate, stream_in, shift_one, scale_one)[
        1
    ](d_act_one)
    d_tokens = d_mid + d_in_norm
    d_mod_tok = jnp.concatenate(
        [d_shift_one, d_scale_one, d_gate_one, d_shift_two, d_scale_two, d_gate_two], axis=1
    )
    image_flag = image_col[:, 0]
    second_flag = is_second[:, 0]
    selector = jnp.stack(
        [
            ~second_flag & image_flag,
            ~second_flag & ~image_flag,
            second_flag & image_flag,
            second_flag & ~image_flag,
        ],
        axis=1,
    ).astype(f32)
    pooled = jnp.einsum("tp,te->pe", selector, d_mod_tok, precision=lax.Precision.HIGHEST)
    gain_sums = jnp.sum(gain_sums.reshape(2, 2, part_width // HD, HD), axis=2)
    gain_part = jnp.concatenate([gain_sums[0], gain_sums[1]], axis=1)
    gain_rows = jnp.concatenate([gain_part, jnp.zeros_like(gain_part)], axis=0)
    leaving = jnp.stack(
        [
            jnp.concatenate([pooled[:, r * mod_cols : (r + 1) * mod_cols], gain_rows], axis=1)
            for r in range(reps)
        ]
    )
    qkv_terms, out_terms, fc1_image, fc1_text, leaving = lax.optimization_barrier(
        (qkv_terms, out_terms, fc1_image, fc1_text, leaving)
    )
    leaving = jnp.broadcast_to(leaving[:, None], (reps, shards, *leaving.shape[1:]))
    came = lax.all_to_all(
        leaving.reshape(device_count, *leaving.shape[2:]), ("rep", "shard"), 0, 0, tiled=True
    )
    out_terms = out_terms.reshape(shards, 2, -1, out_terms.shape[-1])
    g_qkv_group, g_out = ring_scatter(qkv_terms, out_terms)
    g_qkv_group, g_out, came = lax.optimization_barrier((g_qkv_group, g_out, came))
    g_out = turn(g_out)
    g_fc1 = jnp.concatenate([fc1_image, fc1_text], axis=0)
    g_parts = [
        g_qkv_group[:, :, t * part_width : (t + 1) * part_width] for t in range(3)
    ]
    g_parts = rolled(g_parts, (3 - turns) % 3)
    g_qkv = jnp.concatenate(
        [over_rep(g_parts[i], lambda d, i=i: (3 * (d - i)) % reps) for i in range(3)], axis=2
    )

    g_gains = jnp.sum(came[:, :2, mod_cols:], axis=0)
    came = came[:, :, :mod_cols].reshape(2 * device_count, 2, mod_cols)
    seqs = jnp.stack([firsts, seconds], axis=1).reshape(-1)
    hot_seq = (seqs[:, None] == jnp.arange(slot_count, dtype=jnp.int32)).astype(bf16)
    cond_seq = jnp.dot(hot_seq, cond_rows, preferred_element_type=f32)
    g_mod = jnp.stack(
        [
            lax.dot_general(
                cond_seq,
                came[:, s],
                (((0,), (0,)), ((), ())),
                precision=lax.Precision.HIGHEST,
                preferred_element_type=f32,
            )
            for s in range(2)
        ]
    )
    up_mod = adam_step(w_mod, m_mod, v_mod, g_mod, rate_mod)
    up_qkv = adam_step(w_qkv, m_qkv, v_qkv, g_qkv.astype(f32), rate_qkv)
    up_out = adam_step(w_out, m_out, v_out, g_out.astype(f32), rate_out)
    up_fc1 = adam_step(w_fc1, m_fc1, v_fc1, g_fc1.astype(f32), rate_fc1)
    up_gains = adam_step(gains, m_gains, v_gains, g_gains, rate_gains)
    return (
        output.astype(bf16),
        d_tokens,
        *up_mod,
        *up_qkv,
        *up_out,
        *up_fc1,
        *up_fc2,
        *up_gains[:3],
    )


def solution(mesh):
    rows = P(("rep", "shard"), None)
    held = P(None, "shard", "rep")
    return jax.shard_map(
        body,
        mesh=mesh,
        in_specs=(rows, rows, P(), P(), P(("rep", "shard")), *([held] * 15), P(), P(), P()),
        out_specs=(rows, rows, *([held] * 20), P(), P(), P()),
        check_vma=False,
    )
```

```python
import functools

import jax
import jax.numpy as jnp
from jax import lax
from jax.experimental import pallas as pl
from jax.experimental.pallas import tpu as pltpu
from jax.sharding import PartitionSpec as P

HD = 64
MAXLEN = 1178
STEP = 7

norm_eps = 1e-06
adam_eps = 1e-08
score_scale = 0.125
rate_mod = 0.03
rate_qkv = 0.03
rate_out = 0.15
rate_fc1 = 0.03
rate_fc2 = 0.015
rate_gains = 1.0

bf16 = jnp.bfloat16
f32 = jnp.float32
QB = 256
KB = 256
TXT = 154
WINDOW = (TXT + 15 + 15) // 16 * 16
COLS = 512
GELU_A = 0.7978845608028654
GELU_B = 0.044715
NN = (((1,), (0,)), ((), ()))
NT = (((1,), (1,)), ((), ()))
TN = (((0,), (0,)), ((), ()))


def layer_modulate(values, shift, scale):
    centred = values - jnp.mean(values, axis=-1, keepdims=True)
    normed = centred * lax.rsqrt(jnp.mean(centred * centred, axis=-1, keepdims=True) + norm_eps)
    return normed * (1.0 + scale) + shift


def adam_step(weight, moment_one, moment_two, grads, rate):
    new_one = 0.9 * moment_one + 0.1 * grads
    new_two = 0.999 * moment_two + 0.001 * grads * grads
    fixed_one = new_one / (1.0 - 0.9**STEP)
    fixed_two = new_two / (1.0 - 0.999**STEP)
    new_weight = weight - rate * (fixed_one / (jnp.sqrt(fixed_two) + adam_eps) + 0.01 * weight)
    return (new_weight, new_one, new_two, new_weight.astype(bf16))


def segment_index(position, seq_starts, all_tokens):
    counted = jnp.sum((seq_starts[None, :] <= position[:, None]).astype(jnp.int32), axis=1) - 1
    inside = (position >= 0) & (position < all_tokens)
    return jnp.where(inside, counted, -1)


def fill_window(own_ref, before_ref, after_ref, keys, values):
    halo, own = before_ref.shape[0], own_ref.shape[0]
    heads = keys.shape[0]
    width = heads * HD
    parts = ((before_ref, 0, halo), (own_ref, halo, own), (after_ref, halo + own, halo))
    for source, first, count in parts:
        for head in range(heads):
            for index, dest in ((0, keys), (1, values)):
                start = index * width + head * HD
                dest[head, first : first + count, :HD] = source[:, start : start + HD]


def attend_kernel(
    lo_ref, hi_ref, q_ref, own_ref, before_ref, after_ref, qid_ref, kid_ref, o_ref, l_ref, keys, values, acc
):
    step = pl.program_id(0)
    heads = keys.shape[0]

    @pl.when(step == 0)
    def _():
        lane = lax.broadcasted_iota(jnp.int32, values.shape[1:], 1)
        for head in range(heads):
            values[head] = (lane == HD).astype(bf16)
        fill_window(own_ref, before_ref, after_ref, keys, values)

    qid = qid_ref[...]
    diagonal = lax.broadcasted_iota(jnp.int32, (QB, QB), 0) == lax.broadcasted_iota(
        jnp.int32, (QB, QB), 1
    )
    queries = [q_ref[:, head * HD : (head + 1) * HD] for head in range(heads)]
    acc[...] = jnp.zeros_like(acc)

    @pl.loop(lo_ref[step], hi_ref[step])
    def _(block):
        rows = pl.ds(pl.multiple_of(block * KB, KB), KB)
        same = qid == kid_ref[pl.ds(block, 1), :]
        for head in range(heads):
            scores = lax.dot_general(
                queries[head], keys[head, rows, :], NT, preferred_element_type=f32
            )
            lifted = jnp.where(same, jnp.exp(scores), 0.0).astype(bf16)
            acc[head] += jnp.dot(lifted, values[head, rows, :], preferred_element_type=f32)

    for head in range(heads):
        total = acc[head, :, HD : HD + 1]
        o_ref[:, head * HD : (head + 1) * HD] = (acc[head, :, :HD] / total).astype(bf16)
        l_ref[0, head : head + 1, :] = jnp.sum(
            jnp.where(diagonal, jnp.log(total), 0.0), axis=0, keepdims=True
        )


def attend_back_kernel(
    lo_ref,
    hi_ref,
    q_ref,
    own_ref,
    before_ref,
    after_ref,
    do_ref,
    o_ref,
    qid_ref,
    kid_ref,
    l_ref,
    dq_ref,
    d_before_ref,
    d_after_ref,
    d_own_ref,
    keys,
    values,
    d_keys,
    d_values,
    d_query,
):
    step = pl.program_id(0)
    heads = keys.shape[0]
    width = heads * HD

    @pl.when(step == 0)
    def _():
        fill_window(own_ref, before_ref, after_ref, keys, values)
        d_keys[...] = jnp.zeros_like(d_keys)
        d_values[...] = jnp.zeros_like(d_values)

    qid = qid_ref[0]
    ones = jnp.ones((8, HD), bf16)
    queries, outs, dots = [], [], []
    for head in range(heads):
        lanes = slice(head * HD, (head + 1) * HD)
        queries.append(q_ref[:, lanes])
        outs.append(do_ref[:, lanes])
        product = outs[head].astype(f32) * o_ref[:, lanes].astype(f32)
        coarse = product.astype(bf16)
        fine = (product - coarse.astype(f32)).astype(bf16)
        total = lax.dot_general(ones, coarse, NT, preferred_element_type=f32)
        dots.append((total + lax.dot_general(ones, fine, NT, preferred_element_type=f32))[:1])
    d_query[...] = jnp.zeros_like(d_query)

    @pl.loop(lo_ref[step], hi_ref[step])
    def _(block):
        rows = pl.ds(pl.multiple_of(block * KB, KB), KB)
        same = kid_ref[rows, :] == qid
        for head in range(heads):
            key = keys[head, rows, :]
            scores = lax.dot_general(key, queries[head], NT, preferred_element_type=f32)
            probs = jnp.where(same, jnp.exp(scores - l_ref[0, head : head + 1, :]), 0.0)
            d_values[head, rows, :] += jnp.dot(
                probs.astype(bf16), outs[head], preferred_element_type=f32
            )
            d_probs = lax.dot_general(
                values[head, rows, :], outs[head], NT, preferred_element_type=f32
            )
            d_scores = (probs * (d_probs - dots[head])).astype(bf16)
            d_keys[head, rows, :] += jnp.dot(d_scores, queries[head], preferred_element_type=f32)
            d_query[head] += lax.dot_general(d_scores, key, TN, preferred_element_type=f32)

    for head in range(heads):
        dq_ref[:, head * HD : (head + 1) * HD] = (d_query[head] * score_scale).astype(bf16)

    @pl.when(step == pl.num_programs(0) - 1)
    def _():
        halo, own = d_before_ref.shape[0], d_own_ref.shape[0]
        for index, source in ((0, d_keys), (1, d_values)):
            for head in range(heads):
                span = slice(index * width + head * HD, index * width + (head + 1) * HD)
                d_before_ref[:, span] = source[head, :halo, :].astype(bf16)
                d_own_ref[:, span] = source[head, halo : halo + own, :]
                d_after_ref[:, span] = source[head, halo + own :, :].astype(bf16)


def resident(shape):
    return pl.BlockSpec(shape, lambda *index: (0,) * len(shape))


def attention(query, own, before, after, lo, hi, qid, kid):
    count, width = query.shape
    heads = width // HD
    window = count + 2 * before.shape[0]
    steps = count // QB
    return pl.pallas_call(
        attend_kernel,
        grid_spec=pltpu.PrefetchScalarGridSpec(
            num_scalar_prefetch=2,
            grid=(steps,),
            in_specs=[
                pl.BlockSpec((QB, width), lambda i, lo, hi: (i, 0)),
                resident(own.shape),
                resident(before.shape),
                resident(after.shape),
                pl.BlockSpec((QB, 1), lambda i, lo, hi: (i, 0)),
                resident((window // KB, KB)),
            ],
            out_specs=[
                pl.BlockSpec((QB, width), lambda i, lo, hi: (i, 0)),
                pl.BlockSpec((1, 8, QB), lambda i, lo, hi: (i, 0, 0)),
            ],
            scratch_shapes=[
                pltpu.VMEM((heads, window, HD), bf16),
                pltpu.VMEM((heads, window, 2 * HD), bf16),
                pltpu.VMEM((heads, QB, 2 * HD), f32),
            ],
        ),
        out_shape=[
            jax.ShapeDtypeStruct((count, width), bf16),
            jax.ShapeDtypeStruct((steps, 8, QB), f32),
        ],
        compiler_params=pltpu.CompilerParams(vmem_limit_bytes=40 << 20),
        cost_estimate=pl.CostEstimate(flops=1 << 30, bytes_accessed=4 << 20, transcendentals=0),
        name="attend",
    )(lo, hi, query, own, before, after, qid[:, None], kid.reshape(window // KB, KB))


def attention_back(query, own, before, after, d_out, out, lo, hi, qid, kid, logsum):
    count, width = query.shape
    heads = width // HD
    halo = before.shape[0]
    window = count + 2 * halo
    steps = count // QB
    rows = pl.BlockSpec((QB, width), lambda i, lo, hi: (i, 0))
    return pl.pallas_call(
        attend_back_kernel,
        grid_spec=pltpu.PrefetchScalarGridSpec(
            num_scalar_prefetch=2,
            grid=(steps,),
            in_specs=[
                rows,
                resident(own.shape),
                resident(before.shape),
                resident(after.shape),
                rows,
                rows,
                pl.BlockSpec((1, 1, QB), lambda i, lo, hi: (i, 0, 0)),
                resident((window, 1)),
                pl.BlockSpec((1, 8, QB), lambda i, lo, hi: (i, 0, 0)),
            ],
            out_specs=[
                rows,
                resident((halo, 2 * width)),
                resident((halo, 2 * width)),
                resident((count, 2 * width)),
            ],
            scratch_shapes=[pltpu.VMEM((heads, window, HD), bf16)] * 2
            + [pltpu.VMEM((heads, window, HD), f32)] * 2
            + [pltpu.VMEM((heads, QB, HD), f32)],
        ),
        out_shape=[
            jax.ShapeDtypeStruct((count, width), bf16),
            jax.ShapeDtypeStruct((halo, 2 * width), bf16),
            jax.ShapeDtypeStruct((halo, 2 * width), bf16),
            jax.ShapeDtypeStruct((count, 2 * width), f32),
        ],
        compiler_params=pltpu.CompilerParams(vmem_limit_bytes=58 << 20),
        cost_estimate=pl.CostEstimate(flops=24 << 30, bytes_accessed=8 << 20, transcendentals=0),
        name="attend_back",
    )(lo, hi, query, own, before, after, d_out, out, qid.reshape(steps, 1, QB), kid[:, None], logsum)


def text_windows(spots, blocks, count, work):
    for p in range(blocks):

        @pl.when(spots[blocks + p] == 1)
        def _(p=p):
            first = pl.multiple_of(spots[p], 16)
            base = p * (count // blocks)
            work(p, first, pl.ds(pl.multiple_of(base + first, 16), WINDOW))


def flat(value):
    return value.reshape(-1, value.shape[-1])


def product(x_ref, rows, weight, dims):
    total = None
    for cols, get in weight:
        term = lax.dot_general(x_ref[rows, cols], get(), dims, preferred_element_type=f32)
        total = term if total is None else total + term
    return total


def group_sums(values, blocks_of):
    coarse = values.astype(bf16)
    fine = (values - coarse.astype(f32)).astype(bf16)
    return jnp.dot(coarse, blocks_of, preferred_element_type=f32) + jnp.dot(
        fine, blocks_of, preferred_element_type=f32
    )


def head_blocks(width):
    row = lax.broadcasted_iota(jnp.int32, (width, width), 0) // HD
    col = lax.broadcasted_iota(jnp.int32, (width, width), 1) // HD
    return (row == col).astype(bf16)


def qkv_kernel(blocks, spots, x_ref, w0, w1, image_ref, gain_ref, q_ref, kv_ref, pre_ref):
    kind = pl.program_id(0)
    every = slice(None)
    size, width = q_ref.shape[1:]
    rep = spots[2 * blocks]
    spread = head_blocks(2 * width)

    def finish(t, values, gain):
        if t < 2:
            mean = group_sums(values * values, spread) * (1.0 / HD)
            values = values * lax.rsqrt(mean + norm_eps) * gain
        values = values.astype(bf16)
        return values * jnp.asarray(score_scale, bf16) if t == 0 else values

    for t in range(3):

        @pl.when(kind == t)
        def _(t=t):
            packed_ref = kv_ref if t else q_ref
            lanes = slice((t - 1) * width, t * width) if t else slice(0, width)

            @pl.loop(0, blocks)
            def _(p):
                rows = pl.ds(pl.multiple_of(p * size, size), size)
                values = product(x_ref, rows, [(every, lambda: flat(w0[...]))], NN)
                if t < 2:
                    pre_ref[rows, :] = values
                values = finish(t, values, gain_ref[0, :1])
                for g in range(2):
                    packed_ref[pl.ds((rep ^ p) * 2 + g, 1), :, lanes] = values[
                        :, g * width : (g + 1) * width
                    ][None]

            def text(p, first, rows):
                values = product(x_ref, rows, [(every, lambda: flat(w1[...]))], NN)
                image = image_ref[rows, :] == 1
                if t < 2:
                    pre_ref[rows, :] = jnp.where(image, pre_ref[rows, :], values)
                values = finish(t, values, gain_ref[0, 1:])
                for g in range(2):
                    place = (
                        pl.ds((rep ^ p) * 2 + g, 1),
                        pl.ds(first, WINDOW),
                        lanes,
                    )
                    packed_ref[place] = jnp.where(
                        image[None], packed_ref[place], values[:, g * width : (g + 1) * width][None]
                    )

            text_windows(spots, blocks, x_ref.shape[0], text)


def column_weights(weight, tile):
    shards, _, rows, _ = weight.shape
    return [
        pl.BlockSpec((shards, 1, rows, tile), lambda j, s, stream=stream: (0, stream, 0, j))
        for stream in range(2)
    ]


def tiled_gains(gains, heads):
    return jnp.stack([jnp.tile(gains[:, :HD], (1, heads)), jnp.tile(gains[:, HD:], (1, heads))])


def qkv_product(spots, x, weight, image, gains):
    count, depth = x.shape
    blocks = (spots.shape[0] - 1) // 2
    part = weight.shape[3] // 3
    size = count // blocks
    return pl.pallas_call(
        functools.partial(qkv_kernel, blocks),
        grid_spec=pltpu.PrefetchScalarGridSpec(
            num_scalar_prefetch=1,
            grid=(3,),
            in_specs=[
                resident(x.shape),
                *column_weights(weight, part),
                resident(image.shape),
                pl.BlockSpec((1, 2, part), lambda j, s: (jnp.minimum(j, 1), 0, 0)),
            ],
            out_specs=[
                resident((2 * blocks, size, part // 2)),
                resident((2 * blocks, size, part)),
                pl.BlockSpec((count, part), lambda j, s: (0, jnp.minimum(j, 1))),
            ],
        ),
        out_shape=[
            jax.ShapeDtypeStruct((2 * blocks, size, part // 2), bf16),
            jax.ShapeDtypeStruct((2 * blocks, size, part), bf16),
            jax.ShapeDtypeStruct((count, 2 * part), f32),
        ],
        compiler_params=pltpu.CompilerParams(vmem_limit_bytes=40 << 20),
        cost_estimate=pl.CostEstimate(flops=1 << 30, bytes_accessed=4 << 20, transcendentals=0),
        name="qkv_product",
    )(spots, x, weight, weight, image, tiled_gains(gains, part // HD))


def norm_back_kernel(blocks, spots, q_ref, kv_ref, pre_ref, image_ref, gain_ref, out_ref, sum_ref, both):
    @pl.when(pl.program_id(0) == 0)
    def _():
        sum_ref[...] = jnp.zeros_like(sum_ref)

    part = both.shape[1]
    width = part // 2
    image = image_ref[...] == 1
    spread = head_blocks(part)
    for t in range(3):
        came_ref = kv_ref if t else q_ref
        lanes = slice((t - 1) * width, t * width) if t else slice(0, width)
        for g in range(2):
            both[:, g * width : (g + 1) * width] = came_ref[g, :, lanes].astype(f32)
        grad = both[...]
        if t < 2:
            pre = pre_ref[:, t * part : (t + 1) * part]
            scale = lax.rsqrt(group_sums(pre * pre, spread) * (1.0 / HD) + norm_eps)
            gain = jnp.where(image, gain_ref[t, :1], gain_ref[t, 1:])
            each = grad * pre * scale
            total = jnp.sum(each, axis=0, keepdims=True)
            text = jnp.sum(jnp.where(image, 0.0, each), axis=0, keepdims=True)
            sum_ref[2 * t : 2 * t + 1, :] += total - text
            sum_ref[2 * t + 1 : 2 * t + 2, :] += text
            grad = grad * gain
            mean = group_sums(grad * pre, spread) * (1.0 / HD)
            grad = scale * (grad - pre * (scale * scale * mean))
        out_ref[:, t * part : (t + 1) * part] = grad.astype(bf16)


def norm_back(spots, came_query, came_pair, pre, image, gains):
    blocks = (spots.shape[0] - 1) // 2
    _, size, part = came_pair.shape
    tiled = tiled_gains(gains, part // HD)
    return pl.pallas_call(
        functools.partial(norm_back_kernel, blocks),
        grid_spec=pltpu.PrefetchScalarGridSpec(
            num_scalar_prefetch=1,
            grid=(blocks,),
            in_specs=[
                pl.BlockSpec((2, size, part // 2), lambda p, s: (s[2 * blocks] ^ p, 0, 0)),
                pl.BlockSpec((2, size, part), lambda p, s: (s[2 * blocks] ^ p, 0, 0)),
                pl.BlockSpec((size, 2 * part), lambda p, s: (p, 0)),
                pl.BlockSpec((size, 1), lambda p, s: (p, 0)),
                resident(tiled.shape),
            ],
            out_specs=[
                pl.BlockSpec((size, 3 * part), lambda p, s: (p, 0)),
                resident((4, part)),
            ],
            scratch_shapes=[pltpu.VMEM((size, part), f32)],
        ),
        out_shape=[
            jax.ShapeDtypeStruct((blocks * size, 3 * part), bf16),
            jax.ShapeDtypeStruct((4, part), f32),
        ],
        compiler_params=pltpu.CompilerParams(vmem_limit_bytes=32 << 20),
        cost_estimate=pl.CostEstimate(flops=4 << 30, bytes_accessed=12 << 20, transcendentals=0),
        name="norm_back",
    )(spots, came_query, came_pair, pre, image, tiled)


def forward_kernel(blocks, gathers, gelu, spots, x_ref, w0, w1, image_ref, *rest):
    rep = spots[2 * blocks]
    out_ref = rest[0]
    if gathers:
        x_out = rest[1]
        size, width = x_ref.shape[1:]

        @pl.when(pl.program_id(0) == 0)
        def _():
            for p in range(blocks):
                for g in range(2):
                    x_out[p * size : (p + 1) * size, g * width : (g + 1) * width] = x_ref[
                        pl.ds((rep ^ p) * 2 + g, 1)
                    ][0]

        x_ref = x_out
    every = slice(None)
    count = x_ref.shape[0]

    def finish(values):
        if not gelu:
            return (values.astype(bf16),)
        square = values * values
        bend = jnp.tanh(values * (GELU_A + GELU_A * GELU_B * square))
        half = 0.5 * (1.0 + bend)
        slope = half + 0.5 * values * (1.0 - bend * bend) * (GELU_A + 3.0 * GELU_A * GELU_B * square)
        return (values * half).astype(bf16), slope.astype(bf16)

    outs = rest if gelu else (out_ref,)
    chunk = count // (blocks if gelu else 2)

    @pl.loop(0, count // chunk)
    def _(p):
        rows = pl.ds(pl.multiple_of(p * chunk, chunk), chunk)
        values = product(x_ref, rows, [(every, lambda: flat(w0[...]))], NN)
        for out, value in zip(outs, finish(values)):
            out[rows, :] = value

    def text(p, first, rows):
        values = product(x_ref, rows, [(every, lambda: flat(w1[...]))], NN)
        image = image_ref[rows, :] == 1
        for out, value in zip(outs, finish(values)):
            out[rows, :] = jnp.where(image, out[rows, :], value)

    text_windows(spots, blocks, count, text)


def forward_product(spots, x, weight, image, gathers=False, gelu=False):
    blocks = (spots.shape[0] - 1) // 2
    if weight.ndim == 5:
        tiles, q, _, rows, tile = weight.shape
        weights = [
            pl.BlockSpec((1, q, 1, rows, tile), lambda j, s, stream=stream: (j, 0, stream, 0, 0))
            for stream in range(2)
        ]
        depth = q * rows
    else:
        depth, tile = weight.shape[0] * weight.shape[2], COLS
        tiles = weight.shape[3] // tile
        weights = column_weights(weight, tile)
    count = image.shape[0]
    column = pl.BlockSpec((count, tile), lambda j, s: (0, j))
    whole = jax.ShapeDtypeStruct((count, tiles * tile), bf16)
    out_specs, out_shape = [column], [whole]
    if gathers:
        out_specs.append(resident((count, depth)))
        out_shape.append(jax.ShapeDtypeStruct((count, depth), bf16))
    if gelu:
        out_specs.append(column)
        out_shape.append(whole)
    return pl.pallas_call(
        functools.partial(forward_kernel, blocks, gathers, gelu),
        grid_spec=pltpu.PrefetchScalarGridSpec(
            num_scalar_prefetch=1,
            grid=(tiles,),
            in_specs=[resident(x.shape), *weights, resident(image.shape)],
            out_specs=out_specs,
        ),
        out_shape=out_shape,
        compiler_params=pltpu.CompilerParams(vmem_limit_bytes=40 << 20),
        cost_estimate=pl.CostEstimate(
            flops=count * depth // 4 * tiles * tile, bytes_accessed=4 << 20, transcendentals=0
        ),
        name="forward_product",
    )(spots, x, weight, weight, image)


def backward_kernel(blocks, turned, scaled, packs, spots, dy_ref, w0, w1, image_ref, *rest):
    rest = list(rest)
    factor_ref = rest.pop(0) if scaled else None
    out_ref = rest[0]
    if turned:
        tiles, tile = w0.shape[0], w0.shape[4]
        weights = [
            [
                (slice(n * tile, (n + 1) * tile), lambda w=w, n=n: flat(w[n, :, 0]))
                for n in range(tiles)
            ]
            for w in (w0, w1)
        ]
    else:
        every = slice(None)
        weights = [[(every, lambda w=w: flat(w[...]))] for w in (w0, w1)]
    count = dy_ref.shape[0]
    size = count // blocks
    rep = spots[2 * blocks]
    part = pl.program_id(0)

    def finish(rows, values):
        if scaled:
            values = values * factor_ref[rows, :].astype(f32)
        return values.astype(bf16)

    chunk = size if packs or scaled else count // 2

    @pl.loop(0, count // chunk)
    def _(p):
        rows = pl.ds(pl.multiple_of(p * chunk, chunk), chunk)
        values = finish(rows, product(dy_ref, rows, weights[0], NT))
        if packs:
            out_ref[pl.ds((rep ^ p) * 2 + part, 1)] = values[None]
        else:
            out_ref[rows, :] = values

    def text(p, first, rows):
        values = finish(rows, product(dy_ref, rows, weights[1], NT))
        image = image_ref[rows, :] == 1
        if packs:
            place = (pl.ds((rep ^ p) * 2 + part, 1), pl.ds(first, WINDOW), slice(None))
            out_ref[place] = jnp.where(image[None], out_ref[place], values[None])
        else:
            out_ref[rows, :] = jnp.where(image, out_ref[rows, :], values)

    text_windows(spots, blocks, count, text)


def backward_product(spots, dy, weight, image, factor=None, packs=False):
    blocks = (spots.shape[0] - 1) // 2
    turned = weight.ndim == 5
    count = image.shape[0]
    if turned:
        tiles, q, _, rows, tile = weight.shape
        step = q * rows // 2 if packs else min(q * rows, 768)
        grid = (q * rows // step,)
        if rows < step:
            block = (tiles, step // rows, 1, rows, tile)
            weights = [
                pl.BlockSpec(block, lambda j, s, stream=stream: (0, j, stream, 0, 0))
                for stream in range(2)
            ]
        else:
            per = rows // step
            weights = [
                pl.BlockSpec(
                    (tiles, 1, 1, step, tile),
                    lambda j, s, stream=stream: (0, j // per, stream, j % per, 0),
                )
                for stream in range(2)
            ]
        depth = q * rows
    else:
        shards, _, rows, width = weight.shape
        depth = shards * rows
        bunch = max(1, 768 // rows)
        step = bunch * rows
        grid = (depth // step,)
        weights = [
            pl.BlockSpec((bunch, 1, rows, width), lambda j, s, stream=stream: (j, stream, 0, 0))
            for stream in range(2)
        ]
    column = pl.BlockSpec((count, step), lambda j, s: (0, j))
    in_specs = [resident(dy.shape), *weights, resident(image.shape)]
    operands = [spots, dy, weight, weight, image]
    if factor is not None:
        in_specs.append(column)
        operands.append(factor)
    if packs:
        shape = (2 * blocks, count // blocks, step)
        out_spec, out_shape = resident(shape), jax.ShapeDtypeStruct(shape, bf16)
    else:
        out_spec, out_shape = column, jax.ShapeDtypeStruct((count, depth), bf16)
    return pl.pallas_call(
        functools.partial(backward_kernel, blocks, turned, factor is not None, packs),
        grid_spec=pltpu.PrefetchScalarGridSpec(
            num_scalar_prefetch=1,
            grid=grid,
            in_specs=in_specs,
            out_specs=out_spec,
        ),
        out_shape=out_shape,
        compiler_params=pltpu.CompilerParams(vmem_limit_bytes=48 << 20),
        cost_estimate=pl.CostEstimate(
            flops=count * depth // 4 * dy.shape[1], bytes_accessed=4 << 20, transcendentals=0
        ),
        name="backward_product",
    )(*operands)


def gradient_kernel(blocks, spots, x_ref, dy_ref, image_ref, *rest):
    *outs, turned_x, masked, acc = rest
    count, width = dy_ref.shape
    size = count // blocks
    cols_at_once = acc.shape[1]

    @pl.when(pl.program_id(0) == 0)
    def _():
        @pl.loop(0, blocks)
        def _(p):
            rows = pl.ds(pl.multiple_of(p * size, size), size)
            kept = dy_ref[rows, :]
            masked[rows, :] = jnp.where(image_ref[rows, :] == 1, kept, jnp.zeros_like(kept))

    turned_x[...] = x_ref[...].T

    def store(stream, n, values):
        values = values.astype(bf16)
        out = outs[min(stream, len(outs) - 1)]
        stream = stream if len(outs) == 1 else 0
        if len(out.shape) == 5:
            tile, per = out.shape[4], out.shape[3]
            for t in range(cols_at_once // tile):
                for q in range(out.shape[1]):
                    out[n * (cols_at_once // tile) + t, q, stream] = values[
                        q * per : (q + 1) * per, t * tile : (t + 1) * tile
                    ]
        else:
            per = out.shape[2]
            for k in range(out.shape[0]):
                out[k, stream, :, n * cols_at_once : (n + 1) * cols_at_once] = values[
                    k * per : (k + 1) * per
                ]

    for n in range(width // cols_at_once):
        cols = slice(n * cols_at_once, (n + 1) * cols_at_once)
        store(0, n, jnp.dot(turned_x[...], masked[:, cols], preferred_element_type=f32))
        acc[...] = jnp.zeros_like(acc)

        def text(p, first, rows, cols=cols):
            kept = dy_ref[rows, cols]
            kept = jnp.where(image_ref[rows, :] == 1, jnp.zeros_like(kept), kept)
            acc[...] += lax.dot_general(x_ref[rows, :], kept, TN, preferred_element_type=f32)

        text_windows(spots, blocks, count, text)
        store(1, n, acc[...])


def gradient(spots, x, dy, image, shape, split=False):
    blocks = (spots.shape[0] - 1) // 2
    count, depth = x.shape
    width = dy.shape[1]
    step = 384
    cols = 1152 if width % 768 else 768
    if len(shape) == 4:
        per = step // shape[2]
        streams = 1 if split else 2
        out_spec = pl.BlockSpec((per, streams, shape[2], width), lambda j, s: (j, 0, 0, 0))
    else:
        tiles, q, _, rows, tile = shape
        if rows < step:
            block = (tiles, step // rows, 2, rows, tile)
            out_spec = pl.BlockSpec(block, lambda j, s: (0, j, 0, 0, 0))
        else:
            per = rows // step
            out_spec = pl.BlockSpec(
                (tiles, 1, 2, step, tile), lambda j, s: (0, j // per, 0, j % per, 0)
            )
    half = jax.ShapeDtypeStruct((shape[0], 1, *shape[2:]), bf16)
    return pl.pallas_call(
        functools.partial(gradient_kernel, blocks),
        grid_spec=pltpu.PrefetchScalarGridSpec(
            num_scalar_prefetch=1,
            grid=(depth // step,),
            in_specs=[
                pl.BlockSpec((count, step), lambda j, s: (0, j)),
                resident(dy.shape),
                resident(image.shape),
            ],
            out_specs=[out_spec, out_spec] if split else out_spec,
            scratch_shapes=[
                pltpu.VMEM((step, count), bf16),
                pltpu.VMEM((count, width), bf16),
                pltpu.VMEM((step, cols), f32),
            ],
        ),
        out_shape=[half, half] if split else jax.ShapeDtypeStruct(shape, bf16),
        compiler_params=pltpu.CompilerParams(vmem_limit_bytes=48 << 20),
        cost_estimate=pl.CostEstimate(
            flops=count * depth // 4 * width, bytes_accessed=4 << 20, transcendentals=0
        ),
        name="gradient",
    )(spots, x, dy, image)


def over_rep(value, target):
    count = lax.axis_size("rep")
    return lax.ppermute(value, "rep", [(r, target(r)) for r in range(count)])


def sibling(value):
    return over_rep(value, lambda r: r ^ 1)


def across(value):
    return over_rep(value, lambda r: r ^ 2)


def gather_rep(value):
    far = across(value)
    return [value, sibling(value), far, sibling(far)]


def reduce_rep(parts):
    near = sibling((parts[1], parts[3]))
    far = across((parts[2].astype(f32) + near[1].astype(f32)).astype(bf16))
    return parts[0].astype(f32) + near[0].astype(f32) + far.astype(f32)


def turn(value):
    reps, shards = lax.axis_size("rep"), lax.axis_size("shard")
    q = shards // reps
    pairs = []
    for r in range(reps):
        for s in range(shards):
            pairs.append((r * shards + s, (s // q) * shards + r * q + s % q))
    return lax.ppermute(value, ("rep", "shard"), pairs)


def gather_weight(weight_low):
    return lax.all_gather(weight_low, "shard", axis=0, tiled=False)


def gather_turned(moved):
    full = gather_weight(moved)
    reps = lax.axis_size("rep")
    return full.reshape(reps, full.shape[0] // reps, *full.shape[1:])


def ring_place(shards):
    mine = lax.axis_index("shard")
    odd = mine % 2
    return (1 - odd) * (mine // 2) + odd * (shards - 1 - mine // 2)


def ring_owner(place, shards):
    place = (place + 2 * shards) % shards
    back = place // ((shards + 1) // 2)
    return (1 - back) * (2 * place) + back * (2 * (shards - 1 - place) + 1)


def ring_kernel(shards, count, *refs):
    sources, dests = refs[:count], refs[count : 2 * count]
    send_sem, recv_sem, own_sem = refs[2 * count :]
    place = ring_place(shards)
    mine = ring_owner(place, shards)
    peers = [ring_owner(place + 1, shards), ring_owner(place - 1, shards)]

    barrier = pltpu.get_barrier_semaphore()
    for peer in peers:
        pl.semaphore_signal(
            barrier, inc=1, device_id={"shard": peer}, device_id_type=pl.DeviceIdType.MESH
        )
    pl.semaphore_wait(barrier, 2)

    kept = [
        pltpu.make_async_copy(sources[w], dests[w].at[mine], own_sem.at[w]) for w in range(count)
    ]
    for copy in kept:
        copy.start()
    chains = [(w, way) for w in range(count) for way in range(2)]
    copies = {}
    for step in range(shards - 1):
        for chain in chains:
            w, way = chain
            if step:
                copies[chain, step - 1].wait_recv()
            owner = ring_owner(place - step if way == 0 else place + step, shards)
            dest = dests[w].at[owner, way]
            copies[chain, step] = pltpu.make_async_remote_copy(
                src_ref=dest if step else sources[w].at[way],
                dst_ref=dest,
                send_sem=send_sem.at[w, way, step],
                recv_sem=recv_sem.at[w, way, step],
                device_id={"shard": peers[way]},
                device_id_type=pl.DeviceIdType.MESH,
            )
            copies[chain, step].start()
    for chain in chains:
        copies[chain, shards - 2].wait_recv()
        for step in range(shards - 1):
            copies[chain, step].wait_send()
    for copy in kept:
        copy.wait()


def ring_gather(*blocks):
    shards = lax.axis_size("shard")
    count = len(blocks)
    anywhere = pl.BlockSpec(memory_space=pl.ANY)
    return pl.pallas_call(
        functools.partial(ring_kernel, shards, count),
        in_specs=[anywhere] * count,
        out_specs=[anywhere] * count,
        out_shape=[jax.ShapeDtypeStruct((shards, *b.shape), b.dtype) for b in blocks],
        scratch_shapes=[
            pltpu.SemaphoreType.DMA((count, 2, shards - 1)),
            pltpu.SemaphoreType.DMA((count, 2, shards - 1)),
            pltpu.SemaphoreType.DMA((count,)),
        ],
        compiler_params=pltpu.CompilerParams(collective_id=0, has_side_effects=True),
        cost_estimate=pl.CostEstimate(flops=1 << 20, bytes_accessed=256 << 20, transcendentals=0),
        name="ring_gather",
    )(*blocks)


def as_turned(full):
    reps = lax.axis_size("rep")
    return full.reshape(reps, full.shape[0] // reps, *full.shape[1:])


def ring_scatter_kernel(count, *refs):
    sources, outs, helds = refs[:count], refs[count : 2 * count], refs[2 * count : 3 * count]
    send_sem, recv_sem = refs[3 * count :]
    shards = sources[0].shape[0]
    pieces = helds[0].shape[1]
    place = ring_place(shards)
    mine = ring_owner(place, shards)
    peers = [ring_owner(place + 1, shards), ring_owner(place - 1, shards)]

    barrier = pltpu.get_barrier_semaphore()
    for peer in peers:
        pl.semaphore_signal(
            barrier, inc=1, device_id={"shard": peer}, device_id_type=pl.DeviceIdType.MESH
        )
    pl.semaphore_wait(barrier, 2)

    chains = [
        (w, way, piece) for piece in range(pieces) for w in range(count) for way in range(2)
    ]
    copies = {}
    for step in range(shards):
        for chain in chains:
            w, way, piece = chain
            part = sources[w].shape[2] // pieces
            span = slice(piece * part, (piece + 1) * part)
            if step < shards - 1:
                owner = ring_owner(place - 1 - step if way == 0 else place + 1 + step, shards)
            else:
                owner = mine
            source = sources[w].at[owner, way, span]
            if step:
                copies[chain, step - 1].wait_recv()
                arrived = helds[w].at[way, piece, step - 1]
                total = arrived[...].astype(f32) + source[...].astype(f32)
                if step == shards - 1:
                    outs[w][way, span] = total.astype(bf16)
                    continue
                arrived[...] = total.astype(bf16)
                source = arrived
            copies[chain, step] = pltpu.make_async_remote_copy(
                src_ref=source,
                dst_ref=helds[w].at[way, piece, step],
                send_sem=send_sem.at[w, way, piece, step],
                recv_sem=recv_sem.at[w, way, piece, step],
                device_id={"shard": peers[way]},
                device_id_type=pl.DeviceIdType.MESH,
            )
            copies[chain, step].start()
    for copy in copies.values():
        copy.wait_send()


def ring_scatter(*terms):
    shards, _, rows, _ = terms[0].shape
    count = len(terms)
    pieces = 2 if rows % 32 == 0 else 1
    sems = pltpu.SemaphoreType.DMA((count, 2, pieces, shards - 1))
    whole = pl.BlockSpec(memory_space=pltpu.VMEM)
    return pl.pallas_call(
        functools.partial(ring_scatter_kernel, count),
        in_specs=[whole] * count,
        out_specs=[whole] * count,
        out_shape=[jax.ShapeDtypeStruct(t.shape[1:], bf16) for t in terms],
        scratch_shapes=[
            pltpu.VMEM((2, pieces, shards - 1, t.shape[2] // pieces, t.shape[3]), bf16)
            for t in terms
        ]
        + [sems, sems],
        compiler_params=pltpu.CompilerParams(
            collective_id=1, has_side_effects=True, vmem_limit_bytes=36 << 20
        ),
        cost_estimate=pl.CostEstimate(flops=1 << 20, bytes_accessed=256 << 20, transcendentals=0),
        name="ring_scatter",
    )(*terms)


def scatter_weight(terms):
    return lax.psum_scatter(
        terms.reshape(-1, *terms.shape[-2:]), "shard", scatter_dimension=0, tiled=True
    ).reshape(terms.shape[-3:])


def body(
    tokens,
    cotangent,
    cond,
    seq_lengths,
    stream_mask,
    w_mod,
    m_mod,
    v_mod,
    w_qkv,
    m_qkv,
    v_qkv,
    w_out,
    m_out,
    v_out,
    w_fc1,
    m_fc1,
    v_fc1,
    w_fc2,
    m_fc2,
    v_fc2,
    gains,
    m_gains,
    v_gains,
):
    tok_rows, model_width = tokens.shape
    slot_count = seq_lengths.shape[0]
    reps, shards = lax.axis_size("rep"), lax.axis_size("shard")
    rep_index, shard_index = lax.axis_index("rep"), lax.axis_index("shard")
    device_index = rep_index * shards + shard_index
    all_tokens = tok_rows * reps * shards
    reach = (MAXLEN - 2) // tok_rows + 1
    part_width = model_width // reps
    part_rows = w_mod.shape[1]
    mod_cols = w_mod.shape[2]

    seq_starts = jnp.cumsum(seq_lengths) - seq_lengths
    local_pos = device_index * tok_rows + jnp.arange(tok_rows, dtype=jnp.int32)
    seq_ids = segment_index(local_pos, seq_starts, all_tokens)
    image_col = (stream_mask == 1)[:, None]
    image_group = jnp.concatenate(gather_rep(stream_mask)) == 1
    image = image_group[:, None].astype(jnp.int32)
    text_group = ~image_group.reshape(reps, tok_rows)
    text_first = jnp.argmax(text_group, axis=1).astype(jnp.int32)
    spots = jnp.concatenate(
        [
            jnp.minimum(text_first // 16 * 16, tok_rows - WINDOW),
            jnp.any(text_group, axis=1).astype(jnp.int32),
            rep_index[None].astype(jnp.int32),
        ]
    )

    silu_cond = jax.nn.silu(cond).astype(bf16)
    cond_rows = lax.dynamic_slice_in_dim(silu_cond, shard_index * part_rows, part_rows, 1)
    mod_terms = jnp.concatenate(
        [
            jnp.dot(cond_rows, w_mod[s].astype(bf16), preferred_element_type=f32)
            for s in range(2)
        ],
        axis=0,
    ).astype(bf16)
    device_count = reps * shards
    firsts = segment_index(
        jnp.arange(device_count, dtype=jnp.int32) * tok_rows, seq_starts, all_tokens
    )
    seconds = jnp.minimum(firsts + 1, slot_count - 1)
    stream_offset = jnp.arange(2, dtype=jnp.int32) * slot_count
    wanted = jnp.stack([firsts, seconds], axis=1)[:, :, None] + stream_offset
    hot = (wanted.reshape(-1, 1) == jnp.arange(2 * slot_count, dtype=jnp.int32)).astype(bf16)
    mod_sent = jnp.dot(hot, mod_terms, preferred_element_type=f32).astype(bf16)
    mod_got = lax.all_to_all(
        mod_sent.reshape(device_count, 4, mod_cols), ("rep", "shard"), 0, 0, tiled=True
    )
    mod_sum = jnp.sum(mod_got.reshape(reps, shards, 4, mod_cols).astype(f32), axis=1).astype(bf16)
    mod_rows = jnp.concatenate([mod_sum[r] for r in range(reps)], axis=1)

    qkv_low = w_qkv.astype(bf16)
    chunks = [
        over_rep(
            qkv_low[:, :, i * part_width : (i + 1) * part_width],
            lambda r, i=i: (3 * r + i) % reps,
        )
        for i in range(3)
    ]
    turns = rep_index % 3

    def rolled(parts, amount):
        return [
            jnp.where(
                amount == 0,
                parts[t],
                jnp.where(amount == 1, parts[(t + 1) % 3], parts[(t + 2) % 3]),
            )
            for t in range(3)
        ]

    qkv_weights, out_full = ring_gather(
        jnp.concatenate(rolled(chunks, turns), axis=2), turn(w_out.astype(bf16))
    )
    out_weights = as_turned(out_full)
    qkv_weights, mod_rows, fc1_low, fc2_turned = lax.optimization_barrier(
        (qkv_weights, mod_rows, w_fc1.astype(bf16), turn(w_fc2.astype(bf16)))
    )
    fc1_weights = gather_weight(fc1_low)
    first_seq = seq_ids[0]
    second_seq = jnp.minimum(first_seq + 1, slot_count - 1)
    is_second = (seq_ids != first_seq)[:, None]

    def mod_block(index):
        span = slice(index * model_width, (index + 1) * model_width)
        rows = mod_rows[:, span].astype(f32)
        pick = [jnp.where(is_second, rows[2 + s][None], rows[s][None]) for s in range(2)]
        return jnp.where(image_col, pick[0], pick[1])

    shift_one, scale_one, gate_one, shift_two, scale_two, gate_two = [
        mod_block(i) for i in range(6)
    ]
    stream_in = tokens.astype(f32)
    back_out = cotangent.astype(f32)
    act_one = layer_modulate(stream_in, shift_one, scale_one).astype(bf16)
    act_one_group = jnp.concatenate(gather_rep(act_one))
    d_down = (gate_two * back_out).astype(bf16)
    d_down_group = jnp.concatenate(gather_rep(d_down))

    query_sent, pair_sent, qk_pre = qkv_product(spots, act_one_group, qkv_weights, image, gains)

    bunch = 2 * reps
    bunches = shards // bunch
    half_width = part_width // 2
    groups = [[q * bunch + i for i in range(bunch)] for q in range(bunches)]

    def exchange(value):
        return lax.all_to_all(
            value, "shard", 0, 0, axis_index_groups=None if bunches == 1 else groups, tiled=True
        )

    stretch_count = reps * bunches
    stretch_rows = bunch * tok_rows
    halo = reach * tok_rows

    def stretch_shift(value, steps):
        def place(stretch, g):
            return (stretch % bunches) * bunch + (stretch // bunches) * 2 + g

        pairs = [
            (place(t, g), place(t + steps, g))
            for t in range(stretch_count)
            for g in range(2)
            if 0 <= t + steps < stretch_count
        ]
        return lax.ppermute(value, "shard", pairs)

    pair_own = exchange(pair_sent).reshape(stretch_rows, 2 * half_width)
    pair_before = stretch_shift(pair_own[-halo:], 1)
    pair_after = stretch_shift(pair_own[:halo], -1)
    query_sent, pair_before, pair_after = lax.optimization_barrier(
        (query_sent, pair_before, pair_after)
    )
    query_own = exchange(query_sent).reshape(stretch_rows, half_width)
    fc2_turned, query_own, fc1_weights, d_down_group = lax.optimization_barrier(
        (fc2_turned, query_own, fc1_weights, d_down_group)
    )
    fc2_weights = as_turned(gather_weight(fc2_turned))
    window_rows = stretch_rows + 2 * halo
    stretch = ((shard_index % bunch) // 2) * bunches + shard_index // bunch
    stretch_first = stretch * stretch_rows
    qid = segment_index(
        stretch_first + jnp.arange(stretch_rows, dtype=jnp.int32), seq_starts, all_tokens
    )
    kid = segment_index(
        stretch_first - halo + jnp.arange(window_rows, dtype=jnp.int32), seq_starts, all_tokens
    )
    seq_ends = seq_starts + seq_lengths
    low_pos = seq_starts[qid[::QB]] - (stretch_first - halo)
    high_pos = seq_ends[qid[QB - 1 :: QB]] - (stretch_first - halo)
    lo = jnp.clip(low_pos // KB, 0, window_rows // KB).astype(jnp.int32)
    hi = jnp.clip((high_pos + KB - 1) // KB, 0, window_rows // KB).astype(jnp.int32)
    attended_own, logsum = attention(
        query_own, pair_own, pair_before, pair_after, lo, hi, qid, kid
    )
    attended_came = exchange(attended_own.reshape(bunch, tok_rows, half_width))

    def split_group(value):
        return [value[p * tok_rows : (p + 1) * tok_rows] for p in range(reps)]

    branch_terms, attended_low = forward_product(
        spots, attended_came, out_weights, image, gathers=True
    )
    branch = reduce_rep(split_group(branch_terms))
    mid = stream_in + gate_one * branch
    act_two = layer_modulate(mid, shift_two, scale_two).astype(bf16)
    act_two_group = jnp.concatenate(gather_rep(act_two))
    gelu_low, gelu_slope = forward_product(spots, act_two_group, fc1_weights, image, gelu=True)
    down_terms = forward_product(spots, gelu_low, fc2_weights, image)[0]

    fc2_terms = gradient(spots, gelu_low, d_down_group, image, fc2_weights.shape)
    fc2_terms, gelu_slope = lax.optimization_barrier((fc2_terms, gelu_slope))
    fc2_own = scatter_weight(fc2_terms)
    d_up = backward_product(spots, d_down_group, fc2_weights, image, factor=gelu_slope)
    d_act_two = reduce_rep(split_group(backward_product(spots, d_up, fc1_weights, image)))
    d_mid_norm, d_shift_two, d_scale_two = jax.vjp(layer_modulate, mid, shift_two, scale_two)[1](
        d_act_two
    )
    d_mid = back_out + d_mid_norm
    d_branch = (gate_one * d_mid).astype(bf16)
    fc1_image, fc1_text = gradient(
        spots, act_two_group, d_up, image, fc1_weights.shape, split=True
    )
    fc1_image, fc1_text, d_branch = lax.optimization_barrier((fc1_image, fc1_text, d_branch))
    fc1_image = scatter_weight(fc1_image)
    d_gate_one = d_mid * branch
    d_branch_group = jnp.concatenate(gather_rep(d_branch))
    d_attended = backward_product(spots, d_branch_group, out_weights, image, packs=True)
    out_terms = gradient(spots, attended_low, d_branch_group, image, out_weights.shape)
    d_attended_own = exchange(d_attended).reshape(stretch_rows, half_width)
    d_attended_own, out_terms = lax.optimization_barrier((d_attended_own, out_terms))
    d_query_own, d_before, d_after, d_pair_own = attention_back(
        query_own,
        pair_own,
        pair_before,
        pair_after,
        d_attended_own,
        attended_own,
        lo,
        hi,
        qid,
        kid,
        logsum,
    )
    d_query_came = exchange(d_query_own.reshape(bunch, tok_rows, half_width))
    from_later = stretch_shift(d_before, -1).astype(f32)
    from_earlier = stretch_shift(d_after, 1).astype(f32)
    rest = jnp.zeros((stretch_rows - halo, 2 * half_width), f32)
    d_pair_own = (
        d_pair_own
        + jnp.concatenate([rest, from_later], axis=0)
        + jnp.concatenate([from_earlier, rest], axis=0)
    )
    d_pair_came = exchange(d_pair_own.astype(bf16).reshape(bunch, tok_rows, 2 * half_width))
    d_pair_came, down_terms, fc1_text, fc2_own = lax.optimization_barrier(
        (d_pair_came, down_terms, fc1_text, fc2_own)
    )
    g_fc2 = turn(fc2_own)
    fc1_text = scatter_weight(fc1_text)
    down_proj = reduce_rep(split_group(down_terms))
    output = mid + gate_two * down_proj
    d_gate_two = back_out * down_proj
    d_qkv, gain_sums = norm_back(spots, d_query_came, d_pair_came, qk_pre, image, gains)
    d_act_one = reduce_rep(split_group(backward_product(spots, d_qkv, qkv_weights, image)))
    qkv_terms = gradient(spots, act_one_group, d_qkv, image, qkv_weights.shape)
    d_in_norm, d_shift_one, d_scale_one = jax.vjp(layer_modulate, stream_in, shift_one, scale_one)[
        1
    ](d_act_one)
    d_tokens = d_mid + d_in_norm
    d_mod_tok = jnp.concatenate(
        [d_shift_one, d_scale_one, d_gate_one, d_shift_two, d_scale_two, d_gate_two], axis=1
    )
    image_flag = image_col[:, 0]
    second_flag = is_second[:, 0]
    selector = jnp.stack(
        [
            ~second_flag & image_flag,
            ~second_flag & ~image_flag,
            second_flag & image_flag,
            second_flag & ~image_flag,
        ],
        axis=1,
    ).astype(f32)
    pooled = jnp.einsum("tp,te->pe", selector, d_mod_tok, precision=lax.Precision.HIGHEST)
    gain_sums = jnp.sum(gain_sums.reshape(2, 2, part_width // HD, HD), axis=2)
    gain_part = jnp.concatenate([gain_sums[0], gain_sums[1]], axis=1)
    gain_rows = jnp.concatenate([gain_part, jnp.zeros_like(gain_part)], axis=0)
    leaving = jnp.stack(
        [
            jnp.concatenate([pooled[:, r * mod_cols : (r + 1) * mod_cols], gain_rows], axis=1)
            for r in range(reps)
        ]
    )
    qkv_terms, out_terms, fc1_image, fc1_text, g_fc2, leaving = lax.optimization_barrier(
        (qkv_terms, out_terms, fc1_image, fc1_text, g_fc2, leaving)
    )
    leaving = jnp.broadcast_to(leaving[:, None], (reps, shards, *leaving.shape[1:]))
    came = lax.all_to_all(
        leaving.reshape(device_count, *leaving.shape[2:]), ("rep", "shard"), 0, 0, tiled=True
    )
    out_terms = out_terms.reshape(shards, 2, -1, out_terms.shape[-1])
    g_qkv_group, g_out = ring_scatter(qkv_terms, out_terms)
    g_qkv_group, g_out, came = lax.optimization_barrier((g_qkv_group, g_out, came))
    g_out = turn(g_out)
    g_fc1 = jnp.concatenate([fc1_image, fc1_text], axis=0)
    g_parts = [
        g_qkv_group[:, :, t * part_width : (t + 1) * part_width] for t in range(3)
    ]
    g_parts = rolled(g_parts, (3 - turns) % 3)
    g_qkv = jnp.concatenate(
        [over_rep(g_parts[i], lambda d, i=i: (3 * (d - i)) % reps) for i in range(3)], axis=2
    )

    g_gains = jnp.sum(came[:, :2, mod_cols:], axis=0)
    came = came[:, :, :mod_cols].reshape(2 * device_count, 2, mod_cols)
    seqs = jnp.stack([firsts, seconds], axis=1).reshape(-1)
    hot_seq = (seqs[:, None] == jnp.arange(slot_count, dtype=jnp.int32)).astype(bf16)
    cond_seq = jnp.dot(hot_seq, cond_rows, preferred_element_type=f32)
    g_mod = jnp.stack(
        [
            lax.dot_general(
                cond_seq,
                came[:, s],
                (((0,), (0,)), ((), ())),
                precision=lax.Precision.HIGHEST,
                preferred_element_type=f32,
            )
            for s in range(2)
        ]
    )
    up_mod = adam_step(w_mod, m_mod, v_mod, g_mod, rate_mod)
    up_qkv = adam_step(w_qkv, m_qkv, v_qkv, g_qkv.astype(f32), rate_qkv)
    up_out = adam_step(w_out, m_out, v_out, g_out.astype(f32), rate_out)
    up_fc1 = adam_step(w_fc1, m_fc1, v_fc1, g_fc1.astype(f32), rate_fc1)
    up_fc2 = adam_step(w_fc2, m_fc2, v_fc2, g_fc2.astype(f32), rate_fc2)
    up_gains = adam_step(gains, m_gains, v_gains, g_gains, rate_gains)
    return (
        output.astype(bf16),
        d_tokens,
        *up_mod,
        *up_qkv,
        *up_out,
        *up_fc1,
        *up_fc2,
        *up_gains[:3],
    )


def solution(mesh):
    rows = P(("rep", "shard"), None)
    held = P(None, "shard", "rep")
    return jax.shard_map(
        body,
        mesh=mesh,
        in_specs=(rows, rows, P(), P(), P(("rep", "shard")), *([held] * 15), P(), P(), P()),
        out_specs=(rows, rows, *([held] * 20), P(), P(), P()),
        check_vma=False,
    )
```

```python
import functools

import jax
import jax.numpy as jnp
from jax import lax
from jax.experimental import pallas as pl
from jax.experimental.pallas import tpu as pltpu
from jax.sharding import PartitionSpec as P

HD = 64
MAXLEN = 1178
STEP = 7

norm_eps = 1e-06
adam_eps = 1e-08
score_scale = 0.125
rate_mod = 0.03
rate_qkv = 0.03
rate_out = 0.15
rate_fc1 = 0.03
rate_fc2 = 0.015
rate_gains = 1.0

bf16 = jnp.bfloat16
f32 = jnp.float32
QB = 256
KB = 256
TXT = 154
WINDOW = (TXT + 15 + 15) // 16 * 16
COLS = 512
GELU_A = 0.7978845608028654
GELU_B = 0.044715
NN = (((1,), (0,)), ((), ()))
NT = (((1,), (1,)), ((), ()))
TN = (((0,), (0,)), ((), ()))


def layer_modulate(values, shift, scale):
    centred = values - jnp.mean(values, axis=-1, keepdims=True)
    normed = centred * lax.rsqrt(jnp.mean(centred * centred, axis=-1, keepdims=True) + norm_eps)
    return normed * (1.0 + scale) + shift


def adam_step(weight, moment_one, moment_two, grads, rate):
    new_one = 0.9 * moment_one + 0.1 * grads
    new_two = 0.999 * moment_two + 0.001 * grads * grads
    fixed_one = new_one / (1.0 - 0.9**STEP)
    fixed_two = new_two / (1.0 - 0.999**STEP)
    new_weight = weight - rate * (fixed_one / (jnp.sqrt(fixed_two) + adam_eps) + 0.01 * weight)
    return (new_weight, new_one, new_two, new_weight.astype(bf16))


def segment_index(position, seq_starts, all_tokens):
    counted = jnp.sum((seq_starts[None, :] <= position[:, None]).astype(jnp.int32), axis=1) - 1
    inside = (position >= 0) & (position < all_tokens)
    return jnp.where(inside, counted, -1)


def fill_window(own_ref, before_ref, after_ref, keys, values):
    halo, own = before_ref.shape[0], own_ref.shape[0]
    heads = keys.shape[0]
    width = heads * HD
    parts = ((before_ref, 0, halo), (own_ref, halo, own), (after_ref, halo + own, halo))
    for source, first, count in parts:
        for head in range(heads):
            for index, dest in ((0, keys), (1, values)):
                start = index * width + head * HD
                dest[head, first : first + count, :HD] = source[:, start : start + HD]


def attend_kernel(
    lo_ref, hi_ref, q_ref, own_ref, before_ref, after_ref, qid_ref, kid_ref, o_ref, l_ref, keys, values, acc
):
    step = pl.program_id(0)
    heads = keys.shape[0]

    @pl.when(step == 0)
    def _():
        lane = lax.broadcasted_iota(jnp.int32, values.shape[1:], 1)
        for head in range(heads):
            values[head] = (lane == HD).astype(bf16)
        fill_window(own_ref, before_ref, after_ref, keys, values)

    qid = qid_ref[...]
    diagonal = lax.broadcasted_iota(jnp.int32, (QB, QB), 0) == lax.broadcasted_iota(
        jnp.int32, (QB, QB), 1
    )
    queries = [q_ref[:, head * HD : (head + 1) * HD] for head in range(heads)]
    acc[...] = jnp.zeros_like(acc)

    @pl.loop(lo_ref[step], hi_ref[step])
    def _(block):
        rows = pl.ds(pl.multiple_of(block * KB, KB), KB)
        same = qid == kid_ref[pl.ds(block, 1), :]
        for head in range(heads):
            scores = lax.dot_general(
                queries[head], keys[head, rows, :], NT, preferred_element_type=f32
            )
            lifted = jnp.where(same, jnp.exp(scores), 0.0).astype(bf16)
            acc[head] += jnp.dot(lifted, values[head, rows, :], preferred_element_type=f32)

    for head in range(heads):
        total = acc[head, :, HD : HD + 1]
        o_ref[:, head * HD : (head + 1) * HD] = (acc[head, :, :HD] / total).astype(bf16)
        l_ref[0, head : head + 1, :] = jnp.sum(
            jnp.where(diagonal, jnp.log(total), 0.0), axis=0, keepdims=True
        )


def attend_back_kernel(
    lo_ref,
    hi_ref,
    q_ref,
    own_ref,
    before_ref,
    after_ref,
    do_ref,
    o_ref,
    qid_ref,
    kid_ref,
    l_ref,
    dq_ref,
    d_before_ref,
    d_after_ref,
    d_own_ref,
    keys,
    values,
    d_keys,
    d_values,
    d_query,
):
    step = pl.program_id(0)
    heads = keys.shape[0]
    width = heads * HD

    @pl.when(step == 0)
    def _():
        fill_window(own_ref, before_ref, after_ref, keys, values)
        d_keys[...] = jnp.zeros_like(d_keys)
        d_values[...] = jnp.zeros_like(d_values)

    qid = qid_ref[0]
    ones = jnp.ones((8, HD), bf16)
    queries, outs, dots = [], [], []
    for head in range(heads):
        lanes = slice(head * HD, (head + 1) * HD)
        queries.append(q_ref[:, lanes])
        outs.append(do_ref[:, lanes])
        product = outs[head].astype(f32) * o_ref[:, lanes].astype(f32)
        coarse = product.astype(bf16)
        fine = (product - coarse.astype(f32)).astype(bf16)
        total = lax.dot_general(ones, coarse, NT, preferred_element_type=f32)
        dots.append((total + lax.dot_general(ones, fine, NT, preferred_element_type=f32))[:1])
    d_query[...] = jnp.zeros_like(d_query)

    @pl.loop(lo_ref[step], hi_ref[step])
    def _(block):
        rows = pl.ds(pl.multiple_of(block * KB, KB), KB)
        same = kid_ref[rows, :] == qid
        for head in range(heads):
            key = keys[head, rows, :]
            scores = lax.dot_general(key, queries[head], NT, preferred_element_type=f32)
            probs = jnp.where(same, jnp.exp(scores - l_ref[0, head : head + 1, :]), 0.0)
            d_values[head, rows, :] += jnp.dot(
                probs.astype(bf16), outs[head], preferred_element_type=f32
            )
            d_probs = lax.dot_general(
                values[head, rows, :], outs[head], NT, preferred_element_type=f32
            )
            d_scores = (probs * (d_probs - dots[head])).astype(bf16)
            d_keys[head, rows, :] += jnp.dot(d_scores, queries[head], preferred_element_type=f32)
            d_query[head] += lax.dot_general(d_scores, key, TN, preferred_element_type=f32)

    for head in range(heads):
        dq_ref[:, head * HD : (head + 1) * HD] = (d_query[head] * score_scale).astype(bf16)

    @pl.when(step == pl.num_programs(0) - 1)
    def _():
        halo, own = d_before_ref.shape[0], d_own_ref.shape[0]
        for index, source in ((0, d_keys), (1, d_values)):
            for head in range(heads):
                span = slice(index * width + head * HD, index * width + (head + 1) * HD)
                d_before_ref[:, span] = source[head, :halo, :].astype(bf16)
                d_own_ref[:, span] = source[head, halo : halo + own, :]
                d_after_ref[:, span] = source[head, halo + own :, :].astype(bf16)


def resident(shape):
    return pl.BlockSpec(shape, lambda *index: (0,) * len(shape))


def attention(query, own, before, after, lo, hi, qid, kid):
    count, width = query.shape
    heads = width // HD
    window = count + 2 * before.shape[0]
    steps = count // QB
    return pl.pallas_call(
        attend_kernel,
        grid_spec=pltpu.PrefetchScalarGridSpec(
            num_scalar_prefetch=2,
            grid=(steps,),
            in_specs=[
                pl.BlockSpec((QB, width), lambda i, lo, hi: (i, 0)),
                resident(own.shape),
                resident(before.shape),
                resident(after.shape),
                pl.BlockSpec((QB, 1), lambda i, lo, hi: (i, 0)),
                resident((window // KB, KB)),
            ],
            out_specs=[
                pl.BlockSpec((QB, width), lambda i, lo, hi: (i, 0)),
                pl.BlockSpec((1, 8, QB), lambda i, lo, hi: (i, 0, 0)),
            ],
            scratch_shapes=[
                pltpu.VMEM((heads, window, HD), bf16),
                pltpu.VMEM((heads, window, 2 * HD), bf16),
                pltpu.VMEM((heads, QB, 2 * HD), f32),
            ],
        ),
        out_shape=[
            jax.ShapeDtypeStruct((count, width), bf16),
            jax.ShapeDtypeStruct((steps, 8, QB), f32),
        ],
        compiler_params=pltpu.CompilerParams(vmem_limit_bytes=40 << 20),
        cost_estimate=pl.CostEstimate(flops=1 << 30, bytes_accessed=4 << 20, transcendentals=0),
        name="attend",
    )(lo, hi, query, own, before, after, qid[:, None], kid.reshape(window // KB, KB))


def attention_back(query, own, before, after, d_out, out, lo, hi, qid, kid, logsum):
    count, width = query.shape
    heads = width // HD
    halo = before.shape[0]
    window = count + 2 * halo
    steps = count // QB
    rows = pl.BlockSpec((QB, width), lambda i, lo, hi: (i, 0))
    return pl.pallas_call(
        attend_back_kernel,
        grid_spec=pltpu.PrefetchScalarGridSpec(
            num_scalar_prefetch=2,
            grid=(steps,),
            in_specs=[
                rows,
                resident(own.shape),
                resident(before.shape),
                resident(after.shape),
                rows,
                rows,
                pl.BlockSpec((1, 1, QB), lambda i, lo, hi: (i, 0, 0)),
                resident((window, 1)),
                pl.BlockSpec((1, 8, QB), lambda i, lo, hi: (i, 0, 0)),
            ],
            out_specs=[
                rows,
                resident((halo, 2 * width)),
                resident((halo, 2 * width)),
                resident((count, 2 * width)),
            ],
            scratch_shapes=[pltpu.VMEM((heads, window, HD), bf16)] * 2
            + [pltpu.VMEM((heads, window, HD), f32)] * 2
            + [pltpu.VMEM((heads, QB, HD), f32)],
        ),
        out_shape=[
            jax.ShapeDtypeStruct((count, width), bf16),
            jax.ShapeDtypeStruct((halo, 2 * width), bf16),
            jax.ShapeDtypeStruct((halo, 2 * width), bf16),
            jax.ShapeDtypeStruct((count, 2 * width), f32),
        ],
        compiler_params=pltpu.CompilerParams(vmem_limit_bytes=58 << 20),
        cost_estimate=pl.CostEstimate(flops=24 << 30, bytes_accessed=8 << 20, transcendentals=0),
        name="attend_back",
    )(lo, hi, query, own, before, after, d_out, out, qid.reshape(steps, 1, QB), kid[:, None], logsum)


def text_windows(spots, blocks, count, work):
    for p in range(blocks):

        @pl.when(spots[blocks + p] == 1)
        def _(p=p):
            first = pl.multiple_of(spots[p], 16)
            base = p * (count // blocks)
            work(p, first, pl.ds(pl.multiple_of(base + first, 16), WINDOW))


def flat(value):
    return value.reshape(-1, value.shape[-1])


def product(x_ref, rows, weight, dims):
    total = None
    for cols, get in weight:
        term = lax.dot_general(x_ref[rows, cols], get(), dims, preferred_element_type=f32)
        total = term if total is None else total + term
    return total


def group_sums(values, blocks_of):
    coarse = values.astype(bf16)
    fine = (values - coarse.astype(f32)).astype(bf16)
    return jnp.dot(coarse, blocks_of, preferred_element_type=f32) + jnp.dot(
        fine, blocks_of, preferred_element_type=f32
    )


def head_blocks(width):
    row = lax.broadcasted_iota(jnp.int32, (width, width), 0) // HD
    col = lax.broadcasted_iota(jnp.int32, (width, width), 1) // HD
    return (row == col).astype(bf16)


def qkv_kernel(blocks, spots, x_ref, w0, w1, image_ref, gain_ref, q_ref, kv_ref, pre_ref):
    kind = pl.program_id(0)
    every = slice(None)
    size, width = q_ref.shape[1:]
    rep = spots[2 * blocks]
    spread = head_blocks(2 * width)

    def finish(t, values, gain):
        if t < 2:
            mean = group_sums(values * values, spread) * (1.0 / HD)
            values = values * lax.rsqrt(mean + norm_eps) * gain
        values = values.astype(bf16)
        return values * jnp.asarray(score_scale, bf16) if t == 0 else values

    for t in range(3):

        @pl.when(kind == t)
        def _(t=t):
            packed_ref = kv_ref if t else q_ref
            lanes = slice((t - 1) * width, t * width) if t else slice(0, width)

            @pl.loop(0, blocks)
            def _(p):
                rows = pl.ds(pl.multiple_of(p * size, size), size)
                values = product(x_ref, rows, [(every, lambda: flat(w0[...]))], NN)
                if t < 2:
                    pre_ref[rows, :] = values
                values = finish(t, values, gain_ref[0, :1])
                for g in range(2):
                    packed_ref[pl.ds((rep ^ p) * 2 + g, 1), :, lanes] = values[
                        :, g * width : (g + 1) * width
                    ][None]

            def text(p, first, rows):
                values = product(x_ref, rows, [(every, lambda: flat(w1[...]))], NN)
                image = image_ref[rows, :] == 1
                if t < 2:
                    pre_ref[rows, :] = jnp.where(image, pre_ref[rows, :], values)
                values = finish(t, values, gain_ref[0, 1:])
                for g in range(2):
                    place = (
                        pl.ds((rep ^ p) * 2 + g, 1),
                        pl.ds(first, WINDOW),
                        lanes,
                    )
                    packed_ref[place] = jnp.where(
                        image[None], packed_ref[place], values[:, g * width : (g + 1) * width][None]
                    )

            text_windows(spots, blocks, x_ref.shape[0], text)


def column_weights(weight, tile):
    shards, _, rows, _ = weight.shape
    return [
        pl.BlockSpec((shards, 1, rows, tile), lambda j, s, stream=stream: (0, stream, 0, j))
        for stream in range(2)
    ]


def tiled_gains(gains, heads):
    return jnp.stack([jnp.tile(gains[:, :HD], (1, heads)), jnp.tile(gains[:, HD:], (1, heads))])


def qkv_product(spots, x, weight, image, gains):
    count, depth = x.shape
    blocks = (spots.shape[0] - 1) // 2
    part = weight.shape[3] // 3
    size = count // blocks
    return pl.pallas_call(
        functools.partial(qkv_kernel, blocks),
        grid_spec=pltpu.PrefetchScalarGridSpec(
            num_scalar_prefetch=1,
            grid=(3,),
            in_specs=[
                resident(x.shape),
                *column_weights(weight, part),
                resident(image.shape),
                pl.BlockSpec((1, 2, part), lambda j, s: (jnp.minimum(j, 1), 0, 0)),
            ],
            out_specs=[
                resident((2 * blocks, size, part // 2)),
                resident((2 * blocks, size, part)),
                pl.BlockSpec((count, part), lambda j, s: (0, jnp.minimum(j, 1))),
            ],
        ),
        out_shape=[
            jax.ShapeDtypeStruct((2 * blocks, size, part // 2), bf16),
            jax.ShapeDtypeStruct((2 * blocks, size, part), bf16),
            jax.ShapeDtypeStruct((count, 2 * part), f32),
        ],
        compiler_params=pltpu.CompilerParams(vmem_limit_bytes=40 << 20),
        cost_estimate=pl.CostEstimate(flops=1 << 30, bytes_accessed=4 << 20, transcendentals=0),
        name="qkv_product",
    )(spots, x, weight, weight, image, tiled_gains(gains, part // HD))


def norm_back_kernel(blocks, spots, q_ref, kv_ref, pre_ref, image_ref, gain_ref, out_ref, sum_ref, both):
    @pl.when(pl.program_id(0) == 0)
    def _():
        sum_ref[...] = jnp.zeros_like(sum_ref)

    part = both.shape[1]
    width = part // 2
    image = image_ref[...] == 1
    spread = head_blocks(part)
    for t in range(3):
        came_ref = kv_ref if t else q_ref
        lanes = slice((t - 1) * width, t * width) if t else slice(0, width)
        for g in range(2):
            both[:, g * width : (g + 1) * width] = came_ref[g, :, lanes].astype(f32)
        grad = both[...]
        if t < 2:
            pre = pre_ref[:, t * part : (t + 1) * part]
            scale = lax.rsqrt(group_sums(pre * pre, spread) * (1.0 / HD) + norm_eps)
            gain = jnp.where(image, gain_ref[t, :1], gain_ref[t, 1:])
            each = grad * pre * scale
            total = jnp.sum(each, axis=0, keepdims=True)
            text = jnp.sum(jnp.where(image, 0.0, each), axis=0, keepdims=True)
            sum_ref[2 * t : 2 * t + 1, :] += total - text
            sum_ref[2 * t + 1 : 2 * t + 2, :] += text
            grad = grad * gain
            mean = group_sums(grad * pre, spread) * (1.0 / HD)
            grad = scale * (grad - pre * (scale * scale * mean))
        out_ref[:, t * part : (t + 1) * part] = grad.astype(bf16)


def norm_back(spots, came_query, came_pair, pre, image, gains):
    blocks = (spots.shape[0] - 1) // 2
    _, size, part = came_pair.shape
    tiled = tiled_gains(gains, part // HD)
    return pl.pallas_call(
        functools.partial(norm_back_kernel, blocks),
        grid_spec=pltpu.PrefetchScalarGridSpec(
            num_scalar_prefetch=1,
            grid=(blocks,),
            in_specs=[
                pl.BlockSpec((2, size, part // 2), lambda p, s: (s[2 * blocks] ^ p, 0, 0)),
                pl.BlockSpec((2, size, part), lambda p, s: (s[2 * blocks] ^ p, 0, 0)),
                pl.BlockSpec((size, 2 * part), lambda p, s: (p, 0)),
                pl.BlockSpec((size, 1), lambda p, s: (p, 0)),
                resident(tiled.shape),
            ],
            out_specs=[
                pl.BlockSpec((size, 3 * part), lambda p, s: (p, 0)),
                resident((4, part)),
            ],
            scratch_shapes=[pltpu.VMEM((size, part), f32)],
        ),
        out_shape=[
            jax.ShapeDtypeStruct((blocks * size, 3 * part), bf16),
            jax.ShapeDtypeStruct((4, part), f32),
        ],
        compiler_params=pltpu.CompilerParams(vmem_limit_bytes=32 << 20),
        cost_estimate=pl.CostEstimate(flops=4 << 30, bytes_accessed=12 << 20, transcendentals=0),
        name="norm_back",
    )(spots, came_query, came_pair, pre, image, tiled)


def forward_kernel(blocks, gathers, gelu, spots, x_ref, w0, w1, image_ref, *rest):
    rep = spots[2 * blocks]
    out_ref = rest[0]
    if gathers:
        x_out = rest[1]
        size, width = x_ref.shape[1:]

        @pl.when(pl.program_id(0) == 0)
        def _():
            for p in range(blocks):
                for g in range(2):
                    x_out[p * size : (p + 1) * size, g * width : (g + 1) * width] = x_ref[
                        pl.ds((rep ^ p) * 2 + g, 1)
                    ][0]

        x_ref = x_out
    every = slice(None)
    count = x_ref.shape[0]

    def finish(values):
        if not gelu:
            return (values.astype(bf16),)
        square = values * values
        bend = jnp.tanh(values * (GELU_A + GELU_A * GELU_B * square))
        half = 0.5 * (1.0 + bend)
        slope = half + 0.5 * values * (1.0 - bend * bend) * (GELU_A + 3.0 * GELU_A * GELU_B * square)
        return (values * half).astype(bf16), slope.astype(bf16)

    outs = rest if gelu else (out_ref,)
    chunk = count // (blocks if gelu else 2)

    @pl.loop(0, count // chunk)
    def _(p):
        rows = pl.ds(pl.multiple_of(p * chunk, chunk), chunk)
        values = product(x_ref, rows, [(every, lambda: flat(w0[...]))], NN)
        for out, value in zip(outs, finish(values)):
            out[rows, :] = value

    def text(p, first, rows):
        values = product(x_ref, rows, [(every, lambda: flat(w1[...]))], NN)
        image = image_ref[rows, :] == 1
        for out, value in zip(outs, finish(values)):
            out[rows, :] = jnp.where(image, out[rows, :], value)

    text_windows(spots, blocks, count, text)


def forward_product(spots, x, weight, image, gathers=False, gelu=False):
    blocks = (spots.shape[0] - 1) // 2
    if weight.ndim == 5:
        tiles, q, _, rows, tile = weight.shape
        weights = [
            pl.BlockSpec((1, q, 1, rows, tile), lambda j, s, stream=stream: (j, 0, stream, 0, 0))
            for stream in range(2)
        ]
        depth = q * rows
    else:
        depth, tile = weight.shape[0] * weight.shape[2], COLS
        tiles = weight.shape[3] // tile
        weights = column_weights(weight, tile)
    count = image.shape[0]
    column = pl.BlockSpec((count, tile), lambda j, s: (0, j))
    whole = jax.ShapeDtypeStruct((count, tiles * tile), bf16)
    out_specs, out_shape = [column], [whole]
    if gathers:
        out_specs.append(resident((count, depth)))
        out_shape.append(jax.ShapeDtypeStruct((count, depth), bf16))
    if gelu:
        out_specs.append(column)
        out_shape.append(whole)
    return pl.pallas_call(
        functools.partial(forward_kernel, blocks, gathers, gelu),
        grid_spec=pltpu.PrefetchScalarGridSpec(
            num_scalar_prefetch=1,
            grid=(tiles,),
            in_specs=[resident(x.shape), *weights, resident(image.shape)],
            out_specs=out_specs,
        ),
        out_shape=out_shape,
        compiler_params=pltpu.CompilerParams(vmem_limit_bytes=40 << 20),
        cost_estimate=pl.CostEstimate(
            flops=count * depth // 4 * tiles * tile, bytes_accessed=4 << 20, transcendentals=0
        ),
        name="forward_product",
    )(spots, x, weight, weight, image)


def backward_kernel(blocks, turned, scaled, packs, spots, dy_ref, w0, w1, image_ref, *rest):
    rest = list(rest)
    factor_ref = rest.pop(0) if scaled else None
    out_ref = rest[0]
    if turned:
        tiles, tile = w0.shape[0], w0.shape[4]
        weights = [
            [
                (slice(n * tile, (n + 1) * tile), lambda w=w, n=n: flat(w[n, :, 0]))
                for n in range(tiles)
            ]
            for w in (w0, w1)
        ]
    else:
        every = slice(None)
        weights = [[(every, lambda w=w: flat(w[...]))] for w in (w0, w1)]
    count = dy_ref.shape[0]
    size = count // blocks
    rep = spots[2 * blocks]
    part = pl.program_id(0)

    def finish(rows, values):
        if scaled:
            values = values * factor_ref[rows, :].astype(f32)
        return values.astype(bf16)

    chunk = size if packs or scaled else count // 2

    @pl.loop(0, count // chunk)
    def _(p):
        rows = pl.ds(pl.multiple_of(p * chunk, chunk), chunk)
        values = finish(rows, product(dy_ref, rows, weights[0], NT))
        if packs:
            out_ref[pl.ds((rep ^ p) * 2 + part, 1)] = values[None]
        else:
            out_ref[rows, :] = values

    def text(p, first, rows):
        values = finish(rows, product(dy_ref, rows, weights[1], NT))
        image = image_ref[rows, :] == 1
        if packs:
            place = (pl.ds((rep ^ p) * 2 + part, 1), pl.ds(first, WINDOW), slice(None))
            out_ref[place] = jnp.where(image[None], out_ref[place], values[None])
        else:
            out_ref[rows, :] = jnp.where(image, out_ref[rows, :], values)

    text_windows(spots, blocks, count, text)


def backward_product(spots, dy, weight, image, factor=None, packs=False):
    blocks = (spots.shape[0] - 1) // 2
    turned = weight.ndim == 5
    count = image.shape[0]
    if turned:
        tiles, q, _, rows, tile = weight.shape
        step = q * rows // 2 if packs else min(q * rows, 768)
        grid = (q * rows // step,)
        if rows < step:
            block = (tiles, step // rows, 1, rows, tile)
            weights = [
                pl.BlockSpec(block, lambda j, s, stream=stream: (0, j, stream, 0, 0))
                for stream in range(2)
            ]
        else:
            per = rows // step
            weights = [
                pl.BlockSpec(
                    (tiles, 1, 1, step, tile),
                    lambda j, s, stream=stream: (0, j // per, stream, j % per, 0),
                )
                for stream in range(2)
            ]
        depth = q * rows
    else:
        shards, _, rows, width = weight.shape
        depth = shards * rows
        bunch = max(1, 768 // rows)
        step = bunch * rows
        grid = (depth // step,)
        weights = [
            pl.BlockSpec((bunch, 1, rows, width), lambda j, s, stream=stream: (j, stream, 0, 0))
            for stream in range(2)
        ]
    column = pl.BlockSpec((count, step), lambda j, s: (0, j))
    in_specs = [resident(dy.shape), *weights, resident(image.shape)]
    operands = [spots, dy, weight, weight, image]
    if factor is not None:
        in_specs.append(column)
        operands.append(factor)
    if packs:
        shape = (2 * blocks, count // blocks, step)
        out_spec, out_shape = resident(shape), jax.ShapeDtypeStruct(shape, bf16)
    else:
        out_spec, out_shape = column, jax.ShapeDtypeStruct((count, depth), bf16)
    return pl.pallas_call(
        functools.partial(backward_kernel, blocks, turned, factor is not None, packs),
        grid_spec=pltpu.PrefetchScalarGridSpec(
            num_scalar_prefetch=1,
            grid=grid,
            in_specs=in_specs,
            out_specs=out_spec,
        ),
        out_shape=out_shape,
        compiler_params=pltpu.CompilerParams(vmem_limit_bytes=48 << 20),
        cost_estimate=pl.CostEstimate(
            flops=count * depth // 4 * dy.shape[1], bytes_accessed=4 << 20, transcendentals=0
        ),
        name="backward_product",
    )(*operands)


def gradient_kernel(blocks, spots, x_ref, dy_ref, image_ref, *rest):
    *outs, turned_x, masked, acc = rest
    count, width = dy_ref.shape
    size = count // blocks
    cols_at_once = acc.shape[1]

    @pl.when(pl.program_id(0) == 0)
    def _():
        @pl.loop(0, blocks)
        def _(p):
            rows = pl.ds(pl.multiple_of(p * size, size), size)
            kept = dy_ref[rows, :]
            masked[rows, :] = jnp.where(image_ref[rows, :] == 1, kept, jnp.zeros_like(kept))

    turned_x[...] = x_ref[...].T

    def store(stream, n, values):
        values = values.astype(bf16)
        out = outs[min(stream, len(outs) - 1)]
        stream = stream if len(outs) == 1 else 0
        if len(out.shape) == 5:
            tile, per = out.shape[4], out.shape[3]
            for t in range(cols_at_once // tile):
                for q in range(out.shape[1]):
                    out[n * (cols_at_once // tile) + t, q, stream] = values[
                        q * per : (q + 1) * per, t * tile : (t + 1) * tile
                    ]
        else:
            per = out.shape[2]
            for k in range(out.shape[0]):
                out[k, stream, :, n * cols_at_once : (n + 1) * cols_at_once] = values[
                    k * per : (k + 1) * per
                ]

    for n in range(width // cols_at_once):
        cols = slice(n * cols_at_once, (n + 1) * cols_at_once)
        store(0, n, jnp.dot(turned_x[...], masked[:, cols], preferred_element_type=f32))
        acc[...] = jnp.zeros_like(acc)

        def text(p, first, rows, cols=cols):
            kept = dy_ref[rows, cols]
            kept = jnp.where(image_ref[rows, :] == 1, jnp.zeros_like(kept), kept)
            acc[...] += lax.dot_general(x_ref[rows, :], kept, TN, preferred_element_type=f32)

        text_windows(spots, blocks, count, text)
        store(1, n, acc[...])


def gradient(spots, x, dy, image, shape, split=False):
    blocks = (spots.shape[0] - 1) // 2
    count, depth = x.shape
    width = dy.shape[1]
    step = 384
    cols = 1152 if width % 768 else 768
    if len(shape) == 4:
        per = step // shape[2]
        streams = 1 if split else 2
        out_spec = pl.BlockSpec((per, streams, shape[2], width), lambda j, s: (j, 0, 0, 0))
    else:
        tiles, q, _, rows, tile = shape
        if rows < step:
            block = (tiles, step // rows, 2, rows, tile)
            out_spec = pl.BlockSpec(block, lambda j, s: (0, j, 0, 0, 0))
        else:
            per = rows // step
            out_spec = pl.BlockSpec(
                (tiles, 1, 2, step, tile), lambda j, s: (0, j // per, 0, j % per, 0)
            )
    half = jax.ShapeDtypeStruct((shape[0], 1, *shape[2:]), bf16)
    return pl.pallas_call(
        functools.partial(gradient_kernel, blocks),
        grid_spec=pltpu.PrefetchScalarGridSpec(
            num_scalar_prefetch=1,
            grid=(depth // step,),
            in_specs=[
                pl.BlockSpec((count, step), lambda j, s: (0, j)),
                resident(dy.shape),
                resident(image.shape),
            ],
            out_specs=[out_spec, out_spec] if split else out_spec,
            scratch_shapes=[
                pltpu.VMEM((step, count), bf16),
                pltpu.VMEM((count, width), bf16),
                pltpu.VMEM((step, cols), f32),
            ],
        ),
        out_shape=[half, half] if split else jax.ShapeDtypeStruct(shape, bf16),
        compiler_params=pltpu.CompilerParams(vmem_limit_bytes=48 << 20),
        cost_estimate=pl.CostEstimate(
            flops=count * depth // 4 * width, bytes_accessed=4 << 20, transcendentals=0
        ),
        name="gradient",
    )(spots, x, dy, image)


def over_rep(value, target):
    count = lax.axis_size("rep")
    return lax.ppermute(value, "rep", [(r, target(r)) for r in range(count)])


def sibling(value):
    return over_rep(value, lambda r: r ^ 1)


def across(value):
    return over_rep(value, lambda r: r ^ 2)


def gather_rep(value):
    far = across(value)
    return [value, sibling(value), far, sibling(far)]


def reduce_rep(parts):
    near = sibling((parts[1], parts[3]))
    far = across((parts[2].astype(f32) + near[1].astype(f32)).astype(bf16))
    return parts[0].astype(f32) + near[0].astype(f32) + far.astype(f32)


def turn(value):
    reps, shards = lax.axis_size("rep"), lax.axis_size("shard")
    q = shards // reps
    pairs = []
    for r in range(reps):
        for s in range(shards):
            pairs.append((r * shards + s, (s // q) * shards + r * q + s % q))
    return lax.ppermute(value, ("rep", "shard"), pairs)


def gather_weight(weight_low):
    return lax.all_gather(weight_low, "shard", axis=0, tiled=False)


def gather_turned(moved):
    full = gather_weight(moved)
    reps = lax.axis_size("rep")
    return full.reshape(reps, full.shape[0] // reps, *full.shape[1:])


def ring_place(shards):
    mine = lax.axis_index("shard")
    odd = mine % 2
    return (1 - odd) * (mine // 2) + odd * (shards - 1 - mine // 2)


def ring_owner(place, shards):
    place = (place + 2 * shards) % shards
    back = place // ((shards + 1) // 2)
    return (1 - back) * (2 * place) + back * (2 * (shards - 1 - place) + 1)


def ring_kernel(shards, count, *refs):
    sources, dests = refs[:count], refs[count : 2 * count]
    send_sem, recv_sem, own_sem = refs[2 * count :]
    place = ring_place(shards)
    mine = ring_owner(place, shards)
    peers = [ring_owner(place + 1, shards), ring_owner(place - 1, shards)]

    barrier = pltpu.get_barrier_semaphore()
    for peer in peers:
        pl.semaphore_signal(
            barrier, inc=1, device_id={"shard": peer}, device_id_type=pl.DeviceIdType.MESH
        )
    pl.semaphore_wait(barrier, 2)

    kept = [
        pltpu.make_async_copy(sources[w], dests[w].at[mine], own_sem.at[w]) for w in range(count)
    ]
    for copy in kept:
        copy.start()
    chains = [(w, way) for w in range(count) for way in range(2)]
    copies = {}
    for step in range(shards - 1):
        for chain in chains:
            w, way = chain
            if step:
                copies[chain, step - 1].wait_recv()
            owner = ring_owner(place - step if way == 0 else place + step, shards)
            dest = dests[w].at[owner, way]
            copies[chain, step] = pltpu.make_async_remote_copy(
                src_ref=dest if step else sources[w].at[way],
                dst_ref=dest,
                send_sem=send_sem.at[w, way, step],
                recv_sem=recv_sem.at[w, way, step],
                device_id={"shard": peers[way]},
                device_id_type=pl.DeviceIdType.MESH,
            )
            copies[chain, step].start()
    for chain in chains:
        copies[chain, shards - 2].wait_recv()
        for step in range(shards - 1):
            copies[chain, step].wait_send()
    for copy in kept:
        copy.wait()


def ring_gather(*blocks):
    shards = lax.axis_size("shard")
    count = len(blocks)
    anywhere = pl.BlockSpec(memory_space=pl.ANY)
    return pl.pallas_call(
        functools.partial(ring_kernel, shards, count),
        in_specs=[anywhere] * count,
        out_specs=[anywhere] * count,
        out_shape=[jax.ShapeDtypeStruct((shards, *b.shape), b.dtype) for b in blocks],
        scratch_shapes=[
            pltpu.SemaphoreType.DMA((count, 2, shards - 1)),
            pltpu.SemaphoreType.DMA((count, 2, shards - 1)),
            pltpu.SemaphoreType.DMA((count,)),
        ],
        compiler_params=pltpu.CompilerParams(collective_id=0, has_side_effects=True),
        cost_estimate=pl.CostEstimate(flops=1 << 20, bytes_accessed=256 << 20, transcendentals=0),
        name="ring_gather",
    )(*blocks)


def as_turned(full):
    reps = lax.axis_size("rep")
    return full.reshape(reps, full.shape[0] // reps, *full.shape[1:])


def ring_scatter_kernel(count, *refs):
    sources, outs, helds = refs[:count], refs[count : 2 * count], refs[2 * count : 3 * count]
    send_sem, recv_sem = refs[3 * count :]
    shards = sources[0].shape[0]
    pieces = helds[0].shape[1]
    place = ring_place(shards)
    mine = ring_owner(place, shards)
    peers = [ring_owner(place + 1, shards), ring_owner(place - 1, shards)]

    barrier = pltpu.get_barrier_semaphore()
    for peer in peers:
        pl.semaphore_signal(
            barrier, inc=1, device_id={"shard": peer}, device_id_type=pl.DeviceIdType.MESH
        )
    pl.semaphore_wait(barrier, 2)

    chains = [
        (w, way, piece) for piece in range(pieces) for w in range(count) for way in range(2)
    ]
    copies = {}
    for step in range(shards):
        for chain in chains:
            w, way, piece = chain
            part = sources[w].shape[2] // pieces
            span = slice(piece * part, (piece + 1) * part)
            if step < shards - 1:
                owner = ring_owner(place - 1 - step if way == 0 else place + 1 + step, shards)
            else:
                owner = mine
            source = sources[w].at[owner, way, span]
            if step:
                copies[chain, step - 1].wait_recv()
                arrived = helds[w].at[way, piece, step - 1]
                total = arrived[...].astype(f32) + source[...].astype(f32)
                if step == shards - 1:
                    outs[w][way, span] = total.astype(bf16)
                    continue
                arrived[...] = total.astype(bf16)
                source = arrived
            copies[chain, step] = pltpu.make_async_remote_copy(
                src_ref=source,
                dst_ref=helds[w].at[way, piece, step],
                send_sem=send_sem.at[w, way, piece, step],
                recv_sem=recv_sem.at[w, way, piece, step],
                device_id={"shard": peers[way]},
                device_id_type=pl.DeviceIdType.MESH,
            )
            copies[chain, step].start()
    for copy in copies.values():
        copy.wait_send()


def ring_scatter(*terms):
    shards, _, rows, _ = terms[0].shape
    count = len(terms)
    pieces = 2 if rows % 32 == 0 else 1
    sems = pltpu.SemaphoreType.DMA((count, 2, pieces, shards - 1))
    whole = pl.BlockSpec(memory_space=pltpu.VMEM)
    return pl.pallas_call(
        functools.partial(ring_scatter_kernel, count),
        in_specs=[whole] * count,
        out_specs=[whole] * count,
        out_shape=[jax.ShapeDtypeStruct(t.shape[1:], bf16) for t in terms],
        scratch_shapes=[
            pltpu.VMEM((2, pieces, shards - 1, t.shape[2] // pieces, t.shape[3]), bf16)
            for t in terms
        ]
        + [sems, sems],
        compiler_params=pltpu.CompilerParams(
            collective_id=1, has_side_effects=True, vmem_limit_bytes=36 << 20
        ),
        cost_estimate=pl.CostEstimate(flops=1 << 20, bytes_accessed=256 << 20, transcendentals=0),
        name="ring_scatter",
    )(*terms)


def scatter_weight(terms):
    return lax.psum_scatter(
        terms.reshape(-1, *terms.shape[-2:]), "shard", scatter_dimension=0, tiled=True
    ).reshape(terms.shape[-3:])


def body(
    tokens,
    cotangent,
    cond,
    seq_lengths,
    stream_mask,
    w_mod,
    m_mod,
    v_mod,
    w_qkv,
    m_qkv,
    v_qkv,
    w_out,
    m_out,
    v_out,
    w_fc1,
    m_fc1,
    v_fc1,
    w_fc2,
    m_fc2,
    v_fc2,
    gains,
    m_gains,
    v_gains,
):
    tok_rows, model_width = tokens.shape
    slot_count = seq_lengths.shape[0]
    reps, shards = lax.axis_size("rep"), lax.axis_size("shard")
    rep_index, shard_index = lax.axis_index("rep"), lax.axis_index("shard")
    device_index = rep_index * shards + shard_index
    all_tokens = tok_rows * reps * shards
    reach = (MAXLEN - 2) // tok_rows + 1
    part_width = model_width // reps
    part_rows = w_mod.shape[1]
    mod_cols = w_mod.shape[2]

    seq_starts = jnp.cumsum(seq_lengths) - seq_lengths
    local_pos = device_index * tok_rows + jnp.arange(tok_rows, dtype=jnp.int32)
    seq_ids = segment_index(local_pos, seq_starts, all_tokens)
    image_col = (stream_mask == 1)[:, None]
    image_group = jnp.concatenate(gather_rep(stream_mask)) == 1
    image = image_group[:, None].astype(jnp.int32)
    text_group = ~image_group.reshape(reps, tok_rows)
    text_first = jnp.argmax(text_group, axis=1).astype(jnp.int32)
    spots = jnp.concatenate(
        [
            jnp.minimum(text_first // 16 * 16, tok_rows - WINDOW),
            jnp.any(text_group, axis=1).astype(jnp.int32),
            rep_index[None].astype(jnp.int32),
        ]
    )

    silu_cond = jax.nn.silu(cond).astype(bf16)
    cond_rows = lax.dynamic_slice_in_dim(silu_cond, shard_index * part_rows, part_rows, 1)
    mod_terms = jnp.concatenate(
        [
            jnp.dot(cond_rows, w_mod[s].astype(bf16), preferred_element_type=f32)
            for s in range(2)
        ],
        axis=0,
    ).astype(bf16)
    device_count = reps * shards
    firsts = segment_index(
        jnp.arange(device_count, dtype=jnp.int32) * tok_rows, seq_starts, all_tokens
    )
    seconds = jnp.minimum(firsts + 1, slot_count - 1)
    stream_offset = jnp.arange(2, dtype=jnp.int32) * slot_count
    wanted = jnp.stack([firsts, seconds], axis=1)[:, :, None] + stream_offset
    hot = (wanted.reshape(-1, 1) == jnp.arange(2 * slot_count, dtype=jnp.int32)).astype(bf16)
    mod_sent = jnp.dot(hot, mod_terms, preferred_element_type=f32).astype(bf16)
    mod_got = lax.all_to_all(
        mod_sent.reshape(device_count, 4, mod_cols), ("rep", "shard"), 0, 0, tiled=True
    )
    mod_sum = jnp.sum(mod_got.reshape(reps, shards, 4, mod_cols).astype(f32), axis=1).astype(bf16)
    mod_rows = jnp.concatenate([mod_sum[r] for r in range(reps)], axis=1)

    qkv_low = w_qkv.astype(bf16)
    chunks = [
        over_rep(
            qkv_low[:, :, i * part_width : (i + 1) * part_width],
            lambda r, i=i: (3 * r + i) % reps,
        )
        for i in range(3)
    ]
    turns = rep_index % 3

    def rolled(parts, amount):
        return [
            jnp.where(
                amount == 0,
                parts[t],
                jnp.where(amount == 1, parts[(t + 1) % 3], parts[(t + 2) % 3]),
            )
            for t in range(3)
        ]

    out_turned, fc2_low = lax.optimization_barrier(
        (turn(w_out.astype(bf16)), w_fc2.astype(bf16))
    )
    fc2_turned = turn(fc2_low)
    qkv_weights, out_full = ring_gather(
        jnp.concatenate(rolled(chunks, turns), axis=2), out_turned
    )
    out_weights = as_turned(out_full)
    qkv_weights, mod_rows, fc1_low, fc2_turned = lax.optimization_barrier(
        (qkv_weights, mod_rows, w_fc1.astype(bf16), fc2_turned)
    )
    fc1_weights = gather_weight(fc1_low)
    first_seq = seq_ids[0]
    second_seq = jnp.minimum(first_seq + 1, slot_count - 1)
    is_second = (seq_ids != first_seq)[:, None]

    def mod_block(index):
        span = slice(index * model_width, (index + 1) * model_width)
        rows = mod_rows[:, span].astype(f32)
        pick = [jnp.where(is_second, rows[2 + s][None], rows[s][None]) for s in range(2)]
        return jnp.where(image_col, pick[0], pick[1])

    shift_one, scale_one, gate_one, shift_two, scale_two, gate_two = [
        mod_block(i) for i in range(6)
    ]
    stream_in = tokens.astype(f32)
    back_out = cotangent.astype(f32)
    act_one = layer_modulate(stream_in, shift_one, scale_one).astype(bf16)
    act_one_group = jnp.concatenate(gather_rep(act_one))
    d_down = (gate_two * back_out).astype(bf16)
    d_down_group = jnp.concatenate(gather_rep(d_down))

    query_sent, pair_sent, qk_pre = qkv_product(spots, act_one_group, qkv_weights, image, gains)

    bunch = 2 * reps
    bunches = shards // bunch
    half_width = part_width // 2
    groups = [[q * bunch + i for i in range(bunch)] for q in range(bunches)]

    def exchange(value):
        return lax.all_to_all(
            value, "shard", 0, 0, axis_index_groups=None if bunches == 1 else groups, tiled=True
        )

    stretch_count = reps * bunches
    stretch_rows = bunch * tok_rows
    halo = reach * tok_rows

    def stretch_shift(value, steps):
        def place(stretch, g):
            return (stretch % bunches) * bunch + (stretch // bunches) * 2 + g

        pairs = [
            (place(t, g), place(t + steps, g))
            for t in range(stretch_count)
            for g in range(2)
            if 0 <= t + steps < stretch_count
        ]
        return lax.ppermute(value, "shard", pairs)

    pair_own = exchange(pair_sent).reshape(stretch_rows, 2 * half_width)
    pair_before = stretch_shift(pair_own[-halo:], 1)
    pair_after = stretch_shift(pair_own[:halo], -1)
    query_sent, pair_before, pair_after = lax.optimization_barrier(
        (query_sent, pair_before, pair_after)
    )
    query_own = exchange(query_sent).reshape(stretch_rows, half_width)
    fc2_turned, query_own, fc1_weights, d_down_group = lax.optimization_barrier(
        (fc2_turned, query_own, fc1_weights, d_down_group)
    )
    fc2_weights = as_turned(gather_weight(fc2_turned))
    window_rows = stretch_rows + 2 * halo
    stretch = ((shard_index % bunch) // 2) * bunches + shard_index // bunch
    stretch_first = stretch * stretch_rows
    qid = segment_index(
        stretch_first + jnp.arange(stretch_rows, dtype=jnp.int32), seq_starts, all_tokens
    )
    kid = segment_index(
        stretch_first - halo + jnp.arange(window_rows, dtype=jnp.int32), seq_starts, all_tokens
    )
    seq_ends = seq_starts + seq_lengths
    low_pos = seq_starts[qid[::QB]] - (stretch_first - halo)
    high_pos = seq_ends[qid[QB - 1 :: QB]] - (stretch_first - halo)
    lo = jnp.clip(low_pos // KB, 0, window_rows // KB).astype(jnp.int32)
    hi = jnp.clip((high_pos + KB - 1) // KB, 0, window_rows // KB).astype(jnp.int32)
    attended_own, logsum = attention(
        query_own, pair_own, pair_before, pair_after, lo, hi, qid, kid
    )
    attended_came = exchange(attended_own.reshape(bunch, tok_rows, half_width))

    def split_group(value):
        return [value[p * tok_rows : (p + 1) * tok_rows] for p in range(reps)]

    branch_terms, attended_low = forward_product(
        spots, attended_came, out_weights, image, gathers=True
    )
    branch = reduce_rep(split_group(branch_terms))
    mid = stream_in + gate_one * branch
    act_two = layer_modulate(mid, shift_two, scale_two).astype(bf16)
    act_two_group = jnp.concatenate(gather_rep(act_two))
    gelu_low, gelu_slope = forward_product(spots, act_two_group, fc1_weights, image, gelu=True)
    down_terms = forward_product(spots, gelu_low, fc2_weights, image)[0]

    fc2_terms = gradient(spots, gelu_low, d_down_group, image, fc2_weights.shape)
    fc2_terms, gelu_slope = lax.optimization_barrier((fc2_terms, gelu_slope))
    fc2_own = scatter_weight(fc2_terms)
    d_up = backward_product(spots, d_down_group, fc2_weights, image, factor=gelu_slope)
    d_act_two = reduce_rep(split_group(backward_product(spots, d_up, fc1_weights, image)))
    d_mid_norm, d_shift_two, d_scale_two = jax.vjp(layer_modulate, mid, shift_two, scale_two)[1](
        d_act_two
    )
    d_mid = back_out + d_mid_norm
    d_branch = (gate_one * d_mid).astype(bf16)
    fc1_image, fc1_text = gradient(
        spots, act_two_group, d_up, image, fc1_weights.shape, split=True
    )
    fc1_image, fc1_text, d_branch = lax.optimization_barrier((fc1_image, fc1_text, d_branch))
    fc1_image = scatter_weight(fc1_image)
    d_gate_one = d_mid * branch
    d_branch_group = jnp.concatenate(gather_rep(d_branch))
    d_attended = backward_product(spots, d_branch_group, out_weights, image, packs=True)
    out_terms = gradient(spots, attended_low, d_branch_group, image, out_weights.shape)
    d_attended_own = exchange(d_attended).reshape(stretch_rows, half_width)
    d_attended_own, out_terms, fc2_own = lax.optimization_barrier(
        (d_attended_own, out_terms, fc2_own)
    )
    g_fc2 = turn(fc2_own)
    d_query_own, d_before, d_after, d_pair_own = attention_back(
        query_own,
        pair_own,
        pair_before,
        pair_after,
        d_attended_own,
        attended_own,
        lo,
        hi,
        qid,
        kid,
        logsum,
    )
    d_before, d_after, g_fc2 = lax.optimization_barrier((d_before, d_after, g_fc2))
    d_query_came = exchange(d_query_own.reshape(bunch, tok_rows, half_width))
    from_later = stretch_shift(d_before, -1).astype(f32)
    from_earlier = stretch_shift(d_after, 1).astype(f32)
    rest = jnp.zeros((stretch_rows - halo, 2 * half_width), f32)
    d_pair_own = (
        d_pair_own
        + jnp.concatenate([rest, from_later], axis=0)
        + jnp.concatenate([from_earlier, rest], axis=0)
    )
    d_pair_came = exchange(d_pair_own.astype(bf16).reshape(bunch, tok_rows, 2 * half_width))
    d_pair_came, down_terms, fc1_text = lax.optimization_barrier(
        (d_pair_came, down_terms, fc1_text)
    )
    fc1_text = scatter_weight(fc1_text)
    down_proj = reduce_rep(split_group(down_terms))
    output = mid + gate_two * down_proj
    d_gate_two = back_out * down_proj
    d_qkv, gain_sums = norm_back(spots, d_query_came, d_pair_came, qk_pre, image, gains)
    d_act_one = reduce_rep(split_group(backward_product(spots, d_qkv, qkv_weights, image)))
    qkv_terms = gradient(spots, act_one_group, d_qkv, image, qkv_weights.shape)
    d_in_norm, d_shift_one, d_scale_one = jax.vjp(layer_modulate, stream_in, shift_one, scale_one)[
        1
    ](d_act_one)
    d_tokens = d_mid + d_in_norm
    d_mod_tok = jnp.concatenate(
        [d_shift_one, d_scale_one, d_gate_one, d_shift_two, d_scale_two, d_gate_two], axis=1
    )
    image_flag = image_col[:, 0]
    second_flag = is_second[:, 0]
    selector = jnp.stack(
        [
            ~second_flag & image_flag,
            ~second_flag & ~image_flag,
            second_flag & image_flag,
            second_flag & ~image_flag,
        ],
        axis=1,
    ).astype(f32)
    pooled = jnp.einsum("tp,te->pe", selector, d_mod_tok, precision=lax.Precision.HIGHEST)
    gain_sums = jnp.sum(gain_sums.reshape(2, 2, part_width // HD, HD), axis=2)
    gain_part = jnp.concatenate([gain_sums[0], gain_sums[1]], axis=1)
    gain_rows = jnp.concatenate([gain_part, jnp.zeros_like(gain_part)], axis=0)
    leaving = jnp.stack(
        [
            jnp.concatenate([pooled[:, r * mod_cols : (r + 1) * mod_cols], gain_rows], axis=1)
            for r in range(reps)
        ]
    )
    up_fc2 = adam_step(w_fc2, m_fc2, v_fc2, g_fc2.astype(f32), rate_fc2)
    qkv_terms, out_terms, fc1_image, fc1_text, up_fc2, leaving = lax.optimization_barrier(
        (qkv_terms, out_terms, fc1_image, fc1_text, up_fc2, leaving)
    )
    leaving = jnp.broadcast_to(leaving[:, None], (reps, shards, *leaving.shape[1:]))
    came = lax.all_to_all(
        leaving.reshape(device_count, *leaving.shape[2:]), ("rep", "shard"), 0, 0, tiled=True
    )
    out_terms = out_terms.reshape(shards, 2, -1, out_terms.shape[-1])
    g_qkv_group, g_out = ring_scatter(qkv_terms, out_terms)
    g_qkv_group, g_out, came = lax.optimization_barrier((g_qkv_group, g_out, came))
    g_out = turn(g_out)
    g_fc1 = jnp.concatenate([fc1_image, fc1_text], axis=0)
    g_parts = [
        g_qkv_group[:, :, t * part_width : (t + 1) * part_width] for t in range(3)
    ]
    g_parts = rolled(g_parts, (3 - turns) % 3)
    g_qkv = jnp.concatenate(
        [over_rep(g_parts[i], lambda d, i=i: (3 * (d - i)) % reps) for i in range(3)], axis=2
    )

    g_gains = jnp.sum(came[:, :2, mod_cols:], axis=0)
    came = came[:, :, :mod_cols].reshape(2 * device_count, 2, mod_cols)
    seqs = jnp.stack([firsts, seconds], axis=1).reshape(-1)
    hot_seq = (seqs[:, None] == jnp.arange(slot_count, dtype=jnp.int32)).astype(bf16)
    cond_seq = jnp.dot(hot_seq, cond_rows, preferred_element_type=f32)
    g_mod = jnp.stack(
        [
            lax.dot_general(
                cond_seq,
                came[:, s],
                (((0,), (0,)), ((), ())),
                precision=lax.Precision.HIGHEST,
                preferred_element_type=f32,
            )
            for s in range(2)
        ]
    )
    up_mod = adam_step(w_mod, m_mod, v_mod, g_mod, rate_mod)
    up_qkv = adam_step(w_qkv, m_qkv, v_qkv, g_qkv.astype(f32), rate_qkv)
    up_out = adam_step(w_out, m_out, v_out, g_out.astype(f32), rate_out)
    up_fc1 = adam_step(w_fc1, m_fc1, v_fc1, g_fc1.astype(f32), rate_fc1)
    up_gains = adam_step(gains, m_gains, v_gains, g_gains, rate_gains)
    return (
        output.astype(bf16),
        d_tokens,
        *up_mod,
        *up_qkv,
        *up_out,
        *up_fc1,
        *up_fc2,
        *up_gains[:3],
    )


def solution(mesh):
    rows = P(("rep", "shard"), None)
    held = P(None, "shard", "rep")
    return jax.shard_map(
        body,
        mesh=mesh,
        in_specs=(rows, rows, P(), P(), P(("rep", "shard")), *([held] * 15), P(), P(), P()),
        out_specs=(rows, rows, *([held] * 20), P(), P(), P()),
        check_vma=False,
    )
```

```python
import functools

import jax
import jax.numpy as jnp
from jax import lax
from jax.experimental import pallas as pl
from jax.experimental.pallas import tpu as pltpu
from jax.sharding import PartitionSpec as P

HD = 64
MAXLEN = 1178
STEP = 7

norm_eps = 1e-06
adam_eps = 1e-08
score_scale = 0.125
rate_mod = 0.03
rate_qkv = 0.03
rate_out = 0.15
rate_fc1 = 0.03
rate_fc2 = 0.015
rate_gains = 1.0

bf16 = jnp.bfloat16
f32 = jnp.float32
QB = 256
KB = 256
TXT = 154
WINDOW = (TXT + 15 + 15) // 16 * 16
COLS = 512
GELU_A = 0.7978845608028654
GELU_B = 0.044715
NN = (((1,), (0,)), ((), ()))
NT = (((1,), (1,)), ((), ()))
TN = (((0,), (0,)), ((), ()))


def layer_modulate(values, shift, scale):
    centred = values - jnp.mean(values, axis=-1, keepdims=True)
    normed = centred * lax.rsqrt(jnp.mean(centred * centred, axis=-1, keepdims=True) + norm_eps)
    return normed * (1.0 + scale) + shift


def adam_step(weight, moment_one, moment_two, grads, rate):
    new_one = 0.9 * moment_one + 0.1 * grads
    new_two = 0.999 * moment_two + 0.001 * grads * grads
    fixed_one = new_one / (1.0 - 0.9**STEP)
    fixed_two = new_two / (1.0 - 0.999**STEP)
    new_weight = weight - rate * (fixed_one / (jnp.sqrt(fixed_two) + adam_eps) + 0.01 * weight)
    return (new_weight, new_one, new_two, new_weight.astype(bf16))


def segment_index(position, seq_starts, all_tokens):
    counted = jnp.sum((seq_starts[None, :] <= position[:, None]).astype(jnp.int32), axis=1) - 1
    inside = (position >= 0) & (position < all_tokens)
    return jnp.where(inside, counted, -1)


def fill_window(own_ref, before_ref, after_ref, keys, values):
    halo, own = before_ref.shape[0], own_ref.shape[0]
    heads = keys.shape[0]
    width = heads * HD
    parts = ((before_ref, 0, halo), (own_ref, halo, own), (after_ref, halo + own, halo))
    for source, first, count in parts:
        for head in range(heads):
            for index, dest in ((0, keys), (1, values)):
                start = index * width + head * HD
                dest[head, first : first + count, :HD] = source[:, start : start + HD]


def attend_kernel(
    lo_ref, hi_ref, q_ref, own_ref, before_ref, after_ref, qid_ref, kid_ref, o_ref, l_ref, keys, values, acc
):
    step = pl.program_id(0)
    heads = keys.shape[0]

    @pl.when(step == 0)
    def _():
        lane = lax.broadcasted_iota(jnp.int32, values.shape[1:], 1)
        for head in range(heads):
            values[head] = (lane == HD).astype(bf16)
        fill_window(own_ref, before_ref, after_ref, keys, values)

    qid = qid_ref[...]
    diagonal = lax.broadcasted_iota(jnp.int32, (QB, QB), 0) == lax.broadcasted_iota(
        jnp.int32, (QB, QB), 1
    )
    queries = [q_ref[:, head * HD : (head + 1) * HD] for head in range(heads)]
    acc[...] = jnp.zeros_like(acc)

    @pl.loop(lo_ref[step], hi_ref[step])
    def _(block):
        rows = pl.ds(pl.multiple_of(block * KB, KB), KB)
        same = qid == kid_ref[pl.ds(block, 1), :]
        for head in range(heads):
            scores = lax.dot_general(
                queries[head], keys[head, rows, :], NT, preferred_element_type=f32
            )
            lifted = jnp.where(same, jnp.exp(scores), 0.0).astype(bf16)
            acc[head] += jnp.dot(lifted, values[head, rows, :], preferred_element_type=f32)

    for head in range(heads):
        total = acc[head, :, HD : HD + 1]
        o_ref[:, head * HD : (head + 1) * HD] = (acc[head, :, :HD] / total).astype(bf16)
        l_ref[0, head : head + 1, :] = jnp.sum(
            jnp.where(diagonal, jnp.log(total), 0.0), axis=0, keepdims=True
        )


def attend_back_kernel(
    lo_ref,
    hi_ref,
    q_ref,
    own_ref,
    before_ref,
    after_ref,
    do_ref,
    o_ref,
    qid_ref,
    kid_ref,
    l_ref,
    dq_ref,
    d_before_ref,
    d_after_ref,
    d_own_ref,
    keys,
    values,
    d_keys,
    d_values,
    d_query,
):
    step = pl.program_id(0)
    heads = keys.shape[0]
    width = heads * HD

    @pl.when(step == 0)
    def _():
        fill_window(own_ref, before_ref, after_ref, keys, values)
        d_keys[...] = jnp.zeros_like(d_keys)
        d_values[...] = jnp.zeros_like(d_values)

    qid = qid_ref[0]
    ones = jnp.ones((8, HD), bf16)
    queries, outs, dots = [], [], []
    for head in range(heads):
        lanes = slice(head * HD, (head + 1) * HD)
        queries.append(q_ref[:, lanes])
        outs.append(do_ref[:, lanes])
        product = outs[head].astype(f32) * o_ref[:, lanes].astype(f32)
        coarse = product.astype(bf16)
        fine = (product - coarse.astype(f32)).astype(bf16)
        total = lax.dot_general(ones, coarse, NT, preferred_element_type=f32)
        dots.append((total + lax.dot_general(ones, fine, NT, preferred_element_type=f32))[:1])
    d_query[...] = jnp.zeros_like(d_query)

    @pl.loop(lo_ref[step], hi_ref[step])
    def _(block):
        rows = pl.ds(pl.multiple_of(block * KB, KB), KB)
        same = kid_ref[rows, :] == qid
        for head in range(heads):
            key = keys[head, rows, :]
            scores = lax.dot_general(key, queries[head], NT, preferred_element_type=f32)
            probs = jnp.where(same, jnp.exp(scores - l_ref[0, head : head + 1, :]), 0.0)
            d_values[head, rows, :] += jnp.dot(
                probs.astype(bf16), outs[head], preferred_element_type=f32
            )
            d_probs = lax.dot_general(
                values[head, rows, :], outs[head], NT, preferred_element_type=f32
            )
            d_scores = (probs * (d_probs - dots[head])).astype(bf16)
            d_keys[head, rows, :] += jnp.dot(d_scores, queries[head], preferred_element_type=f32)
            d_query[head] += lax.dot_general(d_scores, key, TN, preferred_element_type=f32)

    for head in range(heads):
        dq_ref[:, head * HD : (head + 1) * HD] = (d_query[head] * score_scale).astype(bf16)

    @pl.when(step == pl.num_programs(0) - 1)
    def _():
        halo, own = d_before_ref.shape[0], d_own_ref.shape[0]
        for index, source in ((0, d_keys), (1, d_values)):
            for head in range(heads):
                span = slice(index * width + head * HD, index * width + (head + 1) * HD)
                d_before_ref[:, span] = source[head, :halo, :].astype(bf16)
                d_own_ref[:, span] = source[head, halo : halo + own, :]
                d_after_ref[:, span] = source[head, halo + own :, :].astype(bf16)


def resident(shape):
    return pl.BlockSpec(shape, lambda *index: (0,) * len(shape))


def attention(query, own, before, after, lo, hi, qid, kid):
    count, width = query.shape
    heads = width // HD
    window = count + 2 * before.shape[0]
    steps = count // QB
    return pl.pallas_call(
        attend_kernel,
        grid_spec=pltpu.PrefetchScalarGridSpec(
            num_scalar_prefetch=2,
            grid=(steps,),
            in_specs=[
                pl.BlockSpec((QB, width), lambda i, lo, hi: (i, 0)),
                resident(own.shape),
                resident(before.shape),
                resident(after.shape),
                pl.BlockSpec((QB, 1), lambda i, lo, hi: (i, 0)),
                resident((window // KB, KB)),
            ],
            out_specs=[
                pl.BlockSpec((QB, width), lambda i, lo, hi: (i, 0)),
                pl.BlockSpec((1, 8, QB), lambda i, lo, hi: (i, 0, 0)),
            ],
            scratch_shapes=[
                pltpu.VMEM((heads, window, HD), bf16),
                pltpu.VMEM((heads, window, 2 * HD), bf16),
                pltpu.VMEM((heads, QB, 2 * HD), f32),
            ],
        ),
        out_shape=[
            jax.ShapeDtypeStruct((count, width), bf16),
            jax.ShapeDtypeStruct((steps, 8, QB), f32),
        ],
        compiler_params=pltpu.CompilerParams(vmem_limit_bytes=40 << 20),
        cost_estimate=pl.CostEstimate(flops=1 << 30, bytes_accessed=4 << 20, transcendentals=0),
        name="attend",
    )(lo, hi, query, own, before, after, qid[:, None], kid.reshape(window // KB, KB))


def attention_back(query, own, before, after, d_out, out, lo, hi, qid, kid, logsum):
    count, width = query.shape
    heads = width // HD
    halo = before.shape[0]
    window = count + 2 * halo
    steps = count // QB
    rows = pl.BlockSpec((QB, width), lambda i, lo, hi: (i, 0))
    return pl.pallas_call(
        attend_back_kernel,
        grid_spec=pltpu.PrefetchScalarGridSpec(
            num_scalar_prefetch=2,
            grid=(steps,),
            in_specs=[
                rows,
                resident(own.shape),
                resident(before.shape),
                resident(after.shape),
                rows,
                rows,
                pl.BlockSpec((1, 1, QB), lambda i, lo, hi: (i, 0, 0)),
                resident((window, 1)),
                pl.BlockSpec((1, 8, QB), lambda i, lo, hi: (i, 0, 0)),
            ],
            out_specs=[
                rows,
                resident((halo, 2 * width)),
                resident((halo, 2 * width)),
                resident((count, 2 * width)),
            ],
            scratch_shapes=[pltpu.VMEM((heads, window, HD), bf16)] * 2
            + [pltpu.VMEM((heads, window, HD), f32)] * 2
            + [pltpu.VMEM((heads, QB, HD), f32)],
        ),
        out_shape=[
            jax.ShapeDtypeStruct((count, width), bf16),
            jax.ShapeDtypeStruct((halo, 2 * width), bf16),
            jax.ShapeDtypeStruct((halo, 2 * width), bf16),
            jax.ShapeDtypeStruct((count, 2 * width), f32),
        ],
        compiler_params=pltpu.CompilerParams(vmem_limit_bytes=58 << 20),
        cost_estimate=pl.CostEstimate(flops=24 << 30, bytes_accessed=8 << 20, transcendentals=0),
        name="attend_back",
    )(lo, hi, query, own, before, after, d_out, out, qid.reshape(steps, 1, QB), kid[:, None], logsum)


def text_windows(spots, blocks, count, work):
    for p in range(blocks):

        @pl.when(spots[blocks + p] == 1)
        def _(p=p):
            first = pl.multiple_of(spots[p], 16)
            base = p * (count // blocks)
            work(p, first, pl.ds(pl.multiple_of(base + first, 16), WINDOW))


def flat(value):
    return value.reshape(-1, value.shape[-1])


def product(x_ref, rows, weight, dims):
    total = None
    for cols, get in weight:
        term = lax.dot_general(x_ref[rows, cols], get(), dims, preferred_element_type=f32)
        total = term if total is None else total + term
    return total


def group_sums(values, blocks_of):
    coarse = values.astype(bf16)
    fine = (values - coarse.astype(f32)).astype(bf16)
    return jnp.dot(coarse, blocks_of, preferred_element_type=f32) + jnp.dot(
        fine, blocks_of, preferred_element_type=f32
    )


def head_blocks(width):
    row = lax.broadcasted_iota(jnp.int32, (width, width), 0) // HD
    col = lax.broadcasted_iota(jnp.int32, (width, width), 1) // HD
    return (row == col).astype(bf16)


def qkv_kernel(blocks, spots, x_ref, w0, w1, image_ref, gain_ref, q_ref, kv_ref, pre_ref):
    kind = pl.program_id(0)
    every = slice(None)
    size, width = q_ref.shape[1:]
    rep = spots[2 * blocks]
    spread = head_blocks(2 * width)

    def finish(t, values, gain):
        if t < 2:
            mean = group_sums(values * values, spread) * (1.0 / HD)
            values = values * lax.rsqrt(mean + norm_eps) * gain
        values = values.astype(bf16)
        return values * jnp.asarray(score_scale, bf16) if t == 0 else values

    for t in range(3):

        @pl.when(kind == t)
        def _(t=t):
            packed_ref = kv_ref if t else q_ref
            lanes = slice((t - 1) * width, t * width) if t else slice(0, width)

            @pl.loop(0, blocks)
            def _(p):
                rows = pl.ds(pl.multiple_of(p * size, size), size)
                values = product(x_ref, rows, [(every, lambda: flat(w0[...]))], NN)
                if t < 2:
                    pre_ref[rows, :] = values
                values = finish(t, values, gain_ref[0, :1])
                for g in range(2):
                    packed_ref[pl.ds((rep ^ p) * 2 + g, 1), :, lanes] = values[
                        :, g * width : (g + 1) * width
                    ][None]

            def text(p, first, rows):
                values = product(x_ref, rows, [(every, lambda: flat(w1[...]))], NN)
                image = image_ref[rows, :] == 1
                if t < 2:
                    pre_ref[rows, :] = jnp.where(image, pre_ref[rows, :], values)
                values = finish(t, values, gain_ref[0, 1:])
                for g in range(2):
                    place = (
                        pl.ds((rep ^ p) * 2 + g, 1),
                        pl.ds(first, WINDOW),
                        lanes,
                    )
                    packed_ref[place] = jnp.where(
                        image[None], packed_ref[place], values[:, g * width : (g + 1) * width][None]
                    )

            text_windows(spots, blocks, x_ref.shape[0], text)


def both(weight):
    return weight if isinstance(weight, tuple) else (weight, weight)


def column_weights(weight, tile):
    pair = both(weight)
    shards, _, rows, _ = pair[0].shape
    places = [stream if pair[0].shape[1] == 2 else 0 for stream in range(2)]
    return [
        pl.BlockSpec((shards, 1, rows, tile), lambda j, s, place=place: (0, place, 0, j))
        for place in places
    ]


def tiled_gains(gains, heads):
    return jnp.stack([jnp.tile(gains[:, :HD], (1, heads)), jnp.tile(gains[:, HD:], (1, heads))])


def qkv_product(spots, x, weight, image, gains):
    count, depth = x.shape
    blocks = (spots.shape[0] - 1) // 2
    part = weight.shape[3] // 3
    size = count // blocks
    return pl.pallas_call(
        functools.partial(qkv_kernel, blocks),
        grid_spec=pltpu.PrefetchScalarGridSpec(
            num_scalar_prefetch=1,
            grid=(3,),
            in_specs=[
                resident(x.shape),
                *column_weights(weight, part),
                resident(image.shape),
                pl.BlockSpec((1, 2, part), lambda j, s: (jnp.minimum(j, 1), 0, 0)),
            ],
            out_specs=[
                resident((2 * blocks, size, part // 2)),
                resident((2 * blocks, size, part)),
                pl.BlockSpec((count, part), lambda j, s: (0, jnp.minimum(j, 1))),
            ],
        ),
        out_shape=[
            jax.ShapeDtypeStruct((2 * blocks, size, part // 2), bf16),
            jax.ShapeDtypeStruct((2 * blocks, size, part), bf16),
            jax.ShapeDtypeStruct((count, 2 * part), f32),
        ],
        compiler_params=pltpu.CompilerParams(vmem_limit_bytes=40 << 20),
        cost_estimate=pl.CostEstimate(flops=1 << 30, bytes_accessed=4 << 20, transcendentals=0),
        name="qkv_product",
    )(spots, x, weight, weight, image, tiled_gains(gains, part // HD))


def norm_back_kernel(blocks, spots, q_ref, kv_ref, pre_ref, image_ref, gain_ref, out_ref, sum_ref, both):
    @pl.when(pl.program_id(0) == 0)
    def _():
        sum_ref[...] = jnp.zeros_like(sum_ref)

    part = both.shape[1]
    width = part // 2
    image = image_ref[...] == 1
    spread = head_blocks(part)
    for t in range(3):
        came_ref = kv_ref if t else q_ref
        lanes = slice((t - 1) * width, t * width) if t else slice(0, width)
        for g in range(2):
            both[:, g * width : (g + 1) * width] = came_ref[g, :, lanes].astype(f32)
        grad = both[...]
        if t < 2:
            pre = pre_ref[:, t * part : (t + 1) * part]
            scale = lax.rsqrt(group_sums(pre * pre, spread) * (1.0 / HD) + norm_eps)
            gain = jnp.where(image, gain_ref[t, :1], gain_ref[t, 1:])
            each = grad * pre * scale
            total = jnp.sum(each, axis=0, keepdims=True)
            text = jnp.sum(jnp.where(image, 0.0, each), axis=0, keepdims=True)
            sum_ref[2 * t : 2 * t + 1, :] += total - text
            sum_ref[2 * t + 1 : 2 * t + 2, :] += text
            grad = grad * gain
            mean = group_sums(grad * pre, spread) * (1.0 / HD)
            grad = scale * (grad - pre * (scale * scale * mean))
        out_ref[:, t * part : (t + 1) * part] = grad.astype(bf16)


def norm_back(spots, came_query, came_pair, pre, image, gains):
    blocks = (spots.shape[0] - 1) // 2
    _, size, part = came_pair.shape
    tiled = tiled_gains(gains, part // HD)
    return pl.pallas_call(
        functools.partial(norm_back_kernel, blocks),
        grid_spec=pltpu.PrefetchScalarGridSpec(
            num_scalar_prefetch=1,
            grid=(blocks,),
            in_specs=[
                pl.BlockSpec((2, size, part // 2), lambda p, s: (s[2 * blocks] ^ p, 0, 0)),
                pl.BlockSpec((2, size, part), lambda p, s: (s[2 * blocks] ^ p, 0, 0)),
                pl.BlockSpec((size, 2 * part), lambda p, s: (p, 0)),
                pl.BlockSpec((size, 1), lambda p, s: (p, 0)),
                resident(tiled.shape),
            ],
            out_specs=[
                pl.BlockSpec((size, 3 * part), lambda p, s: (p, 0)),
                resident((4, part)),
            ],
            scratch_shapes=[pltpu.VMEM((size, part), f32)],
        ),
        out_shape=[
            jax.ShapeDtypeStruct((blocks * size, 3 * part), bf16),
            jax.ShapeDtypeStruct((4, part), f32),
        ],
        compiler_params=pltpu.CompilerParams(vmem_limit_bytes=32 << 20),
        cost_estimate=pl.CostEstimate(flops=4 << 30, bytes_accessed=12 << 20, transcendentals=0),
        name="norm_back",
    )(spots, came_query, came_pair, pre, image, tiled)


def forward_kernel(blocks, gathers, gelu, spots, x_ref, w0, w1, image_ref, *rest):
    rep = spots[2 * blocks]
    out_ref = rest[0]
    if gathers:
        x_out = rest[1]
        size, width = x_ref.shape[1:]

        @pl.when(pl.program_id(0) == 0)
        def _():
            for p in range(blocks):
                for g in range(2):
                    x_out[p * size : (p + 1) * size, g * width : (g + 1) * width] = x_ref[
                        pl.ds((rep ^ p) * 2 + g, 1)
                    ][0]

        x_ref = x_out
    every = slice(None)
    count = x_ref.shape[0]

    def finish(values):
        if not gelu:
            return (values.astype(bf16),)
        square = values * values
        bend = jnp.tanh(values * (GELU_A + GELU_A * GELU_B * square))
        half = 0.5 * (1.0 + bend)
        slope = half + 0.5 * values * (1.0 - bend * bend) * (GELU_A + 3.0 * GELU_A * GELU_B * square)
        return (values * half).astype(bf16), slope.astype(bf16)

    outs = rest if gelu else (out_ref,)
    chunk = count // (blocks if gelu else 2)

    @pl.loop(0, count // chunk)
    def _(p):
        rows = pl.ds(pl.multiple_of(p * chunk, chunk), chunk)
        values = product(x_ref, rows, [(every, lambda: flat(w0[...]))], NN)
        for out, value in zip(outs, finish(values)):
            out[rows, :] = value

    def text(p, first, rows):
        values = product(x_ref, rows, [(every, lambda: flat(w1[...]))], NN)
        image = image_ref[rows, :] == 1
        for out, value in zip(outs, finish(values)):
            out[rows, :] = jnp.where(image, out[rows, :], value)

    text_windows(spots, blocks, count, text)


def forward_product(spots, x, weight, image, gathers=False, gelu=False):
    blocks = (spots.shape[0] - 1) // 2
    if both(weight)[0].ndim == 5:
        tiles, q, _, rows, tile = weight.shape
        weights = [
            pl.BlockSpec((1, q, 1, rows, tile), lambda j, s, stream=stream: (j, 0, stream, 0, 0))
            for stream in range(2)
        ]
        depth = q * rows
    else:
        shards, _, rows, width = both(weight)[0].shape
        depth, tile = shards * rows, COLS
        tiles = width // tile
        weights = column_weights(weight, tile)
    count = image.shape[0]
    column = pl.BlockSpec((count, tile), lambda j, s: (0, j))
    whole = jax.ShapeDtypeStruct((count, tiles * tile), bf16)
    out_specs, out_shape = [column], [whole]
    if gathers:
        out_specs.append(resident((count, depth)))
        out_shape.append(jax.ShapeDtypeStruct((count, depth), bf16))
    if gelu:
        out_specs.append(column)
        out_shape.append(whole)
    return pl.pallas_call(
        functools.partial(forward_kernel, blocks, gathers, gelu),
        grid_spec=pltpu.PrefetchScalarGridSpec(
            num_scalar_prefetch=1,
            grid=(tiles,),
            in_specs=[resident(x.shape), *weights, resident(image.shape)],
            out_specs=out_specs,
        ),
        out_shape=out_shape,
        compiler_params=pltpu.CompilerParams(vmem_limit_bytes=40 << 20),
        cost_estimate=pl.CostEstimate(
            flops=count * depth // 4 * tiles * tile, bytes_accessed=4 << 20, transcendentals=0
        ),
        name="forward_product",
    )(spots, x, *both(weight), image)


def backward_kernel(blocks, turned, scaled, packs, spots, dy_ref, w0, w1, image_ref, *rest):
    rest = list(rest)
    factor_ref = rest.pop(0) if scaled else None
    out_ref = rest[0]
    if turned:
        tiles, tile = w0.shape[0], w0.shape[4]
        weights = [
            [
                (slice(n * tile, (n + 1) * tile), lambda w=w, n=n: flat(w[n, :, 0]))
                for n in range(tiles)
            ]
            for w in (w0, w1)
        ]
    else:
        every = slice(None)
        weights = [[(every, lambda w=w: flat(w[...]))] for w in (w0, w1)]
    count = dy_ref.shape[0]
    size = count // blocks
    rep = spots[2 * blocks]
    part = pl.program_id(0)

    def finish(rows, values):
        if scaled:
            values = values * factor_ref[rows, :].astype(f32)
        return values.astype(bf16)

    chunk = size if packs or scaled else count // 2

    @pl.loop(0, count // chunk)
    def _(p):
        rows = pl.ds(pl.multiple_of(p * chunk, chunk), chunk)
        values = finish(rows, product(dy_ref, rows, weights[0], NT))
        if packs:
            out_ref[pl.ds((rep ^ p) * 2 + part, 1)] = values[None]
        else:
            out_ref[rows, :] = values

    def text(p, first, rows):
        values = finish(rows, product(dy_ref, rows, weights[1], NT))
        image = image_ref[rows, :] == 1
        if packs:
            place = (pl.ds((rep ^ p) * 2 + part, 1), pl.ds(first, WINDOW), slice(None))
            out_ref[place] = jnp.where(image[None], out_ref[place], values[None])
        else:
            out_ref[rows, :] = jnp.where(image, out_ref[rows, :], values)

    text_windows(spots, blocks, count, text)


def backward_product(spots, dy, weight, image, factor=None, packs=False):
    blocks = (spots.shape[0] - 1) // 2
    turned = both(weight)[0].ndim == 5
    count = image.shape[0]
    if turned:
        tiles, q, _, rows, tile = weight.shape
        step = q * rows // 2 if packs else min(q * rows, 768)
        grid = (q * rows // step,)
        if rows < step:
            block = (tiles, step // rows, 1, rows, tile)
            weights = [
                pl.BlockSpec(block, lambda j, s, stream=stream: (0, j, stream, 0, 0))
                for stream in range(2)
            ]
        else:
            per = rows // step
            weights = [
                pl.BlockSpec(
                    (tiles, 1, 1, step, tile),
                    lambda j, s, stream=stream: (0, j // per, stream, j % per, 0),
                )
                for stream in range(2)
            ]
        depth = q * rows
    else:
        shards, streams, rows, width = both(weight)[0].shape
        depth = shards * rows
        bunch = max(1, 768 // rows)
        step = bunch * rows
        grid = (depth // step,)
        weights = [
            pl.BlockSpec((bunch, 1, rows, width), lambda j, s, place=place: (j, place, 0, 0))
            for place in (0, streams - 1)
        ]
    column = pl.BlockSpec((count, step), lambda j, s: (0, j))
    in_specs = [resident(dy.shape), *weights, resident(image.shape)]
    operands = [spots, dy, *both(weight), image]
    if factor is not None:
        in_specs.append(column)
        operands.append(factor)
    if packs:
        shape = (2 * blocks, count // blocks, step)
        out_spec, out_shape = resident(shape), jax.ShapeDtypeStruct(shape, bf16)
    else:
        out_spec, out_shape = column, jax.ShapeDtypeStruct((count, depth), bf16)
    return pl.pallas_call(
        functools.partial(backward_kernel, blocks, turned, factor is not None, packs),
        grid_spec=pltpu.PrefetchScalarGridSpec(
            num_scalar_prefetch=1,
            grid=grid,
            in_specs=in_specs,
            out_specs=out_spec,
        ),
        out_shape=out_shape,
        compiler_params=pltpu.CompilerParams(vmem_limit_bytes=48 << 20),
        cost_estimate=pl.CostEstimate(
            flops=count * depth // 4 * dy.shape[1], bytes_accessed=4 << 20, transcendentals=0
        ),
        name="backward_product",
    )(*operands)


def gradient_kernel(blocks, spots, x_ref, dy_ref, image_ref, *rest):
    *outs, turned_x, masked, acc = rest
    count, width = dy_ref.shape
    size = count // blocks
    cols_at_once = acc.shape[1]

    @pl.when(pl.program_id(0) == 0)
    def _():
        @pl.loop(0, blocks)
        def _(p):
            rows = pl.ds(pl.multiple_of(p * size, size), size)
            kept = dy_ref[rows, :]
            masked[rows, :] = jnp.where(image_ref[rows, :] == 1, kept, jnp.zeros_like(kept))

    turned_x[...] = x_ref[...].T

    def store(stream, n, values):
        values = values.astype(bf16)
        out = outs[min(stream, len(outs) - 1)]
        stream = stream if len(outs) == 1 else 0
        if len(out.shape) == 5:
            tile, per = out.shape[4], out.shape[3]
            for t in range(cols_at_once // tile):
                for q in range(out.shape[1]):
                    out[n * (cols_at_once // tile) + t, q, stream] = values[
                        q * per : (q + 1) * per, t * tile : (t + 1) * tile
                    ]
        else:
            per = out.shape[2]
            for k in range(out.shape[0]):
                out[k, stream, :, n * cols_at_once : (n + 1) * cols_at_once] = values[
                    k * per : (k + 1) * per
                ]

    for n in range(width // cols_at_once):
        cols = slice(n * cols_at_once, (n + 1) * cols_at_once)
        store(0, n, jnp.dot(turned_x[...], masked[:, cols], preferred_element_type=f32))
        acc[...] = jnp.zeros_like(acc)

        def text(p, first, rows, cols=cols):
            kept = dy_ref[rows, cols]
            kept = jnp.where(image_ref[rows, :] == 1, jnp.zeros_like(kept), kept)
            acc[...] += lax.dot_general(x_ref[rows, :], kept, TN, preferred_element_type=f32)

        text_windows(spots, blocks, count, text)
        store(1, n, acc[...])


def gradient(spots, x, dy, image, shape, split=False):
    blocks = (spots.shape[0] - 1) // 2
    count, depth = x.shape
    width = dy.shape[1]
    step = 384
    cols = 1152 if width % 768 else 768
    if len(shape) == 4:
        per = step // shape[2]
        streams = 1 if split else 2
        out_spec = pl.BlockSpec((per, streams, shape[2], width), lambda j, s: (j, 0, 0, 0))
    else:
        tiles, q, _, rows, tile = shape
        if rows < step:
            block = (tiles, step // rows, 2, rows, tile)
            out_spec = pl.BlockSpec(block, lambda j, s: (0, j, 0, 0, 0))
        else:
            per = rows // step
            out_spec = pl.BlockSpec(
                (tiles, 1, 2, step, tile), lambda j, s: (0, j // per, 0, j % per, 0)
            )
    half = jax.ShapeDtypeStruct((shape[0], 1, *shape[2:]), bf16)
    return pl.pallas_call(
        functools.partial(gradient_kernel, blocks),
        grid_spec=pltpu.PrefetchScalarGridSpec(
            num_scalar_prefetch=1,
            grid=(depth // step,),
            in_specs=[
                pl.BlockSpec((count, step), lambda j, s: (0, j)),
                resident(dy.shape),
                resident(image.shape),
            ],
            out_specs=[out_spec, out_spec] if split else out_spec,
            scratch_shapes=[
                pltpu.VMEM((step, count), bf16),
                pltpu.VMEM((count, width), bf16),
                pltpu.VMEM((step, cols), f32),
            ],
        ),
        out_shape=[half, half] if split else jax.ShapeDtypeStruct(shape, bf16),
        compiler_params=pltpu.CompilerParams(vmem_limit_bytes=48 << 20),
        cost_estimate=pl.CostEstimate(
            flops=count * depth // 4 * width, bytes_accessed=4 << 20, transcendentals=0
        ),
        name="gradient",
    )(spots, x, dy, image)


def over_rep(value, target):
    count = lax.axis_size("rep")
    return lax.ppermute(value, "rep", [(r, target(r)) for r in range(count)])


def sibling(value):
    return over_rep(value, lambda r: r ^ 1)


def across(value):
    return over_rep(value, lambda r: r ^ 2)


def gather_rep(value):
    far = across(value)
    return [value, sibling(value), far, sibling(far)]


def reduce_rep(parts):
    near = sibling((parts[1], parts[3]))
    far = across((parts[2].astype(f32) + near[1].astype(f32)).astype(bf16))
    return parts[0].astype(f32) + near[0].astype(f32) + far.astype(f32)


def turn(value):
    reps, shards = lax.axis_size("rep"), lax.axis_size("shard")
    q = shards // reps
    pairs = []
    for r in range(reps):
        for s in range(shards):
            pairs.append((r * shards + s, (s // q) * shards + r * q + s % q))
    return lax.ppermute(value, ("rep", "shard"), pairs)


def gather_weight(weight_low):
    return lax.all_gather(weight_low, "shard", axis=0, tiled=False)


def gather_turned(moved):
    full = gather_weight(moved)
    reps = lax.axis_size("rep")
    return full.reshape(reps, full.shape[0] // reps, *full.shape[1:])


def ring_place(shards):
    mine = lax.axis_index("shard")
    odd = mine % 2
    return (1 - odd) * (mine // 2) + odd * (shards - 1 - mine // 2)


def ring_owner(place, shards):
    place = (place + 2 * shards) % shards
    back = place // ((shards + 1) // 2)
    return (1 - back) * (2 * place) + back * (2 * (shards - 1 - place) + 1)


def ring_kernel(shards, count, *refs):
    sources, dests = refs[:count], refs[count : 2 * count]
    send_sem, recv_sem, own_sem = refs[2 * count :]
    place = ring_place(shards)
    mine = ring_owner(place, shards)
    peers = [ring_owner(place + 1, shards), ring_owner(place - 1, shards)]

    barrier = pltpu.get_barrier_semaphore()
    for peer in peers:
        pl.semaphore_signal(
            barrier, inc=1, device_id={"shard": peer}, device_id_type=pl.DeviceIdType.MESH
        )
    pl.semaphore_wait(barrier, 2)

    kept = [
        pltpu.make_async_copy(sources[w], dests[w].at[mine], own_sem.at[w]) for w in range(count)
    ]
    for copy in kept:
        copy.start()
    chains = [(w, way) for w in range(count) for way in range(2)]
    copies = {}
    for step in range(shards - 1):
        for chain in chains:
            w, way = chain
            if step:
                copies[chain, step - 1].wait_recv()
            owner = ring_owner(place - step if way == 0 else place + step, shards)
            dest = dests[w].at[owner, way]
            copies[chain, step] = pltpu.make_async_remote_copy(
                src_ref=dest if step else sources[w].at[way],
                dst_ref=dest,
                send_sem=send_sem.at[w, way, step],
                recv_sem=recv_sem.at[w, way, step],
                device_id={"shard": peers[way]},
                device_id_type=pl.DeviceIdType.MESH,
            )
            copies[chain, step].start()
    for chain in chains:
        copies[chain, shards - 2].wait_recv()
        for step in range(shards - 1):
            copies[chain, step].wait_send()
    for copy in kept:
        copy.wait()


def ring_gather(*blocks):
    shards = lax.axis_size("shard")
    count = len(blocks)
    anywhere = pl.BlockSpec(memory_space=pl.ANY)
    return pl.pallas_call(
        functools.partial(ring_kernel, shards, count),
        in_specs=[anywhere] * count,
        out_specs=[anywhere] * count,
        out_shape=[jax.ShapeDtypeStruct((shards, *b.shape), b.dtype) for b in blocks],
        scratch_shapes=[
            pltpu.SemaphoreType.DMA((count, 2, shards - 1)),
            pltpu.SemaphoreType.DMA((count, 2, shards - 1)),
            pltpu.SemaphoreType.DMA((count,)),
        ],
        compiler_params=pltpu.CompilerParams(collective_id=0, has_side_effects=True),
        cost_estimate=pl.CostEstimate(flops=1 << 20, bytes_accessed=256 << 20, transcendentals=0),
        name="ring_gather",
    )(*blocks)


def as_turned(full):
    reps = lax.axis_size("rep")
    return full.reshape(reps, full.shape[0] // reps, *full.shape[1:])


def ring_scatter_kernel(count, *refs):
    sources, outs, helds = refs[:count], refs[count : 2 * count], refs[2 * count : 3 * count]
    send_sem, recv_sem = refs[3 * count :]
    shards = sources[0].shape[0]
    pieces = helds[0].shape[1]
    place = ring_place(shards)
    mine = ring_owner(place, shards)
    peers = [ring_owner(place + 1, shards), ring_owner(place - 1, shards)]

    barrier = pltpu.get_barrier_semaphore()
    for peer in peers:
        pl.semaphore_signal(
            barrier, inc=1, device_id={"shard": peer}, device_id_type=pl.DeviceIdType.MESH
        )
    pl.semaphore_wait(barrier, 2)

    chains = [
        (w, way, piece) for piece in range(pieces) for w in range(count) for way in range(2)
    ]
    copies = {}
    for step in range(shards):
        for chain in chains:
            w, way, piece = chain
            part = sources[w].shape[2] // pieces
            span = slice(piece * part, (piece + 1) * part)
            if step < shards - 1:
                owner = ring_owner(place - 1 - step if way == 0 else place + 1 + step, shards)
            else:
                owner = mine
            source = sources[w].at[owner, way, span]
            if step:
                copies[chain, step - 1].wait_recv()
                arrived = helds[w].at[way, piece, step - 1]
                total = arrived[...].astype(f32) + source[...].astype(f32)
                if step == shards - 1:
                    outs[w][way, span] = total.astype(bf16)
                    continue
                arrived[...] = total.astype(bf16)
                source = arrived
            copies[chain, step] = pltpu.make_async_remote_copy(
                src_ref=source,
                dst_ref=helds[w].at[way, piece, step],
                send_sem=send_sem.at[w, way, piece, step],
                recv_sem=recv_sem.at[w, way, piece, step],
                device_id={"shard": peers[way]},
                device_id_type=pl.DeviceIdType.MESH,
            )
            copies[chain, step].start()
    for copy in copies.values():
        copy.wait_send()


def ring_scatter(*terms):
    shards, _, rows, _ = terms[0].shape
    count = len(terms)
    pieces = 2 if rows % 32 == 0 else 1
    sems = pltpu.SemaphoreType.DMA((count, 2, pieces, shards - 1))
    whole = pl.BlockSpec(memory_space=pltpu.VMEM)
    return pl.pallas_call(
        functools.partial(ring_scatter_kernel, count),
        in_specs=[whole] * count,
        out_specs=[whole] * count,
        out_shape=[jax.ShapeDtypeStruct(t.shape[1:], bf16) for t in terms],
        scratch_shapes=[
            pltpu.VMEM((2, pieces, shards - 1, t.shape[2] // pieces, t.shape[3]), bf16)
            for t in terms
        ]
        + [sems, sems],
        compiler_params=pltpu.CompilerParams(
            collective_id=1, has_side_effects=True, vmem_limit_bytes=36 << 20
        ),
        cost_estimate=pl.CostEstimate(flops=1 << 20, bytes_accessed=256 << 20, transcendentals=0),
        name="ring_scatter",
    )(*terms)


def scatter_weight(terms):
    return lax.psum_scatter(
        terms.reshape(-1, *terms.shape[-2:]), "shard", scatter_dimension=0, tiled=True
    ).reshape(terms.shape[-3:])


def body(
    tokens,
    cotangent,
    cond,
    seq_lengths,
    stream_mask,
    w_mod,
    m_mod,
    v_mod,
    w_qkv,
    m_qkv,
    v_qkv,
    w_out,
    m_out,
    v_out,
    w_fc1,
    m_fc1,
    v_fc1,
    w_fc2,
    m_fc2,
    v_fc2,
    gains,
    m_gains,
    v_gains,
):
    tok_rows, model_width = tokens.shape
    slot_count = seq_lengths.shape[0]
    reps, shards = lax.axis_size("rep"), lax.axis_size("shard")
    rep_index, shard_index = lax.axis_index("rep"), lax.axis_index("shard")
    device_index = rep_index * shards + shard_index
    all_tokens = tok_rows * reps * shards
    reach = (MAXLEN - 2) // tok_rows + 1
    part_width = model_width // reps
    part_rows = w_mod.shape[1]
    mod_cols = w_mod.shape[2]

    seq_starts = jnp.cumsum(seq_lengths) - seq_lengths
    local_pos = device_index * tok_rows + jnp.arange(tok_rows, dtype=jnp.int32)
    seq_ids = segment_index(local_pos, seq_starts, all_tokens)
    image_col = (stream_mask == 1)[:, None]
    image_group = jnp.concatenate(gather_rep(stream_mask)) == 1
    image = image_group[:, None].astype(jnp.int32)
    text_group = ~image_group.reshape(reps, tok_rows)
    text_first = jnp.argmax(text_group, axis=1).astype(jnp.int32)
    spots = jnp.concatenate(
        [
            jnp.minimum(text_first // 16 * 16, tok_rows - WINDOW),
            jnp.any(text_group, axis=1).astype(jnp.int32),
            rep_index[None].astype(jnp.int32),
        ]
    )

    silu_cond = jax.nn.silu(cond).astype(bf16)
    cond_rows = lax.dynamic_slice_in_dim(silu_cond, shard_index * part_rows, part_rows, 1)
    mod_terms = jnp.concatenate(
        [
            jnp.dot(cond_rows, w_mod[s].astype(bf16), preferred_element_type=f32)
            for s in range(2)
        ],
        axis=0,
    ).astype(bf16)
    device_count = reps * shards
    firsts = segment_index(
        jnp.arange(device_count, dtype=jnp.int32) * tok_rows, seq_starts, all_tokens
    )
    seconds = jnp.minimum(firsts + 1, slot_count - 1)
    stream_offset = jnp.arange(2, dtype=jnp.int32) * slot_count
    wanted = jnp.stack([firsts, seconds], axis=1)[:, :, None] + stream_offset
    hot = (wanted.reshape(-1, 1) == jnp.arange(2 * slot_count, dtype=jnp.int32)).astype(bf16)
    mod_sent = jnp.dot(hot, mod_terms, preferred_element_type=f32).astype(bf16)
    mod_sent, out_turned = lax.optimization_barrier((mod_sent, turn(w_out.astype(bf16))))
    mod_got = lax.all_to_all(
        mod_sent.reshape(device_count, 4, mod_cols), ("rep", "shard"), 0, 0, tiled=True
    )
    mod_sum = jnp.sum(mod_got.reshape(reps, shards, 4, mod_cols).astype(f32), axis=1).astype(bf16)
    mod_rows = jnp.concatenate([mod_sum[r] for r in range(reps)], axis=1)

    qkv_low = w_qkv.astype(bf16)
    chunks = [
        over_rep(
            qkv_low[:, :, i * part_width : (i + 1) * part_width],
            lambda r, i=i: (3 * r + i) % reps,
        )
        for i in range(3)
    ]
    turns = rep_index % 3

    def rolled(parts, amount):
        return [
            jnp.where(
                amount == 0,
                parts[t],
                jnp.where(amount == 1, parts[(t + 1) % 3], parts[(t + 2) % 3]),
            )
            for t in range(3)
        ]

    out_turned, fc2_low = lax.optimization_barrier((out_turned, w_fc2.astype(bf16)))
    fc2_turned = turn(fc2_low)
    qkv_weights, out_full = ring_gather(
        jnp.concatenate(rolled(chunks, turns), axis=2), out_turned
    )
    out_weights = as_turned(out_full)
    qkv_weights, mod_rows, fc1_low, fc2_turned = lax.optimization_barrier(
        (qkv_weights, mod_rows, w_fc1.astype(bf16), fc2_turned)
    )
    fc1_image_weights = gather_weight(fc1_low[:1])
    first_seq = seq_ids[0]
    second_seq = jnp.minimum(first_seq + 1, slot_count - 1)
    is_second = (seq_ids != first_seq)[:, None]

    def mod_block(index):
        span = slice(index * model_width, (index + 1) * model_width)
        rows = mod_rows[:, span].astype(f32)
        pick = [jnp.where(is_second, rows[2 + s][None], rows[s][None]) for s in range(2)]
        return jnp.where(image_col, pick[0], pick[1])

    shift_one, scale_one, gate_one, shift_two, scale_two, gate_two = [
        mod_block(i) for i in range(6)
    ]
    stream_in = tokens.astype(f32)
    back_out = cotangent.astype(f32)
    act_one = layer_modulate(stream_in, shift_one, scale_one).astype(bf16)
    act_one_group = jnp.concatenate(gather_rep(act_one))
    d_down = (gate_two * back_out).astype(bf16)
    d_down_group = jnp.concatenate(gather_rep(d_down))

    query_sent, pair_sent, qk_pre = qkv_product(spots, act_one_group, qkv_weights, image, gains)

    bunch = 2 * reps
    bunches = shards // bunch
    half_width = part_width // 2
    groups = [[q * bunch + i for i in range(bunch)] for q in range(bunches)]

    def exchange(value):
        return lax.all_to_all(
            value, "shard", 0, 0, axis_index_groups=None if bunches == 1 else groups, tiled=True
        )

    stretch_count = reps * bunches
    stretch_rows = bunch * tok_rows
    halo = reach * tok_rows

    def stretch_shift(value, steps):
        def place(stretch, g):
            return (stretch % bunches) * bunch + (stretch // bunches) * 2 + g

        pairs = [
            (place(t, g), place(t + steps, g))
            for t in range(stretch_count)
            for g in range(2)
            if 0 <= t + steps < stretch_count
        ]
        return lax.ppermute(value, "shard", pairs)

    pair_own = exchange(pair_sent).reshape(stretch_rows, 2 * half_width)
    pair_own, fc1_text_low = lax.optimization_barrier((pair_own, fc1_low[1:]))
    pair_before = stretch_shift(pair_own[-halo:], 1)
    pair_after = stretch_shift(pair_own[:halo], -1)
    query_sent, pair_before, pair_after = lax.optimization_barrier(
        (query_sent, pair_before, pair_after)
    )
    fc1_text_weights = gather_weight(fc1_text_low)
    query_own = exchange(query_sent).reshape(stretch_rows, half_width)
    fc2_turned, query_own, fc1_image_weights, d_down_group = lax.optimization_barrier(
        (fc2_turned, query_own, fc1_image_weights, d_down_group)
    )
    fc2_weights = as_turned(gather_weight(fc2_turned))
    window_rows = stretch_rows + 2 * halo
    stretch = ((shard_index % bunch) // 2) * bunches + shard_index // bunch
    stretch_first = stretch * stretch_rows
    qid = segment_index(
        stretch_first + jnp.arange(stretch_rows, dtype=jnp.int32), seq_starts, all_tokens
    )
    kid = segment_index(
        stretch_first - halo + jnp.arange(window_rows, dtype=jnp.int32), seq_starts, all_tokens
    )
    seq_ends = seq_starts + seq_lengths
    low_pos = seq_starts[qid[::QB]] - (stretch_first - halo)
    high_pos = seq_ends[qid[QB - 1 :: QB]] - (stretch_first - halo)
    lo = jnp.clip(low_pos // KB, 0, window_rows // KB).astype(jnp.int32)
    hi = jnp.clip((high_pos + KB - 1) // KB, 0, window_rows // KB).astype(jnp.int32)
    attended_own, logsum = attention(
        query_own, pair_own, pair_before, pair_after, lo, hi, qid, kid
    )
    attended_own, fc1_text_weights = lax.optimization_barrier((attended_own, fc1_text_weights))
    fc1_weights = (fc1_image_weights, fc1_text_weights)
    attended_came = exchange(attended_own.reshape(bunch, tok_rows, half_width))

    def split_group(value):
        return [value[p * tok_rows : (p + 1) * tok_rows] for p in range(reps)]

    branch_terms, attended_low = forward_product(
        spots, attended_came, out_weights, image, gathers=True
    )
    branch = reduce_rep(split_group(branch_terms))
    mid = stream_in + gate_one * branch
    act_two = layer_modulate(mid, shift_two, scale_two).astype(bf16)
    act_two_group = jnp.concatenate(gather_rep(act_two))
    gelu_low, gelu_slope = forward_product(spots, act_two_group, fc1_weights, image, gelu=True)
    down_terms = forward_product(spots, gelu_low, fc2_weights, image)[0]

    fc2_terms = gradient(spots, gelu_low, d_down_group, image, fc2_weights.shape)
    fc2_terms, gelu_slope = lax.optimization_barrier((fc2_terms, gelu_slope))
    fc2_own = scatter_weight(fc2_terms)
    d_up = backward_product(spots, d_down_group, fc2_weights, image, factor=gelu_slope)
    d_act_two = reduce_rep(split_group(backward_product(spots, d_up, fc1_weights, image)))
    d_mid_norm, d_shift_two, d_scale_two = jax.vjp(layer_modulate, mid, shift_two, scale_two)[1](
        d_act_two
    )
    d_mid = back_out + d_mid_norm
    d_branch = (gate_one * d_mid).astype(bf16)
    fc1_image, fc1_text = gradient(
        spots, act_two_group, d_up, image, (shards, 2, *w_fc1.shape[1:]), split=True
    )
    fc1_image, fc1_text, d_branch = lax.optimization_barrier((fc1_image, fc1_text, d_branch))
    fc1_image = scatter_weight(fc1_image)
    d_gate_one = d_mid * branch
    d_branch_group = jnp.concatenate(gather_rep(d_branch))
    d_attended = backward_product(spots, d_branch_group, out_weights, image, packs=True)
    out_terms = gradient(spots, attended_low, d_branch_group, image, out_weights.shape)
    d_attended_own = exchange(d_attended).reshape(stretch_rows, half_width)
    d_attended_own, out_terms, fc2_own = lax.optimization_barrier(
        (d_attended_own, out_terms, fc2_own)
    )
    g_fc2 = turn(fc2_own)
    d_query_own, d_before, d_after, d_pair_own = attention_back(
        query_own,
        pair_own,
        pair_before,
        pair_after,
        d_attended_own,
        attended_own,
        lo,
        hi,
        qid,
        kid,
        logsum,
    )
    d_before, d_after, g_fc2 = lax.optimization_barrier((d_before, d_after, g_fc2))
    d_query_came = exchange(d_query_own.reshape(bunch, tok_rows, half_width))
    from_later = stretch_shift(d_before, -1).astype(f32)
    from_earlier = stretch_shift(d_after, 1).astype(f32)
    rest = jnp.zeros((stretch_rows - halo, 2 * half_width), f32)
    d_pair_own = (
        d_pair_own
        + jnp.concatenate([rest, from_later], axis=0)
        + jnp.concatenate([from_earlier, rest], axis=0)
    )
    d_pair_came = exchange(d_pair_own.astype(bf16).reshape(bunch, tok_rows, 2 * half_width))
    d_pair_came, down_terms, fc1_text = lax.optimization_barrier(
        (d_pair_came, down_terms, fc1_text)
    )
    fc1_text = scatter_weight(fc1_text)
    down_proj = reduce_rep(split_group(down_terms))
    output = mid + gate_two * down_proj
    d_gate_two = back_out * down_proj
    d_qkv, gain_sums = norm_back(spots, d_query_came, d_pair_came, qk_pre, image, gains)
    d_act_one = reduce_rep(split_group(backward_product(spots, d_qkv, qkv_weights, image)))
    qkv_terms = gradient(spots, act_one_group, d_qkv, image, qkv_weights.shape)
    d_in_norm, d_shift_one, d_scale_one = jax.vjp(layer_modulate, stream_in, shift_one, scale_one)[
        1
    ](d_act_one)
    d_tokens = d_mid + d_in_norm
    d_mod_tok = jnp.concatenate(
        [d_shift_one, d_scale_one, d_gate_one, d_shift_two, d_scale_two, d_gate_two], axis=1
    )
    image_flag = image_col[:, 0]
    second_flag = is_second[:, 0]
    selector = jnp.stack(
        [
            ~second_flag & image_flag,
            ~second_flag & ~image_flag,
            second_flag & image_flag,
            second_flag & ~image_flag,
        ],
        axis=1,
    ).astype(f32)
    pooled = jnp.einsum("tp,te->pe", selector, d_mod_tok, precision=lax.Precision.HIGHEST)
    gain_sums = jnp.sum(gain_sums.reshape(2, 2, part_width // HD, HD), axis=2)
    gain_part = jnp.concatenate([gain_sums[0], gain_sums[1]], axis=1)
    gain_rows = jnp.concatenate([gain_part, jnp.zeros_like(gain_part)], axis=0)
    leaving = jnp.stack(
        [
            jnp.concatenate([pooled[:, r * mod_cols : (r + 1) * mod_cols], gain_rows], axis=1)
            for r in range(reps)
        ]
    )
    up_fc2 = adam_step(w_fc2, m_fc2, v_fc2, g_fc2.astype(f32), rate_fc2)
    qkv_terms, out_terms, fc1_image, fc1_text, up_fc2, leaving = lax.optimization_barrier(
        (qkv_terms, out_terms, fc1_image, fc1_text, up_fc2, leaving)
    )
    leaving = jnp.broadcast_to(leaving[:, None], (reps, shards, *leaving.shape[1:]))
    came = lax.all_to_all(
        leaving.reshape(device_count, *leaving.shape[2:]), ("rep", "shard"), 0, 0, tiled=True
    )
    out_terms = out_terms.reshape(shards, 2, -1, out_terms.shape[-1])
    g_qkv_group, g_out = ring_scatter(qkv_terms, out_terms)
    g_qkv_group, g_out, came = lax.optimization_barrier((g_qkv_group, g_out, came))
    g_out = turn(g_out)
    g_fc1 = jnp.concatenate([fc1_image, fc1_text], axis=0)
    g_parts = [
        g_qkv_group[:, :, t * part_width : (t + 1) * part_width] for t in range(3)
    ]
    g_parts = rolled(g_parts, (3 - turns) % 3)
    g_qkv = jnp.concatenate(
        [over_rep(g_parts[i], lambda d, i=i: (3 * (d - i)) % reps) for i in range(3)], axis=2
    )

    g_gains = jnp.sum(came[:, :2, mod_cols:], axis=0)
    came = came[:, :, :mod_cols].reshape(2 * device_count, 2, mod_cols)
    seqs = jnp.stack([firsts, seconds], axis=1).reshape(-1)
    hot_seq = (seqs[:, None] == jnp.arange(slot_count, dtype=jnp.int32)).astype(bf16)
    cond_seq = jnp.dot(hot_seq, cond_rows, preferred_element_type=f32)
    g_mod = jnp.stack(
        [
            lax.dot_general(
                cond_seq,
                came[:, s],
                (((0,), (0,)), ((), ())),
                precision=lax.Precision.HIGHEST,
                preferred_element_type=f32,
            )
            for s in range(2)
        ]
    )
    up_mod = adam_step(w_mod, m_mod, v_mod, g_mod, rate_mod)
    up_qkv = adam_step(w_qkv, m_qkv, v_qkv, g_qkv.astype(f32), rate_qkv)
    up_out = adam_step(w_out, m_out, v_out, g_out.astype(f32), rate_out)
    up_fc1 = adam_step(w_fc1, m_fc1, v_fc1, g_fc1.astype(f32), rate_fc1)
    up_gains = adam_step(gains, m_gains, v_gains, g_gains, rate_gains)
    return (
        output.astype(bf16),
        d_tokens,
        *up_mod,
        *up_qkv,
        *up_out,
        *up_fc1,
        *up_fc2,
        *up_gains[:3],
    )


def solution(mesh):
    rows = P(("rep", "shard"), None)
    held = P(None, "shard", "rep")
    return jax.shard_map(
        body,
        mesh=mesh,
        in_specs=(rows, rows, P(), P(), P(("rep", "shard")), *([held] * 15), P(), P(), P()),
        out_specs=(rows, rows, *([held] * 20), P(), P(), P()),
        check_vma=False,
    )
```

```python
import functools

import jax
import jax.numpy as jnp
from jax import lax
from jax.experimental import pallas as pl
from jax.experimental.pallas import tpu as pltpu
from jax.sharding import PartitionSpec as P

HD = 64
MAXLEN = 1178
STEP = 7

norm_eps = 1e-06
adam_eps = 1e-08
score_scale = 0.125
rate_mod = 0.03
rate_qkv = 0.03
rate_out = 0.15
rate_fc1 = 0.03
rate_fc2 = 0.015
rate_gains = 1.0

bf16 = jnp.bfloat16
f32 = jnp.float32
QB = 256
KB = 256
TXT = 154
WINDOW = (TXT + 15 + 15) // 16 * 16
COLS = 512
GELU_A = 0.7978845608028654
GELU_B = 0.044715
NN = (((1,), (0,)), ((), ()))
NT = (((1,), (1,)), ((), ()))
TN = (((0,), (0,)), ((), ()))


def layer_modulate(values, shift, scale):
    centred = values - jnp.mean(values, axis=-1, keepdims=True)
    normed = centred * lax.rsqrt(jnp.mean(centred * centred, axis=-1, keepdims=True) + norm_eps)
    return normed * (1.0 + scale) + shift


def adam_step(weight, moment_one, moment_two, grads, rate):
    new_one = 0.9 * moment_one + 0.1 * grads
    new_two = 0.999 * moment_two + 0.001 * grads * grads
    fixed_one = new_one / (1.0 - 0.9**STEP)
    fixed_two = new_two / (1.0 - 0.999**STEP)
    new_weight = weight - rate * (fixed_one / (jnp.sqrt(fixed_two) + adam_eps) + 0.01 * weight)
    return (new_weight, new_one, new_two, new_weight.astype(bf16))


def segment_index(position, seq_starts, all_tokens):
    counted = jnp.sum((seq_starts[None, :] <= position[:, None]).astype(jnp.int32), axis=1) - 1
    inside = (position >= 0) & (position < all_tokens)
    return jnp.where(inside, counted, -1)


def fill_window(own_ref, before_ref, after_ref, keys, values):
    halo, own = before_ref.shape[0], own_ref.shape[0]
    heads = keys.shape[0]
    width = heads * HD
    parts = ((before_ref, 0, halo), (own_ref, halo, own), (after_ref, halo + own, halo))
    for source, first, count in parts:
        for head in range(heads):
            for index, dest in ((0, keys), (1, values)):
                start = index * width + head * HD
                dest[head, first : first + count, :HD] = source[:, start : start + HD]


def attend_kernel(
    lo_ref, hi_ref, q_ref, own_ref, before_ref, after_ref, qid_ref, kid_ref, o_ref, l_ref, keys, values, acc
):
    step = pl.program_id(0)
    heads = keys.shape[0]

    @pl.when(step == 0)
    def _():
        lane = lax.broadcasted_iota(jnp.int32, values.shape[1:], 1)
        for head in range(heads):
            values[head] = (lane == HD).astype(bf16)
        fill_window(own_ref, before_ref, after_ref, keys, values)

    qid = qid_ref[...]
    diagonal = lax.broadcasted_iota(jnp.int32, (QB, QB), 0) == lax.broadcasted_iota(
        jnp.int32, (QB, QB), 1
    )
    queries = [q_ref[:, head * HD : (head + 1) * HD] for head in range(heads)]
    acc[...] = jnp.zeros_like(acc)

    @pl.loop(lo_ref[step], hi_ref[step])
    def _(block):
        rows = pl.ds(pl.multiple_of(block * KB, KB), KB)
        same = qid == kid_ref[pl.ds(block, 1), :]
        for head in range(heads):
            scores = lax.dot_general(
                queries[head], keys[head, rows, :], NT, preferred_element_type=f32
            )
            lifted = jnp.where(same, jnp.exp(scores), 0.0).astype(bf16)
            acc[head] += jnp.dot(lifted, values[head, rows, :], preferred_element_type=f32)

    for head in range(heads):
        total = acc[head, :, HD : HD + 1]
        o_ref[:, head * HD : (head + 1) * HD] = (acc[head, :, :HD] / total).astype(bf16)
        l_ref[0, head : head + 1, :] = jnp.sum(
            jnp.where(diagonal, jnp.log(total), 0.0), axis=0, keepdims=True
        )


def attend_back_kernel(
    lo_ref,
    hi_ref,
    q_ref,
    own_ref,
    before_ref,
    after_ref,
    do_ref,
    o_ref,
    qid_ref,
    kid_ref,
    l_ref,
    dq_ref,
    d_before_ref,
    d_after_ref,
    d_own_ref,
    keys,
    values,
    d_keys,
    d_values,
    d_query,
):
    step = pl.program_id(0)
    heads = keys.shape[0]
    width = heads * HD

    @pl.when(step == 0)
    def _():
        fill_window(own_ref, before_ref, after_ref, keys, values)
        d_keys[...] = jnp.zeros_like(d_keys)
        d_values[...] = jnp.zeros_like(d_values)

    qid = qid_ref[0]
    ones = jnp.ones((8, HD), bf16)
    queries, outs, dots = [], [], []
    for head in range(heads):
        lanes = slice(head * HD, (head + 1) * HD)
        queries.append(q_ref[:, lanes])
        outs.append(do_ref[:, lanes])
        product = outs[head].astype(f32) * o_ref[:, lanes].astype(f32)
        coarse = product.astype(bf16)
        fine = (product - coarse.astype(f32)).astype(bf16)
        total = lax.dot_general(ones, coarse, NT, preferred_element_type=f32)
        dots.append((total + lax.dot_general(ones, fine, NT, preferred_element_type=f32))[:1])
    d_query[...] = jnp.zeros_like(d_query)

    @pl.loop(lo_ref[step], hi_ref[step])
    def _(block):
        rows = pl.ds(pl.multiple_of(block * KB, KB), KB)
        same = kid_ref[rows, :] == qid
        for head in range(heads):
            key = keys[head, rows, :]
            scores = lax.dot_general(key, queries[head], NT, preferred_element_type=f32)
            probs = jnp.where(same, jnp.exp(scores - l_ref[0, head : head + 1, :]), 0.0)
            d_values[head, rows, :] += jnp.dot(
                probs.astype(bf16), outs[head], preferred_element_type=f32
            )
            d_probs = lax.dot_general(
                values[head, rows, :], outs[head], NT, preferred_element_type=f32
            )
            d_scores = (probs * (d_probs - dots[head])).astype(bf16)
            d_keys[head, rows, :] += jnp.dot(d_scores, queries[head], preferred_element_type=f32)
            d_query[head] += lax.dot_general(d_scores, key, TN, preferred_element_type=f32)

    for head in range(heads):
        dq_ref[:, head * HD : (head + 1) * HD] = (d_query[head] * score_scale).astype(bf16)

    @pl.when(step == pl.num_programs(0) - 1)
    def _():
        halo, own = d_before_ref.shape[0], d_own_ref.shape[0]
        for index, source in ((0, d_keys), (1, d_values)):
            for head in range(heads):
                span = slice(index * width + head * HD, index * width + (head + 1) * HD)
                d_before_ref[:, span] = source[head, :halo, :].astype(bf16)
                d_own_ref[:, span] = source[head, halo : halo + own, :]
                d_after_ref[:, span] = source[head, halo + own :, :].astype(bf16)


def resident(shape):
    return pl.BlockSpec(shape, lambda *index: (0,) * len(shape))


def attention(query, own, before, after, lo, hi, qid, kid):
    count, width = query.shape
    heads = width // HD
    window = count + 2 * before.shape[0]
    steps = count // QB
    return pl.pallas_call(
        attend_kernel,
        grid_spec=pltpu.PrefetchScalarGridSpec(
            num_scalar_prefetch=2,
            grid=(steps,),
            in_specs=[
                pl.BlockSpec((QB, width), lambda i, lo, hi: (i, 0)),
                resident(own.shape),
                resident(before.shape),
                resident(after.shape),
                pl.BlockSpec((QB, 1), lambda i, lo, hi: (i, 0)),
                resident((window // KB, KB)),
            ],
            out_specs=[
                pl.BlockSpec((QB, width), lambda i, lo, hi: (i, 0)),
                pl.BlockSpec((1, 8, QB), lambda i, lo, hi: (i, 0, 0)),
            ],
            scratch_shapes=[
                pltpu.VMEM((heads, window, HD), bf16),
                pltpu.VMEM((heads, window, 2 * HD), bf16),
                pltpu.VMEM((heads, QB, 2 * HD), f32),
            ],
        ),
        out_shape=[
            jax.ShapeDtypeStruct((count, width), bf16),
            jax.ShapeDtypeStruct((steps, 8, QB), f32),
        ],
        compiler_params=pltpu.CompilerParams(vmem_limit_bytes=40 << 20),
        cost_estimate=pl.CostEstimate(flops=1 << 30, bytes_accessed=4 << 20, transcendentals=0),
        name="attend",
    )(lo, hi, query, own, before, after, qid[:, None], kid.reshape(window // KB, KB))


def attention_back(query, own, before, after, d_out, out, lo, hi, qid, kid, logsum):
    count, width = query.shape
    heads = width // HD
    halo = before.shape[0]
    window = count + 2 * halo
    steps = count // QB
    rows = pl.BlockSpec((QB, width), lambda i, lo, hi: (i, 0))
    return pl.pallas_call(
        attend_back_kernel,
        grid_spec=pltpu.PrefetchScalarGridSpec(
            num_scalar_prefetch=2,
            grid=(steps,),
            in_specs=[
                rows,
                resident(own.shape),
                resident(before.shape),
                resident(after.shape),
                rows,
                rows,
                pl.BlockSpec((1, 1, QB), lambda i, lo, hi: (i, 0, 0)),
                resident((window, 1)),
                pl.BlockSpec((1, 8, QB), lambda i, lo, hi: (i, 0, 0)),
            ],
            out_specs=[
                rows,
                resident((halo, 2 * width)),
                resident((halo, 2 * width)),
                resident((count, 2 * width)),
            ],
            scratch_shapes=[pltpu.VMEM((heads, window, HD), bf16)] * 2
            + [pltpu.VMEM((heads, window, HD), f32)] * 2
            + [pltpu.VMEM((heads, QB, HD), f32)],
        ),
        out_shape=[
            jax.ShapeDtypeStruct((count, width), bf16),
            jax.ShapeDtypeStruct((halo, 2 * width), bf16),
            jax.ShapeDtypeStruct((halo, 2 * width), bf16),
            jax.ShapeDtypeStruct((count, 2 * width), f32),
        ],
        compiler_params=pltpu.CompilerParams(vmem_limit_bytes=58 << 20),
        cost_estimate=pl.CostEstimate(flops=24 << 30, bytes_accessed=8 << 20, transcendentals=0),
        name="attend_back",
    )(lo, hi, query, own, before, after, d_out, out, qid.reshape(steps, 1, QB), kid[:, None], logsum)


def text_windows(spots, blocks, count, work):
    for p in range(blocks):

        @pl.when(spots[blocks + p] == 1)
        def _(p=p):
            first = pl.multiple_of(spots[p], 16)
            base = p * (count // blocks)
            work(p, first, pl.ds(pl.multiple_of(base + first, 16), WINDOW))


def flat(value):
    return value.reshape(-1, value.shape[-1])


def product(x_ref, rows, weight, dims):
    total = None
    for cols, get in weight:
        term = lax.dot_general(x_ref[rows, cols], get(), dims, preferred_element_type=f32)
        total = term if total is None else total + term
    return total


def group_sums(values, blocks_of):
    coarse = values.astype(bf16)
    fine = (values - coarse.astype(f32)).astype(bf16)
    return jnp.dot(coarse, blocks_of, preferred_element_type=f32) + jnp.dot(
        fine, blocks_of, preferred_element_type=f32
    )


def head_blocks(width):
    row = lax.broadcasted_iota(jnp.int32, (width, width), 0) // HD
    col = lax.broadcasted_iota(jnp.int32, (width, width), 1) // HD
    return (row == col).astype(bf16)


def qkv_kernel(blocks, spots, x_ref, w0, w1, image_ref, gain_ref, q_ref, kv_ref, pre_ref):
    kind = pl.program_id(0)
    every = slice(None)
    size, width = q_ref.shape[1:]
    rep = spots[2 * blocks]
    spread = head_blocks(2 * width)

    def finish(t, values, gain):
        if t < 2:
            mean = group_sums(values * values, spread) * (1.0 / HD)
            values = values * lax.rsqrt(mean + norm_eps) * gain
        values = values.astype(bf16)
        return values * jnp.asarray(score_scale, bf16) if t == 0 else values

    for t in range(3):

        @pl.when(kind == t)
        def _(t=t):
            packed_ref = kv_ref if t else q_ref
            lanes = slice((t - 1) * width, t * width) if t else slice(0, width)

            @pl.loop(0, blocks)
            def _(p):
                rows = pl.ds(pl.multiple_of(p * size, size), size)
                values = product(x_ref, rows, [(every, lambda: flat(w0[...]))], NN)
                if t < 2:
                    pre_ref[rows, :] = values
                values = finish(t, values, gain_ref[0, :1])
                for g in range(2):
                    packed_ref[pl.ds((rep ^ p) * 2 + g, 1), :, lanes] = values[
                        :, g * width : (g + 1) * width
                    ][None]

            def text(p, first, rows):
                values = product(x_ref, rows, [(every, lambda: flat(w1[...]))], NN)
                image = image_ref[rows, :] == 1
                if t < 2:
                    pre_ref[rows, :] = jnp.where(image, pre_ref[rows, :], values)
                values = finish(t, values, gain_ref[0, 1:])
                for g in range(2):
                    place = (
                        pl.ds((rep ^ p) * 2 + g, 1),
                        pl.ds(first, WINDOW),
                        lanes,
                    )
                    packed_ref[place] = jnp.where(
                        image[None], packed_ref[place], values[:, g * width : (g + 1) * width][None]
                    )

            text_windows(spots, blocks, x_ref.shape[0], text)


def both(weight):
    return weight if isinstance(weight, tuple) else (weight, weight)


def column_weights(weight, tile):
    pair = both(weight)
    shards, _, rows, _ = pair[0].shape
    places = [stream if pair[0].shape[1] == 2 else 0 for stream in range(2)]
    return [
        pl.BlockSpec((shards, 1, rows, tile), lambda j, s, place=place: (0, place, 0, j))
        for place in places
    ]


def tiled_gains(gains, heads):
    return jnp.stack([jnp.tile(gains[:, :HD], (1, heads)), jnp.tile(gains[:, HD:], (1, heads))])


def qkv_product(spots, x, weight, image, gains):
    count, depth = x.shape
    blocks = (spots.shape[0] - 1) // 2
    part = weight.shape[3] // 3
    size = count // blocks
    return pl.pallas_call(
        functools.partial(qkv_kernel, blocks),
        grid_spec=pltpu.PrefetchScalarGridSpec(
            num_scalar_prefetch=1,
            grid=(3,),
            in_specs=[
                resident(x.shape),
                *column_weights(weight, part),
                resident(image.shape),
                pl.BlockSpec((1, 2, part), lambda j, s: (jnp.minimum(j, 1), 0, 0)),
            ],
            out_specs=[
                resident((2 * blocks, size, part // 2)),
                resident((2 * blocks, size, part)),
                pl.BlockSpec((count, part), lambda j, s: (0, jnp.minimum(j, 1))),
            ],
        ),
        out_shape=[
            jax.ShapeDtypeStruct((2 * blocks, size, part // 2), bf16),
            jax.ShapeDtypeStruct((2 * blocks, size, part), bf16),
            jax.ShapeDtypeStruct((count, 2 * part), f32),
        ],
        compiler_params=pltpu.CompilerParams(vmem_limit_bytes=40 << 20),
        cost_estimate=pl.CostEstimate(flops=1 << 30, bytes_accessed=4 << 20, transcendentals=0),
        name="qkv_product",
    )(spots, x, weight, weight, image, tiled_gains(gains, part // HD))


def norm_back_kernel(blocks, spots, q_ref, kv_ref, pre_ref, image_ref, gain_ref, out_ref, sum_ref, both):
    @pl.when(pl.program_id(0) == 0)
    def _():
        sum_ref[...] = jnp.zeros_like(sum_ref)

    part = both.shape[1]
    width = part // 2
    image = image_ref[...] == 1
    spread = head_blocks(part)
    for t in range(3):
        came_ref = kv_ref if t else q_ref
        lanes = slice((t - 1) * width, t * width) if t else slice(0, width)
        for g in range(2):
            both[:, g * width : (g + 1) * width] = came_ref[g, :, lanes].astype(f32)
        grad = both[...]
        if t < 2:
            pre = pre_ref[:, t * part : (t + 1) * part]
            scale = lax.rsqrt(group_sums(pre * pre, spread) * (1.0 / HD) + norm_eps)
            gain = jnp.where(image, gain_ref[t, :1], gain_ref[t, 1:])
            each = grad * pre * scale
            total = jnp.sum(each, axis=0, keepdims=True)
            text = jnp.sum(jnp.where(image, 0.0, each), axis=0, keepdims=True)
            sum_ref[2 * t : 2 * t + 1, :] += total - text
            sum_ref[2 * t + 1 : 2 * t + 2, :] += text
            grad = grad * gain
            mean = group_sums(grad * pre, spread) * (1.0 / HD)
            grad = scale * (grad - pre * (scale * scale * mean))
        out_ref[:, t * part : (t + 1) * part] = grad.astype(bf16)


def norm_back(spots, came_query, came_pair, pre, image, gains):
    blocks = (spots.shape[0] - 1) // 2
    _, size, part = came_pair.shape
    tiled = tiled_gains(gains, part // HD)
    return pl.pallas_call(
        functools.partial(norm_back_kernel, blocks),
        grid_spec=pltpu.PrefetchScalarGridSpec(
            num_scalar_prefetch=1,
            grid=(blocks,),
            in_specs=[
                pl.BlockSpec((2, size, part // 2), lambda p, s: (s[2 * blocks] ^ p, 0, 0)),
                pl.BlockSpec((2, size, part), lambda p, s: (s[2 * blocks] ^ p, 0, 0)),
                pl.BlockSpec((size, 2 * part), lambda p, s: (p, 0)),
                pl.BlockSpec((size, 1), lambda p, s: (p, 0)),
                resident(tiled.shape),
            ],
            out_specs=[
                pl.BlockSpec((size, 3 * part), lambda p, s: (p, 0)),
                resident((4, part)),
            ],
            scratch_shapes=[pltpu.VMEM((size, part), f32)],
        ),
        out_shape=[
            jax.ShapeDtypeStruct((blocks * size, 3 * part), bf16),
            jax.ShapeDtypeStruct((4, part), f32),
        ],
        compiler_params=pltpu.CompilerParams(vmem_limit_bytes=32 << 20),
        cost_estimate=pl.CostEstimate(flops=4 << 30, bytes_accessed=12 << 20, transcendentals=0),
        name="norm_back",
    )(spots, came_query, came_pair, pre, image, tiled)


def forward_kernel(blocks, gathers, gelu, spots, x_ref, w0, w1, image_ref, *rest):
    rep = spots[2 * blocks]
    out_ref = rest[0]
    if gathers:
        x_out = rest[1]
        size, width = x_ref.shape[1:]

        @pl.when(pl.program_id(0) == 0)
        def _():
            for p in range(blocks):
                for g in range(2):
                    x_out[p * size : (p + 1) * size, g * width : (g + 1) * width] = x_ref[
                        pl.ds((rep ^ p) * 2 + g, 1)
                    ][0]

        x_ref = x_out
    every = slice(None)
    count = x_ref.shape[0]

    def finish(values):
        if not gelu:
            return (values.astype(bf16),)
        square = values * values
        bend = jnp.tanh(values * (GELU_A + GELU_A * GELU_B * square))
        half = 0.5 * (1.0 + bend)
        slope = half + 0.5 * values * (1.0 - bend * bend) * (GELU_A + 3.0 * GELU_A * GELU_B * square)
        return (values * half).astype(bf16), slope.astype(bf16)

    outs = rest if gelu else (out_ref,)
    chunk = count // (blocks if gelu else 2)

    @pl.loop(0, count // chunk)
    def _(p):
        rows = pl.ds(pl.multiple_of(p * chunk, chunk), chunk)
        values = product(x_ref, rows, [(every, lambda: flat(w0[...]))], NN)
        for out, value in zip(outs, finish(values)):
            out[rows, :] = value

    def text(p, first, rows):
        values = product(x_ref, rows, [(every, lambda: flat(w1[...]))], NN)
        image = image_ref[rows, :] == 1
        for out, value in zip(outs, finish(values)):
            out[rows, :] = jnp.where(image, out[rows, :], value)

    text_windows(spots, blocks, count, text)


def forward_product(spots, x, weight, image, gathers=False, gelu=False):
    blocks = (spots.shape[0] - 1) // 2
    if both(weight)[0].ndim == 5:
        tiles, q, _, rows, tile = weight.shape
        weights = [
            pl.BlockSpec((1, q, 1, rows, tile), lambda j, s, stream=stream: (j, 0, stream, 0, 0))
            for stream in range(2)
        ]
        depth = q * rows
    else:
        shards, _, rows, width = both(weight)[0].shape
        depth, tile = shards * rows, COLS
        tiles = width // tile
        weights = column_weights(weight, tile)
    count = image.shape[0]
    column = pl.BlockSpec((count, tile), lambda j, s: (0, j))
    whole = jax.ShapeDtypeStruct((count, tiles * tile), bf16)
    out_specs, out_shape = [column], [whole]
    if gathers:
        out_specs.append(resident((count, depth)))
        out_shape.append(jax.ShapeDtypeStruct((count, depth), bf16))
    if gelu:
        out_specs.append(column)
        out_shape.append(whole)
    return pl.pallas_call(
        functools.partial(forward_kernel, blocks, gathers, gelu),
        grid_spec=pltpu.PrefetchScalarGridSpec(
            num_scalar_prefetch=1,
            grid=(tiles,),
            in_specs=[resident(x.shape), *weights, resident(image.shape)],
            out_specs=out_specs,
        ),
        out_shape=out_shape,
        compiler_params=pltpu.CompilerParams(vmem_limit_bytes=40 << 20),
        cost_estimate=pl.CostEstimate(
            flops=count * depth // 4 * tiles * tile, bytes_accessed=4 << 20, transcendentals=0
        ),
        name="forward_product",
    )(spots, x, *both(weight), image)


def backward_kernel(blocks, turned, scaled, packs, spots, dy_ref, w0, w1, image_ref, *rest):
    rest = list(rest)
    factor_ref = rest.pop(0) if scaled else None
    out_ref = rest[0]
    if turned:
        tiles, tile = w0.shape[0], w0.shape[4]
        weights = [
            [
                (slice(n * tile, (n + 1) * tile), lambda w=w, n=n: flat(w[n, :, 0]))
                for n in range(tiles)
            ]
            for w in (w0, w1)
        ]
    else:
        every = slice(None)
        weights = [[(every, lambda w=w: flat(w[...]))] for w in (w0, w1)]
    count = dy_ref.shape[0]
    size = count // blocks
    rep = spots[2 * blocks]
    part = pl.program_id(0)

    def finish(rows, values):
        if scaled:
            values = values * factor_ref[rows, :].astype(f32)
        return values.astype(bf16)

    chunk = size if packs or scaled else count // 2

    @pl.loop(0, count // chunk)
    def _(p):
        rows = pl.ds(pl.multiple_of(p * chunk, chunk), chunk)
        values = finish(rows, product(dy_ref, rows, weights[0], NT))
        if packs:
            out_ref[pl.ds((rep ^ p) * 2 + part, 1)] = values[None]
        else:
            out_ref[rows, :] = values

    def text(p, first, rows):
        values = finish(rows, product(dy_ref, rows, weights[1], NT))
        image = image_ref[rows, :] == 1
        if packs:
            place = (pl.ds((rep ^ p) * 2 + part, 1), pl.ds(first, WINDOW), slice(None))
            out_ref[place] = jnp.where(image[None], out_ref[place], values[None])
        else:
            out_ref[rows, :] = jnp.where(image, out_ref[rows, :], values)

    text_windows(spots, blocks, count, text)


def backward_product(spots, dy, weight, image, factor=None, packs=False):
    blocks = (spots.shape[0] - 1) // 2
    turned = both(weight)[0].ndim == 5
    count = image.shape[0]
    if turned:
        tiles, q, _, rows, tile = weight.shape
        step = q * rows // 2 if packs else min(q * rows, 768)
        grid = (q * rows // step,)
        if rows < step:
            block = (tiles, step // rows, 1, rows, tile)
            weights = [
                pl.BlockSpec(block, lambda j, s, stream=stream: (0, j, stream, 0, 0))
                for stream in range(2)
            ]
        else:
            per = rows // step
            weights = [
                pl.BlockSpec(
                    (tiles, 1, 1, step, tile),
                    lambda j, s, stream=stream: (0, j // per, stream, j % per, 0),
                )
                for stream in range(2)
            ]
        depth = q * rows
    else:
        shards, streams, rows, width = both(weight)[0].shape
        depth = shards * rows
        bunch = max(1, 768 // rows)
        step = bunch * rows
        grid = (depth // step,)
        weights = [
            pl.BlockSpec((bunch, 1, rows, width), lambda j, s, place=place: (j, place, 0, 0))
            for place in (0, streams - 1)
        ]
    column = pl.BlockSpec((count, step), lambda j, s: (0, j))
    in_specs = [resident(dy.shape), *weights, resident(image.shape)]
    operands = [spots, dy, *both(weight), image]
    if factor is not None:
        in_specs.append(column)
        operands.append(factor)
    if packs:
        shape = (2 * blocks, count // blocks, step)
        out_spec, out_shape = resident(shape), jax.ShapeDtypeStruct(shape, bf16)
    else:
        out_spec, out_shape = column, jax.ShapeDtypeStruct((count, depth), bf16)
    return pl.pallas_call(
        functools.partial(backward_kernel, blocks, turned, factor is not None, packs),
        grid_spec=pltpu.PrefetchScalarGridSpec(
            num_scalar_prefetch=1,
            grid=grid,
            in_specs=in_specs,
            out_specs=out_spec,
        ),
        out_shape=out_shape,
        compiler_params=pltpu.CompilerParams(vmem_limit_bytes=48 << 20),
        cost_estimate=pl.CostEstimate(
            flops=count * depth // 4 * dy.shape[1], bytes_accessed=4 << 20, transcendentals=0
        ),
        name="backward_product",
    )(*operands)


def gradient_kernel(blocks, spots, x_ref, dy_ref, image_ref, *rest):
    *outs, turned_x, masked, acc = rest
    count, width = dy_ref.shape
    size = count // blocks
    cols_at_once = acc.shape[1]

    @pl.when(pl.program_id(0) == 0)
    def _():
        @pl.loop(0, blocks)
        def _(p):
            rows = pl.ds(pl.multiple_of(p * size, size), size)
            kept = dy_ref[rows, :]
            masked[rows, :] = jnp.where(image_ref[rows, :] == 1, kept, jnp.zeros_like(kept))

    turned_x[...] = x_ref[...].T

    def store(stream, n, values):
        values = values.astype(bf16)
        out = outs[min(stream, len(outs) - 1)]
        stream = stream if len(outs) == 1 else 0
        if len(out.shape) == 5:
            tile, per = out.shape[4], out.shape[3]
            for t in range(cols_at_once // tile):
                for q in range(out.shape[1]):
                    out[n * (cols_at_once // tile) + t, q, stream] = values[
                        q * per : (q + 1) * per, t * tile : (t + 1) * tile
                    ]
        else:
            per = out.shape[2]
            for k in range(out.shape[0]):
                out[k, stream, :, n * cols_at_once : (n + 1) * cols_at_once] = values[
                    k * per : (k + 1) * per
                ]

    for n in range(width // cols_at_once):
        cols = slice(n * cols_at_once, (n + 1) * cols_at_once)
        store(0, n, jnp.dot(turned_x[...], masked[:, cols], preferred_element_type=f32))
        acc[...] = jnp.zeros_like(acc)

        def text(p, first, rows, cols=cols):
            kept = dy_ref[rows, cols]
            kept = jnp.where(image_ref[rows, :] == 1, jnp.zeros_like(kept), kept)
            acc[...] += lax.dot_general(x_ref[rows, :], kept, TN, preferred_element_type=f32)

        text_windows(spots, blocks, count, text)
        store(1, n, acc[...])


def gradient(spots, x, dy, image, shape, split=False):
    blocks = (spots.shape[0] - 1) // 2
    count, depth = x.shape
    width = dy.shape[1]
    step = 384
    cols = 1152 if width % 768 else 768
    if len(shape) == 4:
        per = step // shape[2]
        streams = 1 if split else 2
        out_spec = pl.BlockSpec((per, streams, shape[2], width), lambda j, s: (j, 0, 0, 0))
    else:
        tiles, q, _, rows, tile = shape
        if rows < step:
            block = (tiles, step // rows, 2, rows, tile)
            out_spec = pl.BlockSpec(block, lambda j, s: (0, j, 0, 0, 0))
        else:
            per = rows // step
            out_spec = pl.BlockSpec(
                (tiles, 1, 2, step, tile), lambda j, s: (0, j // per, 0, j % per, 0)
            )
    half = jax.ShapeDtypeStruct((shape[0], 1, *shape[2:]), bf16)
    return pl.pallas_call(
        functools.partial(gradient_kernel, blocks),
        grid_spec=pltpu.PrefetchScalarGridSpec(
            num_scalar_prefetch=1,
            grid=(depth // step,),
            in_specs=[
                pl.BlockSpec((count, step), lambda j, s: (0, j)),
                resident(dy.shape),
                resident(image.shape),
            ],
            out_specs=[out_spec, out_spec] if split else out_spec,
            scratch_shapes=[
                pltpu.VMEM((step, count), bf16),
                pltpu.VMEM((count, width), bf16),
                pltpu.VMEM((step, cols), f32),
            ],
        ),
        out_shape=[half, half] if split else jax.ShapeDtypeStruct(shape, bf16),
        compiler_params=pltpu.CompilerParams(vmem_limit_bytes=48 << 20),
        cost_estimate=pl.CostEstimate(
            flops=count * depth // 4 * width, bytes_accessed=4 << 20, transcendentals=0
        ),
        name="gradient",
    )(spots, x, dy, image)


def over_rep(value, target):
    count = lax.axis_size("rep")
    return lax.ppermute(value, "rep", [(r, target(r)) for r in range(count)])


def sibling(value):
    return over_rep(value, lambda r: r ^ 1)


def across(value):
    return over_rep(value, lambda r: r ^ 2)


def gather_rep(value):
    far = across(value)
    return [value, sibling(value), far, sibling(far)]


def reduce_rep(parts):
    near = sibling((parts[1], parts[3]))
    far = across((parts[2].astype(f32) + near[1].astype(f32)).astype(bf16))
    return parts[0].astype(f32) + near[0].astype(f32) + far.astype(f32)


def turn(value):
    reps, shards = lax.axis_size("rep"), lax.axis_size("shard")
    q = shards // reps
    pairs = []
    for r in range(reps):
        for s in range(shards):
            pairs.append((r * shards + s, (s // q) * shards + r * q + s % q))
    return lax.ppermute(value, ("rep", "shard"), pairs)


def gather_weight(weight_low):
    return lax.all_gather(weight_low, "shard", axis=0, tiled=False)


def gather_turned(moved):
    full = gather_weight(moved)
    reps = lax.axis_size("rep")
    return full.reshape(reps, full.shape[0] // reps, *full.shape[1:])


def ring_place(shards):
    mine = lax.axis_index("shard")
    odd = mine % 2
    return (1 - odd) * (mine // 2) + odd * (shards - 1 - mine // 2)


def ring_owner(place, shards):
    place = (place + 2 * shards) % shards
    back = place // ((shards + 1) // 2)
    return (1 - back) * (2 * place) + back * (2 * (shards - 1 - place) + 1)


def ring_kernel(shards, count, *refs):
    sources, dests = refs[:count], refs[count : 2 * count]
    send_sem, recv_sem, own_sem = refs[2 * count :]
    place = ring_place(shards)
    mine = ring_owner(place, shards)
    peers = [ring_owner(place + 1, shards), ring_owner(place - 1, shards)]

    barrier = pltpu.get_barrier_semaphore()
    for peer in peers:
        pl.semaphore_signal(
            barrier, inc=1, device_id={"shard": peer}, device_id_type=pl.DeviceIdType.MESH
        )
    pl.semaphore_wait(barrier, 2)

    kept = [
        pltpu.make_async_copy(sources[w], dests[w].at[mine], own_sem.at[w]) for w in range(count)
    ]
    for copy in kept:
        copy.start()
    chains = [(w, way) for w in range(count) for way in range(2)]
    copies = {}
    for step in range(shards - 1):
        for chain in chains:
            w, way = chain
            if step:
                copies[chain, step - 1].wait_recv()
            owner = ring_owner(place - step if way == 0 else place + step, shards)
            dest = dests[w].at[owner, way]
            copies[chain, step] = pltpu.make_async_remote_copy(
                src_ref=dest if step else sources[w].at[way],
                dst_ref=dest,
                send_sem=send_sem.at[w, way, step],
                recv_sem=recv_sem.at[w, way, step],
                device_id={"shard": peers[way]},
                device_id_type=pl.DeviceIdType.MESH,
            )
            copies[chain, step].start()
    for chain in chains:
        copies[chain, shards - 2].wait_recv()
        for step in range(shards - 1):
            copies[chain, step].wait_send()
    for copy in kept:
        copy.wait()


def ring_gather(*blocks):
    shards = lax.axis_size("shard")
    count = len(blocks)
    anywhere = pl.BlockSpec(memory_space=pl.ANY)
    return pl.pallas_call(
        functools.partial(ring_kernel, shards, count),
        in_specs=[anywhere] * count,
        out_specs=[anywhere] * count,
        out_shape=[jax.ShapeDtypeStruct((shards, *b.shape), b.dtype) for b in blocks],
        scratch_shapes=[
            pltpu.SemaphoreType.DMA((count, 2, shards - 1)),
            pltpu.SemaphoreType.DMA((count, 2, shards - 1)),
            pltpu.SemaphoreType.DMA((count,)),
        ],
        compiler_params=pltpu.CompilerParams(collective_id=0, has_side_effects=True),
        cost_estimate=pl.CostEstimate(flops=1 << 20, bytes_accessed=256 << 20, transcendentals=0),
        name="ring_gather",
    )(*blocks)


def as_turned(full):
    reps = lax.axis_size("rep")
    return full.reshape(reps, full.shape[0] // reps, *full.shape[1:])


def ring_scatter_kernel(count, *refs):
    sources, outs, helds = refs[:count], refs[count : 2 * count], refs[2 * count : 3 * count]
    send_sem, recv_sem = refs[3 * count :]
    shards = sources[0].shape[0]
    pieces = helds[0].shape[1]
    place = ring_place(shards)
    mine = ring_owner(place, shards)
    peers = [ring_owner(place + 1, shards), ring_owner(place - 1, shards)]

    barrier = pltpu.get_barrier_semaphore()
    for peer in peers:
        pl.semaphore_signal(
            barrier, inc=1, device_id={"shard": peer}, device_id_type=pl.DeviceIdType.MESH
        )
    pl.semaphore_wait(barrier, 2)

    chains = [
        (w, way, piece) for piece in range(pieces) for w in range(count) for way in range(2)
    ]
    copies = {}
    for step in range(shards):
        for chain in chains:
            w, way, piece = chain
            part = sources[w].shape[2] // pieces
            span = slice(piece * part, (piece + 1) * part)
            if step < shards - 1:
                owner = ring_owner(place - 1 - step if way == 0 else place + 1 + step, shards)
            else:
                owner = mine
            source = sources[w].at[owner, way, span]
            if step:
                copies[chain, step - 1].wait_recv()
                arrived = helds[w].at[way, piece, step - 1]
                total = arrived[...].astype(f32) + source[...].astype(f32)
                if step == shards - 1:
                    outs[w][way, span] = total.astype(bf16)
                    continue
                arrived[...] = total.astype(bf16)
                source = arrived
            copies[chain, step] = pltpu.make_async_remote_copy(
                src_ref=source,
                dst_ref=helds[w].at[way, piece, step],
                send_sem=send_sem.at[w, way, piece, step],
                recv_sem=recv_sem.at[w, way, piece, step],
                device_id={"shard": peers[way]},
                device_id_type=pl.DeviceIdType.MESH,
            )
            copies[chain, step].start()
    for copy in copies.values():
        copy.wait_send()


def ring_scatter(*terms):
    shards, _, rows, _ = terms[0].shape
    count = len(terms)
    pieces = 2 if rows % 32 == 0 else 1
    sems = pltpu.SemaphoreType.DMA((count, 2, pieces, shards - 1))
    whole = pl.BlockSpec(memory_space=pltpu.VMEM)
    return pl.pallas_call(
        functools.partial(ring_scatter_kernel, count),
        in_specs=[whole] * count,
        out_specs=[whole] * count,
        out_shape=[jax.ShapeDtypeStruct(t.shape[1:], bf16) for t in terms],
        scratch_shapes=[
            pltpu.VMEM((2, pieces, shards - 1, t.shape[2] // pieces, t.shape[3]), bf16)
            for t in terms
        ]
        + [sems, sems],
        compiler_params=pltpu.CompilerParams(
            collective_id=1, has_side_effects=True, vmem_limit_bytes=36 << 20
        ),
        cost_estimate=pl.CostEstimate(flops=1 << 20, bytes_accessed=8 << 20, transcendentals=0),
        name="ring_scatter",
    )(*terms)


def scatter_weight(terms):
    return lax.psum_scatter(
        terms.reshape(-1, *terms.shape[-2:]), "shard", scatter_dimension=0, tiled=True
    ).reshape(terms.shape[-3:])


def body(
    tokens,
    cotangent,
    cond,
    seq_lengths,
    stream_mask,
    w_mod,
    m_mod,
    v_mod,
    w_qkv,
    m_qkv,
    v_qkv,
    w_out,
    m_out,
    v_out,
    w_fc1,
    m_fc1,
    v_fc1,
    w_fc2,
    m_fc2,
    v_fc2,
    gains,
    m_gains,
    v_gains,
):
    tok_rows, model_width = tokens.shape
    slot_count = seq_lengths.shape[0]
    reps, shards = lax.axis_size("rep"), lax.axis_size("shard")
    rep_index, shard_index = lax.axis_index("rep"), lax.axis_index("shard")
    device_index = rep_index * shards + shard_index
    all_tokens = tok_rows * reps * shards
    reach = (MAXLEN - 2) // tok_rows + 1
    part_width = model_width // reps
    part_rows = w_mod.shape[1]
    mod_cols = w_mod.shape[2]

    seq_starts = jnp.cumsum(seq_lengths) - seq_lengths
    local_pos = device_index * tok_rows + jnp.arange(tok_rows, dtype=jnp.int32)
    seq_ids = segment_index(local_pos, seq_starts, all_tokens)
    image_col = (stream_mask == 1)[:, None]
    image_group = jnp.concatenate(gather_rep(stream_mask)) == 1
    image = image_group[:, None].astype(jnp.int32)
    text_group = ~image_group.reshape(reps, tok_rows)
    text_first = jnp.argmax(text_group, axis=1).astype(jnp.int32)
    spots = jnp.concatenate(
        [
            jnp.minimum(text_first // 16 * 16, tok_rows - WINDOW),
            jnp.any(text_group, axis=1).astype(jnp.int32),
            rep_index[None].astype(jnp.int32),
        ]
    )

    silu_cond = jax.nn.silu(cond).astype(bf16)
    cond_rows = lax.dynamic_slice_in_dim(silu_cond, shard_index * part_rows, part_rows, 1)
    mod_terms = jnp.concatenate(
        [
            jnp.dot(cond_rows, w_mod[s].astype(bf16), preferred_element_type=f32)
            for s in range(2)
        ],
        axis=0,
    ).astype(bf16)
    device_count = reps * shards
    firsts = segment_index(
        jnp.arange(device_count, dtype=jnp.int32) * tok_rows, seq_starts, all_tokens
    )
    seconds = jnp.minimum(firsts + 1, slot_count - 1)
    stream_offset = jnp.arange(2, dtype=jnp.int32) * slot_count
    wanted = jnp.stack([firsts, seconds], axis=1)[:, :, None] + stream_offset
    hot = (wanted.reshape(-1, 1) == jnp.arange(2 * slot_count, dtype=jnp.int32)).astype(bf16)
    mod_sent = jnp.dot(hot, mod_terms, preferred_element_type=f32).astype(bf16)
    mod_sent, out_turned = lax.optimization_barrier((mod_sent, turn(w_out.astype(bf16))))
    mod_got = lax.all_to_all(
        mod_sent.reshape(device_count, 4, mod_cols), ("rep", "shard"), 0, 0, tiled=True
    )
    mod_sum = jnp.sum(mod_got.reshape(reps, shards, 4, mod_cols).astype(f32), axis=1).astype(bf16)
    mod_rows = jnp.concatenate([mod_sum[r] for r in range(reps)], axis=1)

    qkv_low = w_qkv.astype(bf16)
    chunks = [
        over_rep(
            qkv_low[:, :, i * part_width : (i + 1) * part_width],
            lambda r, i=i: (3 * r + i) % reps,
        )
        for i in range(3)
    ]
    turns = rep_index % 3

    def rolled(parts, amount):
        return [
            jnp.where(
                amount == 0,
                parts[t],
                jnp.where(amount == 1, parts[(t + 1) % 3], parts[(t + 2) % 3]),
            )
            for t in range(3)
        ]

    out_turned, fc2_low = lax.optimization_barrier((out_turned, w_fc2.astype(bf16)))
    fc2_turned = turn(fc2_low)
    qkv_weights, out_full = ring_gather(
        jnp.concatenate(rolled(chunks, turns), axis=2), out_turned
    )
    out_weights = as_turned(out_full)
    qkv_weights, mod_rows, fc1_low, fc2_turned = lax.optimization_barrier(
        (qkv_weights, mod_rows, w_fc1.astype(bf16), fc2_turned)
    )
    fc1_image_weights = gather_weight(fc1_low[:1])
    first_seq = seq_ids[0]
    second_seq = jnp.minimum(first_seq + 1, slot_count - 1)
    is_second = (seq_ids != first_seq)[:, None]

    def mod_block(index):
        span = slice(index * model_width, (index + 1) * model_width)
        rows = mod_rows[:, span].astype(f32)
        pick = [jnp.where(is_second, rows[2 + s][None], rows[s][None]) for s in range(2)]
        return jnp.where(image_col, pick[0], pick[1])

    shift_one, scale_one, gate_one, shift_two, scale_two, gate_two = [
        mod_block(i) for i in range(6)
    ]
    stream_in = tokens.astype(f32)
    back_out = cotangent.astype(f32)
    act_one = layer_modulate(stream_in, shift_one, scale_one).astype(bf16)
    act_one_group = jnp.concatenate(gather_rep(act_one))
    d_down = (gate_two * back_out).astype(bf16)
    d_down_group = jnp.concatenate(gather_rep(d_down))

    query_sent, pair_sent, qk_pre = qkv_product(spots, act_one_group, qkv_weights, image, gains)

    bunch = 2 * reps
    bunches = shards // bunch
    half_width = part_width // 2
    groups = [[q * bunch + i for i in range(bunch)] for q in range(bunches)]

    def exchange(value):
        return lax.all_to_all(
            value, "shard", 0, 0, axis_index_groups=None if bunches == 1 else groups, tiled=True
        )

    stretch_count = reps * bunches
    stretch_rows = bunch * tok_rows
    halo = reach * tok_rows

    def stretch_shift(value, steps):
        def place(stretch, g):
            return (stretch % bunches) * bunch + (stretch // bunches) * 2 + g

        pairs = [
            (place(t, g), place(t + steps, g))
            for t in range(stretch_count)
            for g in range(2)
            if 0 <= t + steps < stretch_count
        ]
        return lax.ppermute(value, "shard", pairs)

    pair_own = exchange(pair_sent).reshape(stretch_rows, 2 * half_width)
    pair_own, fc1_text_low = lax.optimization_barrier((pair_own, fc1_low[1:]))
    pair_before = stretch_shift(pair_own[-halo:], 1)
    pair_after = stretch_shift(pair_own[:halo], -1)
    query_sent, pair_before, pair_after = lax.optimization_barrier(
        (query_sent, pair_before, pair_after)
    )
    fc1_text_weights = gather_weight(fc1_text_low)
    query_own = exchange(query_sent).reshape(stretch_rows, half_width)
    fc2_turned, query_own, fc1_image_weights, d_down_group = lax.optimization_barrier(
        (fc2_turned, query_own, fc1_image_weights, d_down_group)
    )
    fc2_weights = as_turned(gather_weight(fc2_turned))
    window_rows = stretch_rows + 2 * halo
    stretch = ((shard_index % bunch) // 2) * bunches + shard_index // bunch
    stretch_first = stretch * stretch_rows
    qid = segment_index(
        stretch_first + jnp.arange(stretch_rows, dtype=jnp.int32), seq_starts, all_tokens
    )
    kid = segment_index(
        stretch_first - halo + jnp.arange(window_rows, dtype=jnp.int32), seq_starts, all_tokens
    )
    seq_ends = seq_starts + seq_lengths
    low_pos = seq_starts[qid[::QB]] - (stretch_first - halo)
    high_pos = seq_ends[qid[QB - 1 :: QB]] - (stretch_first - halo)
    lo = jnp.clip(low_pos // KB, 0, window_rows // KB).astype(jnp.int32)
    hi = jnp.clip((high_pos + KB - 1) // KB, 0, window_rows // KB).astype(jnp.int32)
    attended_own, logsum = attention(
        query_own, pair_own, pair_before, pair_after, lo, hi, qid, kid
    )
    attended_own, fc1_text_weights = lax.optimization_barrier((attended_own, fc1_text_weights))
    fc1_weights = (fc1_image_weights, fc1_text_weights)
    attended_came = exchange(attended_own.reshape(bunch, tok_rows, half_width))

    def split_group(value):
        return [value[p * tok_rows : (p + 1) * tok_rows] for p in range(reps)]

    branch_terms, attended_low = forward_product(
        spots, attended_came, out_weights, image, gathers=True
    )
    branch = reduce_rep(split_group(branch_terms))
    mid = stream_in + gate_one * branch
    act_two = layer_modulate(mid, shift_two, scale_two).astype(bf16)
    act_two_group = jnp.concatenate(gather_rep(act_two))
    gelu_low, gelu_slope = forward_product(spots, act_two_group, fc1_weights, image, gelu=True)
    down_terms = forward_product(spots, gelu_low, fc2_weights, image)[0]

    fc2_terms = gradient(spots, gelu_low, d_down_group, image, fc2_weights.shape)
    fc2_terms, gelu_slope = lax.optimization_barrier((fc2_terms, gelu_slope))
    fc2_own = scatter_weight(fc2_terms)
    d_up = backward_product(spots, d_down_group, fc2_weights, image, factor=gelu_slope)
    d_act_two = reduce_rep(split_group(backward_product(spots, d_up, fc1_weights, image)))
    d_mid_norm, d_shift_two, d_scale_two = jax.vjp(layer_modulate, mid, shift_two, scale_two)[1](
        d_act_two
    )
    d_mid = back_out + d_mid_norm
    d_branch = (gate_one * d_mid).astype(bf16)
    fc1_image, fc1_text = gradient(
        spots, act_two_group, d_up, image, (shards, 2, *w_fc1.shape[1:]), split=True
    )
    fc1_image, fc1_text, d_branch = lax.optimization_barrier((fc1_image, fc1_text, d_branch))
    fc1_image = scatter_weight(fc1_image)
    d_gate_one = d_mid * branch
    d_branch_group = jnp.concatenate(gather_rep(d_branch))
    d_attended = backward_product(spots, d_branch_group, out_weights, image, packs=True)
    out_terms = gradient(spots, attended_low, d_branch_group, image, out_weights.shape)
    d_attended_own = exchange(d_attended).reshape(stretch_rows, half_width)
    d_attended_own, out_terms, fc2_own = lax.optimization_barrier(
        (d_attended_own, out_terms, fc2_own)
    )
    g_fc2 = turn(fc2_own)
    d_query_own, d_before, d_after, d_pair_own = attention_back(
        query_own,
        pair_own,
        pair_before,
        pair_after,
        d_attended_own,
        attended_own,
        lo,
        hi,
        qid,
        kid,
        logsum,
    )
    d_before, d_after, g_fc2 = lax.optimization_barrier((d_before, d_after, g_fc2))
    d_query_came = exchange(d_query_own.reshape(bunch, tok_rows, half_width))
    from_later = stretch_shift(d_before, -1).astype(f32)
    from_earlier = stretch_shift(d_after, 1).astype(f32)
    rest = jnp.zeros((stretch_rows - halo, 2 * half_width), f32)
    d_pair_own = (
        d_pair_own
        + jnp.concatenate([rest, from_later], axis=0)
        + jnp.concatenate([from_earlier, rest], axis=0)
    )
    d_pair_came = exchange(d_pair_own.astype(bf16).reshape(bunch, tok_rows, 2 * half_width))
    d_pair_came, down_terms, fc1_text = lax.optimization_barrier(
        (d_pair_came, down_terms, fc1_text)
    )
    fc1_text = scatter_weight(fc1_text)
    down_proj = reduce_rep(split_group(down_terms))
    output = mid + gate_two * down_proj
    d_gate_two = back_out * down_proj
    d_qkv, gain_sums = norm_back(spots, d_query_came, d_pair_came, qk_pre, image, gains)
    d_act_one = reduce_rep(split_group(backward_product(spots, d_qkv, qkv_weights, image)))
    qkv_terms = gradient(spots, act_one_group, d_qkv, image, qkv_weights.shape)
    d_in_norm, d_shift_one, d_scale_one = jax.vjp(layer_modulate, stream_in, shift_one, scale_one)[
        1
    ](d_act_one)
    d_tokens = d_mid + d_in_norm
    d_mod_tok = jnp.concatenate(
        [d_shift_one, d_scale_one, d_gate_one, d_shift_two, d_scale_two, d_gate_two], axis=1
    )
    image_flag = image_col[:, 0]
    second_flag = is_second[:, 0]
    selector = jnp.stack(
        [
            ~second_flag & image_flag,
            ~second_flag & ~image_flag,
            second_flag & image_flag,
            second_flag & ~image_flag,
        ],
        axis=1,
    ).astype(f32)
    pooled = jnp.einsum("tp,te->pe", selector, d_mod_tok, precision=lax.Precision.HIGHEST)
    gain_sums = jnp.sum(gain_sums.reshape(2, 2, part_width // HD, HD), axis=2)
    gain_part = jnp.concatenate([gain_sums[0], gain_sums[1]], axis=1)
    gain_rows = jnp.concatenate([gain_part, jnp.zeros_like(gain_part)], axis=0)
    leaving = jnp.stack(
        [
            jnp.concatenate([pooled[:, r * mod_cols : (r + 1) * mod_cols], gain_rows], axis=1)
            for r in range(reps)
        ]
    )
    up_fc2 = adam_step(w_fc2, m_fc2, v_fc2, g_fc2.astype(f32), rate_fc2)
    qkv_terms, out_terms, fc1_image, up_fc2, leaving = lax.optimization_barrier(
        (qkv_terms, out_terms, fc1_image, up_fc2, leaving)
    )
    leaving = jnp.broadcast_to(leaving[:, None], (reps, shards, *leaving.shape[1:]))
    came = lax.all_to_all(
        leaving.reshape(device_count, *leaving.shape[2:]), ("rep", "shard"), 0, 0, tiled=True
    )
    out_terms = out_terms.reshape(shards, 2, -1, out_terms.shape[-1])
    g_qkv_group, g_out = ring_scatter(qkv_terms, out_terms)
    g_qkv_group, g_out, came, fc1_text = lax.optimization_barrier(
        (g_qkv_group, g_out, came, fc1_text)
    )
    g_out = turn(g_out)
    g_fc1 = jnp.concatenate([fc1_image, fc1_text], axis=0)
    g_parts = [
        g_qkv_group[:, :, t * part_width : (t + 1) * part_width] for t in range(3)
    ]
    g_parts = rolled(g_parts, (3 - turns) % 3)
    g_qkv = jnp.concatenate(
        [over_rep(g_parts[i], lambda d, i=i: (3 * (d - i)) % reps) for i in range(3)], axis=2
    )

    g_gains = jnp.sum(came[:, :2, mod_cols:], axis=0)
    came = came[:, :, :mod_cols].reshape(2 * device_count, 2, mod_cols)
    seqs = jnp.stack([firsts, seconds], axis=1).reshape(-1)
    hot_seq = (seqs[:, None] == jnp.arange(slot_count, dtype=jnp.int32)).astype(bf16)
    cond_seq = jnp.dot(hot_seq, cond_rows, preferred_element_type=f32)
    g_mod = jnp.stack(
        [
            lax.dot_general(
                cond_seq,
                came[:, s],
                (((0,), (0,)), ((), ())),
                precision=lax.Precision.HIGHEST,
                preferred_element_type=f32,
            )
            for s in range(2)
        ]
    )
    up_mod = adam_step(w_mod, m_mod, v_mod, g_mod, rate_mod)
    up_qkv = adam_step(w_qkv, m_qkv, v_qkv, g_qkv.astype(f32), rate_qkv)
    up_out = adam_step(w_out, m_out, v_out, g_out.astype(f32), rate_out)
    up_fc1 = adam_step(w_fc1, m_fc1, v_fc1, g_fc1.astype(f32), rate_fc1)
    up_gains = adam_step(gains, m_gains, v_gains, g_gains, rate_gains)
    return (
        output.astype(bf16),
        d_tokens,
        *up_mod,
        *up_qkv,
        *up_out,
        *up_fc1,
        *up_fc2,
        *up_gains[:3],
    )


def solution(mesh):
    rows = P(("rep", "shard"), None)
    held = P(None, "shard", "rep")
    return jax.shard_map(
        body,
        mesh=mesh,
        in_specs=(rows, rows, P(), P(), P(("rep", "shard")), *([held] * 15), P(), P(), P()),
        out_specs=(rows, rows, *([held] * 20), P(), P(), P()),
        check_vma=False,
    )
```
